32 devices in a mesh: dp: 16 (over z, x, core), blk: 2 (over y).
Axes of the slice: x: 2, y: 2, z: 4, core: 2. Of those that a mesh axis runs over, the one named last changes fastest.
Arguments:
- tokens: bfloat16 [32, 1024, 1024], P('dp', 'blk'), may hold values from -6 to 6
- cotangent: bfloat16 [32, 1024, 1024], P('dp', 'blk'), may hold values from -6 to 6
- doc_lengths: int32 [32, 4], P('dp'), may hold values from 0 to 1024, as said below
- norm1_gain: float32 [1024], replicated, may hold values from 0.5 to 1.5
- norm1_shift: float32 [1024], replicated, may hold values from -1.75 to 1.75
- qkv_weight: bfloat16 [1024, 3072], replicated, may hold values from -0.1875 to 0.1875
- query_bias: float32 [1024], replicated, may hold values from -3 to 3
- value_bias: float32 [1024], replicated, may hold values from -3 to 3
- head_scales: float32 [16], replicated, may hold values from 0.5 to 1.5
- out_weight: bfloat16 [1024, 1024], replicated, may hold values from -0.1875 to 0.1875
- out_bias: float32 [1024], replicated, may hold values from -3 to 3
- attn_gain: float32 [1024], replicated, may hold values from 0.5 to 1.5
- attn_shift: float32 [1024], replicated, may hold values from -1.75 to 1.75
- norm2_gain: float32 [1024], replicated, may hold values from 0.5 to 1.5
- norm2_shift: float32 [1024], replicated, may hold values from -1.75 to 1.75
- fc1_weight: bfloat16 [1024, 4096], replicated, may hold values from -0.1875 to 0.1875
- fc1_bias: float32 [4096], replicated, may hold values from -3 to 3
- mid_gain: float32 [4096], replicated, may hold values from 0.5 to 1.5
- mid_shift: float32 [4096], replicated, may hold values from -1.75 to 1.75
- fc2_weight: bfloat16 [4096, 1024], replicated, may hold values from -0.09375 to 0.09375
- fc2_bias: float32 [1024], replicated, may hold values from -1.75 to 1.75
Outputs:
- output: float32 [32, 1024, 1024], P('dp', 'blk')
- tokens_grad: float32 [32, 1024, 1024], P('dp', 'blk')
- norm1_gain_grad: float32 [1024], replicated
- norm1_shift_grad: float32 [1024], replicated
- qkv_weight_grad: float32 [1024, 3072], P('dp', 'blk')
- query_bias_grad: float32 [1024], replicated
- value_bias_grad: float32 [1024], replicated
- head_scales_grad: float32 [16], replicated
- out_weight_grad: float32 [1024, 1024], P('dp', 'blk')
- out_bias_grad: float32 [1024], replicated
- attn_gain_grad: float32 [1024], replicated
- attn_shift_grad: float32 [1024], replicated
- norm2_gain_grad: float32 [1024], replicated
- norm2_shift_grad: float32 [1024], replicated
- fc1_weight_grad: float32 [1024, 4096], P('dp', 'blk')
- fc1_bias_grad: float32 [4096], replicated
- mid_gain_grad: float32 [4096], replicated
- mid_shift_grad: float32 [4096], replicated
- fc2_weight_grad: float32 [4096, 1024], P('dp', 'blk')
- fc2_bias_grad: float32 [1024], replicated
The draws below stay inside these ranges and needn't reach their ends.
Inputs may be any that keep to these rules, and one draw needn't show every extreme that they name: `doc_lengths`: each row's 4 entries are document lengths in order (0 for an empty slot), each 0, 256, 512 or 1024, summing to 1024. In each aligned block of 2 rows (the rows of one index of dp) one row is a single document of 1024 positions.
All inputs are finite; a program needn't handle non-finite values.
Results may differ from the reference program's by a relative error of at most 0.02.
Values may be sent and summed in bfloat16 or wider, within the bound.
A program may use at most 320 MiB of HBM per device.

```python
import jax
import jax.numpy as jnp
from jax import lax

D = 1024
H = 16
HD = 64
FF = 4096
BATCH = 2
ROW = 1024
ROWS = 32


def draw_doc_lengths(key, part):
    quarter = ROW // 4
    table = jnp.array([[4, 0, 0, 0], [2, 2, 0, 0], [2, 1, 1, 0], [1, 1, 1, 1]], dtype=jnp.int32) * quarter
    key_kind, key_whole, key_order = jax.random.split(jax.random.fold_in(key, 11), 3)
    kinds = jax.random.randint(key_kind, (ROWS,), 0, 4, dtype=jnp.int32)
    chosen = jax.random.randint(key_whole, (ROWS // BATCH,), 0, BATCH, dtype=jnp.int32)
    slots = jnp.arange(ROWS, dtype=jnp.int32) % BATCH
    whole_row = slots == jnp.repeat(chosen, BATCH)
    kinds = jnp.where(whole_row, 0, kinds)
    layouts = table[kinds]
    row_keys = jax.random.split(key_order, ROWS)
    orders = jax.vmap(lambda row_key: jax.random.permutation(row_key, 4))(row_keys)
    return jnp.take_along_axis(layouts, orders.astype(jnp.int32), axis=1)


def shard_levels(own_key, extent, pieces, low, high):
    def one(position, parts):
        heights = jax.random.uniform(jax.random.fold_in(jax.random.fold_in(own_key, 6), position), (parts,), jnp.float32, low / len(pieces), high / len(pieces))
        return jnp.repeat(jnp.exp(heights), extent[position] // parts).reshape((-1,) + (1,) * (len(extent) - position - 1))

    level = one(*pieces[0])
    for cut in pieces[1:]:
        level = level * one(*cut)
    return level


def scatter_about(own_key, dims, width, most, cuts=(), kind=jnp.bfloat16):
    values = width * jax.random.normal(own_key, dims, jnp.float32)
    if cuts:
        values = values * shard_levels(own_key, dims, cuts, -0.22, 0.18)
    return jnp.clip(values, -most, most).astype(kind)


def setup_inputs(seed: int = 0) -> dict:
    keys = jax.random.split(jax.random.key(seed), 22)
    return {
        "tokens": scatter_about(keys[0], (ROWS, ROW, D), 1.0, 6.0, ((0, 16), (1, 2))),
        "cotangent": scatter_about(keys[1], (ROWS, ROW, D), 1.0, 6.0, ((0, 16), (1, 2))),
        "doc_lengths": draw_doc_lengths(jax.random.fold_in(keys[21], 71), 0),
        "norm1_gain": jnp.clip(1.0 + 0.1 * jax.random.normal(keys[3], (D,), jnp.float32), 0.5, 1.5),
        "norm1_shift": scatter_about(keys[4], (D,), 0.3, 1.75, (), jnp.float32),
        "qkv_weight": scatter_about(keys[5], (D, 3 * D), D ** -0.5, 0.1875),
        "query_bias": scatter_about(keys[6], (D,), 0.5, 3.0, (), jnp.float32),
        "value_bias": scatter_about(keys[7], (D,), 0.5, 3.0, (), jnp.float32),
        "head_scales": jnp.clip(jax.random.uniform(keys[8], (H,), jnp.float32, 0.5, 1.5), 0.5, 1.5),
        "out_weight": scatter_about(keys[9], (D, D), D ** -0.5, 0.1875),
        "out_bias": scatter_about(keys[10], (D,), 0.5, 3.0, (), jnp.float32),
        "attn_gain": jnp.clip(1.0 + 0.1 * jax.random.normal(keys[11], (D,), jnp.float32), 0.5, 1.5),
        "attn_shift": scatter_about(keys[12], (D,), 0.3, 1.75, (), jnp.float32),
        "norm2_gain": jnp.clip(1.0 + 0.1 * jax.random.normal(keys[13], (D,), jnp.float32), 0.5, 1.5),
        "norm2_shift": scatter_about(keys[14], (D,), 0.3, 1.75, (), jnp.float32),
        "fc1_weight": scatter_about(keys[15], (D, FF), D ** -0.5, 0.1875),
        "fc1_bias": scatter_about(keys[16], (FF,), 0.5, 3.0, (), jnp.float32),
        "mid_gain": jnp.clip(1.0 + 0.1 * jax.random.normal(keys[17], (FF,), jnp.float32), 0.5, 1.5),
        "mid_shift": scatter_about(keys[18], (FF,), 0.3, 1.75, (), jnp.float32),
        "fc2_weight": scatter_about(keys[19], (FF, D), FF ** -0.5, 0.09375),
        "fc2_bias": scatter_about(keys[20], (D,), 0.3, 1.75, (), jnp.float32),
    }


eps = 1e-05
masked_score = -1e+30
highest = lax.Precision.HIGHEST

@jax.custom_vjp
def low(v):
    return lax.optimization_barrier(v.astype(jnp.bfloat16)).astype(jnp.float32)

@jax.custom_vjp
def low_back(v):
    return v

def low_keep(v):
    return (low(v), None)

def low_pass(kept, grad):
    return (grad,)

def back_keep(v):
    return (v, None)

def back_low(kept, grad):
    return (low(grad),)
low.defvjp(low_keep, low_pass)
low_back.defvjp(back_keep, back_low)

def layer_norm(values, gain, shift):
    average = lax.optimization_barrier(jnp.mean(values, axis=-1, keepdims=True))
    centered = values - average
    inverse = lax.rsqrt(lax.optimization_barrier(jnp.mean(centered * centered, axis=-1, keepdims=True)) + eps)
    return centered * inverse * gain + shift

def forward_row(params, inputs, starts):
    norm1_gain, norm1_shift, qkv_weight, query_bias, value_bias, head_scales, out_weight, out_bias, attn_gain, attn_shift, norm2_gain, norm2_shift, fc1_weight, fc1_bias, mid_gain, mid_shift, fc2_weight, fc2_bias = params
    attn_in = low(layer_norm(inputs, norm1_gain, norm1_shift))
    projected = jnp.dot(attn_in, qkv_weight, precision=highest)
    queries = low(low_back(projected[:, :D] + query_bias)).reshape(ROW, H, HD)
    keys_all = low(low_back(projected[:, D:2 * D])).reshape(ROW, H, HD)
    values_all = low(low_back(projected[:, 2 * D:] + value_bias)).reshape(ROW, H, HD)
    key_pos = jnp.arange(ROW, dtype=jnp.int32)
    block_len = min(512, ROW)

    def one_block(index):
        offset = (index * block_len).astype(jnp.int32)
        query_block = lax.dynamic_slice_in_dim(queries, offset, block_len, 0)
        start_block = lax.dynamic_slice_in_dim(starts, offset, block_len, 0)
        query_pos = offset + jnp.arange(block_len, dtype=jnp.int32)
        scores = jnp.einsum('qhd,khd->hqk', query_block, keys_all, precision=highest) * HD ** (-0.5)
        scores = low_back(scores)
        allowed = (key_pos[None, :] <= query_pos[:, None]) & (key_pos[None, :] >= start_block[:, None])
        scores = jnp.where(allowed[None], scores, masked_score)
        attn_probs = low(jax.nn.softmax(scores, axis=-1))
        return jnp.einsum('hqk,khd->qhd', attn_probs, values_all, precision=highest)
    attended = lax.map(jax.checkpoint(one_block), jnp.arange(ROW // block_len, dtype=jnp.int32))
    attended = low_back(attended.reshape(ROW, H, HD))
    heads_out = low(attended * head_scales[:, None]).reshape(ROW, D)
    projection = low_back(jnp.dot(heads_out, out_weight, precision=highest) + out_bias)
    middle = inputs + layer_norm(projection, attn_gain, attn_shift)
    ffn_in = low(layer_norm(middle, norm2_gain, norm2_shift))
    hidden = low_back(jnp.dot(ffn_in, fc1_weight, precision=highest) + fc1_bias)
    mid_out = low(layer_norm(jax.nn.gelu(hidden, approximate=False), mid_gain, mid_shift))
    return middle + low_back(jnp.dot(mid_out, fc2_weight, precision=highest) + fc2_bias)

def reference(tokens, cotangent, doc_lengths, norm1_gain, norm1_shift, qkv_weight, query_bias, value_bias, head_scales, out_weight, out_bias, attn_gain, attn_shift, norm2_gain, norm2_shift, fc1_weight, fc1_bias, mid_gain, mid_shift, fc2_weight, fc2_bias):
    params = tuple((p.astype(jnp.float32) for p in (norm1_gain, norm1_shift, qkv_weight, query_bias, value_bias, head_scales, out_weight, out_bias, attn_gain, attn_shift, norm2_gain, norm2_shift, fc1_weight, fc1_bias, mid_gain, mid_shift, fc2_weight, fc2_bias)))
    doc_ends = jnp.cumsum(doc_lengths, axis=1, dtype=jnp.int32)
    positions = jnp.arange(ROW, dtype=jnp.int32)
    starts = lax.optimization_barrier(jnp.max(jnp.where(doc_ends[:, None, :] <= positions[None, :, None], doc_ends[:, None, :], 0), axis=2)).astype(jnp.int32)

    def step(totals, item):
        token_row, grad_row, start_row = item

        def run_row(inputs, weights):
            return forward_row(weights, inputs, start_row)
        out_row, backward = jax.vjp(run_row, token_row.astype(jnp.float32), params)
        grad_inputs, grad_params = backward(grad_row.astype(jnp.float32))
        return (jax.tree.map(jnp.add, totals, grad_params), (out_row, grad_inputs))
    zero_grads = jax.tree.map(jnp.zeros_like, params)
    totals, (outputs, input_grads) = lax.scan(step, zero_grads, (tokens, cotangent, starts))
    return (outputs, input_grads, totals[0], totals[1], totals[2], totals[3], totals[4], totals[5], totals[6], totals[7], totals[8], totals[9], totals[10], totals[11], totals[12], totals[13], totals[14], totals[15], totals[16], totals[17])
```

```python
from functools import partial

import jax
import jax.numpy as jnp
from jax import lax
from jax.experimental import pallas as pl
from jax.experimental.pallas import tpu as pltpu
from jax.sharding import PartitionSpec as P

f32 = jnp.float32
bf16 = jnp.bfloat16
eps = 1e-05
masked_score = -1e30
LANES = 128
NT = (((1,), (1,)), ((), ()))
NN = (((1,), (0,)), ((), ()))
TN = (((0,), (0,)), ((), ()))


def mm(a, b, dims=NN):
    return lax.dot_general(a, b, dims, preferred_element_type=f32)


def fold(x):
    total = x[:, :LANES]
    for c in range(LANES, x.shape[1], LANES):
        total = total + x[:, c : c + LANES]
    return total


def row_mean(x):
    return jnp.sum(fold(x), axis=1, keepdims=True) * (1.0 / x.shape[1])


def row_sum(x):
    return jnp.sum(x, axis=0, keepdims=True)


def norm_unit(v):
    centered = v - row_mean(v)
    inverse = lax.rsqrt(row_mean(centered * centered) + eps)
    return centered * inverse, inverse


def norm_back(grad_y, unit, inverse, gain):
    e = grad_y * gain
    return inverse * (e - row_mean(e) - unit * row_mean(e * unit))


def params(mib=None, **more):
    return pltpu.CompilerParams(vmem_limit_bytes=(mib or 60) * 2**20, **more)


def whole(shape):
    return pl.BlockSpec(shape, lambda *_: (0,) * len(shape), pipeline_mode=pl.Buffered(1))


def qkv_body(scale, tok, gain, shift, w, qb, vb, *refs):
    attn_in, qkv = refs[-2:]
    unit, _ = norm_unit(tok[...].astype(f32))
    x = (unit * gain[...] + shift[...]).astype(bf16)
    attn_in[...] = x
    d = x.shape[1]
    q = (mm(x, w[:, :d]) + qb[...]).astype(bf16)
    qkv[:, :d] = (q.astype(f32) * scale).astype(bf16)
    qkv[:, d : 2 * d] = mm(x, w[:, d : 2 * d]).astype(bf16)
    qkv[:, 2 * d :] = (mm(x, w[:, 2 * d :]) + vb[...]).astype(bf16)


def project_qkv(tok, gain, shift, w, qb, vb, scale, slot, total, earlier=(), tb=256):
    n, d = tok.shape
    first = slot * (n // tb)
    held = pl.BlockSpec(memory_space=pl.ANY)
    return pl.pallas_call(
        partial(qkv_body, scale),
        name="project_qkv",
        grid=(n // tb,),
        in_specs=[pl.BlockSpec((tb, d), lambda i: (i, 0))]
        + [whole(a.shape) for a in (gain, shift, w, qb, vb)]
        + [held] * len(earlier),
        out_specs=[
            pl.BlockSpec((tb, d), lambda i: (first + i, 0)),
            pl.BlockSpec((tb, 3 * d), lambda i: (first + i, 0)),
        ],
        out_shape=[
            jax.ShapeDtypeStruct((total, d), bf16),
            jax.ShapeDtypeStruct((total, 3 * d), bf16),
        ],
        input_output_aliases={6 + k: k for k in range(len(earlier))},
        compiler_params=params(),
        cost_estimate=pl.CostEstimate(
            flops=2 * n * d * 3 * d, bytes_accessed=6 * d * d + 10 * n * d, transcendentals=n
        ),
    )(tok, gain, shift, w, qb, vb, *earlier)


def half_slot(own, half):
    return own if half == 0 else 1 - own


def pick(ref, own, block, size):
    half, sub = divmod(block, 2)
    return ref[half_slot(own, half), sub * size : (sub + 1) * size, :]


def head_mask(size):
    return lax.broadcasted_iota(jnp.int32, (size, LANES), 1) < LANES // 2


def block_penalty(tab, i, j):
    return jnp.where(tab[1 + 4 * i + j] > 0, 0.0, masked_score).astype(f32)


def attend_body(tab, q, k, v, head_scale, heads_out, lse):
    size = q.shape[1] // 2
    own = tab[0]
    low = head_mask(size)
    causal = lax.broadcasted_iota(jnp.int32, (size, size), 0) >= lax.broadcasted_iota(
        jnp.int32, (size, size), 1
    )
    lane = lax.broadcasted_iota(jnp.int32, (size, LANES), 1)
    for i in range(4):
        qi = pick(q, own, i, size)
        outs = []
        logs = []
        for h in range(2):
            qm = jnp.where(low if h == 0 else ~low, qi, 0).astype(bf16)
            parts = []
            for j in range(i + 1):
                s = mm(qm, pick(k, own, j, size), NT)
                parts.append(
                    jnp.where(causal, s, masked_score) if j == i else s + block_penalty(tab, i, j)
                )
            top = parts[0]
            for s in parts[1:]:
                top = jnp.maximum(top, s)
            top = jnp.max(top, axis=1, keepdims=True)
            total = None
            out = None
            for j, s in enumerate(parts):
                p = jnp.exp(s - top)
                part_sum = fold(p)
                total = part_sum if total is None else total + part_sum
                part_out = mm(p.astype(bf16), pick(v, own, j, size))
                out = part_out if out is None else out + part_out
            total = jnp.sum(total, axis=1, keepdims=True)
            outs.append(out * (1.0 / total))
            logs.append(top + jnp.log(total))
        both = jnp.where(low, outs[0], outs[1]) * head_scale[...]
        half, sub = divmod(i, 2)
        heads_out[half_slot(own, half), sub * size : (sub + 1) * size, :] = both.astype(bf16)
        columns = jnp.where(lane == 0, logs[0], logs[1])
        lse[0, i] = jnp.transpose(columns)[:8]


def attend(tab, qkv, head_scale_row):
    _, half_len, wide = qkv.shape
    d = wide // 3
    pairs = d // LANES
    size = half_len // 2

    def lanes(first):
        return pl.BlockSpec((2, half_len, LANES), lambda p, t: (0, 0, first + p))

    flops = 16 * half_len * half_len * pairs * LANES
    return pl.pallas_call(
        attend_body,
        name="attend",
        grid_spec=pltpu.PrefetchScalarGridSpec(
            num_scalar_prefetch=1,
            grid=(pairs,),
            in_specs=[
                lanes(0),
                lanes(pairs),
                lanes(2 * pairs),
                pl.BlockSpec((1, LANES), lambda p, t: (0, p)),
            ],
            out_specs=[
                lanes(0),
                pl.BlockSpec((1, 4, 8, size), lambda p, t: (p, 0, 0, 0)),
            ],
        ),
        out_shape=[
            jax.ShapeDtypeStruct((2, half_len, d), bf16),
            jax.ShapeDtypeStruct((pairs, 4, 8, size), f32),
        ],
        compiler_params=params(),
        cost_estimate=pl.CostEstimate(
            flops=flops * 4, bytes_accessed=8 * half_len * wide, transcendentals=8 * half_len * half_len * pairs
        ),
    )(tab, qkv, qkv, qkv, head_scale_row)


def attend_back_body(
    scale, tab, q, k, v, heads_out, d_out, inv_scale, lse, dq, dk, dv, dots, dq_acc
):
    size = q.shape[1] // 2
    own = tab[0]
    low = head_mask(size)
    masks = (low, ~low)
    causal = lax.broadcasted_iota(jnp.int32, (size, size), 0) <= lax.broadcasted_iota(
        jnp.int32, (size, size), 1
    )
    pick_rows = (
        lax.broadcasted_iota(jnp.int32, (8, LANES), 1) // (LANES // 2)
        == lax.broadcasted_iota(jnp.int32, (8, LANES), 0)
    ).astype(f32)
    qs, gs, deltas = {}, {}, []
    for i in range(4):
        qi = pick(q, own, i, size)
        gi = pick(d_out, own, i, size)
        for h in range(2):
            qs[i, h] = jnp.where(masks[h], qi, 0).astype(bf16)
            gs[i, h] = jnp.where(masks[h], gi, 0).astype(bf16)
        product = gi.astype(f32) * pick(heads_out, own, i, size).astype(f32) * inv_scale[...]
        delta = lax.dot_general(
            pick_rows, product, NT, preferred_element_type=f32, precision=lax.Precision.HIGHEST
        )
        deltas.append(delta)
        dots[0, i] = delta
        dq_acc[i] = jnp.zeros((size, LANES), f32)
    for j in range(4):
        kj = pick(k, own, j, size)
        vj = pick(v, own, j, size)
        dk_j = jnp.zeros((size, LANES), f32)
        dv_j = jnp.zeros((size, LANES), f32)
        for h in range(2):
            km = jnp.where(masks[h], kj, 0).astype(bf16)
            for i in range(j, 4):
                logs = lse[0, i, h : h + 1, :]
                if i > j:
                    logs = logs - block_penalty(tab, i, j)
                s = mm(kj, qs[i, h], NT)
                if i == j:
                    s = jnp.where(causal, s, masked_score)
                p = jnp.exp(s - logs)
                gp = mm(vj, gs[i, h], NT)
                ds = (p * (gp - deltas[i][h : h + 1, :])).astype(bf16)
                dv_j = dv_j + mm(p.astype(bf16), gs[i, h])
                dk_j = dk_j + mm(ds, qs[i, h])
                dq_acc[i] += mm(ds, km, TN)
        half, sub = divmod(j, 2)
        where = (half_slot(own, half), slice(sub * size, (sub + 1) * size))
        dk[where[0], where[1], :] = dk_j.astype(bf16)
        dv[where[0], where[1], :] = dv_j.astype(bf16)
    for i in range(4):
        half, sub = divmod(i, 2)
        dq[half_slot(own, half), sub * size : (sub + 1) * size, :] = (dq_acc[i] * scale).astype(bf16)


def attend_back(tab, qkv, heads_out, d_out, inv_scale_row, lse, scale):
    _, half_len, wide = qkv.shape
    d = wide // 3
    pairs = d // LANES
    size = half_len // 2

    def lanes(first):
        return pl.BlockSpec((2, half_len, LANES), lambda p, t: (0, 0, first + p))

    small = pl.BlockSpec((1, 4, 8, size), lambda p, t: (p, 0, 0, 0))
    flops = 16 * half_len * half_len * pairs * LANES
    return pl.pallas_call(
        partial(attend_back_body, scale),
        name="attend_back",
        grid_spec=pltpu.PrefetchScalarGridSpec(
            num_scalar_prefetch=1,
            grid=(pairs,),
            in_specs=[
                lanes(0),
                lanes(pairs),
                lanes(2 * pairs),
                lanes(0),
                lanes(0),
                pl.BlockSpec((1, LANES), lambda p, t: (0, p)),
                small,
            ],
            out_specs=[lanes(0), lanes(0), lanes(0), small],
            scratch_shapes=[pltpu.VMEM((4, size, LANES), f32)],
        ),
        out_shape=[jax.ShapeDtypeStruct((2, half_len, d), bf16)] * 3
        + [jax.ShapeDtypeStruct((pairs, 4, 8, size), f32)],
        compiler_params=params(),
        cost_estimate=pl.CostEstimate(
            flops=flops * 10, bytes_accessed=16 * half_len * wide, transcendentals=8 * half_len * half_len * pairs
        ),
    )(tab, qkv, qkv, qkv, heads_out, d_out, inv_scale_row, lse)


def gelu_parts(v):
    a = jnp.abs(v)
    t = 1.0 / (1.0 + (0.3275911 * 0.7071067811865476) * a)
    bell = jnp.exp(v * v * -0.5)
    poly = ((((1.061405429 * t - 1.453152027) * t + 1.421413741) * t - 0.284496736) * t + 0.254829592) * t
    tail = (0.5 * poly) * bell
    cdf = jnp.where(v < 0, tail, 1.0 - tail)
    return v * cdf, cdf + v * (bell * 0.3989422804014327)


def middle_body(
    ho, tok, cot, out_w, w1, w2, vec, vec4,
    output, grad_middle, ffn_in, mid_out, grad_hidden, grad_proj, d_out, sums, sums4,
    act, slope, back,
):
    step = pl.program_id(0)
    d = ho.shape[1]
    ff = w1.shape[1]
    fc = 512
    chunks = ff // fc

    @pl.when(step == 0)
    def _():
        sums[...] = jnp.zeros_like(sums)
        sums4[...] = jnp.zeros_like(sums4)

    def v(r):
        return vec[r : r + 1, :]

    tokens = tok[...].astype(f32)
    projection = mm(ho[...], out_w[...]) + v(0)
    unit_attn, inverse_attn = norm_unit(projection)
    middle = tokens + (unit_attn * v(1) + v(2))
    unit_two, inverse_two = norm_unit(middle)
    x = (unit_two * v(3) + v(4)).astype(bf16)
    ffn_in[...] = x
    g = cot[...]
    tb = x.shape[0]
    zero = jnp.zeros((tb, LANES), f32)

    def span(c):
        return pl.ds(pl.multiple_of(c * fc, fc), fc)

    def one(c, total):
        s = span(c)
        h = mm(x, w1[:, s]) + vec4[0:1, s]
        back[:, s] = mm(g, w2[s, :], NT)
        a, b = gelu_parts(h)
        act[:, s] = a
        slope[:, s] = b
        return total + fold(a)

    total = lax.fori_loop(0, chunks, one, zero)
    mean = jnp.sum(total, axis=1, keepdims=True) * (1.0 / ff)

    def two(c, total):
        a = act[:, span(c)] - mean
        return total + fold(a * a)

    total = lax.fori_loop(0, chunks, two, zero)
    inverse = lax.rsqrt(jnp.sum(total, axis=1, keepdims=True) * (1.0 / ff) + eps)

    def three(c, carry):
        acc, sum_e, sum_eu = carry
        s = span(c)
        u = (act[:, s] - mean) * inverse
        act[:, s] = u
        gain = vec4[1:2, s]
        m = (u * gain + vec4[2:3, s]).astype(bf16)
        mid_out[:, s] = m
        gm = back[:, s]
        sums4[1:2, s] += row_sum(gm * u)
        sums4[2:3, s] += row_sum(gm)
        e = gm * gain
        return acc + mm(m, w2[s, :]), sum_e + fold(e), sum_eu + fold(e * u)

    acc, sum_e, sum_eu = lax.fori_loop(
        0, chunks, three, (jnp.zeros((tb, d), f32), zero, zero)
    )
    output[...] = middle + acc + v(5)
    mean_e = jnp.sum(sum_e, axis=1, keepdims=True) * (1.0 / ff)
    mean_eu = jnp.sum(sum_eu, axis=1, keepdims=True) * (1.0 / ff)

    def four(c, acc):
        s = span(c)
        e = back[:, s] * vec4[1:2, s]
        grad_act = inverse * (e - mean_e - act[:, s] * mean_eu)
        gh = (grad_act * slope[:, s]).astype(bf16)
        grad_hidden[:, s] = gh
        sums4[0:1, s] += row_sum(gh.astype(f32))
        return acc + mm(gh, w1[:, s], NT)

    grad_ffn_in = lax.fori_loop(0, chunks, four, jnp.zeros((tb, d), f32))
    gout = g.astype(f32)
    sums[5:6, :] += row_sum(gout)
    sums[3:4, :] += row_sum(grad_ffn_in * unit_two)
    sums[4:5, :] += row_sum(grad_ffn_in)
    gmid = gout + norm_back(grad_ffn_in, unit_two, inverse_two, v(3))
    grad_middle[...] = gmid
    sums[1:2, :] += row_sum(gmid * unit_attn)
    sums[2:3, :] += row_sum(gmid)
    gp = norm_back(gmid, unit_attn, inverse_attn, v(1)).astype(bf16)
    grad_proj[...] = gp
    sums[0:1, :] += row_sum(gp.astype(f32))
    d_out[...] = (mm(gp, out_w[...], NT) * v(6)).astype(bf16)


def middle_pass(ho, tok, cot, out_w, w1, w2, vec, vec4, tb=256):
    n, d = ho.shape
    ff = w1.shape[1]
    rows = pl.BlockSpec((tb, d), lambda i: (i, 0))
    wide = pl.BlockSpec((tb, ff), lambda i: (i, 0))
    return pl.pallas_call(
        middle_body,
        name="middle_pass",
        grid=(n // tb,),
        in_specs=[rows, rows, rows] + [whole(a.shape) for a in (out_w, w1, w2, vec, vec4)],
        out_specs=[rows, rows, rows, wide, wide, rows, rows, whole((8, d)), whole((8, ff))],
        out_shape=[
            jax.ShapeDtypeStruct((n, d), f32),
            jax.ShapeDtypeStruct((n, d), f32),
            jax.ShapeDtypeStruct((n, d), bf16),
            jax.ShapeDtypeStruct((n, ff), bf16),
            jax.ShapeDtypeStruct((n, ff), bf16),
            jax.ShapeDtypeStruct((n, d), bf16),
            jax.ShapeDtypeStruct((n, d), bf16),
            jax.ShapeDtypeStruct((8, d), f32),
            jax.ShapeDtypeStruct((8, ff), f32),
        ],
        scratch_shapes=[pltpu.VMEM((tb, ff), f32)] * 3,
        compiler_params=params(),
        cost_estimate=pl.CostEstimate(
            flops=8 * n * d * ff + 4 * n * d * d,
            bytes_accessed=4 * d * ff + 2 * d * d + 4 * n * ff + 20 * n * d,
            transcendentals=2 * n * ff,
        ),
    )(ho, tok, cot, out_w, w1, w2, vec, vec4)


def first_back_body(dq, dk, dv, w, tok, grad_middle, gain, tokens_grad, sums):
    @pl.when(pl.program_id(0) == 0)
    def _():
        sums[...] = jnp.zeros_like(sums)

    d = dq.shape[1]
    grad = mm(dq[...], w[:, :d], NT) + mm(dk[...], w[:, d : 2 * d], NT) + mm(dv[...], w[:, 2 * d :], NT)
    unit, inverse = norm_unit(tok[...].astype(f32))
    sums[0:1, :] += row_sum(grad * unit)
    sums[1:2, :] += row_sum(grad)
    sums[2:3, :] += row_sum(dq[...].astype(f32))
    sums[3:4, :] += row_sum(dv[...].astype(f32))
    tokens_grad[...] = grad_middle[...] + norm_back(grad, unit, inverse, gain[...])


def first_back(dq, dk, dv, w, tok, grad_middle, gain, tb=256):
    n, d = dq.shape
    rows = pl.BlockSpec((tb, d), lambda i: (i, 0))
    return pl.pallas_call(
        first_back_body,
        name="first_back",
        grid=(n // tb,),
        in_specs=[rows, rows, rows, whole(w.shape), rows, rows, whole(gain.shape)],
        out_specs=[rows, whole((8, d))],
        out_shape=[jax.ShapeDtypeStruct((n, d), f32), jax.ShapeDtypeStruct((8, d), f32)],
        compiler_params=params(),
        cost_estimate=pl.CostEstimate(
            flops=6 * n * d * d, bytes_accessed=6 * d * d + 16 * n * d, transcendentals=n
        ),
    )(dq, dk, dv, w, tok, grad_middle, gain)


def weight_grad_body(a, b, out):
    out[...] = mm(a[...], b[...], TN).astype(bf16)


def weight_grad(a, b, tm=512, tn=1024):
    t, m = a.shape
    n = b.shape[1]
    return pl.pallas_call(
        weight_grad_body,
        name="weight_grad",
        grid=(m // tm, n // tn),
        in_specs=[
            pl.BlockSpec((t, tm), lambda i, j: (0, i)),
            pl.BlockSpec((t, tn), lambda i, j: (0, j)),
        ],
        out_specs=pl.BlockSpec((tm, tn), lambda i, j: (i, j)),
        out_shape=jax.ShapeDtypeStruct((m, n), bf16),
        compiler_params=params(),
        cost_estimate=pl.CostEstimate(
            flops=2 * t * m * n, bytes_accessed=2 * (t * m + t * n + m * n), transcendentals=0
        ),
    )(a, b)


def running_sums(lengths):
    count = lengths.shape[1]
    upto = jnp.arange(count)[:, None] >= jnp.arange(count)[None, :]
    return jnp.sum(jnp.where(upto[None], lengths[:, None, :], 0), axis=2).astype(jnp.int32)


def norm_forward(values, gain, shift):
    average = jnp.mean(values, axis=-1, keepdims=True)
    centered = values - average
    inverse = lax.rsqrt(jnp.mean(centered * centered, axis=-1, keepdims=True) + eps)
    normed = centered * inverse
    return (normed * gain + shift, normed, inverse)


def norm_backward(grad_y, normed, inverse, gain):
    scaled = grad_y * gain
    grad_in = inverse * (
        scaled
        - jnp.mean(scaled, axis=-1, keepdims=True)
        - normed * jnp.mean(scaled * normed, axis=-1, keepdims=True)
    )
    return (grad_in, jnp.sum(grad_y * normed, axis=(0, 1)), jnp.sum(grad_y, axis=(0, 1)))


def local_general(
    tokens,
    cotangent,
    doc_lengths,
    norm1_gain,
    norm1_shift,
    qkv_weight,
    query_bias,
    value_bias,
    head_scales,
    out_weight,
    out_bias,
    attn_gain,
    attn_shift,
    norm2_gain,
    norm2_shift,
    fc1_weight,
    fc1_bias,
    mid_gain,
    mid_shift,
    fc2_weight,
    fc2_bias,
):
    f32 = jnp.float32
    bf16 = jnp.bfloat16
    batch_size, local_len, model_width = tokens.shape
    head_count = head_scales.shape[0]
    head_dim = model_width // head_count
    score_scale = head_dim ** (-0.5)
    row_len = local_len * lax.axis_size("blk")
    row_first = lax.axis_index("blk") * local_len
    query_pos = row_first + jnp.arange(local_len, dtype=jnp.int32)
    doc_ends = running_sums(doc_lengths)
    starts = jnp.max(
        jnp.where(doc_ends[:, None, :] <= query_pos[None, :, None], doc_ends[:, None, :], 0), axis=2
    )
    lowest = jnp.min(starts[:, 0])
    query_last = row_first + local_len - 1
    inputs = tokens.astype(f32)
    attn_norm, unit_one, inverse_one = norm_forward(inputs, norm1_gain, norm1_shift)
    attn_in = attn_norm.astype(bf16)
    projected = jnp.dot(attn_in, qkv_weight, preferred_element_type=f32)
    queries = (
        (projected[..., :model_width] + query_bias)
        .astype(bf16)
        .reshape(batch_size, local_len, head_count, head_dim)
    )
    keys_low = projected[..., model_width : 2 * model_width].astype(bf16)
    values_low = (projected[..., 2 * model_width :] + value_bias).astype(bf16)

    def block_scores(key_piece, offset):
        key_len = key_piece.shape[1]
        keys_head = key_piece.reshape(batch_size, key_len, head_count, head_dim)
        raw_scores = (
            jnp.einsum("bqhd,bkhd->bhqk", queries, keys_head, preferred_element_type=f32)
            * score_scale
        )
        key_pos = offset + jnp.arange(key_len, dtype=jnp.int32)
        allowed = (key_pos[None, None, :] <= query_pos[None, :, None]) & (
            key_pos[None, None, :] >= starts[:, :, None]
        )
        return (jnp.where(allowed[:, None], raw_scores, masked_score), keys_head)

    def is_live(offset, key_len):
        return (offset <= query_last) & (offset + key_len - 1 >= lowest)

    def attend_slab(running, key_piece, value_piece, offset):
        key_len = key_piece.shape[1]

        def attend_compute(state):
            running_max, running_sum, weighted = state
            scores, keys_head = block_scores(key_piece, offset)
            new_max = jnp.maximum(running_max, jnp.max(scores, axis=3))
            rescale = jnp.exp(running_max - new_max)
            weights = jnp.exp(scores - new_max[..., None])
            values_head = value_piece.reshape(batch_size, key_len, head_count, head_dim)
            update = jnp.einsum(
                "bhqk,bkhd->bqhd", weights.astype(bf16), values_head, preferred_element_type=f32
            )
            rescale_t = jnp.transpose(rescale, (0, 2, 1))[..., None]
            return (
                new_max,
                running_sum * rescale + jnp.sum(weights, axis=3),
                weighted * rescale_t + update,
            )

        return lax.cond(is_live(offset, key_len), attend_compute, lambda state: state, running)

    start_state = (
        jnp.full((batch_size, head_count, local_len), masked_score, f32),
        jnp.zeros((batch_size, head_count, local_len), f32),
        jnp.zeros((batch_size, local_len, head_count, head_dim), f32),
    )
    key_piece = lax.all_gather(keys_low, "blk", axis=1, tiled=True)
    value_piece = lax.all_gather(values_low, "blk", axis=1, tiled=True)
    turns = key_piece.shape[1] // local_len

    def one_turn(index, state):
        begin = index * local_len
        key_slab = lax.dynamic_slice_in_dim(key_piece, begin, local_len, 1)
        value_slab = lax.dynamic_slice_in_dim(value_piece, begin, local_len, 1)
        return attend_slab(state, key_slab, value_slab, begin)

    running_max, running_sum, weighted = lax.fori_loop(0, turns, one_turn, start_state)
    attended = weighted / jnp.transpose(running_sum, (0, 2, 1))[..., None]
    log_total = running_max + jnp.log(running_sum)
    heads_out = (
        (attended * head_scales[:, None]).reshape(batch_size, local_len, model_width).astype(bf16)
    )
    projection = jnp.dot(heads_out, out_weight, preferred_element_type=f32) + out_bias
    branch, unit_attn, inverse_attn = norm_forward(projection, attn_gain, attn_shift)
    middle = inputs + branch
    ffn_norm, unit_two, inverse_two = norm_forward(middle, norm2_gain, norm2_shift)
    ffn_in = ffn_norm.astype(bf16)
    hidden = jnp.dot(ffn_in, fc1_weight, preferred_element_type=f32) + fc1_bias
    activated, gelu_grad = jax.vjp(partial(jax.nn.gelu, approximate=False), hidden)
    mid_norm, unit_mid, inverse_mid = norm_forward(activated, mid_gain, mid_shift)
    mid_out = mid_norm.astype(bf16)
    output = middle + jnp.dot(mid_out, fc2_weight, preferred_element_type=f32) + fc2_bias
    grad_output = cotangent.astype(f32)
    fc2_weight_grad = jnp.einsum("bcf,bcd->fd", mid_out, cotangent, preferred_element_type=f32)
    fc2_bias_grad = jnp.sum(grad_output, axis=(0, 1))
    grad_mid = jnp.einsum("bcd,fd->bcf", cotangent, fc2_weight, preferred_element_type=f32)
    grad_act, mid_gain_grad, mid_shift_grad = norm_backward(
        grad_mid, unit_mid, inverse_mid, mid_gain
    )
    grad_hidden = gelu_grad(grad_act)[0].astype(bf16)
    fc1_weight_grad = jnp.einsum("bcd,bcf->df", ffn_in, grad_hidden, preferred_element_type=f32)
    fc1_bias_grad = jnp.sum(grad_hidden.astype(f32), axis=(0, 1))
    grad_ffn_in = jnp.einsum("bcf,df->bcd", grad_hidden, fc1_weight, preferred_element_type=f32)
    grad_two, norm2_gain_grad, norm2_shift_grad = norm_backward(
        grad_ffn_in, unit_two, inverse_two, norm2_gain
    )
    grad_middle = grad_output + grad_two
    grad_proj_f, attn_gain_grad, attn_shift_grad = norm_backward(
        grad_middle, unit_attn, inverse_attn, attn_gain
    )
    grad_projection = grad_proj_f.astype(bf16)
    out_weight_grad = jnp.einsum(
        "bcd,bce->de", heads_out, grad_projection, preferred_element_type=f32
    )
    out_bias_grad = jnp.sum(grad_projection.astype(f32), axis=(0, 1))
    grad_heads = jnp.einsum(
        "bce,de->bcd", grad_projection, out_weight, preferred_element_type=f32
    ).reshape(batch_size, local_len, head_count, head_dim)
    head_scales_grad = jnp.sum(grad_heads * attended, axis=(0, 1, 3))
    grad_attended = (grad_heads * head_scales[:, None]).astype(bf16)
    row_dot = jnp.transpose(jnp.sum(grad_attended.astype(f32) * attended, axis=3), (0, 2, 1))

    def back_slab(running, key_piece, value_piece, offset):
        key_len = key_piece.shape[1]

        def back_compute(state):
            grad_queries, kv_buffer = state
            scores, keys_head = block_scores(key_piece, offset)
            attn_probs = jnp.exp(scores - log_total[..., None])
            values_head = value_piece.reshape(batch_size, key_len, head_count, head_dim)
            grad_probs = jnp.einsum(
                "bqhd,bkhd->bhqk", grad_attended, values_head, preferred_element_type=f32
            )
            grad_scores = (attn_probs * (grad_probs - row_dot[..., None])).astype(bf16)
            grad_queries = (
                grad_queries
                + jnp.einsum("bhqk,bkhd->bqhd", grad_scores, keys_head, preferred_element_type=f32)
                * score_scale
            )
            grad_keys = (
                jnp.einsum("bhqk,bqhd->bkhd", grad_scores, queries, preferred_element_type=f32)
                * score_scale
            )
            grad_values = jnp.einsum(
                "bhqk,bqhd->bkhd",
                attn_probs.astype(bf16),
                grad_attended,
                preferred_element_type=f32,
            )
            addition = jnp.concatenate(
                [
                    grad_keys.reshape(batch_size, key_len, model_width),
                    grad_values.reshape(batch_size, key_len, model_width),
                ],
                axis=2,
            )
            previous = lax.dynamic_slice_in_dim(kv_buffer, offset, key_len, 1)
            return (
                grad_queries,
                lax.dynamic_update_slice_in_dim(kv_buffer, previous + addition, offset, 1),
            )

        return lax.cond(is_live(offset, key_len), back_compute, lambda state: state, running)

    back_state = (
        jnp.zeros((batch_size, local_len, head_count, head_dim), f32),
        jnp.zeros((batch_size, row_len, 2 * model_width), f32),
    )
    attend_key_piece = lax.all_gather(keys_low, "blk", axis=1, tiled=True)
    attend_value_piece = lax.all_gather(values_low, "blk", axis=1, tiled=True)
    turns = attend_key_piece.shape[1] // local_len

    def one_turn(index, state):
        begin = index * local_len
        key_slab = lax.dynamic_slice_in_dim(attend_key_piece, begin, local_len, 1)
        value_slab = lax.dynamic_slice_in_dim(attend_value_piece, begin, local_len, 1)
        return back_slab(state, key_slab, value_slab, begin)

    grad_queries, kv_buffer = lax.fori_loop(0, turns, one_turn, back_state)
    grad_kv = lax.psum_scatter(
        kv_buffer.astype(jnp.bfloat16), "blk", scatter_dimension=1, tiled=True
    ).astype(jnp.float32)
    grad_qkv = jnp.concatenate(
        [grad_queries.reshape(batch_size, local_len, model_width), grad_kv], axis=2
    ).astype(bf16)
    qkv_weight_grad = jnp.einsum("bcd,bce->de", attn_in, grad_qkv, preferred_element_type=f32)
    query_bias_grad = jnp.sum(grad_qkv[..., :model_width].astype(f32), axis=(0, 1))
    value_bias_grad = jnp.sum(grad_qkv[..., 2 * model_width :].astype(f32), axis=(0, 1))
    grad_attn_in = jnp.einsum("bce,de->bcd", grad_qkv, qkv_weight, preferred_element_type=f32)
    grad_one, norm1_gain_grad, norm1_shift_grad = norm_backward(
        grad_attn_in, unit_one, inverse_one, norm1_gain
    )
    tokens_grad = grad_middle + grad_one
    matrix_grads = (qkv_weight_grad, out_weight_grad, fc1_weight_grad, fc2_weight_grad)
    reduced = (
        lax.psum_scatter(
            matrix_grads[0].astype(jnp.bfloat16), "dp", scatter_dimension=0, tiled=True
        ).astype(jnp.float32),
        lax.psum_scatter(
            matrix_grads[1].astype(jnp.bfloat16), "dp", scatter_dimension=0, tiled=True
        ).astype(jnp.float32),
        lax.psum_scatter(
            matrix_grads[2].astype(jnp.bfloat16), "dp", scatter_dimension=0, tiled=True
        ).astype(jnp.float32),
        lax.psum_scatter(
            matrix_grads[3].astype(jnp.bfloat16), "dp", scatter_dimension=0, tiled=True
        ).astype(jnp.float32),
    )
    reduced = (
        lax.psum_scatter(
            reduced[0].astype(jnp.bfloat16), "blk", scatter_dimension=1, tiled=True
        ).astype(jnp.float32),
        lax.psum_scatter(
            reduced[1].astype(jnp.bfloat16), "blk", scatter_dimension=1, tiled=True
        ).astype(jnp.float32),
        lax.psum_scatter(
            reduced[2].astype(jnp.bfloat16), "blk", scatter_dimension=1, tiled=True
        ).astype(jnp.float32),
        lax.psum_scatter(
            reduced[3].astype(jnp.bfloat16), "blk", scatter_dimension=1, tiled=True
        ).astype(jnp.float32),
    )
    small_sums = lax.psum(
        (
            norm1_gain_grad,
            norm1_shift_grad,
            query_bias_grad,
            value_bias_grad,
            head_scales_grad,
            out_bias_grad,
            attn_gain_grad,
            attn_shift_grad,
            norm2_gain_grad,
            norm2_shift_grad,
            fc1_bias_grad,
            mid_gain_grad,
            mid_shift_grad,
            fc2_bias_grad,
        ),
        ("dp", "blk"),
    )
    return (
        output,
        tokens_grad,
        small_sums[0],
        small_sums[1],
        reduced[0],
        small_sums[2],
        small_sums[3],
        small_sums[4],
        reduced[1],
        small_sums[5],
        small_sums[6],
        small_sums[7],
        small_sums[8],
        small_sums[9],
        reduced[2],
        small_sums[10],
        small_sums[11],
        small_sums[12],
        reduced[3],
        small_sums[13],
    )


swap = ((0, 1), (1, 0))


def exchange(x):
    return lax.ppermute(x, "blk", swap)


def local_rows(
    tokens,
    cotangent,
    doc_lengths,
    norm1_gain,
    norm1_shift,
    qkv_weight,
    query_bias,
    value_bias,
    head_scales,
    out_weight,
    out_bias,
    attn_gain,
    attn_shift,
    norm2_gain,
    norm2_shift,
    fc1_weight,
    fc1_bias,
    mid_gain,
    mid_shift,
    fc2_weight,
    fc2_bias,
):
    _, half_len, d = tokens.shape
    ff = fc1_weight.shape[1]
    heads = head_scales.shape[0]
    head_dim = d // heads
    scale = head_dim**-0.5
    n = 2 * half_len
    b = lax.axis_index("blk")

    def split(x):
        return (
            lax.dynamic_index_in_dim(x, b, 0, keepdims=False),
            lax.dynamic_index_in_dim(x, 1 - b, 0, keepdims=False),
        )

    def assemble(x):
        kept = x[:half_len]
        back = exchange(x[half_len:].astype(bf16)).astype(f32)
        return jnp.where(b == 0, jnp.stack([kept, back]), jnp.stack([back, kept]))

    tok_own, tok_other = split(tokens)
    cot_own, cot_other = split(cotangent)
    tok_in = exchange(tok_other)
    cot_in = exchange(cot_other)

    lengths = lax.dynamic_slice_in_dim(doc_lengths, b, 1, 0)
    ends = running_sums(lengths)[0]
    firsts = (half_len // 2) * jnp.arange(4, dtype=jnp.int32)
    starts = jnp.max(jnp.where(ends[None, :] <= firsts[:, None], ends[None, :], 0), axis=1)
    allowed = (firsts[None, :] >= starts[:, None]).astype(jnp.int32)
    tab = jnp.concatenate([b.astype(jnp.int32)[None], allowed.reshape(16)])

    def line(x):
        return x.reshape(1, -1)

    scale_row = jnp.broadcast_to(head_scales[:, None], (heads, head_dim)).reshape(1, d)
    vec = jnp.stack(
        [out_bias, attn_gain, attn_shift, norm2_gain, norm2_shift, fc2_bias, scale_row[0], out_bias]
    )
    vec4 = jnp.stack([fc1_bias, mid_gain, mid_shift, fc1_bias])

    first_args = (line(norm1_gain), line(norm1_shift), qkv_weight, line(query_bias), line(value_bias))
    early = project_qkv(tok_own, *first_args, scale, 0, n)
    attn_in, qkv = project_qkv(tok_in, *first_args, scale, 1, n, early)
    qkv = qkv.reshape(2, half_len, 3 * d)
    tok = jnp.concatenate([tok_own, tok_in])
    cot = jnp.concatenate([cot_own, cot_in])
    heads_out, logs = attend(tab, qkv, scale_row)
    output, grad_middle, ffn_in, mid_out, grad_hidden, grad_proj, d_out, sums, sums4 = middle_pass(
        heads_out.reshape(n, d), tok, cot, out_weight, fc1_weight, fc2_weight, vec, vec4
    )
    output = assemble(output)
    fc2_weight_grad = weight_grad(mid_out, cot)
    fc1_weight_grad = weight_grad(ffn_in, grad_hidden)
    out_weight_grad = weight_grad(heads_out.reshape(n, d), grad_proj)
    dq, dk, dv, dots = attend_back(
        tab, qkv, heads_out, d_out.reshape(2, half_len, d), 1.0 / scale_row, logs, scale
    )
    dq, dk, dv = (x.reshape(n, d) for x in (dq, dk, dv))
    qkv_weight_grad = jnp.concatenate([weight_grad(attn_in, x) for x in (dq, dk, dv)], axis=1)
    tokens_grad, first_sums = first_back(
        dq, dk, dv, qkv_weight, tok, grad_middle, line(norm1_gain)
    )
    tokens_grad = assemble(tokens_grad)
    head_scales_grad = jnp.sum(dots[:, :, :2, :], axis=(1, 3)).reshape(heads) / head_scales

    def scatter(x):
        x = lax.psum_scatter(x, "dp", scatter_dimension=0, tiled=True)
        return lax.psum_scatter(x, "blk", scatter_dimension=1, tiled=True).astype(f32)

    small = lax.psum(
        (first_sums, sums, sums4, head_scales_grad),
        ("dp", "blk"),
    )
    first_sums, sums, sums4, head_scales_grad = small
    return (
        output,
        tokens_grad,
        first_sums[0],
        first_sums[1],
        scatter(qkv_weight_grad),
        first_sums[2],
        first_sums[3],
        head_scales_grad,
        scatter(out_weight_grad),
        sums[0],
        sums[1],
        sums[2],
        sums[3],
        sums[4],
        scatter(fc1_weight_grad),
        sums4[0],
        sums4[1],
        sums4[2],
        scatter(fc2_weight_grad),
        sums[5],
    )


def solution(mesh):
    rows_fit = mesh.shape["blk"] == 2
    local = local_rows if rows_fit else local_general
    placed = (
        P("dp", "blk", None),
        P("dp", "blk", None),
        P("dp", None),
        P(),
        P(),
        P(),
        P(),
        P(),
        P(),
        P(),
        P(),
        P(),
        P(),
        P(),
        P(),
        P(),
        P(),
        P(),
        P(),
        P(),
        P(),
    )
    return jax.shard_map(
        local,
        mesh=mesh,
        in_specs=placed,
        out_specs=(
            P("dp", "blk", None),
            P("dp", "blk", None),
            P(),
            P(),
            P("dp", "blk"),
            P(),
            P(),
            P(),
            P("dp", "blk"),
            P(),
            P(),
            P(),
            P(),
            P(),
            P("dp", "blk"),
            P(),
            P(),
            P(),
            P("dp", "blk"),
            P(),
        ),
        check_vma=False,
    )
```

```python
from functools import partial

import jax
import jax.numpy as jnp
from jax import lax
from jax.experimental import pallas as pl
from jax.experimental.pallas import tpu as pltpu
from jax.sharding import PartitionSpec as P

f32 = jnp.float32
bf16 = jnp.bfloat16
eps = 1e-05
masked_score = -1e30
LANES = 128
NT = (((1,), (1,)), ((), ()))
NN = (((1,), (0,)), ((), ()))
TN = (((0,), (0,)), ((), ()))


def mm(a, b, dims=NN):
    return lax.dot_general(a, b, dims, preferred_element_type=f32)


def fold(x):
    total = x[:, :LANES]
    for c in range(LANES, x.shape[1], LANES):
        total = total + x[:, c : c + LANES]
    return total


def row_mean(x):
    return jnp.sum(fold(x), axis=1, keepdims=True) * (1.0 / x.shape[1])


def row_sum(x):
    return jnp.sum(x, axis=0, keepdims=True)


def norm_unit(v):
    centered = v - row_mean(v)
    inverse = lax.rsqrt(row_mean(centered * centered) + eps)
    return centered * inverse, inverse


def norm_back(grad_y, unit, inverse, gain):
    e = grad_y * gain
    return inverse * (e - row_mean(e) - unit * row_mean(e * unit))


def params(mib=None, **more):
    return pltpu.CompilerParams(vmem_limit_bytes=(mib or 60) * 2**20, **more)


def whole(shape):
    return pl.BlockSpec(shape, lambda *_: (0,) * len(shape), pipeline_mode=pl.Buffered(1))


def core_split(x):
    low = lax.broadcasted_iota(jnp.int32, (x.shape[0], LANES), 1) < LANES // 2
    even, odd = [], []
    for c in range(0, x.shape[1], 2 * LANES):
        a = x[:, c : c + LANES].astype(f32)
        b = x[:, c + LANES : c + 2 * LANES].astype(f32)
        even.append(jnp.where(low, a, pltpu.roll(b, LANES // 2, 1)))
        odd.append(jnp.where(low, pltpu.roll(a, LANES // 2, 1), b))
    return (jnp.concatenate(y, axis=1).astype(bf16) for y in (even, odd))


def qkv_body(scale, tok, gain, shift, w, qb, vb, *refs):
    attn_in, qkv = refs[-2:]
    unit, _ = norm_unit(tok[...].astype(f32))
    x = (unit * gain[...] + shift[...]).astype(bf16)
    attn_in[0], attn_in[1] = core_split(x)
    d = x.shape[1]
    q = (mm(x, w[:, :d]) + qb[...]).astype(bf16)
    qkv[:, :d] = (q.astype(f32) * scale).astype(bf16)
    qkv[:, d : 2 * d] = mm(x, w[:, d : 2 * d]).astype(bf16)
    qkv[:, 2 * d :] = (mm(x, w[:, 2 * d :]) + vb[...]).astype(bf16)


def project_qkv(tok, gain, shift, w, qb, vb, scale, slot, total, earlier=(), tb=256):
    n, d = tok.shape
    first = slot * (n // tb)
    held = pl.BlockSpec(memory_space=pl.ANY)
    return pl.pallas_call(
        partial(qkv_body, scale),
        name="project_qkv",
        grid=(n // tb,),
        in_specs=[pl.BlockSpec((tb, d), lambda i: (i, 0))]
        + [whole(a.shape) for a in (gain, shift, w, qb, vb)]
        + [held] * len(earlier),
        out_specs=[
            pl.BlockSpec((2, tb, d // 2), lambda i: (0, first + i, 0)),
            pl.BlockSpec((tb, 3 * d), lambda i: (first + i, 0)),
        ],
        out_shape=[
            jax.ShapeDtypeStruct((2, total, d // 2), bf16),
            jax.ShapeDtypeStruct((total, 3 * d), bf16),
        ],
        input_output_aliases={6 + k: k for k in range(len(earlier))},
        compiler_params=params(),
        cost_estimate=pl.CostEstimate(
            flops=2 * n * d * 3 * d, bytes_accessed=6 * d * d + 10 * n * d, transcendentals=n
        ),
    )(tok, gain, shift, w, qb, vb, *earlier)


def half_slot(own, half):
    return own if half == 0 else 1 - own


def pick(ref, own, block, size):
    half, sub = divmod(block, 2)
    return ref[half_slot(own, half), sub * size : (sub + 1) * size, :]


def head_mask(size):
    return lax.broadcasted_iota(jnp.int32, (size, LANES), 1) < LANES // 2


def block_penalty(tab, i, j):
    return jnp.where(tab[1 + 4 * i + j] > 0, 0.0, masked_score).astype(f32)


def attend_body(tab, q, k, v, head_scale, heads_out, lse):
    size = q.shape[1] // 2
    own = tab[0]
    low = head_mask(size)
    causal = lax.broadcasted_iota(jnp.int32, (size, size), 0) >= lax.broadcasted_iota(
        jnp.int32, (size, size), 1
    )
    lane = lax.broadcasted_iota(jnp.int32, (size, LANES), 1)
    for i in range(4):
        qi = pick(q, own, i, size)
        outs = []
        logs = []
        for h in range(2):
            qm = jnp.where(low if h == 0 else ~low, qi, 0).astype(bf16)
            parts = []
            for j in range(i + 1):
                s = mm(qm, pick(k, own, j, size), NT)
                parts.append(
                    jnp.where(causal, s, masked_score) if j == i else s + block_penalty(tab, i, j)
                )
            top = parts[0]
            for s in parts[1:]:
                top = jnp.maximum(top, s)
            top = jnp.max(top, axis=1, keepdims=True)
            total = None
            out = None
            for j, s in enumerate(parts):
                p = jnp.exp(s - top)
                part_sum = fold(p)
                total = part_sum if total is None else total + part_sum
                part_out = mm(p.astype(bf16), pick(v, own, j, size))
                out = part_out if out is None else out + part_out
            total = jnp.sum(total, axis=1, keepdims=True)
            outs.append(out * (1.0 / total))
            logs.append(top + jnp.log(total))
        both = jnp.where(low, outs[0], outs[1]) * head_scale[...]
        half, sub = divmod(i, 2)
        heads_out[half_slot(own, half), sub * size : (sub + 1) * size, :] = both.astype(bf16)
        columns = jnp.where(lane == 0, logs[0], logs[1])
        lse[0, i] = jnp.transpose(columns)[:8]


def attend(tab, qkv, head_scale_row):
    _, half_len, wide = qkv.shape
    d = wide // 3
    pairs = d // LANES
    size = half_len // 2

    def lanes(first):
        return pl.BlockSpec((2, half_len, LANES), lambda p, t: (0, 0, first + p))

    flops = 16 * half_len * half_len * pairs * LANES
    return pl.pallas_call(
        attend_body,
        name="attend",
        grid_spec=pltpu.PrefetchScalarGridSpec(
            num_scalar_prefetch=1,
            grid=(pairs,),
            in_specs=[
                lanes(0),
                lanes(pairs),
                lanes(2 * pairs),
                pl.BlockSpec((1, LANES), lambda p, t: (0, p)),
            ],
            out_specs=[
                lanes(0),
                pl.BlockSpec((1, 4, 8, size), lambda p, t: (p, 0, 0, 0)),
            ],
        ),
        out_shape=[
            jax.ShapeDtypeStruct((2, half_len, d), bf16),
            jax.ShapeDtypeStruct((pairs, 4, 8, size), f32),
        ],
        compiler_params=params(),
        cost_estimate=pl.CostEstimate(
            flops=flops * 4, bytes_accessed=8 * half_len * wide, transcendentals=8 * half_len * half_len * pairs
        ),
    )(tab, qkv, qkv, qkv, head_scale_row)


def attend_back_body(
    scale, tab, q, k, v, heads_out, d_out, inv_scale, lse, dqkv, dots, dq_acc
):
    size = q.shape[1] // 2
    own = tab[0]
    low = head_mask(size)
    masks = (low, ~low)
    causal = lax.broadcasted_iota(jnp.int32, (size, size), 0) <= lax.broadcasted_iota(
        jnp.int32, (size, size), 1
    )
    pick_rows = (
        lax.broadcasted_iota(jnp.int32, (8, LANES), 1) // (LANES // 2)
        == lax.broadcasted_iota(jnp.int32, (8, LANES), 0)
    ).astype(f32)
    qs, gs, deltas = {}, {}, []
    for i in range(4):
        qi = pick(q, own, i, size)
        gi = pick(d_out, own, i, size)
        for h in range(2):
            qs[i, h] = jnp.where(masks[h], qi, 0).astype(bf16)
            gs[i, h] = jnp.where(masks[h], gi, 0).astype(bf16)
        product = gi.astype(f32) * pick(heads_out, own, i, size).astype(f32) * inv_scale[...]
        delta = lax.dot_general(
            pick_rows, product, NT, preferred_element_type=f32, precision=lax.Precision.HIGHEST
        )
        deltas.append(delta)
        dots[0, i] = delta
        dq_acc[i] = jnp.zeros((size, LANES), f32)
    for j in range(4):
        kj = pick(k, own, j, size)
        vj = pick(v, own, j, size)
        dk_j = jnp.zeros((size, LANES), f32)
        dv_j = jnp.zeros((size, LANES), f32)
        for h in range(2):
            km = jnp.where(masks[h], kj, 0).astype(bf16)
            for i in range(j, 4):
                logs = lse[0, i, h : h + 1, :]
                if i > j:
                    logs = logs - block_penalty(tab, i, j)
                s = mm(kj, qs[i, h], NT)
                if i == j:
                    s = jnp.where(causal, s, masked_score)
                p = jnp.exp(s - logs)
                gp = mm(vj, gs[i, h], NT)
                ds = (p * (gp - deltas[i][h : h + 1, :])).astype(bf16)
                dv_j = dv_j + mm(p.astype(bf16), gs[i, h])
                dk_j = dk_j + mm(ds, qs[i, h])
                dq_acc[i] += mm(ds, km, TN)
        half, sub = divmod(j, 2)
        where = (half_slot(own, half), slice(sub * size, (sub + 1) * size))
        dqkv[1, where[0], where[1], :] = dk_j.astype(bf16)
        dqkv[2, where[0], where[1], :] = dv_j.astype(bf16)
    for i in range(4):
        half, sub = divmod(i, 2)
        dqkv[0, half_slot(own, half), sub * size : (sub + 1) * size, :] = (dq_acc[i] * scale).astype(bf16)


def attend_back(tab, qkv, heads_out, d_out, inv_scale_row, lse, scale, group):
    _, half_len, wide = qkv.shape
    d = wide // 3
    every = d // LANES
    pairs = every // 2
    size = half_len // 2

    def pair(p):
        return p + 2 * (p // 2) + 2 * group

    def lanes(first):
        return pl.BlockSpec((2, half_len, LANES), lambda p, t: (0, 0, first + pair(p)))

    flops = 16 * half_len * half_len * pairs * LANES
    return pl.pallas_call(
        partial(attend_back_body, scale),
        name="attend_back",
        grid_spec=pltpu.PrefetchScalarGridSpec(
            num_scalar_prefetch=1,
            grid=(pairs,),
            in_specs=[
                lanes(0),
                lanes(every),
                lanes(2 * every),
                lanes(0),
                lanes(0),
                pl.BlockSpec((1, LANES), lambda p, t: (0, pair(p))),
                pl.BlockSpec((1, 4, 8, size), lambda p, t: (pair(p), 0, 0, 0)),
            ],
            out_specs=[
                pl.BlockSpec((3, 2, half_len, LANES), lambda p, t: (0, 0, 0, p)),
                pl.BlockSpec((1, 4, 8, size), lambda p, t: (p, 0, 0, 0)),
            ],
            scratch_shapes=[pltpu.VMEM((4, size, LANES), f32)],
        ),
        out_shape=[
            jax.ShapeDtypeStruct((3, 2, half_len, d // 2), bf16),
            jax.ShapeDtypeStruct((pairs, 4, 8, size), f32),
        ],
        compiler_params=params(),
        cost_estimate=pl.CostEstimate(
            flops=flops * 10, bytes_accessed=8 * half_len * wide, transcendentals=8 * half_len * half_len * pairs
        ),
    )(tab, qkv, qkv, qkv, heads_out, d_out, inv_scale_row, lse)


def gelu_parts(v):
    a = jnp.abs(v)
    t = 1.0 / (1.0 + (0.3275911 * 0.7071067811865476) * a)
    bell = jnp.exp(v * v * -0.5)
    poly = ((((1.061405429 * t - 1.453152027) * t + 1.421413741) * t - 0.284496736) * t + 0.254829592) * t
    tail = (0.5 * poly) * bell
    cdf = jnp.where(v < 0, tail, 1.0 - tail)
    return v * cdf, cdf + v * (bell * 0.3989422804014327)


def middle_body(
    ho, tok, cot, out_w, w1, w2, vec, vec4,
    output, grad_middle, ffn_in, heads_in, mid_out, grad_hidden, grad_proj, d_out, sums, sums4,
    act, slope, back,
):
    step = pl.program_id(0)
    d = ho.shape[1]
    ff = w1.shape[1]
    fc = 512
    chunks = ff // fc

    @pl.when(step == 0)
    def _():
        sums[...] = jnp.zeros_like(sums)
        sums4[...] = jnp.zeros_like(sums4)

    def v(r):
        return vec[r : r + 1, :]

    tokens = tok[...].astype(f32)
    projection = mm(ho[...], out_w[...]) + v(0)
    unit_attn, inverse_attn = norm_unit(projection)
    middle = tokens + (unit_attn * v(1) + v(2))
    unit_two, inverse_two = norm_unit(middle)
    x = (unit_two * v(3) + v(4)).astype(bf16)
    ffn_in[0], ffn_in[1] = core_split(x)
    heads_in[0], heads_in[1] = core_split(ho[...])
    g = cot[...]
    tb = x.shape[0]
    zero = jnp.zeros((tb, LANES), f32)

    def span(c):
        return pl.ds(pl.multiple_of(c * fc, fc), fc)

    def one(c, total):
        s = span(c)
        h = mm(x, w1[:, s]) + vec4[0:1, s]
        back[:, s] = mm(g, w2[s, :], NT)
        a, b = gelu_parts(h)
        act[:, s] = a
        slope[:, s] = b
        return total + fold(a)

    total = lax.fori_loop(0, chunks, one, zero)
    mean = jnp.sum(total, axis=1, keepdims=True) * (1.0 / ff)

    def two(c, total):
        a = act[:, span(c)] - mean
        return total + fold(a * a)

    total = lax.fori_loop(0, chunks, two, zero)
    inverse = lax.rsqrt(jnp.sum(total, axis=1, keepdims=True) * (1.0 / ff) + eps)

    def three(c, carry):
        acc, sum_e, sum_eu = carry
        s = span(c)
        u = (act[:, s] - mean) * inverse
        act[:, s] = u
        gain = vec4[1:2, s]
        m = (u * gain + vec4[2:3, s]).astype(bf16)
        mid_out[:, s] = m
        gm = back[:, s]
        sums4[1:2, s] += row_sum(gm * u)
        sums4[2:3, s] += row_sum(gm)
        e = gm * gain
        return acc + mm(m, w2[s, :]), sum_e + fold(e), sum_eu + fold(e * u)

    acc, sum_e, sum_eu = lax.fori_loop(
        0, chunks, three, (jnp.zeros((tb, d), f32), zero, zero)
    )
    output[...] = middle + acc + v(5)
    mean_e = jnp.sum(sum_e, axis=1, keepdims=True) * (1.0 / ff)
    mean_eu = jnp.sum(sum_eu, axis=1, keepdims=True) * (1.0 / ff)

    def four(c, acc):
        s = span(c)
        e = back[:, s] * vec4[1:2, s]
        grad_act = inverse * (e - mean_e - act[:, s] * mean_eu)
        gh = (grad_act * slope[:, s]).astype(bf16)
        grad_hidden[:, s] = gh
        sums4[0:1, s] += row_sum(gh.astype(f32))
        return acc + mm(gh, w1[:, s], NT)

    grad_ffn_in = lax.fori_loop(0, chunks, four, jnp.zeros((tb, d), f32))
    gout = g.astype(f32)
    sums[5:6, :] += row_sum(gout)
    sums[3:4, :] += row_sum(grad_ffn_in * unit_two)
    sums[4:5, :] += row_sum(grad_ffn_in)
    gmid = gout + norm_back(grad_ffn_in, unit_two, inverse_two, v(3))
    grad_middle[...] = gmid
    sums[1:2, :] += row_sum(gmid * unit_attn)
    sums[2:3, :] += row_sum(gmid)
    gp = norm_back(gmid, unit_attn, inverse_attn, v(1)).astype(bf16)
    grad_proj[...] = gp
    sums[0:1, :] += row_sum(gp.astype(f32))
    d_out[...] = (mm(gp, out_w[...], NT) * v(6)).astype(bf16)


def middle_pass(ho, tok, cot, out_w, w1, w2, vec, vec4, tb=256):
    n, d = ho.shape
    ff = w1.shape[1]
    rows = pl.BlockSpec((tb, d), lambda i: (i, 0))
    wide = pl.BlockSpec((tb, ff), lambda i: (i, 0))
    split = pl.BlockSpec((2, tb, d // 2), lambda i: (0, i, 0))
    return pl.pallas_call(
        middle_body,
        name="middle_pass",
        grid=(n // tb,),
        in_specs=[rows, rows, rows] + [whole(a.shape) for a in (out_w, w1, w2, vec, vec4)],
        out_specs=[rows, rows, split, split, wide, wide, rows, rows, whole((8, d)), whole((8, ff))],
        out_shape=[
            jax.ShapeDtypeStruct((n, d), f32),
            jax.ShapeDtypeStruct((n, d), f32),
            jax.ShapeDtypeStruct((2, n, d // 2), bf16),
            jax.ShapeDtypeStruct((2, n, d // 2), bf16),
            jax.ShapeDtypeStruct((n, ff), bf16),
            jax.ShapeDtypeStruct((n, ff), bf16),
            jax.ShapeDtypeStruct((n, d), bf16),
            jax.ShapeDtypeStruct((n, d), bf16),
            jax.ShapeDtypeStruct((8, d), f32),
            jax.ShapeDtypeStruct((8, ff), f32),
        ],
        scratch_shapes=[pltpu.VMEM((tb, ff), f32)] * 3,
        compiler_params=params(),
        cost_estimate=pl.CostEstimate(
            flops=8 * n * d * ff + 4 * n * d * d,
            bytes_accessed=4 * d * ff + 2 * d * d + 4 * n * ff + 20 * n * d,
            transcendentals=2 * n * ff,
        ),
    )(ho, tok, cot, out_w, w1, w2, vec, vec4)


def first_back_body(even, odd, w, tok, grad_middle, gain, tokens_grad, sums):
    @pl.when(pl.program_id(0) == 0)
    def _():
        sums[...] = jnp.zeros_like(sums)

    d = w.shape[0]
    run = d // 4
    grad = None
    for part in range(3):
        for r in range(4):
            piece = (even, odd)[r % 2][part, :, (r // 2) * run : (r // 2 + 1) * run]
            here = r * run
            term = mm(piece, w[:, part * d + here : part * d + here + run], NT)
            grad = term if grad is None else grad + term
            if part != 1:
                at = 2 + part // 2
                sums[at : at + 1, here : here + run] += row_sum(piece.astype(f32))
    unit, inverse = norm_unit(tok[...].astype(f32))
    sums[0:1, :] += row_sum(grad * unit)
    sums[1:2, :] += row_sum(grad)
    whole_grad = grad_middle[...] + norm_back(grad, unit, inverse, gain[...])
    tokens_grad[...] = whole_grad.astype(tokens_grad.dtype)


def first_back(even, odd, w, tok, grad_middle, gain, slot, kind, tb=256):
    d = w.shape[0]
    n = even.shape[1] // 2
    first = slot * (n // tb)
    rows = pl.BlockSpec((tb, d), lambda i: (first + i, 0))
    half = pl.BlockSpec((3, tb, d // 2), lambda i: (0, first + i, 0))
    return pl.pallas_call(
        first_back_body,
        name="first_back",
        grid=(n // tb,),
        in_specs=[half, half, whole(w.shape), rows, rows, whole(gain.shape)],
        out_specs=[pl.BlockSpec((tb, d), lambda i: (i, 0)), whole((8, d))],
        out_shape=[jax.ShapeDtypeStruct((n, d), kind), jax.ShapeDtypeStruct((8, d), f32)],
        compiler_params=params(),
        cost_estimate=pl.CostEstimate(
            flops=6 * n * d * d, bytes_accessed=6 * d * d + 16 * n * d, transcendentals=n
        ),
    )(even, odd, w, tok, grad_middle, gain)


def after(x, *others):
    return lax.optimization_barrier((x,) + others)[0]


def weight_grad_body(a_lead, b_lead, tab, a, b, *refs):
    lhs = a[0] if a_lead else a[...]
    rhs = b[0] if b_lead else b[...]
    total = mm(lhs, rhs, TN)
    if len(refs) == 1:
        refs[0][0] = total.astype(bf16)
        return
    received, send, keep = refs
    total = (total + received[0].astype(f32)).astype(bf16)

    @pl.when(pl.program_id(0) == 0)
    def _():
        send[...] = total

    @pl.when(pl.program_id(0) == 1)
    def _():
        keep[...] = total


def weight_grad(tab, a, b, a_block, b_block, out_block, shape, steps, received=None):
    flops = 2 * a.shape[-2] * 2 * shape[0] * shape[1]
    out_index = out_block[1]
    moved = 2 * (a.size + b.size) + 4 * shape[0] * shape[1]
    common = dict(
        name="weight_grad",
        compiler_params=params(),
        cost_estimate=pl.CostEstimate(flops=flops, bytes_accessed=moved, transcendentals=0),
    )
    part = pl.BlockSpec((1,) + out_block[0], lambda s, i, t: (s,) + out_index(i))
    in_specs = [pl.BlockSpec(*a_block), pl.BlockSpec(*b_block)]
    args = [tab, a, b]
    if received is None:
        out_specs = part
        out_shape = jax.ShapeDtypeStruct((2,) + shape, bf16)
    else:
        in_specs.append(part)
        args.append(received)
        last = steps - 1
        out_specs = [
            pl.BlockSpec(out_block[0], lambda s, i, t: out_index(jnp.where(s == 0, i, last))),
            pl.BlockSpec(out_block[0], lambda s, i, t: out_index(jnp.where(s == 0, 0, i))),
        ]
        out_shape = [jax.ShapeDtypeStruct(shape, bf16)] * 2
    return pl.pallas_call(
        partial(weight_grad_body, len(a_block[0]) == 3, len(b_block[0]) == 3),
        grid_spec=pltpu.PrefetchScalarGridSpec(
            num_scalar_prefetch=1, grid=(2, steps), in_specs=in_specs, out_specs=out_specs
        ),
        out_shape=out_shape,
        **common,
    )(*args)


def running_sums(lengths):
    count = lengths.shape[1]
    upto = jnp.arange(count)[:, None] >= jnp.arange(count)[None, :]
    return jnp.sum(jnp.where(upto[None], lengths[:, None, :], 0), axis=2).astype(jnp.int32)


def norm_forward(values, gain, shift):
    average = jnp.mean(values, axis=-1, keepdims=True)
    centered = values - average
    inverse = lax.rsqrt(jnp.mean(centered * centered, axis=-1, keepdims=True) + eps)
    normed = centered * inverse
    return (normed * gain + shift, normed, inverse)


def norm_backward(grad_y, normed, inverse, gain):
    scaled = grad_y * gain
    grad_in = inverse * (
        scaled
        - jnp.mean(scaled, axis=-1, keepdims=True)
        - normed * jnp.mean(scaled * normed, axis=-1, keepdims=True)
    )
    return (grad_in, jnp.sum(grad_y * normed, axis=(0, 1)), jnp.sum(grad_y, axis=(0, 1)))


def local_general(
    tokens,
    cotangent,
    doc_lengths,
    norm1_gain,
    norm1_shift,
    qkv_weight,
    query_bias,
    value_bias,
    head_scales,
    out_weight,
    out_bias,
    attn_gain,
    attn_shift,
    norm2_gain,
    norm2_shift,
    fc1_weight,
    fc1_bias,
    mid_gain,
    mid_shift,
    fc2_weight,
    fc2_bias,
):
    f32 = jnp.float32
    bf16 = jnp.bfloat16
    batch_size, local_len, model_width = tokens.shape
    head_count = head_scales.shape[0]
    head_dim = model_width // head_count
    score_scale = head_dim ** (-0.5)
    row_len = local_len * lax.axis_size("blk")
    row_first = lax.axis_index("blk") * local_len
    query_pos = row_first + jnp.arange(local_len, dtype=jnp.int32)
    doc_ends = running_sums(doc_lengths)
    starts = jnp.max(
        jnp.where(doc_ends[:, None, :] <= query_pos[None, :, None], doc_ends[:, None, :], 0), axis=2
    )
    lowest = jnp.min(starts[:, 0])
    query_last = row_first + local_len - 1
    inputs = tokens.astype(f32)
    attn_norm, unit_one, inverse_one = norm_forward(inputs, norm1_gain, norm1_shift)
    attn_in = attn_norm.astype(bf16)
    projected = jnp.dot(attn_in, qkv_weight, preferred_element_type=f32)
    queries = (
        (projected[..., :model_width] + query_bias)
        .astype(bf16)
        .reshape(batch_size, local_len, head_count, head_dim)
    )
    keys_low = projected[..., model_width : 2 * model_width].astype(bf16)
    values_low = (projected[..., 2 * model_width :] + value_bias).astype(bf16)

    def block_scores(key_piece, offset):
        key_len = key_piece.shape[1]
        keys_head = key_piece.reshape(batch_size, key_len, head_count, head_dim)
        raw_scores = (
            jnp.einsum("bqhd,bkhd->bhqk", queries, keys_head, preferred_element_type=f32)
            * score_scale
        )
        key_pos = offset + jnp.arange(key_len, dtype=jnp.int32)
        allowed = (key_pos[None, None, :] <= query_pos[None, :, None]) & (
            key_pos[None, None, :] >= starts[:, :, None]
        )
        return (jnp.where(allowed[:, None], raw_scores, masked_score), keys_head)

    def is_live(offset, key_len):
        return (offset <= query_last) & (offset + key_len - 1 >= lowest)

    def attend_slab(running, key_piece, value_piece, offset):
        key_len = key_piece.shape[1]

        def attend_compute(state):
            running_max, running_sum, weighted = state
            scores, keys_head = block_scores(key_piece, offset)
            new_max = jnp.maximum(running_max, jnp.max(scores, axis=3))
            rescale = jnp.exp(running_max - new_max)
            weights = jnp.exp(scores - new_max[..., None])
            values_head = value_piece.reshape(batch_size, key_len, head_count, head_dim)
            update = jnp.einsum(
                "bhqk,bkhd->bqhd", weights.astype(bf16), values_head, preferred_element_type=f32
            )
            rescale_t = jnp.transpose(rescale, (0, 2, 1))[..., None]
            return (
                new_max,
                running_sum * rescale + jnp.sum(weights, axis=3),
                weighted * rescale_t + update,
            )

        return lax.cond(is_live(offset, key_len), attend_compute, lambda state: state, running)

    start_state = (
        jnp.full((batch_size, head_count, local_len), masked_score, f32),
        jnp.zeros((batch_size, head_count, local_len), f32),
        jnp.zeros((batch_size, local_len, head_count, head_dim), f32),
    )
    key_piece = lax.all_gather(keys_low, "blk", axis=1, tiled=True)
    value_piece = lax.all_gather(values_low, "blk", axis=1, tiled=True)
    turns = key_piece.shape[1] // local_len

    def one_turn(index, state):
        begin = index * local_len
        key_slab = lax.dynamic_slice_in_dim(key_piece, begin, local_len, 1)
        value_slab = lax.dynamic_slice_in_dim(value_piece, begin, local_len, 1)
        return attend_slab(state, key_slab, value_slab, begin)

    running_max, running_sum, weighted = lax.fori_loop(0, turns, one_turn, start_state)
    attended = weighted / jnp.transpose(running_sum, (0, 2, 1))[..., None]
    log_total = running_max + jnp.log(running_sum)
    heads_out = (
        (attended * head_scales[:, None]).reshape(batch_size, local_len, model_width).astype(bf16)
    )
    projection = jnp.dot(heads_out, out_weight, preferred_element_type=f32) + out_bias
    branch, unit_attn, inverse_attn = norm_forward(projection, attn_gain, attn_shift)
    middle = inputs + branch
    ffn_norm, unit_two, inverse_two = norm_forward(middle, norm2_gain, norm2_shift)
    ffn_in = ffn_norm.astype(bf16)
    hidden = jnp.dot(ffn_in, fc1_weight, preferred_element_type=f32) + fc1_bias
    activated, gelu_grad = jax.vjp(partial(jax.nn.gelu, approximate=False), hidden)
    mid_norm, unit_mid, inverse_mid = norm_forward(activated, mid_gain, mid_shift)
    mid_out = mid_norm.astype(bf16)
    output = middle + jnp.dot(mid_out, fc2_weight, preferred_element_type=f32) + fc2_bias
    grad_output = cotangent.astype(f32)
    fc2_weight_grad = jnp.einsum("bcf,bcd->fd", mid_out, cotangent, preferred_element_type=f32)
    fc2_bias_grad = jnp.sum(grad_output, axis=(0, 1))
    grad_mid = jnp.einsum("bcd,fd->bcf", cotangent, fc2_weight, preferred_element_type=f32)
    grad_act, mid_gain_grad, mid_shift_grad = norm_backward(
        grad_mid, unit_mid, inverse_mid, mid_gain
    )
    grad_hidden = gelu_grad(grad_act)[0].astype(bf16)
    fc1_weight_grad = jnp.einsum("bcd,bcf->df", ffn_in, grad_hidden, preferred_element_type=f32)
    fc1_bias_grad = jnp.sum(grad_hidden.astype(f32), axis=(0, 1))
    grad_ffn_in = jnp.einsum("bcf,df->bcd", grad_hidden, fc1_weight, preferred_element_type=f32)
    grad_two, norm2_gain_grad, norm2_shift_grad = norm_backward(
        grad_ffn_in, unit_two, inverse_two, norm2_gain
    )
    grad_middle = grad_output + grad_two
    grad_proj_f, attn_gain_grad, attn_shift_grad = norm_backward(
        grad_middle, unit_attn, inverse_attn, attn_gain
    )
    grad_projection = grad_proj_f.astype(bf16)
    out_weight_grad = jnp.einsum(
        "bcd,bce->de", heads_out, grad_projection, preferred_element_type=f32
    )
    out_bias_grad = jnp.sum(grad_projection.astype(f32), axis=(0, 1))
    grad_heads = jnp.einsum(
        "bce,de->bcd", grad_projection, out_weight, preferred_element_type=f32
    ).reshape(batch_size, local_len, head_count, head_dim)
    head_scales_grad = jnp.sum(grad_heads * attended, axis=(0, 1, 3))
    grad_attended = (grad_heads * head_scales[:, None]).astype(bf16)
    row_dot = jnp.transpose(jnp.sum(grad_attended.astype(f32) * attended, axis=3), (0, 2, 1))

    def back_slab(running, key_piece, value_piece, offset):
        key_len = key_piece.shape[1]

        def back_compute(state):
            grad_queries, kv_buffer = state
            scores, keys_head = block_scores(key_piece, offset)
            attn_probs = jnp.exp(scores - log_total[..., None])
            values_head = value_piece.reshape(batch_size, key_len, head_count, head_dim)
            grad_probs = jnp.einsum(
                "bqhd,bkhd->bhqk", grad_attended, values_head, preferred_element_type=f32
            )
            grad_scores = (attn_probs * (grad_probs - row_dot[..., None])).astype(bf16)
            grad_queries = (
                grad_queries
                + jnp.einsum("bhqk,bkhd->bqhd", grad_scores, keys_head, preferred_element_type=f32)
                * score_scale
            )
            grad_keys = (
                jnp.einsum("bhqk,bqhd->bkhd", grad_scores, queries, preferred_element_type=f32)
                * score_scale
            )
            grad_values = jnp.einsum(
                "bhqk,bqhd->bkhd",
                attn_probs.astype(bf16),
                grad_attended,
                preferred_element_type=f32,
            )
            addition = jnp.concatenate(
                [
                    grad_keys.reshape(batch_size, key_len, model_width),
                    grad_values.reshape(batch_size, key_len, model_width),
                ],
                axis=2,
            )
            previous = lax.dynamic_slice_in_dim(kv_buffer, offset, key_len, 1)
            return (
                grad_queries,
                lax.dynamic_update_slice_in_dim(kv_buffer, previous + addition, offset, 1),
            )

        return lax.cond(is_live(offset, key_len), back_compute, lambda state: state, running)

    back_state = (
        jnp.zeros((batch_size, local_len, head_count, head_dim), f32),
        jnp.zeros((batch_size, row_len, 2 * model_width), f32),
    )
    attend_key_piece = lax.all_gather(keys_low, "blk", axis=1, tiled=True)
    attend_value_piece = lax.all_gather(values_low, "blk", axis=1, tiled=True)
    turns = attend_key_piece.shape[1] // local_len

    def one_turn(index, state):
        begin = index * local_len
        key_slab = lax.dynamic_slice_in_dim(attend_key_piece, begin, local_len, 1)
        value_slab = lax.dynamic_slice_in_dim(attend_value_piece, begin, local_len, 1)
        return back_slab(state, key_slab, value_slab, begin)

    grad_queries, kv_buffer = lax.fori_loop(0, turns, one_turn, back_state)
    grad_kv = lax.psum_scatter(
        kv_buffer.astype(jnp.bfloat16), "blk", scatter_dimension=1, tiled=True
    ).astype(jnp.float32)
    grad_qkv = jnp.concatenate(
        [grad_queries.reshape(batch_size, local_len, model_width), grad_kv], axis=2
    ).astype(bf16)
    qkv_weight_grad = jnp.einsum("bcd,bce->de", attn_in, grad_qkv, preferred_element_type=f32)
    query_bias_grad = jnp.sum(grad_qkv[..., :model_width].astype(f32), axis=(0, 1))
    value_bias_grad = jnp.sum(grad_qkv[..., 2 * model_width :].astype(f32), axis=(0, 1))
    grad_attn_in = jnp.einsum("bce,de->bcd", grad_qkv, qkv_weight, preferred_element_type=f32)
    grad_one, norm1_gain_grad, norm1_shift_grad = norm_backward(
        grad_attn_in, unit_one, inverse_one, norm1_gain
    )
    tokens_grad = grad_middle + grad_one
    matrix_grads = (qkv_weight_grad, out_weight_grad, fc1_weight_grad, fc2_weight_grad)
    reduced = (
        lax.psum_scatter(
            matrix_grads[0].astype(jnp.bfloat16), "dp", scatter_dimension=0, tiled=True
        ).astype(jnp.float32),
        lax.psum_scatter(
            matrix_grads[1].astype(jnp.bfloat16), "dp", scatter_dimension=0, tiled=True
        ).astype(jnp.float32),
        lax.psum_scatter(
            matrix_grads[2].astype(jnp.bfloat16), "dp", scatter_dimension=0, tiled=True
        ).astype(jnp.float32),
        lax.psum_scatter(
            matrix_grads[3].astype(jnp.bfloat16), "dp", scatter_dimension=0, tiled=True
        ).astype(jnp.float32),
    )
    reduced = (
        lax.psum_scatter(
            reduced[0].astype(jnp.bfloat16), "blk", scatter_dimension=1, tiled=True
        ).astype(jnp.float32),
        lax.psum_scatter(
            reduced[1].astype(jnp.bfloat16), "blk", scatter_dimension=1, tiled=True
        ).astype(jnp.float32),
        lax.psum_scatter(
            reduced[2].astype(jnp.bfloat16), "blk", scatter_dimension=1, tiled=True
        ).astype(jnp.float32),
        lax.psum_scatter(
            reduced[3].astype(jnp.bfloat16), "blk", scatter_dimension=1, tiled=True
        ).astype(jnp.float32),
    )
    small_sums = lax.psum(
        (
            norm1_gain_grad,
            norm1_shift_grad,
            query_bias_grad,
            value_bias_grad,
            head_scales_grad,
            out_bias_grad,
            attn_gain_grad,
            attn_shift_grad,
            norm2_gain_grad,
            norm2_shift_grad,
            fc1_bias_grad,
            mid_gain_grad,
            mid_shift_grad,
            fc2_bias_grad,
        ),
        ("dp", "blk"),
    )
    return (
        output,
        tokens_grad,
        small_sums[0],
        small_sums[1],
        reduced[0],
        small_sums[2],
        small_sums[3],
        small_sums[4],
        reduced[1],
        small_sums[5],
        small_sums[6],
        small_sums[7],
        small_sums[8],
        small_sums[9],
        reduced[2],
        small_sums[10],
        small_sums[11],
        small_sums[12],
        reduced[3],
        small_sums[13],
    )


swap = ((0, 1), (1, 0))


def exchange(x):
    return lax.ppermute(x, "blk", swap)


def flip(x, bit):
    return lax.ppermute(x, "dp", [(i, i ^ bit) for i in range(16)])


def local_rows(
    tokens,
    cotangent,
    doc_lengths,
    norm1_gain,
    norm1_shift,
    qkv_weight,
    query_bias,
    value_bias,
    head_scales,
    out_weight,
    out_bias,
    attn_gain,
    attn_shift,
    norm2_gain,
    norm2_shift,
    fc1_weight,
    fc1_bias,
    mid_gain,
    mid_shift,
    fc2_weight,
    fc2_bias,
):
    _, half_len, d = tokens.shape
    ff = fc1_weight.shape[1]
    heads = head_scales.shape[0]
    head_dim = d // heads
    scale = head_dim**-0.5
    n = 2 * half_len
    b = lax.axis_index("blk")

    def split(x):
        return (
            lax.dynamic_index_in_dim(x, b, 0, keepdims=False),
            lax.dynamic_index_in_dim(x, 1 - b, 0, keepdims=False),
        )

    def assemble(kept, sent):
        back = exchange(sent).astype(f32)
        return jnp.where(b == 0, jnp.stack([kept, back]), jnp.stack([back, kept]))

    tok_own, tok_other = split(tokens)
    cot_own, cot_other = split(cotangent)
    tok_in = exchange(tok_other)
    cot_in = exchange(cot_other)

    lengths = lax.dynamic_slice_in_dim(doc_lengths, b, 1, 0)
    ends = running_sums(lengths)[0]
    firsts = (half_len // 2) * jnp.arange(4, dtype=jnp.int32)
    starts = jnp.max(jnp.where(ends[None, :] <= firsts[:, None], ends[None, :], 0), axis=1)
    allowed = (firsts[None, :] >= starts[:, None]).astype(jnp.int32)
    tab = jnp.concatenate([b.astype(jnp.int32)[None], allowed.reshape(16)])

    def line(x):
        return x.reshape(1, -1)

    scale_row = jnp.broadcast_to(head_scales[:, None], (heads, head_dim)).reshape(1, d)
    vec = jnp.stack(
        [out_bias, attn_gain, attn_shift, norm2_gain, norm2_shift, fc2_bias, scale_row[0], out_bias]
    )
    vec4 = jnp.stack([fc1_bias, mid_gain, mid_shift, fc1_bias])

    first_args = (line(norm1_gain), line(norm1_shift), qkv_weight, line(query_bias), line(value_bias))
    early = project_qkv(tok_own, *first_args, scale, 0, n)
    attn_in, qkv = project_qkv(tok_in, *first_args, scale, 1, n, early)
    qkv = qkv.reshape(2, half_len, 3 * d)
    tok = jnp.concatenate([tok_own, tok_in])
    cot = jnp.concatenate([cot_own, cot_in])
    heads_out, logs = attend(tab, qkv, scale_row)
    output, grad_middle, ffn_in, heads_in, mid_out, grad_hidden, grad_proj, d_out, sums, sums4 = middle_pass(
        heads_out.reshape(n, d), tok, cot, out_weight, fc1_weight, fc2_weight, vec, vec4
    )
    output = assemble(output[:half_len], output[half_len:].astype(bf16))
    dp = lax.axis_index("dp").astype(jnp.int32)
    core, x, y = dp % 2, (dp // 2) % 2, b.astype(jnp.int32)
    z = dp // 4
    theirs = jnp.stack([1 - core, x, y])
    mine = jnp.stack([core, x, y])

    def part_of(s, t, at):
        return jnp.where(s == 0, 1 - t[at], t[at])

    tall = ff // 16
    tall_how = (
        ((n, tall), lambda s, i, t: (0, (i * 2 + part_of(s, t, 1)) * 2 + t[0])),
        ((n, d), lambda s, i, t: (0, 0)),
        ((tall, d), lambda i: (i, 0)),
        (4 * tall, d),
        4,
    )

    def flat_how(width):
        tn = d // 2
        steps = width // (2 * tn)
        return (
            ((1, n, d // 2), lambda s, i, t: (t[0], 0, 0)),
            ((n, tn), lambda s, i, t: (0, part_of(s, t, 2) * steps + i)),
            ((d // 2, tn), lambda i: (0, i)),
            (d // 2, steps * tn),
            steps,
        )

    run = d // 4
    qkv_how = (
        ((1, n, d // 2), lambda s, i, t: (t[0], 0, 0)),
        (
            (1, n, run),
            lambda s, i, t: ((part_of(s, t, 2) * 3 + i) // 2, 0, (part_of(s, t, 2) * 3 + i) % 2),
        ),
        ((d // 2, run), lambda i: (0, i)),
        (d // 2, 3 * run),
        3,
    )

    def z_stage(parts):
        total = lax.dynamic_index_in_dim(parts, z, 0, keepdims=False).astype(f32)
        for k in (1, 2, 3):
            total = total + flip(lax.dynamic_index_in_dim(parts, z ^ k, 0, keepdims=False), 4 * k).astype(f32)
        return total

    def along_y(send, keep):
        total = (keep.astype(f32) + flip(send, 2).astype(f32)).astype(bf16).reshape(4, -1, d)
        return (
            lax.dynamic_slice_in_dim(total, (1 - y) * (d // 2), d // 2, 2),
            lax.dynamic_slice_in_dim(total, y * (d // 2), d // 2, 2),
        )

    def along_x(send, keep):
        total = keep.astype(f32) + exchange(send).astype(f32)
        total = total.astype(bf16).reshape(4, 2, d // 16, -1)
        return (
            lax.dynamic_index_in_dim(total, 1 - x, 1, keepdims=False),
            lax.dynamic_index_in_dim(total, x, 1, keepdims=False),
        )

    def end_y(send, keep):
        return z_stage((keep.astype(f32) + exchange(send).astype(f32)).astype(bf16))

    def end_x(send, keep):
        return z_stage((keep.astype(f32) + flip(send, 2).astype(f32)).astype(bf16))

    flat4, flat1 = flat_how(ff), flat_how(d)
    fc2_theirs = weight_grad(theirs, mid_out, cot, *tall_how)
    ffn_in = after(ffn_in, fc2_theirs)
    fc1_theirs = weight_grad(theirs, ffn_in, grad_hidden, *flat4)
    heads_in = after(heads_in, fc1_theirs)
    out_theirs = weight_grad(theirs, heads_in, grad_proj, *flat1)
    mid_out = after(mid_out, out_theirs)
    fc2_parts = weight_grad(mine, mid_out, cot, *tall_how, flip(fc2_theirs, 1))
    ffn_in = after(ffn_in, *fc2_parts)
    fc1_parts = weight_grad(mine, ffn_in, grad_hidden, *flat4, flip(fc1_theirs, 1))
    heads_in = after(heads_in, *fc1_parts)
    out_parts = weight_grad(mine, heads_in, grad_proj, *flat1, flip(out_theirs, 1))
    d_out = after(d_out, *out_parts).reshape(2, half_len, d)
    back_args = (1.0 / scale_row, logs, scale)
    even, dots_even = attend_back(tab, qkv, heads_out, d_out, *back_args, 0)
    even = even.reshape(3, n, d // 2)
    fc2_parts = along_y(fc2_parts[0], after(fc2_parts[1], even))
    fc1_parts = along_x(fc1_parts[0], after(fc1_parts[1], even))
    out_parts = along_x(out_parts[0], after(out_parts[1], even))
    even_theirs = weight_grad(theirs, attn_in, even, *qkv_how)
    d_out = after(d_out, even_theirs, *fc2_parts, *fc1_parts, *out_parts)
    odd, dots_odd = attend_back(tab, qkv, heads_out, d_out, *back_args, 1)
    odd = odd.reshape(3, n, d // 2)
    odd_theirs = weight_grad(theirs, attn_in, odd, *qkv_how)
    attn_in = after(attn_in, odd_theirs)
    even_parts = weight_grad(mine, attn_in, even, *qkv_how, flip(even_theirs, 1))
    first_rest = (odd, qkv_weight, tok, grad_middle, line(norm1_gain))
    grad_sent, sums_sent = first_back(after(even, *even_parts), *first_rest, 1, bf16)
    attn_in = after(attn_in, grad_sent)
    odd_parts = weight_grad(mine, attn_in, odd, *qkv_how, flip(odd_theirs, 1))
    grad_kept, sums_kept = first_back(after(even, *odd_parts), *first_rest, 0, f32)
    fc2_weight_grad = end_y(fc2_parts[0], after(fc2_parts[1], odd))
    fc1_weight_grad = end_x(fc1_parts[0], after(fc1_parts[1], odd))
    out_weight_grad = end_x(out_parts[0], after(out_parts[1], odd))
    even_parts = along_x(even_parts[0], after(even_parts[1], grad_kept))
    odd_parts = along_x(odd_parts[0], after(odd_parts[1], grad_kept))
    even_grad, odd_grad = end_x(*even_parts), end_x(*odd_parts)
    qkv_weight_grad = jnp.stack(
        [even_grad.reshape(-1, 3, run), odd_grad.reshape(-1, 3, run)], axis=2
    ).reshape(-1, 6 * run)
    first_sums = sums_sent + sums_kept
    tokens_grad = assemble(grad_kept, grad_sent)
    dots = jnp.stack([dots_even.reshape(2, 2, 4, 8, -1), dots_odd.reshape(2, 2, 4, 8, -1)], axis=1)
    head_scales_grad = jnp.sum(dots[..., :2, :], axis=(3, 5)).reshape(heads) / head_scales
    head_scales_grad = jnp.pad(head_scales_grad, (0, d - heads))

    def everywhere(v):
        for move in (partial(flip, bit=1), partial(flip, bit=2), exchange, partial(flip, bit=4), partial(flip, bit=8)):
            v = v + move(v)
        return v

    sums = everywhere(jnp.concatenate([sums.reshape(8, d), sums4.reshape(8 * ff // d, d)[: 3 * ff // d]]))
    sums4 = sums[8:].reshape(3, ff)
    first_sums = everywhere(jnp.concatenate([first_sums[:4], head_scales_grad[None]]))
    return (
        output,
        tokens_grad,
        first_sums[0],
        first_sums[1],
        qkv_weight_grad,
        first_sums[2],
        first_sums[3],
        first_sums[4, :heads],
        out_weight_grad,
        sums[0],
        sums[1],
        sums[2],
        sums[3],
        sums[4],
        fc1_weight_grad,
        sums4[0],
        sums4[1],
        sums4[2],
        fc2_weight_grad,
        sums[5],
    )


def solution(mesh):
    rows_fit = dict(mesh.shape) == {"dp": 16, "blk": 2}
    local = local_rows if rows_fit else local_general
    placed = (
        P("dp", "blk", None),
        P("dp", "blk", None),
        P("dp", None),
        P(),
        P(),
        P(),
        P(),
        P(),
        P(),
        P(),
        P(),
        P(),
        P(),
        P(),
        P(),
        P(),
        P(),
        P(),
        P(),
        P(),
        P(),
    )
    return jax.shard_map(
        local,
        mesh=mesh,
        in_specs=placed,
        out_specs=(
            P("dp", "blk", None),
            P("dp", "blk", None),
            P(),
            P(),
            P("dp", "blk"),
            P(),
            P(),
            P(),
            P("dp", "blk"),
            P(),
            P(),
            P(),
            P(),
            P(),
            P("dp", "blk"),
            P(),
            P(),
            P(),
            P("dp", "blk"),
            P(),
        ),
        check_vma=False,
    )
```

```python
from functools import partial

import jax
import jax.numpy as jnp
from jax import lax
from jax.experimental import pallas as pl
from jax.experimental.pallas import tpu as pltpu
from jax.sharding import PartitionSpec as P

f32 = jnp.float32
bf16 = jnp.bfloat16
eps = 1e-05
masked_score = -1e30
LANES = 128
NT = (((1,), (1,)), ((), ()))
NN = (((1,), (0,)), ((), ()))
TN = (((0,), (0,)), ((), ()))


def mm(a, b, dims=NN):
    return lax.dot_general(a, b, dims, preferred_element_type=f32)


def fold(x):
    total = x[:, :LANES]
    for c in range(LANES, x.shape[1], LANES):
        total = total + x[:, c : c + LANES]
    return total


def row_mean(x):
    return jnp.sum(fold(x), axis=1, keepdims=True) * (1.0 / x.shape[1])


def row_sum(x):
    return jnp.sum(x, axis=0, keepdims=True)


def norm_unit(v):
    centered = v - row_mean(v)
    inverse = lax.rsqrt(row_mean(centered * centered) + eps)
    return centered * inverse, inverse


def norm_back(grad_y, unit, inverse, gain):
    e = grad_y * gain
    return inverse * (e - row_mean(e) - unit * row_mean(e * unit))


def params(mib=None, **more):
    return pltpu.CompilerParams(vmem_limit_bytes=(mib or 60) * 2**20, **more)


def whole(shape):
    return pl.BlockSpec(shape, lambda *_: (0,) * len(shape), pipeline_mode=pl.Buffered(1))


def core_split(x):
    low = lax.broadcasted_iota(jnp.int32, (x.shape[0], LANES), 1) < LANES // 2
    even, odd = [], []
    for c in range(0, x.shape[1], 2 * LANES):
        a = x[:, c : c + LANES].astype(f32)
        b = x[:, c + LANES : c + 2 * LANES].astype(f32)
        even.append(jnp.where(low, a, pltpu.roll(b, LANES // 2, 1)))
        odd.append(jnp.where(low, pltpu.roll(a, LANES // 2, 1), b))
    return (jnp.concatenate(y, axis=1).astype(bf16) for y in (even, odd))


def qkv_body(scale, at, tok, gain, shift, w, bias, *refs):
    attn_in, qkv, x, ws, sems = refs[-5:]
    step = pl.program_id(0)
    steps, d, cols = ws.shape
    half = cols // 2

    def fetch(k, h):
        columns = pl.ds(pl.multiple_of(k * cols + h * half, half), half)
        return pltpu.make_async_copy(
            w.at[:, columns], ws.at[k, :, pl.ds(h * half, half)], sems.at[k, h]
        )

    @pl.when(step == 0)
    def _():
        for k in range(steps):
            for h in range(2):
                fetch(k, h).start()
        unit, _ = norm_unit(tok[0].astype(f32))
        here = (unit * gain[...] + shift[...]).astype(bf16)
        x[...] = here
        attn_in[0], attn_in[1] = core_split(here)

    for h in range(2):
        fetch(step, h).wait()
    total = (mm(x[...], ws[step]) + bias[...]).astype(bf16)
    qkv[...] = (total.astype(f32) * jnp.where(step == 0, scale, 1.0)).astype(bf16)


def project_qkv(at, tok, gain, shift, w, bias, scale, slot, total, earlier=()):
    _, n, d = tok.shape
    held = pl.BlockSpec(memory_space=pl.ANY)
    return pl.pallas_call(
        partial(qkv_body, scale),
        name="project_qkv",
        grid_spec=pltpu.PrefetchScalarGridSpec(
            num_scalar_prefetch=1,
            grid=(3,),
            in_specs=[
                pl.BlockSpec((1, n, d), lambda i, at: (at[0], 0, 0), pipeline_mode=pl.Buffered(1)),
                whole(gain.shape),
                whole(shift.shape),
                held,
                pl.BlockSpec((1, d), lambda i, at: (0, i)),
            ]
            + [held] * len(earlier),
            out_specs=[
                pl.BlockSpec((2, n, d // 2), lambda i, at: (0, slot, 0)),
                pl.BlockSpec((n, d), lambda i, at: (slot, i)),
            ],
            scratch_shapes=[
                pltpu.VMEM((n, d), bf16),
                pltpu.VMEM((3, d, d), bf16),
                pltpu.SemaphoreType.DMA((3, 2)),
            ],
        ),
        out_shape=[
            jax.ShapeDtypeStruct((2, total, d // 2), bf16),
            jax.ShapeDtypeStruct((total, 3 * d), bf16),
        ],
        input_output_aliases={6 + k: k for k in range(len(earlier))},
        compiler_params=params(),
        cost_estimate=pl.CostEstimate(
            flops=2 * n * d * 3 * d, bytes_accessed=6 * d * d + 10 * n * d, transcendentals=n
        ),
    )(at, tok, gain, shift, w, bias, *earlier)


def half_slot(own, half):
    return own if half == 0 else 1 - own


def pick(ref, own, block, size):
    half, sub = divmod(block, 2)
    return ref[half_slot(own, half), sub * size : (sub + 1) * size, :]


def head_mask(size):
    return lax.broadcasted_iota(jnp.int32, (size, LANES), 1) < LANES // 2


def block_penalty(tab, i, j):
    return jnp.where(tab[1 + 4 * i + j] > 0, 0.0, masked_score).astype(f32)


def stack_heads(x, low):
    zero = jnp.zeros_like(x)
    return jnp.concatenate([jnp.where(low, x, zero), jnp.where(low, zero, x)], axis=0)


def place(ref, own, *targets):
    half = ref.shape[1]
    for h in range(2):
        targets[0][h * half : (h + 1) * half, :] = ref[half_slot(own, h)]


def attend_body(tab, q, k, v, head_scale, heads_out, lse, kp, vp):
    size = q.shape[1] // 2
    own = tab[0]
    low = head_mask(size)
    causal = lax.broadcasted_iota(jnp.int32, (2 * size, size), 0) % size >= lax.broadcasted_iota(
        jnp.int32, (2 * size, size), 1
    )
    lane = lax.broadcasted_iota(jnp.int32, (size, LANES), 1)
    place(k, own, kp)
    place(v, own, vp)
    for i in range(4):
        width = (i + 1) * size
        s = mm(stack_heads(pick(q, own, i, size), low), kp[:width, :], NT)
        parts = [s[:, j * size : (j + 1) * size] + block_penalty(tab, i, j) for j in range(i)]
        parts.append(jnp.where(causal, s[:, i * size :], masked_score))
        top = parts[0]
        for part in parts[1:]:
            top = jnp.maximum(top, part)
        top = jnp.max(top, axis=1, keepdims=True)
        parts = [jnp.exp(part - top) for part in parts]
        total = fold(parts[0])
        for part in parts[1:]:
            total = total + fold(part)
        total = jnp.sum(total, axis=1, keepdims=True)
        p = jnp.concatenate([part.astype(bf16) for part in parts], axis=1)
        out = mm(p, vp[:width, :]) * (1.0 / total)
        both = jnp.where(low, out[:size], out[size:]) * head_scale[...]
        half, sub = divmod(i, 2)
        heads_out[half_slot(own, half), sub * size : (sub + 1) * size, :] = both.astype(bf16)
        logs = top + jnp.log(total)
        columns = jnp.where(lane == 0, logs[:size], logs[size:])
        lse[0, i] = jnp.transpose(columns)[:8]


def attend(tab, qkv, head_scale_row):
    _, half_len, wide = qkv.shape
    d = wide // 3
    pairs = d // LANES
    size = half_len // 2

    def lanes(first):
        return pl.BlockSpec((2, half_len, LANES), lambda p, t: (0, 0, first + p))

    flops = 16 * half_len * half_len * pairs * LANES
    return pl.pallas_call(
        attend_body,
        name="attend",
        grid_spec=pltpu.PrefetchScalarGridSpec(
            num_scalar_prefetch=1,
            grid=(pairs,),
            in_specs=[
                lanes(0),
                lanes(pairs),
                lanes(2 * pairs),
                pl.BlockSpec((1, LANES), lambda p, t: (0, p)),
            ],
            out_specs=[
                lanes(0),
                pl.BlockSpec((1, 4, 8, size), lambda p, t: (p, 0, 0, 0)),
            ],
            scratch_shapes=[pltpu.VMEM((2 * half_len, LANES), bf16)] * 2,
        ),
        out_shape=[
            jax.ShapeDtypeStruct((2, half_len, d), bf16),
            jax.ShapeDtypeStruct((pairs, 4, 8, size), f32),
        ],
        compiler_params=params(),
        cost_estimate=pl.CostEstimate(
            flops=flops * 4, bytes_accessed=8 * half_len * wide, transcendentals=8 * half_len * half_len * pairs
        ),
    )(tab, qkv, qkv, qkv, head_scale_row)


def attend_back_body(
    scale, tab, q, k, v, heads_out, d_out, inv_scale, lse, dqkv, dots, kp, vp, dk, dv
):
    size = q.shape[1] // 2
    own = tab[0]
    low = head_mask(size)
    causal = lax.broadcasted_iota(jnp.int32, (2 * size, size), 0) % size >= lax.broadcasted_iota(
        jnp.int32, (2 * size, size), 1
    )
    place(k, own, kp)
    place(v, own, vp)
    dots[...] = jnp.zeros_like(dots)
    for i in range(3, -1, -1):
        width = (i + 1) * size
        q2 = stack_heads(pick(q, own, i, size), low)
        gi = pick(d_out, own, i, size)
        g2 = stack_heads(gi, low)
        product = gi.astype(f32) * pick(heads_out, own, i, size).astype(f32) * inv_scale[...]
        dots[0, 0:1, :] += row_sum(product)
        zero = jnp.zeros_like(product)
        delta = jnp.concatenate(
            [
                jnp.sum(jnp.where(low, product, zero), axis=1, keepdims=True),
                jnp.sum(jnp.where(low, zero, product), axis=1, keepdims=True),
            ],
            axis=0,
        )
        columns = jnp.transpose(lse[0, i])
        logs = jnp.concatenate([columns[:, 0:1], columns[:, 1:2]], axis=0)
        s = mm(q2, kp[:width, :], NT)
        g = mm(g2, vp[:width, :], NT)
        ps, ds = [], []
        for j in range(i + 1):
            here = slice(j * size, (j + 1) * size)
            if j < i:
                p = jnp.exp(s[:, here] - (logs - block_penalty(tab, i, j)))
            else:
                p = jnp.exp(jnp.where(causal, s[:, here], masked_score) - logs)
            ps.append(p.astype(bf16))
            ds.append((p * (g[:, here] - delta)).astype(bf16))
        p = jnp.concatenate(ps, axis=1)
        d = jnp.concatenate(ds, axis=1)
        dv_part = mm(p, g2, TN)
        dk_part = mm(d, q2, TN)
        if i == 3:
            dv[...] = dv_part
            dk[...] = dk_part
        else:
            dv[:width, :] += dv_part
            dk[:width, :] += dk_part
        dq = mm(d, kp[:width, :]) * scale
        half, sub = divmod(i, 2)
        dqkv[0, half_slot(own, half), sub * size : (sub + 1) * size, :] = jnp.where(
            low, dq[:size], dq[size:]
        ).astype(bf16)
    for half in range(2):
        here = slice(half * 2 * size, (half + 1) * 2 * size)
        dqkv[1, half_slot(own, half)] = dk[here, :].astype(bf16)
        dqkv[2, half_slot(own, half)] = dv[here, :].astype(bf16)


def attend_back(tab, qkv, heads_out, d_out, inv_scale_row, lse, scale, group):
    _, half_len, wide = qkv.shape
    d = wide // 3
    every = d // LANES
    pairs = every // 2
    size = half_len // 2

    def pair(p):
        return p + 2 * (p // 2) + 2 * group

    def lanes(first):
        return pl.BlockSpec((2, half_len, LANES), lambda p, t: (0, 0, first + pair(p)))

    flops = 16 * half_len * half_len * pairs * LANES
    return pl.pallas_call(
        partial(attend_back_body, scale),
        name="attend_back",
        grid_spec=pltpu.PrefetchScalarGridSpec(
            num_scalar_prefetch=1,
            grid=(pairs,),
            in_specs=[
                lanes(0),
                lanes(every),
                lanes(2 * every),
                lanes(0),
                lanes(0),
                pl.BlockSpec((1, LANES), lambda p, t: (0, pair(p))),
                pl.BlockSpec((1, 4, 8, size), lambda p, t: (pair(p), 0, 0, 0)),
            ],
            out_specs=[
                pl.BlockSpec((3, 2, half_len, LANES), lambda p, t: (0, 0, 0, p)),
                pl.BlockSpec((1, 8, LANES), lambda p, t: (p, 0, 0)),
            ],
            scratch_shapes=[pltpu.VMEM((2 * half_len, LANES), bf16)] * 2
            + [pltpu.VMEM((2 * half_len, LANES), f32)] * 2,
        ),
        out_shape=[
            jax.ShapeDtypeStruct((3, 2, half_len, d // 2), bf16),
            jax.ShapeDtypeStruct((pairs, 8, LANES), f32),
        ],
        compiler_params=params(),
        cost_estimate=pl.CostEstimate(
            flops=flops * 10, bytes_accessed=8 * half_len * wide, transcendentals=8 * half_len * half_len * pairs
        ),
    )(tab, qkv, qkv, qkv, heads_out, d_out, inv_scale_row, lse)


def gelu_parts(v):
    a = jnp.abs(v)
    t = 1.0 / (1.0 + (0.3275911 * 0.7071067811865476) * a)
    bell = jnp.exp(v * v * -0.5)
    poly = ((((1.061405429 * t - 1.453152027) * t + 1.421413741) * t - 0.284496736) * t + 0.254829592) * t
    tail = (0.5 * poly) * bell
    cdf = jnp.where(v < 0, tail, 1.0 - tail)
    return v * cdf, cdf + v * (bell * 0.3989422804014327)


def middle_body(
    at, ho, tok, cot, out_w, w1, w2, vec, vec4, *refs
):
    (
        output, grad_middle, sums, sums4, ffn_in, heads_in, mid_out, grad_hidden, grad_proj, d_out,
        act, slope, back, acc, unit_b, stats, total, total_u, w1s, w2s, sems,
    ) = refs[-21:]
    ho, tok, cot, d_out = (ref.at[0] for ref in (ho, tok, cot, d_out))
    output = output.at[0] if len(output.shape) == 3 else output
    step = pl.program_id(0)
    n, d = ho.shape
    chunks, _, fc = w1s.shape
    ff = fc * chunks
    c = step % chunks
    ahead = 2

    def fetch(k):
        columns = pl.ds(pl.multiple_of(k * fc, fc), fc)
        return (
            pltpu.make_async_copy(w1.at[:, columns], w1s.at[k], sems.at[0, k]),
            pltpu.make_async_copy(w2.at[columns, :], w2s.at[k], sems.at[1, k]),
        )
    strip = 128
    strips = n // strip

    def v(r):
        return vec[r : r + 1, :]

    def rows(t):
        return pl.ds(pl.multiple_of(t * strip, strip), strip)

    @pl.when(step == 0)
    def _():
        for k in range(ahead):
            for copy in fetch(k):
                copy.start()
        sums[...] = jnp.zeros_like(sums)
        acc[...] = mm(ho[...], out_w[...])

        def one(t, _):
            r = rows(t)
            unit_attn, inverse_attn = norm_unit(acc[r, :] + v(0))
            middle = tok[r, :].astype(f32) + (unit_attn * v(1) + v(2))
            unit_two, inverse_two = norm_unit(middle)
            x = (unit_two * v(3) + v(4)).astype(bf16)
            grad_middle[r, :] = unit_attn
            unit_b[r, :] = unit_two
            stats[r, 0:1] = inverse_attn
            stats[r, 1:2] = inverse_two
            acc[r, :] = middle + v(5)
            d_out[r, :] = x
            ffn_in[0, r, :], ffn_in[1, r, :] = core_split(x)
            heads_in[0, r, :], heads_in[1, r, :] = core_split(ho[r, :])
            return 0

        lax.fori_loop(0, strips, one, 0)

    @pl.when(step < chunks - ahead)
    def _():
        for copy in fetch(step + ahead):
            copy.start()

    @pl.when(step < chunks)
    def _():
        for copy in fetch(step):
            copy.wait()
        h = mm(d_out[...], w1s[c]) + vec4[0:1, :]
        back[c] = mm(cot[...], w2s[c], NT).astype(back.dtype)
        a, b = gelu_parts(h)
        act[c] = a
        slope[c] = b.astype(slope.dtype)

    @pl.when(step == 0)
    def _():
        total[...] = jnp.zeros_like(total)

    @pl.when(step < chunks)
    def _():
        total[...] += fold(act[c])

    @pl.when(step == chunks)
    def _():
        mean = jnp.sum(total[...], axis=1, keepdims=True) * (1.0 / ff)

        def one(k, t):
            centered = act[k] - mean
            return t + fold(centered * centered)

        square = lax.fori_loop(0, chunks, one, jnp.zeros_like(total))
        stats[:, 2:3] = mean
        stats[:, 3:4] = lax.rsqrt(jnp.sum(square, axis=1, keepdims=True) * (1.0 / ff) + eps)
        total[...] = jnp.zeros_like(total)
        total_u[...] = jnp.zeros_like(total_u)

    here = pl.ds(pl.multiple_of(c * fc, fc), fc)

    @pl.when((step >= chunks) & (step < 2 * chunks))
    def _():
        u = (act[c] - stats[:, 2:3]) * stats[:, 3:4]
        act[c] = u
        gain = vec4[1:2, :]
        m = (u * gain + vec4[2:3, :]).astype(bf16)
        mid_out[...] = m
        acc[...] += mm(m, w2s[c])
        gm = back[c].astype(f32)
        gmu = gm * u
        sums4[1:2, here] = row_sum(gmu)
        sums4[2:3, here] = row_sum(gm)
        total[...] += fold(gm * gain)
        total_u[...] += fold(gmu * gain)

    @pl.when(step == 2 * chunks)
    def _():
        stats[:, 4:5] = jnp.sum(total[...], axis=1, keepdims=True) * (1.0 / ff)
        stats[:, 5:6] = jnp.sum(total_u[...], axis=1, keepdims=True) * (1.0 / ff)
        output[...] = acc[...].astype(output.dtype)
        acc[...] = jnp.zeros_like(acc)

    @pl.when(step >= 2 * chunks)
    def _():
        e = back[c].astype(f32) * vec4[1:2, :]
        grad_act = stats[:, 3:4] * (e - stats[:, 4:5] - act[c] * stats[:, 5:6])
        gh = (grad_act * slope[c].astype(f32)).astype(bf16)
        grad_hidden[...] = gh
        sums4[0:1, here] = row_sum(gh.astype(f32))
        acc[...] += mm(gh, w1s[c], NT)

    @pl.when(step == 3 * chunks - 1)
    def _():
        def one(t, _):
            r = rows(t)
            grad_ffn_in = acc[r, :]
            unit_two = unit_b[r, :]
            unit_attn = grad_middle[r, :]
            gout = cot[r, :].astype(f32)
            sums[5:6, :] += row_sum(gout)
            sums[3:4, :] += row_sum(grad_ffn_in * unit_two)
            sums[4:5, :] += row_sum(grad_ffn_in)
            gmid = gout + norm_back(grad_ffn_in, unit_two, stats[r, 1:2], v(3))
            grad_middle[r, :] = gmid
            sums[1:2, :] += row_sum(gmid * unit_attn)
            sums[2:3, :] += row_sum(gmid)
            gp = norm_back(gmid, unit_attn, stats[r, 0:1], v(1)).astype(bf16)
            grad_proj[r, :] = gp
            sums[0:1, :] += row_sum(gp.astype(f32))
            return 0

        lax.fori_loop(0, strips, one, 0)
        d_out[...] = (mm(grad_proj[...], out_w[...], NT) * v(6)).astype(bf16)


def middle_pass(at, ho, tok, cot, out_w, w1, w2, vec, vec4, slot, last_part, earlier=(), fc=1024):
    _, n, d = ho.shape
    ff = w1.shape[1]
    chunks = ff // fc
    last = chunks - 1
    rows = whole((n, d))
    held = pl.BlockSpec(memory_space=pl.ANY)

    def once(shape, index):
        return pl.BlockSpec(shape, index, pipeline_mode=pl.Buffered(1))

    in_place = once((1, n, d), lambda t, at: (at[0], 0, 0))
    in_slot = once((1, n, d), lambda t, at: (slot, 0, 0))
    split = once((2, n, d // 2), lambda t, at: (0, slot, 0))
    kind = f32 if last_part else bf16
    return pl.pallas_call(
        middle_body,
        name="middle_pass",
        grid_spec=pltpu.PrefetchScalarGridSpec(
            num_scalar_prefetch=1,
            grid=(3 * chunks,),
            in_specs=[
                in_slot,
                in_place,
                in_place,
                whole(out_w.shape),
                held,
                held,
                whole(vec.shape),
                pl.BlockSpec((vec4.shape[0], fc), lambda t, at: (0, t % chunks)),
            ]
            + [held] * len(earlier),
            out_specs=[
                in_place if last_part else rows,
                rows,
                whole((8, d)),
                whole((8, ff)),
                split,
                split,
                pl.BlockSpec((n, fc), lambda t, at: (slot, jnp.clip(t - chunks, 0, last))),
                pl.BlockSpec((n, fc), lambda t, at: (slot, jnp.clip(t - 2 * chunks, 0, last))),
                once((n, d), lambda t, at: (slot, 0)),
                in_slot,
            ],
            scratch_shapes=[
                pltpu.VMEM((chunks, n, fc), f32),
                pltpu.VMEM((chunks, n, fc), bf16),
                pltpu.VMEM((chunks, n, fc), bf16),
                pltpu.VMEM((n, d), f32),
                pltpu.VMEM((n, d), f32),
                pltpu.VMEM((n, LANES), f32),
                pltpu.VMEM((n, LANES), f32),
                pltpu.VMEM((n, LANES), f32),
                pltpu.VMEM((chunks, d, fc), bf16),
                pltpu.VMEM((chunks, fc, d), bf16),
                pltpu.SemaphoreType.DMA((2, chunks)),
            ],
        ),
        out_shape=[
            jax.ShapeDtypeStruct((2, n, d) if last_part else (n, d), kind),
            jax.ShapeDtypeStruct((n, d), f32),
            jax.ShapeDtypeStruct((8, d), f32),
            jax.ShapeDtypeStruct((8, ff), f32),
            jax.ShapeDtypeStruct((2, 2 * n, d // 2), bf16),
            jax.ShapeDtypeStruct((2, 2 * n, d // 2), bf16),
            jax.ShapeDtypeStruct((2 * n, ff), bf16),
            jax.ShapeDtypeStruct((2 * n, ff), bf16),
            jax.ShapeDtypeStruct((2 * n, d), bf16),
            jax.ShapeDtypeStruct((2, n, d), bf16),
        ],
        input_output_aliases={9 + k: 4 + k for k in range(len(earlier))},
        compiler_params=params(62),
        cost_estimate=pl.CostEstimate(
            flops=8 * n * d * ff + 4 * n * d * d,
            bytes_accessed=4 * d * ff + 2 * d * d + 4 * n * ff + 20 * n * d,
            transcendentals=2 * n * ff,
        ),
    )(at, ho, tok, cot, out_w, w1, w2, vec, vec4, *earlier)


def first_back_body(at, even, odd, w, tok, grad_middle, gain, tokens_grad, sums):
    @pl.when(pl.program_id(0) == 0)
    def _():
        sums[...] = jnp.zeros_like(sums)

    d = w.shape[0]
    run = d // 4
    grad = None
    for part in range(3):
        for r in range(4):
            piece = (even, odd)[r % 2][part, :, (r // 2) * run : (r // 2 + 1) * run]
            here = r * run
            term = mm(piece, w[:, part * d + here : part * d + here + run], NT)
            grad = term if grad is None else grad + term
            if part != 1:
                at = 2 + part // 2
                sums[at : at + 1, here : here + run] += row_sum(piece.astype(f32))
    unit, inverse = norm_unit(tok[0].astype(f32))
    sums[0:1, :] += row_sum(grad * unit)
    sums[1:2, :] += row_sum(grad)
    whole_grad = grad_middle[...] + norm_back(grad, unit, inverse, gain[...])
    if len(tokens_grad.shape) == 3:
        tokens_grad[0] = whole_grad
    else:
        tokens_grad[...] = whole_grad.astype(tokens_grad.dtype)


def first_back(at, even, odd, w, tok, grad_middle, gain, slot, last_part, tb=256):
    d = w.shape[0]
    n = even.shape[1] // 2
    first = slot * (n // tb)
    half = pl.BlockSpec((3, tb, d // 2), lambda i, at: (0, first + i, 0))
    rows = pl.BlockSpec((tb, d), lambda i, at: (i, 0))
    in_place = pl.BlockSpec((1, tb, d), lambda i, at: (at[0], i, 0))
    return pl.pallas_call(
        first_back_body,
        name="first_back",
        grid_spec=pltpu.PrefetchScalarGridSpec(
            num_scalar_prefetch=1,
            grid=(n // tb,),
            in_specs=[half, half, whole(w.shape), in_place, rows, whole(gain.shape)],
            out_specs=[in_place if last_part else rows, whole((8, d))],
        ),
        out_shape=[
            jax.ShapeDtypeStruct((2, n, d), f32) if last_part else jax.ShapeDtypeStruct((n, d), bf16),
            jax.ShapeDtypeStruct((8, d), f32),
        ],
        compiler_params=params(),
        cost_estimate=pl.CostEstimate(
            flops=6 * n * d * d, bytes_accessed=6 * d * d + 16 * n * d, transcendentals=n
        ),
    )(at, even, odd, w, tok, grad_middle, gain)


def after(x, *others):
    return lax.optimization_barrier((x,) + others)[0]


def weight_grad_body(a_count, b_count, halves, received_too, tab, *refs):
    def joined(parts, axis=1):
        parts = [x[0] if len(x.shape) == 3 else x[...] for x in parts]
        return parts[0] if len(parts) == 1 else jnp.concatenate(parts, axis=axis)

    rhs = joined(refs[a_count : a_count + b_count], 0 if halves else 1)
    total = mm(joined(refs[:a_count]), rhs, TN)
    if not received_too:
        refs[-1][0] = total.astype(bf16)
        return
    received, send, keep = refs[-3:]
    total = (total + received[0].astype(f32)).astype(bf16)

    @pl.when(pl.program_id(0) == 0)
    def _():
        send[...] = total

    @pl.when(pl.program_id(0) == 1)
    def _():
        keep[...] = total


def weight_grad(tab, a, b, a_blocks, b_blocks, out_block, shape, steps, received=None):
    flops = 2 * a.shape[-2] * 2 * shape[0] * shape[1]
    out_index = out_block[1]
    halves = isinstance(b, tuple)
    bs = b if halves else (b,) * len(b_blocks)
    moved = 2 * (a.size + bs[0].size) + 4 * shape[0] * shape[1]
    part = pl.BlockSpec((1,) + out_block[0], lambda s, i, t: (s,) + out_index(i))
    in_specs = [pl.BlockSpec(*spec) for spec in (*a_blocks, *b_blocks)]
    args = [tab] + [a] * len(a_blocks) + list(bs)
    if received is None:
        out_specs = part
        out_shape = jax.ShapeDtypeStruct((2,) + shape, bf16)
    else:
        in_specs.append(part)
        args.append(received)
        last = steps - 1
        out_specs = [
            pl.BlockSpec(out_block[0], lambda s, i, t: out_index(jnp.where(s == 0, i, last))),
            pl.BlockSpec(out_block[0], lambda s, i, t: out_index(jnp.where(s == 0, 0, i))),
        ]
        out_shape = [jax.ShapeDtypeStruct(shape, bf16)] * 2
    return pl.pallas_call(
        partial(weight_grad_body, len(a_blocks), len(b_blocks), halves, received is not None),
        name="weight_grad",
        grid_spec=pltpu.PrefetchScalarGridSpec(
            num_scalar_prefetch=1, grid=(2, steps), in_specs=in_specs, out_specs=out_specs
        ),
        out_shape=out_shape,
        compiler_params=params(),
        cost_estimate=pl.CostEstimate(flops=flops, bytes_accessed=moved, transcendentals=0),
    )(*args)


def part_of(s, t, at):
    return jnp.where(s == 0, 1 - t[at], t[at])


def tall_how(n, d, ff):
    tall = ff // 16

    def run(k):
        return ((n, tall), lambda s, i, t: (0, ((2 * i + k) * 2 + part_of(s, t, 1)) * 2 + t[0]))

    return (
        [run(0), run(1)],
        [
            ((1, n // 2, d), lambda s, i, t: (t[2], 0, 0)),
            ((1, n // 2, d), lambda s, i, t: (0, 0, 0)),
        ],
        ((2 * tall, d), lambda i: (i, 0)),
        (4 * tall, d),
        2,
    )


def flat_how(n, d, width):
    tn = d // 2
    count = 2 if width > 2 * d else 1
    steps = width // (2 * tn * count)

    def columns(k):
        return ((n, tn), lambda s, i, t: (0, (part_of(s, t, 2) * steps + i) * count + k))

    return (
        [((1, n, d // 2), lambda s, i, t: (t[0], 0, 0))],
        [columns(k) for k in range(count)],
        ((d // 2, tn * count), lambda i: (0, i)),
        (d // 2, steps * tn * count),
        steps,
    )


def qkv_how(n, d):
    run = d // 4

    def columns(k):
        def index(s, i, t):
            at = part_of(s, t, 2) * 3 + k
            return at // 2, 0, at % 2

        return ((1, n, run), index)

    return (
        [((1, n, d // 2), lambda s, i, t: (t[0], 0, 0))],
        [columns(k) for k in range(3)],
        ((d // 2, 3 * run), lambda i: (0, 0)),
        (d // 2, 3 * run),
        1,
    )


def running_sums(lengths):
    count = lengths.shape[1]
    upto = jnp.arange(count)[:, None] >= jnp.arange(count)[None, :]
    return jnp.sum(jnp.where(upto[None], lengths[:, None, :], 0), axis=2).astype(jnp.int32)


def norm_forward(values, gain, shift):
    average = jnp.mean(values, axis=-1, keepdims=True)
    centered = values - average
    inverse = lax.rsqrt(jnp.mean(centered * centered, axis=-1, keepdims=True) + eps)
    normed = centered * inverse
    return (normed * gain + shift, normed, inverse)


def norm_backward(grad_y, normed, inverse, gain):
    scaled = grad_y * gain
    grad_in = inverse * (
        scaled
        - jnp.mean(scaled, axis=-1, keepdims=True)
        - normed * jnp.mean(scaled * normed, axis=-1, keepdims=True)
    )
    return (grad_in, jnp.sum(grad_y * normed, axis=(0, 1)), jnp.sum(grad_y, axis=(0, 1)))


def local_general(
    tokens,
    cotangent,
    doc_lengths,
    norm1_gain,
    norm1_shift,
    qkv_weight,
    query_bias,
    value_bias,
    head_scales,
    out_weight,
    out_bias,
    attn_gain,
    attn_shift,
    norm2_gain,
    norm2_shift,
    fc1_weight,
    fc1_bias,
    mid_gain,
    mid_shift,
    fc2_weight,
    fc2_bias,
):
    f32 = jnp.float32
    bf16 = jnp.bfloat16
    batch_size, local_len, model_width = tokens.shape
    head_count = head_scales.shape[0]
    head_dim = model_width // head_count
    score_scale = head_dim ** (-0.5)
    row_len = local_len * lax.axis_size("blk")
    row_first = lax.axis_index("blk") * local_len
    query_pos = row_first + jnp.arange(local_len, dtype=jnp.int32)
    doc_ends = running_sums(doc_lengths)
    starts = jnp.max(
        jnp.where(doc_ends[:, None, :] <= query_pos[None, :, None], doc_ends[:, None, :], 0), axis=2
    )
    lowest = jnp.min(starts[:, 0])
    query_last = row_first + local_len - 1
    inputs = tokens.astype(f32)
    attn_norm, unit_one, inverse_one = norm_forward(inputs, norm1_gain, norm1_shift)
    attn_in = attn_norm.astype(bf16)
    projected = jnp.dot(attn_in, qkv_weight, preferred_element_type=f32)
    queries = (
        (projected[..., :model_width] + query_bias)
        .astype(bf16)
        .reshape(batch_size, local_len, head_count, head_dim)
    )
    keys_low = projected[..., model_width : 2 * model_width].astype(bf16)
    values_low = (projected[..., 2 * model_width :] + value_bias).astype(bf16)

    def block_scores(key_piece, offset):
        key_len = key_piece.shape[1]
        keys_head = key_piece.reshape(batch_size, key_len, head_count, head_dim)
        raw_scores = (
            jnp.einsum("bqhd,bkhd->bhqk", queries, keys_head, preferred_element_type=f32)
            * score_scale
        )
        key_pos = offset + jnp.arange(key_len, dtype=jnp.int32)
        allowed = (key_pos[None, None, :] <= query_pos[None, :, None]) & (
            key_pos[None, None, :] >= starts[:, :, None]
        )
        return (jnp.where(allowed[:, None], raw_scores, masked_score), keys_head)

    def is_live(offset, key_len):
        return (offset <= query_last) & (offset + key_len - 1 >= lowest)

    def attend_slab(running, key_piece, value_piece, offset):
        key_len = key_piece.shape[1]

        def attend_compute(state):
            running_max, running_sum, weighted = state
            scores, keys_head = block_scores(key_piece, offset)
            new_max = jnp.maximum(running_max, jnp.max(scores, axis=3))
            rescale = jnp.exp(running_max - new_max)
            weights = jnp.exp(scores - new_max[..., None])
            values_head = value_piece.reshape(batch_size, key_len, head_count, head_dim)
            update = jnp.einsum(
                "bhqk,bkhd->bqhd", weights.astype(bf16), values_head, preferred_element_type=f32
            )
            rescale_t = jnp.transpose(rescale, (0, 2, 1))[..., None]
            return (
                new_max,
                running_sum * rescale + jnp.sum(weights, axis=3),
                weighted * rescale_t + update,
            )

        return lax.cond(is_live(offset, key_len), attend_compute, lambda state: state, running)

    start_state = (
        jnp.full((batch_size, head_count, local_len), masked_score, f32),
        jnp.zeros((batch_size, head_count, local_len), f32),
        jnp.zeros((batch_size, local_len, head_count, head_dim), f32),
    )
    key_piece = lax.all_gather(keys_low, "blk", axis=1, tiled=True)
    value_piece = lax.all_gather(values_low, "blk", axis=1, tiled=True)
    turns = key_piece.shape[1] // local_len

    def one_turn(index, state):
        begin = index * local_len
        key_slab = lax.dynamic_slice_in_dim(key_piece, begin, local_len, 1)
        value_slab = lax.dynamic_slice_in_dim(value_piece, begin, local_len, 1)
        return attend_slab(state, key_slab, value_slab, begin)

    running_max, running_sum, weighted = lax.fori_loop(0, turns, one_turn, start_state)
    attended = weighted / jnp.transpose(running_sum, (0, 2, 1))[..., None]
    log_total = running_max + jnp.log(running_sum)
    heads_out = (
        (attended * head_scales[:, None]).reshape(batch_size, local_len, model_width).astype(bf16)
    )
    projection = jnp.dot(heads_out, out_weight, preferred_element_type=f32) + out_bias
    branch, unit_attn, inverse_attn = norm_forward(projection, attn_gain, attn_shift)
    middle = inputs + branch
    ffn_norm, unit_two, inverse_two = norm_forward(middle, norm2_gain, norm2_shift)
    ffn_in = ffn_norm.astype(bf16)
    hidden = jnp.dot(ffn_in, fc1_weight, preferred_element_type=f32) + fc1_bias
    activated, gelu_grad = jax.vjp(partial(jax.nn.gelu, approximate=False), hidden)
    mid_norm, unit_mid, inverse_mid = norm_forward(activated, mid_gain, mid_shift)
    mid_out = mid_norm.astype(bf16)
    output = middle + jnp.dot(mid_out, fc2_weight, preferred_element_type=f32) + fc2_bias
    grad_output = cotangent.astype(f32)
    fc2_weight_grad = jnp.einsum("bcf,bcd->fd", mid_out, cotangent, preferred_element_type=f32)
    fc2_bias_grad = jnp.sum(grad_output, axis=(0, 1))
    grad_mid = jnp.einsum("bcd,fd->bcf", cotangent, fc2_weight, preferred_element_type=f32)
    grad_act, mid_gain_grad, mid_shift_grad = norm_backward(
        grad_mid, unit_mid, inverse_mid, mid_gain
    )
    grad_hidden = gelu_grad(grad_act)[0].astype(bf16)
    fc1_weight_grad = jnp.einsum("bcd,bcf->df", ffn_in, grad_hidden, preferred_element_type=f32)
    fc1_bias_grad = jnp.sum(grad_hidden.astype(f32), axis=(0, 1))
    grad_ffn_in = jnp.einsum("bcf,df->bcd", grad_hidden, fc1_weight, preferred_element_type=f32)
    grad_two, norm2_gain_grad, norm2_shift_grad = norm_backward(
        grad_ffn_in, unit_two, inverse_two, norm2_gain
    )
    grad_middle = grad_output + grad_two
    grad_proj_f, attn_gain_grad, attn_shift_grad = norm_backward(
        grad_middle, unit_attn, inverse_attn, attn_gain
    )
    grad_projection = grad_proj_f.astype(bf16)
    out_weight_grad = jnp.einsum(
        "bcd,bce->de", heads_out, grad_projection, preferred_element_type=f32
    )
    out_bias_grad = jnp.sum(grad_projection.astype(f32), axis=(0, 1))
    grad_heads = jnp.einsum(
        "bce,de->bcd", grad_projection, out_weight, preferred_element_type=f32
    ).reshape(batch_size, local_len, head_count, head_dim)
    head_scales_grad = jnp.sum(grad_heads * attended, axis=(0, 1, 3))
    grad_attended = (grad_heads * head_scales[:, None]).astype(bf16)
    row_dot = jnp.transpose(jnp.sum(grad_attended.astype(f32) * attended, axis=3), (0, 2, 1))

    def back_slab(running, key_piece, value_piece, offset):
        key_len = key_piece.shape[1]

        def back_compute(state):
            grad_queries, kv_buffer = state
            scores, keys_head = block_scores(key_piece, offset)
            attn_probs = jnp.exp(scores - log_total[..., None])
            values_head = value_piece.reshape(batch_size, key_len, head_count, head_dim)
            grad_probs = jnp.einsum(
                "bqhd,bkhd->bhqk", grad_attended, values_head, preferred_element_type=f32
            )
            grad_scores = (attn_probs * (grad_probs - row_dot[..., None])).astype(bf16)
            grad_queries = (
                grad_queries
                + jnp.einsum("bhqk,bkhd->bqhd", grad_scores, keys_head, preferred_element_type=f32)
                * score_scale
            )
            grad_keys = (
                jnp.einsum("bhqk,bqhd->bkhd", grad_scores, queries, preferred_element_type=f32)
                * score_scale
            )
            grad_values = jnp.einsum(
                "bhqk,bqhd->bkhd",
                attn_probs.astype(bf16),
                grad_attended,
                preferred_element_type=f32,
            )
            addition = jnp.concatenate(
                [
                    grad_keys.reshape(batch_size, key_len, model_width),
                    grad_values.reshape(batch_size, key_len, model_width),
                ],
                axis=2,
            )
            previous = lax.dynamic_slice_in_dim(kv_buffer, offset, key_len, 1)
            return (
                grad_queries,
                lax.dynamic_update_slice_in_dim(kv_buffer, previous + addition, offset, 1),
            )

        return lax.cond(is_live(offset, key_len), back_compute, lambda state: state, running)

    back_state = (
        jnp.zeros((batch_size, local_len, head_count, head_dim), f32),
        jnp.zeros((batch_size, row_len, 2 * model_width), f32),
    )
    attend_key_piece = lax.all_gather(keys_low, "blk", axis=1, tiled=True)
    attend_value_piece = lax.all_gather(values_low, "blk", axis=1, tiled=True)
    turns = attend_key_piece.shape[1] // local_len

    def one_turn(index, state):
        begin = index * local_len
        key_slab = lax.dynamic_slice_in_dim(attend_key_piece, begin, local_len, 1)
        value_slab = lax.dynamic_slice_in_dim(attend_value_piece, begin, local_len, 1)
        return back_slab(state, key_slab, value_slab, begin)

    grad_queries, kv_buffer = lax.fori_loop(0, turns, one_turn, back_state)
    grad_kv = lax.psum_scatter(
        kv_buffer.astype(jnp.bfloat16), "blk", scatter_dimension=1, tiled=True
    ).astype(jnp.float32)
    grad_qkv = jnp.concatenate(
        [grad_queries.reshape(batch_size, local_len, model_width), grad_kv], axis=2
    ).astype(bf16)
    qkv_weight_grad = jnp.einsum("bcd,bce->de", attn_in, grad_qkv, preferred_element_type=f32)
    query_bias_grad = jnp.sum(grad_qkv[..., :model_width].astype(f32), axis=(0, 1))
    value_bias_grad = jnp.sum(grad_qkv[..., 2 * model_width :].astype(f32), axis=(0, 1))
    grad_attn_in = jnp.einsum("bce,de->bcd", grad_qkv, qkv_weight, preferred_element_type=f32)
    grad_one, norm1_gain_grad, norm1_shift_grad = norm_backward(
        grad_attn_in, unit_one, inverse_one, norm1_gain
    )
    tokens_grad = grad_middle + grad_one
    matrix_grads = (qkv_weight_grad, out_weight_grad, fc1_weight_grad, fc2_weight_grad)
    reduced = (
        lax.psum_scatter(
            matrix_grads[0].astype(jnp.bfloat16), "dp", scatter_dimension=0, tiled=True
        ).astype(jnp.float32),
        lax.psum_scatter(
            matrix_grads[1].astype(jnp.bfloat16), "dp", scatter_dimension=0, tiled=True
        ).astype(jnp.float32),
        lax.psum_scatter(
            matrix_grads[2].astype(jnp.bfloat16), "dp", scatter_dimension=0, tiled=True
        ).astype(jnp.float32),
        lax.psum_scatter(
            matrix_grads[3].astype(jnp.bfloat16), "dp", scatter_dimension=0, tiled=True
        ).astype(jnp.float32),
    )
    reduced = (
        lax.psum_scatter(
            reduced[0].astype(jnp.bfloat16), "blk", scatter_dimension=1, tiled=True
        ).astype(jnp.float32),
        lax.psum_scatter(
            reduced[1].astype(jnp.bfloat16), "blk", scatter_dimension=1, tiled=True
        ).astype(jnp.float32),
        lax.psum_scatter(
            reduced[2].astype(jnp.bfloat16), "blk", scatter_dimension=1, tiled=True
        ).astype(jnp.float32),
        lax.psum_scatter(
            reduced[3].astype(jnp.bfloat16), "blk", scatter_dimension=1, tiled=True
        ).astype(jnp.float32),
    )
    small_sums = lax.psum(
        (
            norm1_gain_grad,
            norm1_shift_grad,
            query_bias_grad,
            value_bias_grad,
            head_scales_grad,
            out_bias_grad,
            attn_gain_grad,
            attn_shift_grad,
            norm2_gain_grad,
            norm2_shift_grad,
            fc1_bias_grad,
            mid_gain_grad,
            mid_shift_grad,
            fc2_bias_grad,
        ),
        ("dp", "blk"),
    )
    return (
        output,
        tokens_grad,
        small_sums[0],
        small_sums[1],
        reduced[0],
        small_sums[2],
        small_sums[3],
        small_sums[4],
        reduced[1],
        small_sums[5],
        small_sums[6],
        small_sums[7],
        small_sums[8],
        small_sums[9],
        reduced[2],
        small_sums[10],
        small_sums[11],
        small_sums[12],
        reduced[3],
        small_sums[13],
    )


swap = ((0, 1), (1, 0))


def exchange(x):
    return lax.ppermute(x, "blk", swap)


def flip(x, bit):
    return lax.ppermute(x, "dp", [(i, i ^ bit) for i in range(16)])


def local_rows(
    tokens,
    cotangent,
    doc_lengths,
    norm1_gain,
    norm1_shift,
    qkv_weight,
    query_bias,
    value_bias,
    head_scales,
    out_weight,
    out_bias,
    attn_gain,
    attn_shift,
    norm2_gain,
    norm2_shift,
    fc1_weight,
    fc1_bias,
    mid_gain,
    mid_shift,
    fc2_weight,
    fc2_bias,
):
    _, half_len, d = tokens.shape
    ff = fc1_weight.shape[1]
    heads = head_scales.shape[0]
    head_dim = d // heads
    scale = head_dim**-0.5
    n = 2 * half_len
    b = lax.axis_index("blk").astype(jnp.int32)
    dp = lax.axis_index("dp").astype(jnp.int32)
    core, x, z, y = dp % 2, (dp // 2) % 2, dp // 4, b

    tok_in = exchange(lax.dynamic_slice_in_dim(tokens, 1 - b, 1, 0))
    cot_in = exchange(lax.dynamic_slice_in_dim(cotangent, 1 - b, 1, 0))
    kept_at = b[None]
    sent_at = jnp.zeros((1,), jnp.int32)

    lengths = lax.dynamic_slice_in_dim(doc_lengths, b, 1, 0)
    ends = running_sums(lengths)[0]
    firsts = (half_len // 2) * jnp.arange(4, dtype=jnp.int32)
    starts = jnp.max(jnp.where(ends[None, :] <= firsts[:, None], ends[None, :], 0), axis=1)
    allowed = (firsts[None, :] >= starts[:, None]).astype(jnp.int32)
    tab = jnp.concatenate([b[None], allowed.reshape(16)])
    theirs = jnp.stack([1 - core, x, y])
    mine = jnp.stack([core, x, y])

    def line(v):
        return v.reshape(1, -1)

    scale_row = jnp.broadcast_to(head_scales[:, None], (heads, head_dim)).reshape(1, d)
    vec = jnp.stack(
        [out_bias, attn_gain, attn_shift, norm2_gain, norm2_shift, fc2_bias, scale_row[0], out_bias]
    )
    vec4 = jnp.stack([fc1_bias, mid_gain, mid_shift, fc1_bias])
    qkv_bias = jnp.concatenate([query_bias, jnp.zeros_like(query_bias), value_bias])

    first_args = (line(norm1_gain), line(norm1_shift), qkv_weight, line(qkv_bias), scale)
    early = project_qkv(kept_at, tokens, *first_args, 0, n)
    attn_in, qkv = project_qkv(sent_at, tok_in, *first_args, 1, n, early)
    qkv = qkv.reshape(2, half_len, 3 * d)
    heads_out, logs = attend(tab, qkv, scale_row)

    weights = (out_weight, fc1_weight, fc2_weight, vec, vec4)
    out_sent, mid_sent, *more = middle_pass(sent_at, heads_out, tok_in, cot_in, *weights, 1, False)
    sums, sums4, *earlier = more
    out_back = exchange(out_sent)
    output, mid_kept, *more = middle_pass(
        kept_at, heads_out, tokens, cotangent, *weights, 0, True, earlier
    )
    sums = sums + more[0]
    sums4 = sums4 + more[1]
    ffn_in, heads_in, mid_out, grad_hidden, grad_proj, d_out = more[2:]

    def fill(kept, back):
        return lax.dynamic_update_slice_in_dim(kept, back.astype(f32)[None], 1 - b, 0)

    def z_stage(parts):
        total = lax.dynamic_index_in_dim(parts, z, 0, keepdims=False).astype(f32)
        for k in (1, 2, 3):
            total = total + flip(lax.dynamic_index_in_dim(parts, z ^ k, 0, keepdims=False), 4 * k).astype(f32)
        return total

    def rows_by_x(total):
        total = total.astype(bf16).reshape(4, 2, -1, total.shape[1])
        return (
            lax.dynamic_index_in_dim(total, 1 - x, 1, keepdims=False),
            lax.dynamic_index_in_dim(total, x, 1, keepdims=False),
        )

    def columns_by_y(total):
        total = total.astype(bf16)
        total = total.reshape(4, -1, total.shape[-1])
        width = total.shape[2] // 2
        return (
            lax.dynamic_slice_in_dim(total, (1 - y) * width, width, 2),
            lax.dynamic_slice_in_dim(total, y * width, width, 2),
        )

    def add_x(send, keep):
        return keep.astype(f32) + flip(send, 2).astype(f32)

    def add_y(send, keep):
        return keep.astype(f32) + exchange(send).astype(f32)

    tall, flat4, flat1, qkv3 = (
        tall_how(n, d, ff), flat_how(n, d, ff), flat_how(n, d, d), qkv_how(n, d)
    )
    cots = (cotangent, cot_in)
    fc2_theirs = weight_grad(theirs, mid_out, cots, *tall)
    ffn_in = after(ffn_in, fc2_theirs)
    fc1_theirs = weight_grad(theirs, ffn_in, grad_hidden, *flat4)
    mid_out = after(mid_out, fc1_theirs)
    fc2_parts = weight_grad(mine, mid_out, cots, *tall, flip(fc2_theirs, 1))
    heads_in = after(heads_in, *fc2_parts)
    out_theirs = weight_grad(theirs, heads_in, grad_proj, *flat1)
    ffn_in = after(ffn_in, out_theirs)
    fc1_parts = weight_grad(mine, ffn_in, grad_hidden, *flat4, flip(fc1_theirs, 1))

    sums = jnp.concatenate([sums, sums4.reshape(8 * ff // d, d)[: 3 * ff // d]])
    steps = (
        (partial(flip, bit=1), fc2_theirs),
        (partial(flip, bit=2), fc1_theirs),
        (exchange, fc2_parts[0]),
        (partial(flip, bit=4), fc1_parts[0]),
    )
    for move, done in steps:
        sums = after(sums, done) + move(sums)

    d_out = after(d_out, *fc1_parts)
    back_args = (1.0 / scale_row, logs, scale)
    even, dots_even = attend_back(tab, qkv, heads_out, d_out, *back_args, 0)
    even = even.reshape(3, n, d // 2)
    sums = after(sums, even) + flip(sums, 8)
    output = fill(after(output, even), out_back)
    out_parts = weight_grad(mine, after(heads_in, even), grad_proj, *flat1, flip(out_theirs, 1))
    even_theirs = weight_grad(theirs, after(attn_in, *out_parts), even, *qkv3)
    fc2_parts = columns_by_y(add_x(fc2_parts[0], after(fc2_parts[1], even_theirs)))
    fc1_parts = rows_by_x(add_y(fc1_parts[0], after(fc1_parts[1], even_theirs)))
    d_out = after(d_out, even_theirs, *fc2_parts, *fc1_parts)
    odd, dots_odd = attend_back(tab, qkv, heads_out, d_out, *back_args, 1)
    odd = odd.reshape(3, n, d // 2)
    odd_theirs = weight_grad(theirs, attn_in, odd, *qkv3)
    attn_in = after(attn_in, odd_theirs)
    even_parts = weight_grad(mine, attn_in, even, *qkv3, flip(even_theirs, 1))
    grad_sent, sums_sent = first_back(
        sent_at, after(even, *even_parts), odd, qkv_weight, tok_in, mid_sent, line(norm1_gain), 1, False
    )
    grad_back = exchange(grad_sent)
    odd_parts = weight_grad(mine, after(attn_in, grad_sent), odd, *qkv3, flip(odd_theirs, 1))
    tokens_grad, sums_kept = first_back(
        kept_at, after(even, *odd_parts), odd, qkv_weight, tokens, mid_kept, line(norm1_gain), 0, True
    )
    fc2_weight_grad = z_stage(add_y(fc2_parts[0], after(fc2_parts[1], grad_sent)).astype(bf16))
    fc1_weight_grad = z_stage(add_x(fc1_parts[0], after(fc1_parts[1], grad_sent)).astype(bf16))
    out_parts = rows_by_x(add_y(out_parts[0], after(out_parts[1], odd)))
    out_weight_grad = z_stage(add_x(out_parts[0], after(out_parts[1], grad_sent)).astype(bf16))
    even_parts = rows_by_x(add_y(even_parts[0], after(even_parts[1], tokens_grad)))
    odd_parts = rows_by_x(add_y(odd_parts[0], after(odd_parts[1], tokens_grad)))
    even_grad, odd_grad = (z_stage(add_x(*parts).astype(bf16)) for parts in (even_parts, odd_parts))
    run = d // 4
    qkv_weight_grad = jnp.stack(
        [even_grad.reshape(-1, 3, run), odd_grad.reshape(-1, 3, run)], axis=2
    ).reshape(-1, 6 * run)
    tokens_grad = fill(tokens_grad, grad_back)
    dots = jnp.stack([dots_even[:, 0].reshape(2, 4, head_dim), dots_odd[:, 0].reshape(2, 4, head_dim)], axis=1)
    head_scales_grad = jnp.sum(dots, axis=3).reshape(heads) / head_scales
    head_scales_grad = jnp.pad(head_scales_grad, (0, d - heads))
    first_sums = jnp.concatenate([(sums_sent + sums_kept)[:4], head_scales_grad[None]])
    for move in (partial(flip, bit=1), partial(flip, bit=2), exchange, partial(flip, bit=4), partial(flip, bit=8)):
        first_sums = first_sums + move(first_sums)
    sums4 = sums[8:].reshape(3, ff)
    return (
        output,
        tokens_grad,
        first_sums[0],
        first_sums[1],
        qkv_weight_grad,
        first_sums[2],
        first_sums[3],
        first_sums[4, :heads],
        out_weight_grad,
        sums[0],
        sums[1],
        sums[2],
        sums[3],
        sums[4],
        fc1_weight_grad,
        sums4[0],
        sums4[1],
        sums4[2],
        fc2_weight_grad,
        sums[5],
    )


def solution(mesh):
    rows_fit = dict(mesh.shape) == {"dp": 16, "blk": 2}
    local = local_rows if rows_fit else local_general
    placed = (
        P("dp", "blk", None),
        P("dp", "blk", None),
        P("dp", None),
        P(),
        P(),
        P(),
        P(),
        P(),
        P(),
        P(),
        P(),
        P(),
        P(),
        P(),
        P(),
        P(),
        P(),
        P(),
        P(),
        P(),
        P(),
    )
    return jax.shard_map(
        local,
        mesh=mesh,
        in_specs=placed,
        out_specs=(
            P("dp", "blk", None),
            P("dp", "blk", None),
            P(),
            P(),
            P("dp", "blk"),
            P(),
            P(),
            P(),
            P("dp", "blk"),
            P(),
            P(),
            P(),
            P(),
            P(),
            P("dp", "blk"),
            P(),
            P(),
            P(),
            P("dp", "blk"),
            P(),
        ),
        check_vma=False,
    )
```

```python
from functools import partial

import jax
import jax.numpy as jnp
from jax import lax
from jax.experimental import pallas as pl
from jax.experimental.pallas import tpu as pltpu
from jax.sharding import PartitionSpec as P

f32 = jnp.float32
bf16 = jnp.bfloat16
eps = 1e-05
masked_score = -1e30
LANES = 128
NT = (((1,), (1,)), ((), ()))
NN = (((1,), (0,)), ((), ()))
TN = (((0,), (0,)), ((), ()))


def mm(a, b, dims=NN):
    return lax.dot_general(a, b, dims, preferred_element_type=f32)


def fold(x):
    total = x[:, :LANES]
    for c in range(LANES, x.shape[1], LANES):
        total = total + x[:, c : c + LANES]
    return total


def row_mean(x):
    return jnp.sum(fold(x), axis=1, keepdims=True) * (1.0 / x.shape[1])


def row_sum(x):
    return jnp.sum(x, axis=0, keepdims=True)


def norm_unit(v):
    centered = v - row_mean(v)
    inverse = lax.rsqrt(row_mean(centered * centered) + eps)
    return centered * inverse, inverse


def norm_back(grad_y, unit, inverse, gain):
    e = grad_y * gain
    return inverse * (e - row_mean(e) - unit * row_mean(e * unit))


def params(mib=None, **more):
    return pltpu.CompilerParams(vmem_limit_bytes=(mib or 60) * 2**20, **more)


def cost(flops, moved):
    return pl.CostEstimate(flops=flops, bytes_accessed=moved, transcendentals=0)


def whole(shape):
    return pl.BlockSpec(shape, lambda *_: (0,) * len(shape), pipeline_mode=pl.Buffered(1))


def core_split(x):
    low = lax.broadcasted_iota(jnp.int32, (x.shape[0], LANES), 1) < LANES // 2
    even, odd = [], []
    for c in range(0, x.shape[1], 2 * LANES):
        a = x[:, c : c + LANES].astype(f32)
        b = x[:, c + LANES : c + 2 * LANES].astype(f32)
        even.append(jnp.where(low, a, pltpu.roll(b, LANES // 2, 1)))
        odd.append(jnp.where(low, pltpu.roll(a, LANES // 2, 1), b))
    return (jnp.concatenate(y, axis=1).astype(bf16) for y in (even, odd))


def qkv_body(scale, at, tok, gain, shift, w, bias, *refs):
    attn_in, qkv, x, ws, sems = refs[-5:]
    step = pl.program_id(0)
    steps, d, cols = ws.shape
    half = cols // 2

    def fetch(k, h):
        columns = pl.ds(pl.multiple_of(k * cols + h * half, half), half)
        return pltpu.make_async_copy(
            w.at[:, columns], ws.at[k, :, pl.ds(h * half, half)], sems.at[k, h]
        )

    @pl.when(step == 0)
    def _():
        for k in range(steps):
            for h in range(2):
                fetch(k, h).start()
        unit, _ = norm_unit(tok[0].astype(f32))
        here = (unit * gain[...] + shift[...]).astype(bf16)
        x[...] = here
        attn_in[0], attn_in[1] = core_split(here)

    for h in range(2):
        fetch(step, h).wait()
    total = (mm(x[...], ws[step]) + bias[...]).astype(bf16)
    qkv[...] = (total.astype(f32) * jnp.where(step == 0, scale, 1.0)).astype(bf16)


def project_qkv(at, tok, gain, shift, w, bias, scale, slot, total, earlier=()):
    _, n, d = tok.shape
    held = pl.BlockSpec(memory_space=pl.ANY)
    return pl.pallas_call(
        partial(qkv_body, scale),
        name="project_qkv",
        grid_spec=pltpu.PrefetchScalarGridSpec(
            num_scalar_prefetch=1,
            grid=(3,),
            in_specs=[
                pl.BlockSpec((1, n, d), lambda i, at: (at[0], 0, 0), pipeline_mode=pl.Buffered(1)),
                whole(gain.shape),
                whole(shift.shape),
                held,
                pl.BlockSpec((1, d), lambda i, at: (0, i)),
            ]
            + [held] * len(earlier),
            out_specs=[
                pl.BlockSpec((2, n, d // 2), lambda i, at: (0, slot, 0)),
                pl.BlockSpec((n, d), lambda i, at: (slot, i)),
            ],
            scratch_shapes=[
                pltpu.VMEM((n, d), bf16),
                pltpu.VMEM((3, d, d), bf16),
                pltpu.SemaphoreType.DMA((3, 2)),
            ],
        ),
        out_shape=[
            jax.ShapeDtypeStruct((2, total, d // 2), bf16),
            jax.ShapeDtypeStruct((total, 3 * d), bf16),
        ],
        input_output_aliases={6 + k: k for k in range(len(earlier))},
        compiler_params=params(),
        cost_estimate=cost(2 * n * d * 3 * d, 6 * d * d + 10 * n * d),
    )(at, tok, gain, shift, w, bias, *earlier)


def half_slot(own, half):
    return own if half == 0 else 1 - own


def pick(ref, own, block, size):
    half, sub = divmod(block, 2)
    return ref[half_slot(own, half), sub * size : (sub + 1) * size, :]


def head_mask(size):
    return lax.broadcasted_iota(jnp.int32, (size, LANES), 1) < LANES // 2


def block_penalty(tab, i, j):
    return jnp.where(tab[1 + 4 * i + j] > 0, 0.0, masked_score).astype(f32)


def stack_heads(x, low):
    zero = jnp.zeros_like(x)
    return jnp.concatenate([jnp.where(low, x, zero), jnp.where(low, zero, x)], axis=0)


def place(ref, own, *targets):
    half = ref.shape[1]
    for h in range(2):
        targets[0][h * half : (h + 1) * half, :] = ref[half_slot(own, h)]


def attend_body(tab, q, k, v, head_scale, heads_out, lse, kp, vp):
    size = q.shape[1] // 2
    own = tab[0]
    low = head_mask(size)
    causal = lax.broadcasted_iota(jnp.int32, (2 * size, size), 0) % size >= lax.broadcasted_iota(
        jnp.int32, (2 * size, size), 1
    )
    lane = lax.broadcasted_iota(jnp.int32, (size, LANES), 1)
    place(k, own, kp)
    place(v, own, vp)
    for i in range(4):
        width = (i + 1) * size
        s = mm(stack_heads(pick(q, own, i, size), low), kp[:width, :], NT)
        parts = [s[:, j * size : (j + 1) * size] + block_penalty(tab, i, j) for j in range(i)]
        parts.append(jnp.where(causal, s[:, i * size :], masked_score))
        top = parts[0]
        for part in parts[1:]:
            top = jnp.maximum(top, part)
        top = jnp.max(top, axis=1, keepdims=True)
        parts = [jnp.exp(part - top) for part in parts]
        total = fold(parts[0])
        for part in parts[1:]:
            total = total + fold(part)
        total = jnp.sum(total, axis=1, keepdims=True)
        p = jnp.concatenate([part.astype(bf16) for part in parts], axis=1)
        out = mm(p, vp[:width, :]) * (1.0 / total)
        both = jnp.where(low, out[:size], out[size:]) * head_scale[...]
        half, sub = divmod(i, 2)
        heads_out[half_slot(own, half), sub * size : (sub + 1) * size, :] = both.astype(bf16)
        logs = top + jnp.log(total)
        columns = jnp.where(lane == 0, logs[:size], logs[size:])
        lse[0, i] = jnp.transpose(columns)[:8]


def attend(tab, qkv, head_scale_row):
    _, half_len, wide = qkv.shape
    d = wide // 3
    pairs = d // LANES
    size = half_len // 2

    def lanes(first):
        return pl.BlockSpec((2, half_len, LANES), lambda p, t: (0, 0, first + p))

    flops = 16 * half_len * half_len * pairs * LANES
    return pl.pallas_call(
        attend_body,
        name="attend",
        grid_spec=pltpu.PrefetchScalarGridSpec(
            num_scalar_prefetch=1,
            grid=(pairs,),
            in_specs=[
                lanes(0),
                lanes(pairs),
                lanes(2 * pairs),
                pl.BlockSpec((1, LANES), lambda p, t: (0, p)),
            ],
            out_specs=[
                lanes(0),
                pl.BlockSpec((1, 4, 8, size), lambda p, t: (p, 0, 0, 0)),
            ],
            scratch_shapes=[pltpu.VMEM((2 * half_len, LANES), bf16)] * 2,
        ),
        out_shape=[
            jax.ShapeDtypeStruct((2, half_len, d), bf16),
            jax.ShapeDtypeStruct((pairs, 4, 8, size), f32),
        ],
        compiler_params=params(),
        cost_estimate=cost(flops * 4, 8 * half_len * wide),
    )(tab, qkv, qkv, qkv, head_scale_row)


def attend_back_body(
    scale, tab, q, k, v, heads_out, d_out, inv_scale, lse, dqkv, dots, kp, vp, dk, dv
):
    size = q.shape[1] // 2
    own = tab[0]
    low = head_mask(size)
    causal = lax.broadcasted_iota(jnp.int32, (2 * size, size), 0) % size >= lax.broadcasted_iota(
        jnp.int32, (2 * size, size), 1
    )
    place(k, own, kp)
    place(v, own, vp)
    dots[...] = jnp.zeros_like(dots)
    for i in range(3, -1, -1):
        width = (i + 1) * size
        q2 = stack_heads(pick(q, own, i, size), low)
        gi = pick(d_out, own, i, size)
        g2 = stack_heads(gi, low)
        product = gi.astype(f32) * pick(heads_out, own, i, size).astype(f32) * inv_scale[...]
        dots[0, 0:1, :] += row_sum(product)
        zero = jnp.zeros_like(product)
        delta = jnp.concatenate(
            [
                jnp.sum(jnp.where(low, product, zero), axis=1, keepdims=True),
                jnp.sum(jnp.where(low, zero, product), axis=1, keepdims=True),
            ],
            axis=0,
        )
        columns = jnp.transpose(lse[0, i])
        logs = jnp.concatenate([columns[:, 0:1], columns[:, 1:2]], axis=0)
        s = mm(q2, kp[:width, :], NT)
        g = mm(g2, vp[:width, :], NT)
        ps, ds = [], []
        for j in range(i + 1):
            here = slice(j * size, (j + 1) * size)
            if j < i:
                p = jnp.exp(s[:, here] - (logs - block_penalty(tab, i, j)))
            else:
                p = jnp.exp(jnp.where(causal, s[:, here], masked_score) - logs)
            ps.append(p.astype(bf16))
            ds.append((p * (g[:, here] - delta)).astype(bf16))
        p = jnp.concatenate(ps, axis=1)
        d = jnp.concatenate(ds, axis=1)
        dv_part = mm(p, g2, TN)
        dk_part = mm(d, q2, TN)
        if i == 3:
            dv[...] = dv_part
            dk[...] = dk_part
        else:
            dv[:width, :] += dv_part
            dk[:width, :] += dk_part
        dq = mm(d, kp[:width, :]) * scale
        half, sub = divmod(i, 2)
        dqkv[0, half_slot(own, half), sub * size : (sub + 1) * size, :] = jnp.where(
            low, dq[:size], dq[size:]
        ).astype(bf16)
    for half in range(2):
        here = slice(half * 2 * size, (half + 1) * 2 * size)
        dqkv[1, half_slot(own, half)] = dk[here, :].astype(bf16)
        dqkv[2, half_slot(own, half)] = dv[here, :].astype(bf16)


def attend_back(tab, qkv, heads_out, d_out, inv_scale_row, lse, scale, group):
    _, half_len, wide = qkv.shape
    d = wide // 3
    every = d // LANES
    pairs = every // 2
    size = half_len // 2

    def pair(p):
        return p + 2 * (p // 2) + 2 * group

    def lanes(first):
        return pl.BlockSpec((2, half_len, LANES), lambda p, t: (0, 0, first + pair(p)))

    flops = 16 * half_len * half_len * pairs * LANES
    return pl.pallas_call(
        partial(attend_back_body, scale),
        name="attend_back",
        grid_spec=pltpu.PrefetchScalarGridSpec(
            num_scalar_prefetch=1,
            grid=(pairs,),
            in_specs=[
                lanes(0),
                lanes(every),
                lanes(2 * every),
                lanes(0),
                lanes(0),
                pl.BlockSpec((1, LANES), lambda p, t: (0, pair(p))),
                pl.BlockSpec((1, 4, 8, size), lambda p, t: (pair(p), 0, 0, 0)),
            ],
            out_specs=[
                pl.BlockSpec((3, 2, half_len, LANES), lambda p, t: (0, 0, 0, p)),
                pl.BlockSpec((1, 8, LANES), lambda p, t: (p, 0, 0)),
            ],
            scratch_shapes=[pltpu.VMEM((2 * half_len, LANES), bf16)] * 2
            + [pltpu.VMEM((2 * half_len, LANES), f32)] * 2,
        ),
        out_shape=[
            jax.ShapeDtypeStruct((3, 2, half_len, d // 2), bf16),
            jax.ShapeDtypeStruct((pairs, 8, LANES), f32),
        ],
        compiler_params=params(),
        cost_estimate=cost(flops * 10, 8 * half_len * wide),
    )(tab, qkv, qkv, qkv, heads_out, d_out, inv_scale_row, lse)


def gelu_parts(v):
    a = jnp.abs(v)
    t = 1.0 / (1.0 + (0.3275911 * 0.7071067811865476) * a)
    bell = jnp.exp(v * v * -0.5)
    poly = ((((1.061405429 * t - 1.453152027) * t + 1.421413741) * t - 0.284496736) * t + 0.254829592) * t
    tail = (0.5 * poly) * bell
    cdf = jnp.where(v < 0, tail, 1.0 - tail)
    return v * cdf, cdf + v * (bell * 0.3989422804014327)


def middle_body(
    at, ho, tok, cot, out_w, w1, w2, vec, vec4, *refs
):
    (
        output, grad_middle, sums, sums4, ffn_in, heads_in, mid_out, grad_hidden, grad_proj, d_out,
        act, slope, back, acc, unit_b, stats, total, total_u, w1s, w2s, sems,
    ) = refs[-21:]
    ho, tok, cot, d_out = (ref.at[0] for ref in (ho, tok, cot, d_out))
    output = output.at[0] if len(output.shape) == 3 else output
    step = pl.program_id(0)
    n, d = ho.shape
    chunks, _, fc = w1s.shape
    ff = fc * chunks
    c = step % chunks
    ahead = 2

    def fetch(k):
        columns = pl.ds(pl.multiple_of(k * fc, fc), fc)
        return (
            pltpu.make_async_copy(w1.at[:, columns], w1s.at[k], sems.at[0, k]),
            pltpu.make_async_copy(w2.at[columns, :], w2s.at[k], sems.at[1, k]),
        )
    strip = 128
    strips = n // strip

    def v(r):
        return vec[r : r + 1, :]

    def rows(t):
        return pl.ds(pl.multiple_of(t * strip, strip), strip)

    @pl.when(step == 0)
    def _():
        for k in range(ahead):
            for copy in fetch(k):
                copy.start()
        sums[...] = jnp.zeros_like(sums)
        acc[...] = mm(ho[...], out_w[...])

        def one(t, _):
            r = rows(t)
            unit_attn, inverse_attn = norm_unit(acc[r, :] + v(0))
            middle = tok[r, :].astype(f32) + (unit_attn * v(1) + v(2))
            unit_two, inverse_two = norm_unit(middle)
            x = (unit_two * v(3) + v(4)).astype(bf16)
            grad_middle[r, :] = unit_attn
            unit_b[r, :] = unit_two
            stats[r, 0:1] = inverse_attn
            stats[r, 1:2] = inverse_two
            acc[r, :] = middle + v(5)
            d_out[r, :] = x
            ffn_in[0, r, :], ffn_in[1, r, :] = core_split(x)
            heads_in[0, r, :], heads_in[1, r, :] = core_split(ho[r, :])
            return 0

        lax.fori_loop(0, strips, one, 0)

    @pl.when(step < chunks - ahead)
    def _():
        for copy in fetch(step + ahead):
            copy.start()

    @pl.when(step < chunks)
    def _():
        for copy in fetch(step):
            copy.wait()
        h = mm(d_out[...], w1s[c]) + vec4[0:1, :]
        back[c] = mm(cot[...], w2s[c], NT).astype(back.dtype)
        a, b = gelu_parts(h)
        act[c] = a
        slope[c] = b.astype(slope.dtype)

    @pl.when(step == 0)
    def _():
        total[...] = jnp.zeros_like(total)

    @pl.when(step < chunks)
    def _():
        total[...] += fold(act[c])

    @pl.when(step == chunks)
    def _():
        mean = jnp.sum(total[...], axis=1, keepdims=True) * (1.0 / ff)

        def one(k, t):
            centered = act[k] - mean
            return t + fold(centered * centered)

        square = lax.fori_loop(0, chunks, one, jnp.zeros_like(total))
        stats[:, 2:3] = mean
        stats[:, 3:4] = lax.rsqrt(jnp.sum(square, axis=1, keepdims=True) * (1.0 / ff) + eps)
        total[...] = jnp.zeros_like(total)
        total_u[...] = jnp.zeros_like(total_u)

    here = pl.ds(pl.multiple_of(c * fc, fc), fc)

    @pl.when((step >= chunks) & (step < 2 * chunks))
    def _():
        u = (act[c] - stats[:, 2:3]) * stats[:, 3:4]
        act[c] = u
        gain = vec4[1:2, :]
        m = (u * gain + vec4[2:3, :]).astype(bf16)
        mid_out[...] = m
        acc[...] += mm(m, w2s[c])
        gm = back[c].astype(f32)
        gmu = gm * u
        sums4[1:2, here] = row_sum(gmu)
        sums4[2:3, here] = row_sum(gm)
        total[...] += fold(gm * gain)
        total_u[...] += fold(gmu * gain)

    @pl.when(step == 2 * chunks)
    def _():
        stats[:, 4:5] = jnp.sum(total[...], axis=1, keepdims=True) * (1.0 / ff)
        stats[:, 5:6] = jnp.sum(total_u[...], axis=1, keepdims=True) * (1.0 / ff)
        output[...] = acc[...].astype(output.dtype)
        acc[...] = jnp.zeros_like(acc)

    @pl.when(step >= 2 * chunks)
    def _():
        e = back[c].astype(f32) * vec4[1:2, :]
        grad_act = stats[:, 3:4] * (e - stats[:, 4:5] - act[c] * stats[:, 5:6])
        gh = (grad_act * slope[c].astype(f32)).astype(bf16)
        grad_hidden[...] = gh
        sums4[0:1, here] = row_sum(gh.astype(f32))
        acc[...] += mm(gh, w1s[c], NT)

    @pl.when(step == 3 * chunks - 1)
    def _():
        def one(t, _):
            r = rows(t)
            grad_ffn_in = acc[r, :]
            unit_two = unit_b[r, :]
            unit_attn = grad_middle[r, :]
            gout = cot[r, :].astype(f32)
            sums[5:6, :] += row_sum(gout)
            sums[3:4, :] += row_sum(grad_ffn_in * unit_two)
            sums[4:5, :] += row_sum(grad_ffn_in)
            gmid = gout + norm_back(grad_ffn_in, unit_two, stats[r, 1:2], v(3))
            grad_middle[r, :] = gmid
            sums[1:2, :] += row_sum(gmid * unit_attn)
            sums[2:3, :] += row_sum(gmid)
            gp = norm_back(gmid, unit_attn, stats[r, 0:1], v(1)).astype(bf16)
            grad_proj[r, :] = gp
            sums[0:1, :] += row_sum(gp.astype(f32))
            return 0

        lax.fori_loop(0, strips, one, 0)
        d_out[...] = (mm(grad_proj[...], out_w[...], NT) * v(6)).astype(bf16)


def middle_pass(at, ho, tok, cot, out_w, w1, w2, vec, vec4, slot, last_part, earlier=(), fc=1024):
    _, n, d = ho.shape
    ff = w1.shape[1]
    chunks = ff // fc
    last = chunks - 1
    rows = whole((n, d))
    held = pl.BlockSpec(memory_space=pl.ANY)

    def once(shape, index):
        return pl.BlockSpec(shape, index, pipeline_mode=pl.Buffered(1))

    in_place = once((1, n, d), lambda t, at: (at[0], 0, 0))
    in_slot = once((1, n, d), lambda t, at: (slot, 0, 0))
    split = once((2, n, d // 2), lambda t, at: (0, slot, 0))
    kind = f32 if last_part else bf16
    return pl.pallas_call(
        middle_body,
        name="middle_pass",
        grid_spec=pltpu.PrefetchScalarGridSpec(
            num_scalar_prefetch=1,
            grid=(3 * chunks,),
            in_specs=[
                in_slot,
                in_place,
                in_place,
                whole(out_w.shape),
                held,
                held,
                whole(vec.shape),
                pl.BlockSpec((vec4.shape[0], fc), lambda t, at: (0, t % chunks)),
            ]
            + [held] * len(earlier),
            out_specs=[
                in_place if last_part else rows,
                rows,
                whole((8, d)),
                whole((8, ff)),
                split,
                split,
                pl.BlockSpec((n, fc), lambda t, at: (slot, jnp.clip(t - chunks, 0, last))),
                pl.BlockSpec((n, fc), lambda t, at: (slot, jnp.clip(t - 2 * chunks, 0, last))),
                once((n, d), lambda t, at: (slot, 0)),
                in_slot,
            ],
            scratch_shapes=[
                pltpu.VMEM((chunks, n, fc), f32),
                pltpu.VMEM((chunks, n, fc), bf16),
                pltpu.VMEM((chunks, n, fc), bf16),
                pltpu.VMEM((n, d), f32),
                pltpu.VMEM((n, d), f32),
                pltpu.VMEM((n, LANES), f32),
                pltpu.VMEM((n, LANES), f32),
                pltpu.VMEM((n, LANES), f32),
                pltpu.VMEM((chunks, d, fc), bf16),
                pltpu.VMEM((chunks, fc, d), bf16),
                pltpu.SemaphoreType.DMA((2, chunks)),
            ],
        ),
        out_shape=[
            jax.ShapeDtypeStruct((2, n, d) if last_part else (n, d), kind),
            jax.ShapeDtypeStruct((n, d), f32),
            jax.ShapeDtypeStruct((8, d), f32),
            jax.ShapeDtypeStruct((8, ff), f32),
            jax.ShapeDtypeStruct((2, 2 * n, d // 2), bf16),
            jax.ShapeDtypeStruct((2, 2 * n, d // 2), bf16),
            jax.ShapeDtypeStruct((2 * n, ff), bf16),
            jax.ShapeDtypeStruct((2 * n, ff), bf16),
            jax.ShapeDtypeStruct((2 * n, d), bf16),
            jax.ShapeDtypeStruct((2, n, d), bf16),
        ],
        input_output_aliases={9 + k: 4 + k for k in range(len(earlier))},
        compiler_params=params(62),
        cost_estimate=cost(
            8 * n * d * ff + 4 * n * d * d, 4 * d * ff + 2 * d * d + 4 * n * ff + 20 * n * d
        ),
    )(at, ho, tok, cot, out_w, w1, w2, vec, vec4, *earlier)


def first_back_body(at, even, odd, w, tok, grad_middle, gain, tokens_grad, sums):
    @pl.when(pl.program_id(0) == 0)
    def _():
        sums[...] = jnp.zeros_like(sums)

    d = w.shape[0]
    run = d // 4
    grad = None
    for part in range(3):
        for r in range(4):
            piece = (even, odd)[r % 2][part, :, (r // 2) * run : (r // 2 + 1) * run]
            here = r * run
            term = mm(piece, w[:, part * d + here : part * d + here + run], NT)
            grad = term if grad is None else grad + term
            if part != 1:
                at = 2 + part // 2
                sums[at : at + 1, here : here + run] += row_sum(piece.astype(f32))
    unit, inverse = norm_unit(tok[0].astype(f32))
    sums[0:1, :] += row_sum(grad * unit)
    sums[1:2, :] += row_sum(grad)
    whole_grad = grad_middle[...] + norm_back(grad, unit, inverse, gain[...])
    if len(tokens_grad.shape) == 3:
        tokens_grad[0] = whole_grad
    else:
        tokens_grad[...] = whole_grad.astype(tokens_grad.dtype)


def first_back(at, even, odd, w, tok, grad_middle, gain, slot, last_part, tb=256):
    d = w.shape[0]
    n = even.shape[1] // 2
    first = slot * (n // tb)
    half = pl.BlockSpec((3, tb, d // 2), lambda i, at: (0, first + i, 0))
    rows = pl.BlockSpec((tb, d), lambda i, at: (i, 0))
    in_place = pl.BlockSpec((1, tb, d), lambda i, at: (at[0], i, 0))
    return pl.pallas_call(
        first_back_body,
        name="first_back",
        grid_spec=pltpu.PrefetchScalarGridSpec(
            num_scalar_prefetch=1,
            grid=(n // tb,),
            in_specs=[half, half, whole(w.shape), in_place, rows, whole(gain.shape)],
            out_specs=[in_place if last_part else rows, whole((8, d))],
        ),
        out_shape=[
            jax.ShapeDtypeStruct((2, n, d), f32) if last_part else jax.ShapeDtypeStruct((n, d), bf16),
            jax.ShapeDtypeStruct((8, d), f32),
        ],
        compiler_params=params(),
        cost_estimate=cost(6 * n * d * d, 6 * d * d + 16 * n * d),
    )(at, even, odd, w, tok, grad_middle, gain)


def after(x, *others):
    return lax.optimization_barrier((x,) + others)[0]


def emit(at_low, low, high, received, outs):
    send, keep = jnp.where(at_low, high, low), jnp.where(at_low, low, high)
    if received is None:
        outs[-1][0] = send.astype(bf16)
        outs[-1][1] = keep.astype(bf16)
    else:
        outs[-2][...] = (send + received[0].astype(f32)).astype(bf16)
        outs[-1][...] = (keep + received[1].astype(f32)).astype(bf16)


def tall_grad_body(received_too, tab, *refs):
    runs, halves = refs[:2], refs[2:4]
    a = jnp.concatenate([r[...] for r in runs], axis=1)
    total = mm(a, jnp.concatenate([h[0] for h in halves], axis=0), TN)
    wide = total.shape[1] // 2
    emit(tab[2] == 0, total[:, :wide], total[:, wide:], refs[4] if received_too else None, refs)


def tall_grad(tab, a, b, received=None):
    n, wide = a.shape
    d = b[0].shape[2]
    tall = wide // 16
    steps = 4

    def run(k):
        return pl.BlockSpec((n, tall), lambda i, t: (0, (2 * i + k) * 2 + t[0]))

    in_specs = [
        run(0),
        run(1),
        pl.BlockSpec((1, n // 2, d), lambda i, t: (t[2], 0, 0), pipeline_mode=pl.Buffered(1)),
        pl.BlockSpec((1, n // 2, d), lambda i, t: (0, 0, 0), pipeline_mode=pl.Buffered(1)),
    ]
    both = pl.BlockSpec((2, 2 * tall, d // 2), lambda i, t: (0, i, 0))
    one = pl.BlockSpec((2 * tall, d // 2), lambda i, t: (i, 0))
    args = [tab, a, a, *b]
    if received is not None:
        in_specs.append(both)
        args.append(received)
    shape = (wide // 2, d // 2)
    return pl.pallas_call(
        partial(tall_grad_body, received is not None),
        name="tall_grad",
        grid_spec=pltpu.PrefetchScalarGridSpec(
            num_scalar_prefetch=1,
            grid=(steps,),
            in_specs=in_specs,
            out_specs=both if received is None else [one, one],
        ),
        out_shape=jax.ShapeDtypeStruct((2,) + shape, bf16)
        if received is None
        else [jax.ShapeDtypeStruct(shape, bf16)] * 2,
        compiler_params=params(),
        cost_estimate=cost(2 * n * wide * d // 2, n * wide + 2 * n * d + 8 * wide * d // 4),
    )(*args)


def flat_grad_body(counts, received_too, tab, *refs):
    step = pl.program_id(0)
    parts = len(counts)
    lhs, rhs = refs[:parts], refs[parts : 2 * parts]
    first = 0
    for k, count in enumerate(counts):

        @pl.when((step >= first) & (step < first + count))
        def _(k=k):
            b = rhs[k][0] if len(rhs[k].shape) == 3 else rhs[k][...]
            total = mm(lhs[k][0], b, TN)
            run = total.shape[0] // 8
            low, high = (
                jnp.concatenate([total[(2 * z + h) * run : (2 * z + h + 1) * run] for z in range(4)])
                for h in range(2)
            )
            emit(tab[1] == 0, low, high, refs[2 * parts] if received_too else None, refs)

        first += count


def flat_grad(tab, pairs, tn, received=None):
    counts = [b.shape[0] if b.ndim == 3 else b.shape[1] // tn for _, b in pairs]
    steps = sum(counts)
    n, wide = pairs[0][0].shape[1:]
    in_specs = [
        pl.BlockSpec((1, n, wide), lambda i, t: (t[0], 0, 0), pipeline_mode=pl.Buffered(1))
    ] * len(pairs)
    first = 0
    for (_, b), count in zip(pairs, counts):
        at = partial(lambda first, last, i: jnp.clip(i - first, 0, last), first, count - 1)
        if b.ndim == 3:
            in_specs.append(pl.BlockSpec((1, n, tn), lambda i, t, at=at: (at(i), 0, 0)))
        else:
            in_specs.append(pl.BlockSpec((n, tn), lambda i, t, at=at: (0, at(i))))
        first += count
    both = pl.BlockSpec((2, wide // 2, tn), lambda i, t: (0, 0, i))
    one = pl.BlockSpec((wide // 2, tn), lambda i, t: (0, i))
    args = [tab] + [a for a, _ in pairs] + [b for _, b in pairs]
    if received is not None:
        in_specs.append(both)
        args.append(received)
    shape = (wide // 2, steps * tn)
    weight = 16 if pairs[0][1].ndim == 3 else 1
    return pl.pallas_call(
        partial(flat_grad_body, counts, received is not None),
        name="flat_grad",
        grid_spec=pltpu.PrefetchScalarGridSpec(
            num_scalar_prefetch=1,
            grid=(steps,),
            in_specs=in_specs,
            out_specs=both if received is None else [one, one],
        ),
        out_shape=jax.ShapeDtypeStruct((2,) + shape, bf16)
        if received is None
        else [jax.ShapeDtypeStruct(shape, bf16)] * 2,
        compiler_params=params(),
        cost_estimate=cost(2 * n * wide * shape[1] // weight, (2 * n * (wide + shape[1]) + 8 * wide * shape[1]) // weight),
    )(*args)


def running_sums(lengths):
    count = lengths.shape[1]
    upto = jnp.arange(count)[:, None] >= jnp.arange(count)[None, :]
    return jnp.sum(jnp.where(upto[None], lengths[:, None, :], 0), axis=2).astype(jnp.int32)


def norm_forward(values, gain, shift):
    average = jnp.mean(values, axis=-1, keepdims=True)
    centered = values - average
    inverse = lax.rsqrt(jnp.mean(centered * centered, axis=-1, keepdims=True) + eps)
    normed = centered * inverse
    return (normed * gain + shift, normed, inverse)


def norm_backward(grad_y, normed, inverse, gain):
    scaled = grad_y * gain
    grad_in = inverse * (
        scaled
        - jnp.mean(scaled, axis=-1, keepdims=True)
        - normed * jnp.mean(scaled * normed, axis=-1, keepdims=True)
    )
    return (grad_in, jnp.sum(grad_y * normed, axis=(0, 1)), jnp.sum(grad_y, axis=(0, 1)))


def local_general(
    tokens,
    cotangent,
    doc_lengths,
    norm1_gain,
    norm1_shift,
    qkv_weight,
    query_bias,
    value_bias,
    head_scales,
    out_weight,
    out_bias,
    attn_gain,
    attn_shift,
    norm2_gain,
    norm2_shift,
    fc1_weight,
    fc1_bias,
    mid_gain,
    mid_shift,
    fc2_weight,
    fc2_bias,
):
    f32 = jnp.float32
    bf16 = jnp.bfloat16
    batch_size, local_len, model_width = tokens.shape
    head_count = head_scales.shape[0]
    head_dim = model_width // head_count
    score_scale = head_dim ** (-0.5)
    row_len = local_len * lax.axis_size("blk")
    row_first = lax.axis_index("blk") * local_len
    query_pos = row_first + jnp.arange(local_len, dtype=jnp.int32)
    doc_ends = running_sums(doc_lengths)
    starts = jnp.max(
        jnp.where(doc_ends[:, None, :] <= query_pos[None, :, None], doc_ends[:, None, :], 0), axis=2
    )
    lowest = jnp.min(starts[:, 0])
    query_last = row_first + local_len - 1
    inputs = tokens.astype(f32)
    attn_norm, unit_one, inverse_one = norm_forward(inputs, norm1_gain, norm1_shift)
    attn_in = attn_norm.astype(bf16)
    projected = jnp.dot(attn_in, qkv_weight, preferred_element_type=f32)
    queries = (
        (projected[..., :model_width] + query_bias)
        .astype(bf16)
        .reshape(batch_size, local_len, head_count, head_dim)
    )
    keys_low = projected[..., model_width : 2 * model_width].astype(bf16)
    values_low = (projected[..., 2 * model_width :] + value_bias).astype(bf16)

    def block_scores(key_piece, offset):
        key_len = key_piece.shape[1]
        keys_head = key_piece.reshape(batch_size, key_len, head_count, head_dim)
        raw_scores = (
            jnp.einsum("bqhd,bkhd->bhqk", queries, keys_head, preferred_element_type=f32)
            * score_scale
        )
        key_pos = offset + jnp.arange(key_len, dtype=jnp.int32)
        allowed = (key_pos[None, None, :] <= query_pos[None, :, None]) & (
            key_pos[None, None, :] >= starts[:, :, None]
        )
        return (jnp.where(allowed[:, None], raw_scores, masked_score), keys_head)

    def is_live(offset, key_len):
        return (offset <= query_last) & (offset + key_len - 1 >= lowest)

    def attend_slab(running, key_piece, value_piece, offset):
        key_len = key_piece.shape[1]

        def attend_compute(state):
            running_max, running_sum, weighted = state
            scores, keys_head = block_scores(key_piece, offset)
            new_max = jnp.maximum(running_max, jnp.max(scores, axis=3))
            rescale = jnp.exp(running_max - new_max)
            weights = jnp.exp(scores - new_max[..., None])
            values_head = value_piece.reshape(batch_size, key_len, head_count, head_dim)
            update = jnp.einsum(
                "bhqk,bkhd->bqhd", weights.astype(bf16), values_head, preferred_element_type=f32
            )
            rescale_t = jnp.transpose(rescale, (0, 2, 1))[..., None]
            return (
                new_max,
                running_sum * rescale + jnp.sum(weights, axis=3),
                weighted * rescale_t + update,
            )

        return lax.cond(is_live(offset, key_len), attend_compute, lambda state: state, running)

    start_state = (
        jnp.full((batch_size, head_count, local_len), masked_score, f32),
        jnp.zeros((batch_size, head_count, local_len), f32),
        jnp.zeros((batch_size, local_len, head_count, head_dim), f32),
    )
    key_piece = lax.all_gather(keys_low, "blk", axis=1, tiled=True)
    value_piece = lax.all_gather(values_low, "blk", axis=1, tiled=True)
    turns = key_piece.shape[1] // local_len

    def one_turn(index, state):
        begin = index * local_len
        key_slab = lax.dynamic_slice_in_dim(key_piece, begin, local_len, 1)
        value_slab = lax.dynamic_slice_in_dim(value_piece, begin, local_len, 1)
        return attend_slab(state, key_slab, value_slab, begin)

    running_max, running_sum, weighted = lax.fori_loop(0, turns, one_turn, start_state)
    attended = weighted / jnp.transpose(running_sum, (0, 2, 1))[..., None]
    log_total = running_max + jnp.log(running_sum)
    heads_out = (
        (attended * head_scales[:, None]).reshape(batch_size, local_len, model_width).astype(bf16)
    )
    projection = jnp.dot(heads_out, out_weight, preferred_element_type=f32) + out_bias
    branch, unit_attn, inverse_attn = norm_forward(projection, attn_gain, attn_shift)
    middle = inputs + branch
    ffn_norm, unit_two, inverse_two = norm_forward(middle, norm2_gain, norm2_shift)
    ffn_in = ffn_norm.astype(bf16)
    hidden = jnp.dot(ffn_in, fc1_weight, preferred_element_type=f32) + fc1_bias
    activated, gelu_grad = jax.vjp(partial(jax.nn.gelu, approximate=False), hidden)
    mid_norm, unit_mid, inverse_mid = norm_forward(activated, mid_gain, mid_shift)
    mid_out = mid_norm.astype(bf16)
    output = middle + jnp.dot(mid_out, fc2_weight, preferred_element_type=f32) + fc2_bias
    grad_output = cotangent.astype(f32)
    fc2_weight_grad = jnp.einsum("bcf,bcd->fd", mid_out, cotangent, preferred_element_type=f32)
    fc2_bias_grad = jnp.sum(grad_output, axis=(0, 1))
    grad_mid = jnp.einsum("bcd,fd->bcf", cotangent, fc2_weight, preferred_element_type=f32)
    grad_act, mid_gain_grad, mid_shift_grad = norm_backward(
        grad_mid, unit_mid, inverse_mid, mid_gain
    )
    grad_hidden = gelu_grad(grad_act)[0].astype(bf16)
    fc1_weight_grad = jnp.einsum("bcd,bcf->df", ffn_in, grad_hidden, preferred_element_type=f32)
    fc1_bias_grad = jnp.sum(grad_hidden.astype(f32), axis=(0, 1))
    grad_ffn_in = jnp.einsum("bcf,df->bcd", grad_hidden, fc1_weight, preferred_element_type=f32)
    grad_two, norm2_gain_grad, norm2_shift_grad = norm_backward(
        grad_ffn_in, unit_two, inverse_two, norm2_gain
    )
    grad_middle = grad_output + grad_two
    grad_proj_f, attn_gain_grad, attn_shift_grad = norm_backward(
        grad_middle, unit_attn, inverse_attn, attn_gain
    )
    grad_projection = grad_proj_f.astype(bf16)
    out_weight_grad = jnp.einsum(
        "bcd,bce->de", heads_out, grad_projection, preferred_element_type=f32
    )
    out_bias_grad = jnp.sum(grad_projection.astype(f32), axis=(0, 1))
    grad_heads = jnp.einsum(
        "bce,de->bcd", grad_projection, out_weight, preferred_element_type=f32
    ).reshape(batch_size, local_len, head_count, head_dim)
    head_scales_grad = jnp.sum(grad_heads * attended, axis=(0, 1, 3))
    grad_attended = (grad_heads * head_scales[:, None]).astype(bf16)
    row_dot = jnp.transpose(jnp.sum(grad_attended.astype(f32) * attended, axis=3), (0, 2, 1))

    def back_slab(running, key_piece, value_piece, offset):
        key_len = key_piece.shape[1]

        def back_compute(state):
            grad_queries, kv_buffer = state
            scores, keys_head = block_scores(key_piece, offset)
            attn_probs = jnp.exp(scores - log_total[..., None])
            values_head = value_piece.reshape(batch_size, key_len, head_count, head_dim)
            grad_probs = jnp.einsum(
                "bqhd,bkhd->bhqk", grad_attended, values_head, preferred_element_type=f32
            )
            grad_scores = (attn_probs * (grad_probs - row_dot[..., None])).astype(bf16)
            grad_queries = (
                grad_queries
                + jnp.einsum("bhqk,bkhd->bqhd", grad_scores, keys_head, preferred_element_type=f32)
                * score_scale
            )
            grad_keys = (
                jnp.einsum("bhqk,bqhd->bkhd", grad_scores, queries, preferred_element_type=f32)
                * score_scale
            )
            grad_values = jnp.einsum(
                "bhqk,bqhd->bkhd",
                attn_probs.astype(bf16),
                grad_attended,
                preferred_element_type=f32,
            )
            addition = jnp.concatenate(
                [
                    grad_keys.reshape(batch_size, key_len, model_width),
                    grad_values.reshape(batch_size, key_len, model_width),
                ],
                axis=2,
            )
            previous = lax.dynamic_slice_in_dim(kv_buffer, offset, key_len, 1)
            return (
                grad_queries,
                lax.dynamic_update_slice_in_dim(kv_buffer, previous + addition, offset, 1),
            )

        return lax.cond(is_live(offset, key_len), back_compute, lambda state: state, running)

    back_state = (
        jnp.zeros((batch_size, local_len, head_count, head_dim), f32),
        jnp.zeros((batch_size, row_len, 2 * model_width), f32),
    )
    attend_key_piece = lax.all_gather(keys_low, "blk", axis=1, tiled=True)
    attend_value_piece = lax.all_gather(values_low, "blk", axis=1, tiled=True)
    turns = attend_key_piece.shape[1] // local_len

    def one_turn(index, state):
        begin = index * local_len
        key_slab = lax.dynamic_slice_in_dim(attend_key_piece, begin, local_len, 1)
        value_slab = lax.dynamic_slice_in_dim(attend_value_piece, begin, local_len, 1)
        return back_slab(state, key_slab, value_slab, begin)

    grad_queries, kv_buffer = lax.fori_loop(0, turns, one_turn, back_state)
    grad_kv = lax.psum_scatter(
        kv_buffer.astype(jnp.bfloat16), "blk", scatter_dimension=1, tiled=True
    ).astype(jnp.float32)
    grad_qkv = jnp.concatenate(
        [grad_queries.reshape(batch_size, local_len, model_width), grad_kv], axis=2
    ).astype(bf16)
    qkv_weight_grad = jnp.einsum("bcd,bce->de", attn_in, grad_qkv, preferred_element_type=f32)
    query_bias_grad = jnp.sum(grad_qkv[..., :model_width].astype(f32), axis=(0, 1))
    value_bias_grad = jnp.sum(grad_qkv[..., 2 * model_width :].astype(f32), axis=(0, 1))
    grad_attn_in = jnp.einsum("bce,de->bcd", grad_qkv, qkv_weight, preferred_element_type=f32)
    grad_one, norm1_gain_grad, norm1_shift_grad = norm_backward(
        grad_attn_in, unit_one, inverse_one, norm1_gain
    )
    tokens_grad = grad_middle + grad_one
    matrix_grads = (qkv_weight_grad, out_weight_grad, fc1_weight_grad, fc2_weight_grad)
    reduced = (
        lax.psum_scatter(
            matrix_grads[0].astype(jnp.bfloat16), "dp", scatter_dimension=0, tiled=True
        ).astype(jnp.float32),
        lax.psum_scatter(
            matrix_grads[1].astype(jnp.bfloat16), "dp", scatter_dimension=0, tiled=True
        ).astype(jnp.float32),
        lax.psum_scatter(
            matrix_grads[2].astype(jnp.bfloat16), "dp", scatter_dimension=0, tiled=True
        ).astype(jnp.float32),
        lax.psum_scatter(
            matrix_grads[3].astype(jnp.bfloat16), "dp", scatter_dimension=0, tiled=True
        ).astype(jnp.float32),
    )
    reduced = (
        lax.psum_scatter(
            reduced[0].astype(jnp.bfloat16), "blk", scatter_dimension=1, tiled=True
        ).astype(jnp.float32),
        lax.psum_scatter(
            reduced[1].astype(jnp.bfloat16), "blk", scatter_dimension=1, tiled=True
        ).astype(jnp.float32),
        lax.psum_scatter(
            reduced[2].astype(jnp.bfloat16), "blk", scatter_dimension=1, tiled=True
        ).astype(jnp.float32),
        lax.psum_scatter(
            reduced[3].astype(jnp.bfloat16), "blk", scatter_dimension=1, tiled=True
        ).astype(jnp.float32),
    )
    small_sums = lax.psum(
        (
            norm1_gain_grad,
            norm1_shift_grad,
            query_bias_grad,
            value_bias_grad,
            head_scales_grad,
            out_bias_grad,
            attn_gain_grad,
            attn_shift_grad,
            norm2_gain_grad,
            norm2_shift_grad,
            fc1_bias_grad,
            mid_gain_grad,
            mid_shift_grad,
            fc2_bias_grad,
        ),
        ("dp", "blk"),
    )
    return (
        output,
        tokens_grad,
        small_sums[0],
        small_sums[1],
        reduced[0],
        small_sums[2],
        small_sums[3],
        small_sums[4],
        reduced[1],
        small_sums[5],
        small_sums[6],
        small_sums[7],
        small_sums[8],
        small_sums[9],
        reduced[2],
        small_sums[10],
        small_sums[11],
        small_sums[12],
        reduced[3],
        small_sums[13],
    )


swap = ((0, 1), (1, 0))


def exchange(x):
    return lax.ppermute(x, "blk", swap)


def flip(x, bit):
    return lax.ppermute(x, "dp", [(i, i ^ bit) for i in range(16)])


def local_rows(
    tokens,
    cotangent,
    doc_lengths,
    norm1_gain,
    norm1_shift,
    qkv_weight,
    query_bias,
    value_bias,
    head_scales,
    out_weight,
    out_bias,
    attn_gain,
    attn_shift,
    norm2_gain,
    norm2_shift,
    fc1_weight,
    fc1_bias,
    mid_gain,
    mid_shift,
    fc2_weight,
    fc2_bias,
):
    _, half_len, d = tokens.shape
    ff = fc1_weight.shape[1]
    heads = head_scales.shape[0]
    head_dim = d // heads
    scale = head_dim**-0.5
    n = 2 * half_len
    b = lax.axis_index("blk").astype(jnp.int32)
    dp = lax.axis_index("dp").astype(jnp.int32)
    core, x, z, y = dp % 2, (dp // 2) % 2, dp // 4, b

    tok_in = exchange(lax.dynamic_slice_in_dim(tokens, 1 - b, 1, 0))
    cot_in = exchange(lax.dynamic_slice_in_dim(cotangent, 1 - b, 1, 0))
    kept_at = b[None]
    sent_at = jnp.zeros((1,), jnp.int32)

    lengths = lax.dynamic_slice_in_dim(doc_lengths, b, 1, 0)
    ends = running_sums(lengths)[0]
    firsts = (half_len // 2) * jnp.arange(4, dtype=jnp.int32)
    starts = jnp.max(jnp.where(ends[None, :] <= firsts[:, None], ends[None, :], 0), axis=1)
    allowed = (firsts[None, :] >= starts[:, None]).astype(jnp.int32)
    tab = jnp.concatenate([b[None], allowed.reshape(16)])
    theirs = jnp.stack([1 - core, x, y])
    mine = jnp.stack([core, x, y])

    def line(v):
        return v.reshape(1, -1)

    scale_row = jnp.broadcast_to(head_scales[:, None], (heads, head_dim)).reshape(1, d)
    vec = jnp.stack(
        [out_bias, attn_gain, attn_shift, norm2_gain, norm2_shift, fc2_bias, scale_row[0], out_bias]
    )
    vec4 = jnp.stack([fc1_bias, mid_gain, mid_shift, fc1_bias])
    qkv_bias = jnp.concatenate([query_bias, jnp.zeros_like(query_bias), value_bias])

    first_args = (line(norm1_gain), line(norm1_shift), qkv_weight, line(qkv_bias), scale)
    early = project_qkv(kept_at, tokens, *first_args, 0, n)
    attn_in, qkv = project_qkv(sent_at, tok_in, *first_args, 1, n, early)
    qkv = qkv.reshape(2, half_len, 3 * d)
    heads_out, logs = attend(tab, qkv, scale_row)

    weights = (out_weight, fc1_weight, fc2_weight, vec, vec4)
    out_sent, mid_sent, *more = middle_pass(sent_at, heads_out, tok_in, cot_in, *weights, 1, False)
    sums, sums4, *earlier = more
    out_back = exchange(out_sent)
    output, mid_kept, *more = middle_pass(
        kept_at, heads_out, tokens, cotangent, *weights, 0, True, earlier
    )
    sums = sums + more[0]
    sums4 = sums4 + more[1]
    ffn_in, heads_in, mid_out, grad_hidden, grad_proj, d_out = more[2:]

    def fill(kept, back):
        return lax.dynamic_update_slice_in_dim(kept, back.astype(f32)[None], 1 - b, 0)

    def near_z(total):
        total = total.astype(bf16).reshape((2, 2) + total.shape[1:])
        odd = z % 2
        return (
            lax.dynamic_index_in_dim(total, 1 - odd, 1, keepdims=False),
            lax.dynamic_index_in_dim(total, odd, 1, keepdims=False),
        )

    def far_z(total):
        total = total.astype(bf16)
        high = z // 2
        return (
            lax.dynamic_index_in_dim(total, 1 - high, 0, keepdims=False),
            lax.dynamic_index_in_dim(total, high, 0, keepdims=False),
        )

    def add_z(move, send, keep):
        return keep.astype(f32) + flip(send, move).astype(f32)

    def held(parts, *others):
        return parts[0], after(parts[1], *others)

    def rows_by_x(total):
        total = total.astype(bf16).reshape(4, 2, -1, total.shape[1])
        return (
            lax.dynamic_index_in_dim(total, 1 - x, 1, keepdims=False),
            lax.dynamic_index_in_dim(total, x, 1, keepdims=False),
        )

    def columns_by_y(total, *cuts):
        total = total.astype(bf16).reshape(4, -1, total.shape[1])
        out = []
        for at in (1 - y, y):
            groups = []
            for first, last in zip((0,) + cuts, cuts + (total.shape[2],)):
                width = (last - first) // 2
                groups.append(lax.dynamic_slice_in_dim(total, first + at * width, width, 2))
            out.append(jnp.concatenate(groups, axis=2) if cuts else groups[0])
        return out

    def add_x(send, keep):
        return keep.astype(f32) + flip(send, 2).astype(f32)

    def add_y(send, keep):
        return keep.astype(f32) + exchange(send).astype(f32)

    cots = (cotangent, cot_in)
    output = fill(output, out_back)
    wide_pairs = [(after(ffn_in, output), grad_hidden), (heads_in, grad_proj)]
    wide_theirs = flat_grad(theirs, wide_pairs, d)
    fc2_theirs = tall_grad(theirs, after(mid_out, wide_theirs), cots)
    wide_pairs = [(after(ffn_in, fc2_theirs), grad_hidden), (heads_in, grad_proj)]
    wide_parts = flat_grad(mine, wide_pairs, d, flip(wide_theirs, 1))
    fc2_parts = tall_grad(mine, after(mid_out, *wide_parts), cots, flip(fc2_theirs, 1))
    d_out = after(d_out, *fc2_parts)
    back_args = (1.0 / scale_row, logs, scale)
    even, dots_even = attend_back(tab, qkv, heads_out, d_out, *back_args, 0)
    even = even.reshape(3, n, d // 2)
    even_theirs = flat_grad(theirs, [(after(attn_in, even), even)], d // 2)
    d_out = after(d_out, even_theirs)
    odd, dots_odd = attend_back(tab, qkv, heads_out, d_out, *back_args, 1)
    odd = odd.reshape(3, n, d // 2)
    wide_parts = columns_by_y(add_x(*held(wide_parts, odd)), ff)
    fc2_parts = rows_by_x(add_y(*held(fc2_parts, odd)))
    odd_theirs = flat_grad(theirs, [(after(attn_in, *wide_parts, *fc2_parts), odd)], d // 2)
    even_parts = flat_grad(mine, [(after(attn_in, odd_theirs), even)], d // 2, flip(even_theirs, 1))
    grad_sent, sums_sent = first_back(
        sent_at, after(even, *even_parts), odd, qkv_weight, tok_in, mid_sent, line(norm1_gain), 1, False
    )
    grad_back = exchange(grad_sent)
    fc2_parts = near_z(add_x(*held(fc2_parts, grad_sent)))
    odd_parts = flat_grad(
        mine, [(after(attn_in, grad_sent, *fc2_parts), odd)], d // 2, flip(odd_theirs, 1)
    )
    wide_parts = near_z(add_y(*held(wide_parts, *odd_parts)))
    tokens_grad, sums_kept = first_back(
        kept_at, after(even, *wide_parts), odd, qkv_weight, tokens, mid_kept, line(norm1_gain), 0, True
    )
    fc2_parts = far_z(add_z(4, *held(fc2_parts, tokens_grad)))
    even_parts = columns_by_y(add_x(*held(even_parts, tokens_grad)))
    wide_parts = far_z(add_z(4, *held(wide_parts, *fc2_parts, *even_parts)))
    tokens_grad = fill(tokens_grad, grad_back)
    fc2_weight_grad = add_z(8, *fc2_parts)
    odd_parts = columns_by_y(add_x(*odd_parts))
    even_parts = near_z(add_y(*even_parts))
    wide_grad = add_z(8, *wide_parts)
    fc1_weight_grad, out_weight_grad = wide_grad[:, : ff // 2], wide_grad[:, ff // 2 :]
    even_parts = far_z(add_z(4, *even_parts))
    odd_parts = far_z(add_z(4, *near_z(add_y(*odd_parts))))
    even_grad, odd_grad = (add_z(8, *parts) for parts in (even_parts, odd_parts))
    run = d // 4
    qkv_weight_grad = jnp.stack(
        [even_grad.reshape(-1, 3, run), odd_grad.reshape(-1, 3, run)], axis=2
    ).reshape(-1, 6 * run)
    tokens_grad = fill(tokens_grad, grad_back)
    dots = jnp.stack([dots_even[:, 0].reshape(2, 4, head_dim), dots_odd[:, 0].reshape(2, 4, head_dim)], axis=1)
    head_scales_grad = jnp.sum(dots, axis=3).reshape(heads) / head_scales
    head_scales_grad = jnp.pad(head_scales_grad, (0, d - heads))
    first_sums = (sums_sent + sums_kept)[:4]
    total = jnp.concatenate(
        [first_sums, head_scales_grad[None], sums[:6], sums4.reshape(8 * ff // d, d)[: 3 * ff // d]]
    )
    for move in (partial(flip, bit=1), partial(flip, bit=4), partial(flip, bit=8), partial(flip, bit=2), exchange):
        total = total + move(total)
    first_sums, sums, sums4 = total[:5], total[5:11], total[11:].reshape(3, ff)
    return (
        output,
        tokens_grad,
        first_sums[0],
        first_sums[1],
        qkv_weight_grad,
        first_sums[2],
        first_sums[3],
        first_sums[4, :heads],
        out_weight_grad,
        sums[0],
        sums[1],
        sums[2],
        sums[3],
        sums[4],
        fc1_weight_grad,
        sums4[0],
        sums4[1],
        sums4[2],
        fc2_weight_grad,
        sums[5],
    )


def solution(mesh):
    rows_fit = dict(mesh.shape) == {"dp": 16, "blk": 2}
    local = local_rows if rows_fit else local_general
    placed = (
        P("dp", "blk", None),
        P("dp", "blk", None),
        P("dp", None),
        P(),
        P(),
        P(),
        P(),
        P(),
        P(),
        P(),
        P(),
        P(),
        P(),
        P(),
        P(),
        P(),
        P(),
        P(),
        P(),
        P(),
        P(),
    )
    return jax.shard_map(
        local,
        mesh=mesh,
        in_specs=placed,
        out_specs=(
            P("dp", "blk", None),
            P("dp", "blk", None),
            P(),
            P(),
            P("dp", "blk"),
            P(),
            P(),
            P(),
            P("dp", "blk"),
            P(),
            P(),
            P(),
            P(),
            P(),
            P("dp", "blk"),
            P(),
            P(),
            P(),
            P("dp", "blk"),
            P(),
        ),
        check_vma=False,
    )
```

```python
from functools import partial

import jax
import jax.numpy as jnp
from jax import lax
from jax.experimental import pallas as pl
from jax.experimental.pallas import tpu as pltpu
from jax.sharding import PartitionSpec as P

f32 = jnp.float32
bf16 = jnp.bfloat16
eps = 1e-05
masked_score = -1e30
LANES = 128
NT = (((1,), (1,)), ((), ()))
NN = (((1,), (0,)), ((), ()))
TN = (((0,), (0,)), ((), ()))


def mm(a, b, dims=NN):
    return lax.dot_general(a, b, dims, preferred_element_type=f32)


def fold(x):
    total = x[:, :LANES]
    for c in range(LANES, x.shape[1], LANES):
        total = total + x[:, c : c + LANES]
    return total


def row_mean(x):
    return jnp.sum(fold(x), axis=1, keepdims=True) * (1.0 / x.shape[1])


def row_sum(x):
    return jnp.sum(x, axis=0, keepdims=True)


def norm_unit(v):
    centered = v - row_mean(v)
    inverse = lax.rsqrt(row_mean(centered * centered) + eps)
    return centered * inverse, inverse


def norm_back(grad_y, unit, inverse, gain):
    e = grad_y * gain
    return inverse * (e - row_mean(e) - unit * row_mean(e * unit))


def params(mib=None, **more):
    return pltpu.CompilerParams(vmem_limit_bytes=(mib or 60) * 2**20, **more)


def cost(flops, moved):
    return pl.CostEstimate(flops=flops, bytes_accessed=moved, transcendentals=0)


def whole(shape):
    return pl.BlockSpec(shape, lambda *_: (0,) * len(shape), pipeline_mode=pl.Buffered(1))


def core_split(x):
    low = lax.broadcasted_iota(jnp.int32, (x.shape[0], LANES), 1) < LANES // 2
    even, odd = [], []
    for c in range(0, x.shape[1], 2 * LANES):
        a = x[:, c : c + LANES].astype(f32)
        b = x[:, c + LANES : c + 2 * LANES].astype(f32)
        even.append(jnp.where(low, a, pltpu.roll(b, LANES // 2, 1)))
        odd.append(jnp.where(low, pltpu.roll(a, LANES // 2, 1), b))
    return (jnp.concatenate(y, axis=1).astype(bf16) for y in (even, odd))


def qkv_body(scale, at, tok, gain, shift, w, bias, *refs):
    attn_in, qkv, x, ws, sems = refs[-5:]
    step = pl.program_id(0)
    steps, d, cols = ws.shape
    half = cols // 2

    def fetch(k, h):
        columns = pl.ds(pl.multiple_of(k * cols + h * half, half), half)
        return pltpu.make_async_copy(
            w.at[:, columns], ws.at[k, :, pl.ds(h * half, half)], sems.at[k, h]
        )

    @pl.when(step == 0)
    def _():
        for k in range(steps):
            for h in range(2):
                fetch(k, h).start()
        unit, _ = norm_unit(tok[0].astype(f32))
        here = (unit * gain[...] + shift[...]).astype(bf16)
        x[...] = here
        attn_in[0], attn_in[1] = core_split(here)

    for h in range(2):
        fetch(step, h).wait()
    total = (mm(x[...], ws[step]) + bias[...]).astype(bf16)
    qkv[...] = (total.astype(f32) * jnp.where(step == 0, scale, 1.0)).astype(bf16)


def project_qkv(at, tok, gain, shift, w, bias, scale, slot, total, earlier=()):
    _, n, d = tok.shape
    held = pl.BlockSpec(memory_space=pl.ANY)
    return pl.pallas_call(
        partial(qkv_body, scale),
        name="project_qkv",
        grid_spec=pltpu.PrefetchScalarGridSpec(
            num_scalar_prefetch=1,
            grid=(3,),
            in_specs=[
                pl.BlockSpec((1, n, d), lambda i, at: (at[0], 0, 0), pipeline_mode=pl.Buffered(1)),
                whole(gain.shape),
                whole(shift.shape),
                held,
                pl.BlockSpec((1, d), lambda i, at: (0, i)),
            ]
            + [held] * len(earlier),
            out_specs=[
                pl.BlockSpec((2, n, d // 2), lambda i, at: (0, slot, 0)),
                pl.BlockSpec((n, d), lambda i, at: (slot, i)),
            ],
            scratch_shapes=[
                pltpu.VMEM((n, d), bf16),
                pltpu.VMEM((3, d, d), bf16),
                pltpu.SemaphoreType.DMA((3, 2)),
            ],
        ),
        out_shape=[
            jax.ShapeDtypeStruct((2, total, d // 2), bf16),
            jax.ShapeDtypeStruct((total, 3 * d), bf16),
        ],
        input_output_aliases={6 + k: k for k in range(len(earlier))},
        compiler_params=params(),
        cost_estimate=cost(2 * n * d * 3 * d, 6 * d * d + 10 * n * d),
    )(at, tok, gain, shift, w, bias, *earlier)


def half_slot(own, half):
    return own if half == 0 else 1 - own


def pick(ref, own, block, size):
    half, sub = divmod(block, 2)
    return ref[half_slot(own, half), sub * size : (sub + 1) * size, :]


def head_mask(size):
    return lax.broadcasted_iota(jnp.int32, (size, LANES), 1) < LANES // 2


def block_penalty(tab, i, j):
    return jnp.where(tab[1 + 4 * i + j] > 0, 0.0, masked_score).astype(f32)


def stack_heads(x, low):
    zero = jnp.zeros_like(x)
    return jnp.concatenate([jnp.where(low, x, zero), jnp.where(low, zero, x)], axis=0)


def place(ref, own, *targets):
    half = ref.shape[1]
    for h in range(2):
        targets[0][h * half : (h + 1) * half, :] = ref[half_slot(own, h)]


def attend_body(tab, q, k, v, head_scale, heads_out, lse, kp, vp):
    size = q.shape[1] // 2
    own = tab[0]
    low = head_mask(size)
    causal = lax.broadcasted_iota(jnp.int32, (2 * size, size), 0) % size >= lax.broadcasted_iota(
        jnp.int32, (2 * size, size), 1
    )
    lane = lax.broadcasted_iota(jnp.int32, (size, LANES), 1)
    place(k, own, kp)
    place(v, own, vp)
    for i in range(4):
        width = (i + 1) * size
        s = mm(stack_heads(pick(q, own, i, size), low), kp[:width, :], NT)
        parts = [s[:, j * size : (j + 1) * size] + block_penalty(tab, i, j) for j in range(i)]
        parts.append(jnp.where(causal, s[:, i * size :], masked_score))
        top = parts[0]
        for part in parts[1:]:
            top = jnp.maximum(top, part)
        top = jnp.max(top, axis=1, keepdims=True)
        parts = [jnp.exp(part - top) for part in parts]
        total = fold(parts[0])
        for part in parts[1:]:
            total = total + fold(part)
        total = jnp.sum(total, axis=1, keepdims=True)
        p = jnp.concatenate([part.astype(bf16) for part in parts], axis=1)
        out = mm(p, vp[:width, :]) * (1.0 / total)
        both = jnp.where(low, out[:size], out[size:]) * head_scale[...]
        half, sub = divmod(i, 2)
        heads_out[half_slot(own, half), sub * size : (sub + 1) * size, :] = both.astype(bf16)
        logs = top + jnp.log(total)
        columns = jnp.where(lane == 0, logs[:size], logs[size:])
        lse[0, i] = jnp.transpose(columns)[:8]


def attend(tab, qkv, head_scale_row):
    _, half_len, wide = qkv.shape
    d = wide // 3
    pairs = d // LANES
    size = half_len // 2

    def lanes(first):
        return pl.BlockSpec((2, half_len, LANES), lambda p, t: (0, 0, first + p))

    flops = 16 * half_len * half_len * pairs * LANES
    return pl.pallas_call(
        attend_body,
        name="attend",
        grid_spec=pltpu.PrefetchScalarGridSpec(
            num_scalar_prefetch=1,
            grid=(pairs,),
            in_specs=[
                lanes(0),
                lanes(pairs),
                lanes(2 * pairs),
                pl.BlockSpec((1, LANES), lambda p, t: (0, p)),
            ],
            out_specs=[
                lanes(0),
                pl.BlockSpec((1, 4, 8, size), lambda p, t: (p, 0, 0, 0)),
            ],
            scratch_shapes=[pltpu.VMEM((2 * half_len, LANES), bf16)] * 2,
        ),
        out_shape=[
            jax.ShapeDtypeStruct((2, half_len, d), bf16),
            jax.ShapeDtypeStruct((pairs, 4, 8, size), f32),
        ],
        compiler_params=params(),
        cost_estimate=cost(flops * 4, 8 * half_len * wide),
    )(tab, qkv, qkv, qkv, head_scale_row)


def attend_back_body(
    scale, tab, q, k, v, heads_out, d_out, inv_scale, lse, dqkv, dots, kp, vp, dk, dv
):
    size = q.shape[1] // 2
    own = tab[0]
    low = head_mask(size)
    causal = lax.broadcasted_iota(jnp.int32, (2 * size, size), 0) % size >= lax.broadcasted_iota(
        jnp.int32, (2 * size, size), 1
    )
    place(k, own, kp)
    place(v, own, vp)
    dots[...] = jnp.zeros_like(dots)
    for i in range(3, -1, -1):
        width = (i + 1) * size
        q2 = stack_heads(pick(q, own, i, size), low)
        gi = pick(d_out, own, i, size)
        g2 = stack_heads(gi, low)
        product = gi.astype(f32) * pick(heads_out, own, i, size).astype(f32) * inv_scale[...]
        dots[0, 0:1, :] += row_sum(product)
        zero = jnp.zeros_like(product)
        delta = jnp.concatenate(
            [
                jnp.sum(jnp.where(low, product, zero), axis=1, keepdims=True),
                jnp.sum(jnp.where(low, zero, product), axis=1, keepdims=True),
            ],
            axis=0,
        )
        columns = jnp.transpose(lse[0, i])
        logs = jnp.concatenate([columns[:, 0:1], columns[:, 1:2]], axis=0)
        s = mm(q2, kp[:width, :], NT)
        g = mm(g2, vp[:width, :], NT)
        ps, ds = [], []
        for j in range(i + 1):
            here = slice(j * size, (j + 1) * size)
            if j < i:
                p = jnp.exp(s[:, here] - (logs - block_penalty(tab, i, j)))
            else:
                p = jnp.exp(jnp.where(causal, s[:, here], masked_score) - logs)
            ps.append(p.astype(bf16))
            ds.append((p * (g[:, here] - delta)).astype(bf16))
        p = jnp.concatenate(ps, axis=1)
        d = jnp.concatenate(ds, axis=1)
        dv_part = mm(p, g2, TN)
        dk_part = mm(d, q2, TN)
        if i == 3:
            dv[...] = dv_part
            dk[...] = dk_part
        else:
            dv[:width, :] += dv_part
            dk[:width, :] += dk_part
        dq = mm(d, kp[:width, :]) * scale
        half, sub = divmod(i, 2)
        dqkv[0, half_slot(own, half), sub * size : (sub + 1) * size, :] = jnp.where(
            low, dq[:size], dq[size:]
        ).astype(bf16)
    for half in range(2):
        here = slice(half * 2 * size, (half + 1) * 2 * size)
        dqkv[1, half_slot(own, half)] = dk[here, :].astype(bf16)
        dqkv[2, half_slot(own, half)] = dv[here, :].astype(bf16)


def attend_back(tab, qkv, heads_out, d_out, inv_scale_row, lse, scale, group):
    _, half_len, wide = qkv.shape
    d = wide // 3
    every = d // LANES
    pairs = every // 2
    size = half_len // 2

    def pair(p):
        return p + 2 * (p // 2) + 2 * group

    def lanes(first):
        return pl.BlockSpec((2, half_len, LANES), lambda p, t: (0, 0, first + pair(p)))

    flops = 16 * half_len * half_len * pairs * LANES
    return pl.pallas_call(
        partial(attend_back_body, scale),
        name="attend_back",
        grid_spec=pltpu.PrefetchScalarGridSpec(
            num_scalar_prefetch=1,
            grid=(pairs,),
            in_specs=[
                lanes(0),
                lanes(every),
                lanes(2 * every),
                lanes(0),
                lanes(0),
                pl.BlockSpec((1, LANES), lambda p, t: (0, pair(p))),
                pl.BlockSpec((1, 4, 8, size), lambda p, t: (pair(p), 0, 0, 0)),
            ],
            out_specs=[
                pl.BlockSpec((3, 2, half_len, LANES), lambda p, t: (0, 0, 0, p)),
                pl.BlockSpec((1, 8, LANES), lambda p, t: (p, 0, 0)),
            ],
            scratch_shapes=[pltpu.VMEM((2 * half_len, LANES), bf16)] * 2
            + [pltpu.VMEM((2 * half_len, LANES), f32)] * 2,
        ),
        out_shape=[
            jax.ShapeDtypeStruct((3, 2, half_len, d // 2), bf16),
            jax.ShapeDtypeStruct((pairs, 8, LANES), f32),
        ],
        compiler_params=params(),
        cost_estimate=cost(flops * 10, 8 * half_len * wide),
    )(tab, qkv, qkv, qkv, heads_out, d_out, inv_scale_row, lse)


def gelu_parts(v):
    a = jnp.abs(v)
    t = 1.0 / (1.0 + (0.3275911 * 0.7071067811865476) * a)
    bell = jnp.exp(v * v * -0.5)
    poly = ((((1.061405429 * t - 1.453152027) * t + 1.421413741) * t - 0.284496736) * t + 0.254829592) * t
    tail = (0.5 * poly) * bell
    cdf = jnp.where(v < 0, tail, 1.0 - tail)
    return v * cdf, cdf + v * (bell * 0.3989422804014327)


def middle_body(
    at, ho, tok, cot, out_w, w1, w2, vec, vec4, *refs
):
    (
        output, grad_middle, sums, sums4, ffn_in, heads_in, mid_out, grad_hidden, grad_proj, d_out,
        act, slope, back, acc, unit_b, stats, total, total_u, w1s, w2s, sems,
    ) = refs[-21:]
    ho, tok, cot, d_out = (ref.at[0] for ref in (ho, tok, cot, d_out))
    output = output.at[0] if len(output.shape) == 3 else output
    step = pl.program_id(0)
    n, d = ho.shape
    chunks, _, fc = w1s.shape
    ff = fc * chunks
    ahead = 2

    def fetch(k):
        columns = pl.ds(pl.multiple_of(k * fc, fc), fc)
        return (
            pltpu.make_async_copy(w1.at[:, columns], w1s.at[k], sems.at[0, k]),
            pltpu.make_async_copy(w2.at[columns, :], w2s.at[k], sems.at[1, k]),
        )
    strip = 128
    strips = n // strip

    def v(r):
        return vec[r : r + 1, :]

    def rows(t):
        return pl.ds(pl.multiple_of(t * strip, strip), strip)

    @pl.when(step == 0)
    def _():
        for k in range(ahead):
            for copy in fetch(k):
                copy.start()
        sums[...] = jnp.zeros_like(sums)
        acc[...] = mm(ho[...], out_w[...])

        def one(t, _):
            r = rows(t)
            unit_attn, inverse_attn = norm_unit(acc[r, :] + v(0))
            middle = tok[r, :].astype(f32) + (unit_attn * v(1) + v(2))
            unit_two, inverse_two = norm_unit(middle)
            x = (unit_two * v(3) + v(4)).astype(bf16)
            grad_middle[r, :] = unit_attn
            unit_b[r, :] = unit_two
            stats[r, 0:1] = inverse_attn
            stats[r, 1:2] = inverse_two
            acc[r, :] = middle + v(5)
            d_out[r, :] = x
            ffn_in[0, r, :], ffn_in[1, r, :] = core_split(x)
            heads_in[0, r, :], heads_in[1, r, :] = core_split(ho[r, :])
            return 0

        lax.fori_loop(0, strips, one, 0)

    @pl.when(step == 0)
    def _():
        total[...] = jnp.zeros_like(total)

    @pl.when(step < chunks - ahead)
    def _():
        for copy in fetch(step + ahead):
            copy.start()

    sub = 256

    def first_phase(k):
        for copy in fetch(k):
            copy.wait()
        for at in range(0, fc, sub):
            cs = slice(at, at + sub)
            h = mm(d_out[...], w1s[k, :, cs]) + vec4[0:1, cs]
            a, b = gelu_parts(h)
            act[k, :, cs] = a
            slope[k, :, cs] = b.astype(slope.dtype)
            total[...] += fold(a)
            back[k, :, cs] = mm(cot[...], w2s[k, cs, :], NT).astype(back.dtype)

    def second_phase(k):
        here = slice(k * fc, (k + 1) * fc)
        u = (act[k] - stats[:, 2:3]) * stats[:, 3:4]
        act[k] = u
        gain = vec4[1:2, :]
        m = (u * gain + vec4[2:3, :]).astype(bf16)
        mid_out[...] = m
        acc[...] += mm(m, w2s[k])
        gm = back[k].astype(f32)
        gmu = gm * u
        sums4[1:2, here] = row_sum(gmu)
        sums4[2:3, here] = row_sum(gm)
        total[...] += fold(gm * gain)
        total_u[...] += fold(gmu * gain)

    def third_phase(k):
        here = slice(k * fc, (k + 1) * fc)
        e = back[k].astype(f32) * vec4[1:2, :]
        grad_act = stats[:, 3:4] * (e - stats[:, 4:5] - act[k] * stats[:, 5:6])
        gh = (grad_act * slope[k].astype(f32)).astype(bf16)
        grad_hidden[...] = gh
        sums4[0:1, here] = row_sum(gh.astype(f32))
        acc[...] += mm(gh, w1s[k], NT)

    @pl.when(step == chunks)
    def _():
        mean = jnp.sum(total[...], axis=1, keepdims=True) * (1.0 / ff)
        square = jnp.zeros_like(total)
        for k in range(chunks):
            centered = act[k] - mean
            square = square + fold(centered * centered)
        stats[:, 2:3] = mean
        stats[:, 3:4] = lax.rsqrt(jnp.sum(square, axis=1, keepdims=True) * (1.0 / ff) + eps)
        total[...] = jnp.zeros_like(total)
        total_u[...] = jnp.zeros_like(total_u)

    @pl.when(step == 2 * chunks)
    def _():
        stats[:, 4:5] = jnp.sum(total[...], axis=1, keepdims=True) * (1.0 / ff)
        stats[:, 5:6] = jnp.sum(total_u[...], axis=1, keepdims=True) * (1.0 / ff)
        output[...] = acc[...].astype(output.dtype)
        acc[...] = jnp.zeros_like(acc)

    for phase, body in enumerate((first_phase, second_phase, third_phase)):
        for k in range(chunks):
            pl.when(step == phase * chunks + k)(partial(body, k))

    @pl.when(step == 3 * chunks - 1)
    def _():
        def one(t, _):
            r = rows(t)
            grad_ffn_in = acc[r, :]
            unit_two = unit_b[r, :]
            unit_attn = grad_middle[r, :]
            gout = cot[r, :].astype(f32)
            sums[5:6, :] += row_sum(gout)
            sums[3:4, :] += row_sum(grad_ffn_in * unit_two)
            sums[4:5, :] += row_sum(grad_ffn_in)
            gmid = gout + norm_back(grad_ffn_in, unit_two, stats[r, 1:2], v(3))
            grad_middle[r, :] = gmid
            sums[1:2, :] += row_sum(gmid * unit_attn)
            sums[2:3, :] += row_sum(gmid)
            gp = norm_back(gmid, unit_attn, stats[r, 0:1], v(1)).astype(bf16)
            grad_proj[r, :] = gp
            sums[0:1, :] += row_sum(gp.astype(f32))
            return 0

        lax.fori_loop(0, strips, one, 0)
        d_out[...] = (mm(grad_proj[...], out_w[...], NT) * v(6)).astype(bf16)


def middle_pass(at, ho, tok, cot, out_w, w1, w2, vec, vec4, slot, last_part, earlier=(), fc=1024):
    _, n, d = ho.shape
    ff = w1.shape[1]
    chunks = ff // fc
    last = chunks - 1
    rows = whole((n, d))
    held = pl.BlockSpec(memory_space=pl.ANY)

    def once(shape, index):
        return pl.BlockSpec(shape, index, pipeline_mode=pl.Buffered(1))

    in_place = once((1, n, d), lambda t, at: (at[0], 0, 0))
    in_slot = once((1, n, d), lambda t, at: (slot, 0, 0))
    split = once((2, n, d // 2), lambda t, at: (0, slot, 0))
    kind = f32 if last_part else bf16
    return pl.pallas_call(
        middle_body,
        name="middle_pass",
        grid_spec=pltpu.PrefetchScalarGridSpec(
            num_scalar_prefetch=1,
            grid=(3 * chunks,),
            in_specs=[
                in_slot,
                in_place,
                in_place,
                whole(out_w.shape),
                held,
                held,
                whole(vec.shape),
                pl.BlockSpec((vec4.shape[0], fc), lambda t, at: (0, t % chunks)),
            ]
            + [held] * len(earlier),
            out_specs=[
                in_place if last_part else rows,
                rows,
                whole((8, d)),
                whole((8, ff)),
                split,
                split,
                pl.BlockSpec((n, fc), lambda t, at: (slot, jnp.clip(t - chunks, 0, last))),
                pl.BlockSpec((n, fc), lambda t, at: (slot, jnp.clip(t - 2 * chunks, 0, last))),
                once((n, d), lambda t, at: (slot, 0)),
                in_slot,
            ],
            scratch_shapes=[
                pltpu.VMEM((chunks, n, fc), f32),
                pltpu.VMEM((chunks, n, fc), bf16),
                pltpu.VMEM((chunks, n, fc), bf16),
                pltpu.VMEM((n, d), f32),
                pltpu.VMEM((n, d), f32),
                pltpu.VMEM((n, LANES), f32),
                pltpu.VMEM((n, LANES), f32),
                pltpu.VMEM((n, LANES), f32),
                pltpu.VMEM((chunks, d, fc), bf16),
                pltpu.VMEM((chunks, fc, d), bf16),
                pltpu.SemaphoreType.DMA((2, chunks)),
            ],
        ),
        out_shape=[
            jax.ShapeDtypeStruct((2, n, d) if last_part else (n, d), kind),
            jax.ShapeDtypeStruct((n, d), f32),
            jax.ShapeDtypeStruct((8, d), f32),
            jax.ShapeDtypeStruct((8, ff), f32),
            jax.ShapeDtypeStruct((2, 2 * n, d // 2), bf16),
            jax.ShapeDtypeStruct((2, 2 * n, d // 2), bf16),
            jax.ShapeDtypeStruct((2 * n, ff), bf16),
            jax.ShapeDtypeStruct((2 * n, ff), bf16),
            jax.ShapeDtypeStruct((2 * n, d), bf16),
            jax.ShapeDtypeStruct((2, n, d), bf16),
        ],
        input_output_aliases={9 + k: 4 + k for k in range(len(earlier))},
        compiler_params=params(62),
        cost_estimate=cost(
            8 * n * d * ff + 4 * n * d * d, 4 * d * ff + 2 * d * d + 4 * n * ff + 20 * n * d
        ),
    )(at, ho, tok, cot, out_w, w1, w2, vec, vec4, *earlier)


def first_back_body(at, even, odd, w, tok, grad_middle, gain, tokens_grad, sums):
    @pl.when(pl.program_id(0) == 0)
    def _():
        sums[...] = jnp.zeros_like(sums)

    d = w.shape[0]
    run = d // 4
    grad = None
    for part in range(3):
        for r in range(4):
            piece = (even, odd)[r % 2][part, :, (r // 2) * run : (r // 2 + 1) * run]
            here = r * run
            term = mm(piece, w[:, part * d + here : part * d + here + run], NT)
            grad = term if grad is None else grad + term
            if part != 1:
                at = 2 + part // 2
                sums[at : at + 1, here : here + run] += row_sum(piece.astype(f32))
    unit, inverse = norm_unit(tok[0].astype(f32))
    sums[0:1, :] += row_sum(grad * unit)
    sums[1:2, :] += row_sum(grad)
    whole_grad = grad_middle[...] + norm_back(grad, unit, inverse, gain[...])
    if len(tokens_grad.shape) == 3:
        tokens_grad[0] = whole_grad
    else:
        tokens_grad[...] = whole_grad.astype(tokens_grad.dtype)


def first_back(at, even, odd, w, tok, grad_middle, gain, slot, last_part, tb=256):
    d = w.shape[0]
    n = even.shape[1] // 2
    first = slot * (n // tb)
    half = pl.BlockSpec((3, tb, d // 2), lambda i, at: (0, first + i, 0))
    rows = pl.BlockSpec((tb, d), lambda i, at: (i, 0))
    in_place = pl.BlockSpec((1, tb, d), lambda i, at: (at[0], i, 0))
    return pl.pallas_call(
        first_back_body,
        name="first_back",
        grid_spec=pltpu.PrefetchScalarGridSpec(
            num_scalar_prefetch=1,
            grid=(n // tb,),
            in_specs=[half, half, whole(w.shape), in_place, rows, whole(gain.shape)],
            out_specs=[in_place if last_part else rows, whole((8, d))],
        ),
        out_shape=[
            jax.ShapeDtypeStruct((2, n, d), f32) if last_part else jax.ShapeDtypeStruct((n, d), bf16),
            jax.ShapeDtypeStruct((8, d), f32),
        ],
        compiler_params=params(),
        cost_estimate=cost(6 * n * d * d, 6 * d * d + 16 * n * d),
    )(at, even, odd, w, tok, grad_middle, gain)


def after(x, *others):
    return lax.optimization_barrier((x,) + others)[0]


def emit(at_low, low, high, received, outs):
    send, keep = jnp.where(at_low, high, low), jnp.where(at_low, low, high)
    if received is None:
        outs[-1][0] = send.astype(bf16)
        outs[-1][1] = keep.astype(bf16)
    else:
        outs[-2][...] = (send + received[0].astype(f32)).astype(bf16)
        outs[-1][...] = (keep + received[1].astype(f32)).astype(bf16)


def tall_grad_body(received_too, tab, *refs):
    runs, halves = refs[:2], refs[2:4]
    a = jnp.concatenate([r[...] for r in runs], axis=1)
    total = mm(a, jnp.concatenate([h[0] for h in halves], axis=0), TN)
    wide = total.shape[1] // 2
    emit(tab[2] == 0, total[:, :wide], total[:, wide:], refs[4] if received_too else None, refs)


def tall_grad(tab, a, b, received=None):
    n, wide = a.shape
    d = b[0].shape[2]
    tall = wide // 16
    steps = 4

    def run(k):
        return pl.BlockSpec((n, tall), lambda i, t: (0, (2 * i + k) * 2 + t[0]))

    in_specs = [
        run(0),
        run(1),
        pl.BlockSpec((1, n // 2, d), lambda i, t: (t[2], 0, 0), pipeline_mode=pl.Buffered(1)),
        pl.BlockSpec((1, n // 2, d), lambda i, t: (0, 0, 0), pipeline_mode=pl.Buffered(1)),
    ]
    both = pl.BlockSpec((2, 2 * tall, d // 2), lambda i, t: (0, i, 0))
    one = pl.BlockSpec((2 * tall, d // 2), lambda i, t: (i, 0))
    args = [tab, a, a, *b]
    if received is not None:
        in_specs.append(both)
        args.append(received)
    shape = (wide // 2, d // 2)
    return pl.pallas_call(
        partial(tall_grad_body, received is not None),
        name="tall_grad",
        grid_spec=pltpu.PrefetchScalarGridSpec(
            num_scalar_prefetch=1,
            grid=(steps,),
            in_specs=in_specs,
            out_specs=both if received is None else [one, one],
        ),
        out_shape=jax.ShapeDtypeStruct((2,) + shape, bf16)
        if received is None
        else [jax.ShapeDtypeStruct(shape, bf16)] * 2,
        compiler_params=params(),
        cost_estimate=cost(2 * n * wide * d // 2, n * wide + 2 * n * d + 8 * wide * d // 4),
    )(*args)


def flat_grad_body(counts, received_too, tab, *refs):
    step = pl.program_id(0)
    parts = len(counts)
    lhs, rhs = refs[:parts], refs[parts : 2 * parts]
    first = 0
    for k, count in enumerate(counts):

        @pl.when((step >= first) & (step < first + count))
        def _(k=k):
            b = rhs[k][0] if len(rhs[k].shape) == 3 else rhs[k][...]
            total = mm(lhs[k][0], b, TN)
            run = total.shape[0] // 8
            low, high = (
                jnp.concatenate([total[(2 * z + h) * run : (2 * z + h + 1) * run] for z in range(4)])
                for h in range(2)
            )
            emit(tab[1] == 0, low, high, refs[2 * parts] if received_too else None, refs)

        first += count


def flat_grad(tab, pairs, tn, received=None):
    counts = [b.shape[0] if b.ndim == 3 else b.shape[1] // tn for _, b in pairs]
    steps = sum(counts)
    n, wide = pairs[0][0].shape[1:]
    in_specs = [
        pl.BlockSpec((1, n, wide), lambda i, t: (t[0], 0, 0), pipeline_mode=pl.Buffered(1))
    ] * len(pairs)
    first = 0
    for (_, b), count in zip(pairs, counts):
        at = partial(lambda first, last, i: jnp.clip(i - first, 0, last), first, count - 1)
        if b.ndim == 3:
            in_specs.append(pl.BlockSpec((1, n, tn), lambda i, t, at=at: (at(i), 0, 0)))
        else:
            in_specs.append(pl.BlockSpec((n, tn), lambda i, t, at=at: (0, at(i))))
        first += count
    both = pl.BlockSpec((2, wide // 2, tn), lambda i, t: (0, 0, i))
    one = pl.BlockSpec((wide // 2, tn), lambda i, t: (0, i))
    args = [tab] + [a for a, _ in pairs] + [b for _, b in pairs]
    if received is not None:
        in_specs.append(both)
        args.append(received)
    shape = (wide // 2, steps * tn)
    weight = 16 if pairs[0][1].ndim == 3 else 1
    return pl.pallas_call(
        partial(flat_grad_body, counts, received is not None),
        name="flat_grad",
        grid_spec=pltpu.PrefetchScalarGridSpec(
            num_scalar_prefetch=1,
            grid=(steps,),
            in_specs=in_specs,
            out_specs=both if received is None else [one, one],
        ),
        out_shape=jax.ShapeDtypeStruct((2,) + shape, bf16)
        if received is None
        else [jax.ShapeDtypeStruct(shape, bf16)] * 2,
        compiler_params=params(),
        cost_estimate=cost(2 * n * wide * shape[1] // weight, (2 * n * (wide + shape[1]) + 8 * wide * shape[1]) // weight),
    )(*args)


def running_sums(lengths):
    count = lengths.shape[1]
    upto = jnp.arange(count)[:, None] >= jnp.arange(count)[None, :]
    return jnp.sum(jnp.where(upto[None], lengths[:, None, :], 0), axis=2).astype(jnp.int32)


def norm_forward(values, gain, shift):
    average = jnp.mean(values, axis=-1, keepdims=True)
    centered = values - average
    inverse = lax.rsqrt(jnp.mean(centered * centered, axis=-1, keepdims=True) + eps)
    normed = centered * inverse
    return (normed * gain + shift, normed, inverse)


def norm_backward(grad_y, normed, inverse, gain):
    scaled = grad_y * gain
    grad_in = inverse * (
        scaled
        - jnp.mean(scaled, axis=-1, keepdims=True)
        - normed * jnp.mean(scaled * normed, axis=-1, keepdims=True)
    )
    return (grad_in, jnp.sum(grad_y * normed, axis=(0, 1)), jnp.sum(grad_y, axis=(0, 1)))


def local_general(
    tokens,
    cotangent,
    doc_lengths,
    norm1_gain,
    norm1_shift,
    qkv_weight,
    query_bias,
    value_bias,
    head_scales,
    out_weight,
    out_bias,
    attn_gain,
    attn_shift,
    norm2_gain,
    norm2_shift,
    fc1_weight,
    fc1_bias,
    mid_gain,
    mid_shift,
    fc2_weight,
    fc2_bias,
):
    f32 = jnp.float32
    bf16 = jnp.bfloat16
    batch_size, local_len, model_width = tokens.shape
    head_count = head_scales.shape[0]
    head_dim = model_width // head_count
    score_scale = head_dim ** (-0.5)
    row_len = local_len * lax.axis_size("blk")
    row_first = lax.axis_index("blk") * local_len
    query_pos = row_first + jnp.arange(local_len, dtype=jnp.int32)
    doc_ends = running_sums(doc_lengths)
    starts = jnp.max(
        jnp.where(doc_ends[:, None, :] <= query_pos[None, :, None], doc_ends[:, None, :], 0), axis=2
    )
    lowest = jnp.min(starts[:, 0])
    query_last = row_first + local_len - 1
    inputs = tokens.astype(f32)
    attn_norm, unit_one, inverse_one = norm_forward(inputs, norm1_gain, norm1_shift)
    attn_in = attn_norm.astype(bf16)
    projected = jnp.dot(attn_in, qkv_weight, preferred_element_type=f32)
    queries = (
        (projected[..., :model_width] + query_bias)
        .astype(bf16)
        .reshape(batch_size, local_len, head_count, head_dim)
    )
    keys_low = projected[..., model_width : 2 * model_width].astype(bf16)
    values_low = (projected[..., 2 * model_width :] + value_bias).astype(bf16)

    def block_scores(key_piece, offset):
        key_len = key_piece.shape[1]
        keys_head = key_piece.reshape(batch_size, key_len, head_count, head_dim)
        raw_scores = (
            jnp.einsum("bqhd,bkhd->bhqk", queries, keys_head, preferred_element_type=f32)
            * score_scale
        )
        key_pos = offset + jnp.arange(key_len, dtype=jnp.int32)
        allowed = (key_pos[None, None, :] <= query_pos[None, :, None]) & (
            key_pos[None, None, :] >= starts[:, :, None]
        )
        return (jnp.where(allowed[:, None], raw_scores, masked_score), keys_head)

    def is_live(offset, key_len):
        return (offset <= query_last) & (offset + key_len - 1 >= lowest)

    def attend_slab(running, key_piece, value_piece, offset):
        key_len = key_piece.shape[1]

        def attend_compute(state):
            running_max, running_sum, weighted = state
            scores, keys_head = block_scores(key_piece, offset)
            new_max = jnp.maximum(running_max, jnp.max(scores, axis=3))
            rescale = jnp.exp(running_max - new_max)
            weights = jnp.exp(scores - new_max[..., None])
            values_head = value_piece.reshape(batch_size, key_len, head_count, head_dim)
            update = jnp.einsum(
                "bhqk,bkhd->bqhd", weights.astype(bf16), values_head, preferred_element_type=f32
            )
            rescale_t = jnp.transpose(rescale, (0, 2, 1))[..., None]
            return (
                new_max,
                running_sum * rescale + jnp.sum(weights, axis=3),
                weighted * rescale_t + update,
            )

        return lax.cond(is_live(offset, key_len), attend_compute, lambda state: state, running)

    start_state = (
        jnp.full((batch_size, head_count, local_len), masked_score, f32),
        jnp.zeros((batch_size, head_count, local_len), f32),
        jnp.zeros((batch_size, local_len, head_count, head_dim), f32),
    )
    key_piece = lax.all_gather(keys_low, "blk", axis=1, tiled=True)
    value_piece = lax.all_gather(values_low, "blk", axis=1, tiled=True)
    turns = key_piece.shape[1] // local_len

    def one_turn(index, state):
        begin = index * local_len
        key_slab = lax.dynamic_slice_in_dim(key_piece, begin, local_len, 1)
        value_slab = lax.dynamic_slice_in_dim(value_piece, begin, local_len, 1)
        return attend_slab(state, key_slab, value_slab, begin)

    running_max, running_sum, weighted = lax.fori_loop(0, turns, one_turn, start_state)
    attended = weighted / jnp.transpose(running_sum, (0, 2, 1))[..., None]
    log_total = running_max + jnp.log(running_sum)
    heads_out = (
        (attended * head_scales[:, None]).reshape(batch_size, local_len, model_width).astype(bf16)
    )
    projection = jnp.dot(heads_out, out_weight, preferred_element_type=f32) + out_bias
    branch, unit_attn, inverse_attn = norm_forward(projection, attn_gain, attn_shift)
    middle = inputs + branch
    ffn_norm, unit_two, inverse_two = norm_forward(middle, norm2_gain, norm2_shift)
    ffn_in = ffn_norm.astype(bf16)
    hidden = jnp.dot(ffn_in, fc1_weight, preferred_element_type=f32) + fc1_bias
    activated, gelu_grad = jax.vjp(partial(jax.nn.gelu, approximate=False), hidden)
    mid_norm, unit_mid, inverse_mid = norm_forward(activated, mid_gain, mid_shift)
    mid_out = mid_norm.astype(bf16)
    output = middle + jnp.dot(mid_out, fc2_weight, preferred_element_type=f32) + fc2_bias
    grad_output = cotangent.astype(f32)
    fc2_weight_grad = jnp.einsum("bcf,bcd->fd", mid_out, cotangent, preferred_element_type=f32)
    fc2_bias_grad = jnp.sum(grad_output, axis=(0, 1))
    grad_mid = jnp.einsum("bcd,fd->bcf", cotangent, fc2_weight, preferred_element_type=f32)
    grad_act, mid_gain_grad, mid_shift_grad = norm_backward(
        grad_mid, unit_mid, inverse_mid, mid_gain
    )
    grad_hidden = gelu_grad(grad_act)[0].astype(bf16)
    fc1_weight_grad = jnp.einsum("bcd,bcf->df", ffn_in, grad_hidden, preferred_element_type=f32)
    fc1_bias_grad = jnp.sum(grad_hidden.astype(f32), axis=(0, 1))
    grad_ffn_in = jnp.einsum("bcf,df->bcd", grad_hidden, fc1_weight, preferred_element_type=f32)
    grad_two, norm2_gain_grad, norm2_shift_grad = norm_backward(
        grad_ffn_in, unit_two, inverse_two, norm2_gain
    )
    grad_middle = grad_output + grad_two
    grad_proj_f, attn_gain_grad, attn_shift_grad = norm_backward(
        grad_middle, unit_attn, inverse_attn, attn_gain
    )
    grad_projection = grad_proj_f.astype(bf16)
    out_weight_grad = jnp.einsum(
        "bcd,bce->de", heads_out, grad_projection, preferred_element_type=f32
    )
    out_bias_grad = jnp.sum(grad_projection.astype(f32), axis=(0, 1))
    grad_heads = jnp.einsum(
        "bce,de->bcd", grad_projection, out_weight, preferred_element_type=f32
    ).reshape(batch_size, local_len, head_count, head_dim)
    head_scales_grad = jnp.sum(grad_heads * attended, axis=(0, 1, 3))
    grad_attended = (grad_heads * head_scales[:, None]).astype(bf16)
    row_dot = jnp.transpose(jnp.sum(grad_attended.astype(f32) * attended, axis=3), (0, 2, 1))

    def back_slab(running, key_piece, value_piece, offset):
        key_len = key_piece.shape[1]

        def back_compute(state):
            grad_queries, kv_buffer = state
            scores, keys_head = block_scores(key_piece, offset)
            attn_probs = jnp.exp(scores - log_total[..., None])
            values_head = value_piece.reshape(batch_size, key_len, head_count, head_dim)
            grad_probs = jnp.einsum(
                "bqhd,bkhd->bhqk", grad_attended, values_head, preferred_element_type=f32
            )
            grad_scores = (attn_probs * (grad_probs - row_dot[..., None])).astype(bf16)
            grad_queries = (
                grad_queries
                + jnp.einsum("bhqk,bkhd->bqhd", grad_scores, keys_head, preferred_element_type=f32)
                * score_scale
            )
            grad_keys = (
                jnp.einsum("bhqk,bqhd->bkhd", grad_scores, queries, preferred_element_type=f32)
                * score_scale
            )
            grad_values = jnp.einsum(
                "bhqk,bqhd->bkhd",
                attn_probs.astype(bf16),
                grad_attended,
                preferred_element_type=f32,
            )
            addition = jnp.concatenate(
                [
                    grad_keys.reshape(batch_size, key_len, model_width),
                    grad_values.reshape(batch_size, key_len, model_width),
                ],
                axis=2,
            )
            previous = lax.dynamic_slice_in_dim(kv_buffer, offset, key_len, 1)
            return (
                grad_queries,
                lax.dynamic_update_slice_in_dim(kv_buffer, previous + addition, offset, 1),
            )

        return lax.cond(is_live(offset, key_len), back_compute, lambda state: state, running)

    back_state = (
        jnp.zeros((batch_size, local_len, head_count, head_dim), f32),
        jnp.zeros((batch_size, row_len, 2 * model_width), f32),
    )
    attend_key_piece = lax.all_gather(keys_low, "blk", axis=1, tiled=True)
    attend_value_piece = lax.all_gather(values_low, "blk", axis=1, tiled=True)
    turns = attend_key_piece.shape[1] // local_len

    def one_turn(index, state):
        begin = index * local_len
        key_slab = lax.dynamic_slice_in_dim(attend_key_piece, begin, local_len, 1)
        value_slab = lax.dynamic_slice_in_dim(attend_value_piece, begin, local_len, 1)
        return back_slab(state, key_slab, value_slab, begin)

    grad_queries, kv_buffer = lax.fori_loop(0, turns, one_turn, back_state)
    grad_kv = lax.psum_scatter(
        kv_buffer.astype(jnp.bfloat16), "blk", scatter_dimension=1, tiled=True
    ).astype(jnp.float32)
    grad_qkv = jnp.concatenate(
        [grad_queries.reshape(batch_size, local_len, model_width), grad_kv], axis=2
    ).astype(bf16)
    qkv_weight_grad = jnp.einsum("bcd,bce->de", attn_in, grad_qkv, preferred_element_type=f32)
    query_bias_grad = jnp.sum(grad_qkv[..., :model_width].astype(f32), axis=(0, 1))
    value_bias_grad = jnp.sum(grad_qkv[..., 2 * model_width :].astype(f32), axis=(0, 1))
    grad_attn_in = jnp.einsum("bce,de->bcd", grad_qkv, qkv_weight, preferred_element_type=f32)
    grad_one, norm1_gain_grad, norm1_shift_grad = norm_backward(
        grad_attn_in, unit_one, inverse_one, norm1_gain
    )
    tokens_grad = grad_middle + grad_one
    matrix_grads = (qkv_weight_grad, out_weight_grad, fc1_weight_grad, fc2_weight_grad)
    reduced = (
        lax.psum_scatter(
            matrix_grads[0].astype(jnp.bfloat16), "dp", scatter_dimension=0, tiled=True
        ).astype(jnp.float32),
        lax.psum_scatter(
            matrix_grads[1].astype(jnp.bfloat16), "dp", scatter_dimension=0, tiled=True
        ).astype(jnp.float32),
        lax.psum_scatter(
            matrix_grads[2].astype(jnp.bfloat16), "dp", scatter_dimension=0, tiled=True
        ).astype(jnp.float32),
        lax.psum_scatter(
            matrix_grads[3].astype(jnp.bfloat16), "dp", scatter_dimension=0, tiled=True
        ).astype(jnp.float32),
    )
    reduced = (
        lax.psum_scatter(
            reduced[0].astype(jnp.bfloat16), "blk", scatter_dimension=1, tiled=True
        ).astype(jnp.float32),
        lax.psum_scatter(
            reduced[1].astype(jnp.bfloat16), "blk", scatter_dimension=1, tiled=True
        ).astype(jnp.float32),
        lax.psum_scatter(
            reduced[2].astype(jnp.bfloat16), "blk", scatter_dimension=1, tiled=True
        ).astype(jnp.float32),
        lax.psum_scatter(
            reduced[3].astype(jnp.bfloat16), "blk", scatter_dimension=1, tiled=True
        ).astype(jnp.float32),
    )
    small_sums = lax.psum(
        (
            norm1_gain_grad,
            norm1_shift_grad,
            query_bias_grad,
            value_bias_grad,
            head_scales_grad,
            out_bias_grad,
            attn_gain_grad,
            attn_shift_grad,
            norm2_gain_grad,
            norm2_shift_grad,
            fc1_bias_grad,
            mid_gain_grad,
            mid_shift_grad,
            fc2_bias_grad,
        ),
        ("dp", "blk"),
    )
    return (
        output,
        tokens_grad,
        small_sums[0],
        small_sums[1],
        reduced[0],
        small_sums[2],
        small_sums[3],
        small_sums[4],
        reduced[1],
        small_sums[5],
        small_sums[6],
        small_sums[7],
        small_sums[8],
        small_sums[9],
        reduced[2],
        small_sums[10],
        small_sums[11],
        small_sums[12],
        reduced[3],
        small_sums[13],
    )


swap = ((0, 1), (1, 0))


def exchange(x):
    return lax.ppermute(x, "blk", swap)


def flip(x, bit):
    return lax.ppermute(x, "dp", [(i, i ^ bit) for i in range(16)])


def local_rows(
    tokens,
    cotangent,
    doc_lengths,
    norm1_gain,
    norm1_shift,
    qkv_weight,
    query_bias,
    value_bias,
    head_scales,
    out_weight,
    out_bias,
    attn_gain,
    attn_shift,
    norm2_gain,
    norm2_shift,
    fc1_weight,
    fc1_bias,
    mid_gain,
    mid_shift,
    fc2_weight,
    fc2_bias,
):
    _, half_len, d = tokens.shape
    ff = fc1_weight.shape[1]
    heads = head_scales.shape[0]
    head_dim = d // heads
    scale = head_dim**-0.5
    n = 2 * half_len
    b = lax.axis_index("blk").astype(jnp.int32)
    dp = lax.axis_index("dp").astype(jnp.int32)
    core, x, z, y = dp % 2, (dp // 2) % 2, dp // 4, b

    tok_in = exchange(lax.dynamic_slice_in_dim(tokens, 1 - b, 1, 0))
    cot_in = exchange(lax.dynamic_slice_in_dim(cotangent, 1 - b, 1, 0))
    kept_at = b[None]
    sent_at = jnp.zeros((1,), jnp.int32)

    def line(v):
        return v.reshape(1, -1)

    qkv_bias = jnp.concatenate([query_bias, jnp.zeros_like(query_bias), value_bias])
    first_args = (line(norm1_gain), line(norm1_shift), qkv_weight, line(qkv_bias), scale)
    early = project_qkv(kept_at, tokens, *first_args, 0, n)

    def later(v):
        return after(v, early[0])

    lengths = lax.dynamic_slice_in_dim(later(doc_lengths), b, 1, 0)
    ends = running_sums(lengths)[0]
    firsts = (half_len // 2) * jnp.arange(4, dtype=jnp.int32)
    starts = jnp.max(jnp.where(ends[None, :] <= firsts[:, None], ends[None, :], 0), axis=1)
    allowed = (firsts[None, :] >= starts[:, None]).astype(jnp.int32)
    tab = jnp.concatenate([b[None], allowed.reshape(16)])
    theirs = jnp.stack([1 - core, x, y])
    mine = jnp.stack([core, x, y])
    head_scales = later(head_scales)
    scale_row = jnp.broadcast_to(head_scales[:, None], (heads, head_dim)).reshape(1, d)
    vec = jnp.stack(
        [later(out_bias), attn_gain, attn_shift, norm2_gain, norm2_shift, fc2_bias, scale_row[0], out_bias]
    )
    fc1_bias = later(fc1_bias)
    vec4 = jnp.stack([fc1_bias, mid_gain, mid_shift, fc1_bias])

    made = after(sent_at, tab, theirs, mine, scale_row, vec, vec4)
    attn_in, qkv = project_qkv(made, tok_in, *first_args, 1, n, early)
    qkv = qkv.reshape(2, half_len, 3 * d)
    heads_out, logs = attend(tab, qkv, scale_row)

    weights = (out_weight, fc1_weight, fc2_weight, vec, vec4)
    out_sent, mid_sent, *more = middle_pass(sent_at, heads_out, tok_in, cot_in, *weights, 1, False)
    sums, sums4, *earlier = more
    out_back = exchange(out_sent)
    output, mid_kept, *more = middle_pass(
        kept_at, heads_out, tokens, cotangent, *weights, 0, True, earlier
    )
    sums = sums + more[0]
    sums4 = sums4 + more[1]
    ffn_in, heads_in, mid_out, grad_hidden, grad_proj, d_out = more[2:]

    def fill(kept, back):
        return lax.dynamic_update_slice_in_dim(kept, back.astype(f32)[None], 1 - b, 0)

    def near_z(total):
        total = total.astype(bf16).reshape((2, 2) + total.shape[1:])
        odd = z % 2
        return (
            lax.dynamic_index_in_dim(total, 1 - odd, 1, keepdims=False),
            lax.dynamic_index_in_dim(total, odd, 1, keepdims=False),
        )

    def far_z(total):
        total = total.astype(bf16)
        high = z // 2
        return (
            lax.dynamic_index_in_dim(total, 1 - high, 0, keepdims=False),
            lax.dynamic_index_in_dim(total, high, 0, keepdims=False),
        )

    def add_z(move, send, keep):
        return keep.astype(f32) + flip(send, move).astype(f32)

    def held(parts, *others):
        return parts[0], after(parts[1], *others)

    def rows_by_x(total):
        total = total.astype(bf16).reshape(4, 2, -1, total.shape[1])
        return (
            lax.dynamic_index_in_dim(total, 1 - x, 1, keepdims=False),
            lax.dynamic_index_in_dim(total, x, 1, keepdims=False),
        )

    def columns_by_y(total, *cuts):
        total = total.astype(bf16).reshape(4, -1, total.shape[1])
        out = []
        for at in (1 - y, y):
            groups = []
            for first, last in zip((0,) + cuts, cuts + (total.shape[2],)):
                width = (last - first) // 2
                groups.append(lax.dynamic_slice_in_dim(total, first + at * width, width, 2))
            out.append(jnp.concatenate(groups, axis=2) if cuts else groups[0])
        return out

    def add_x(send, keep):
        return keep.astype(f32) + flip(send, 2).astype(f32)

    def add_y(send, keep):
        return keep.astype(f32) + exchange(send).astype(f32)

    cots = (cotangent, cot_in)
    output = fill(output, out_back)
    wide_pairs = [(after(ffn_in, output), grad_hidden), (heads_in, grad_proj)]
    wide_theirs = flat_grad(theirs, wide_pairs, d)
    fc2_theirs = tall_grad(theirs, after(mid_out, wide_theirs), cots)
    wide_pairs = [(after(ffn_in, fc2_theirs), grad_hidden), (heads_in, grad_proj)]
    wide_parts = flat_grad(mine, wide_pairs, d, flip(wide_theirs, 1))
    fc2_parts = tall_grad(mine, after(mid_out, *wide_parts), cots, flip(fc2_theirs, 1))
    d_out = after(d_out, *fc2_parts)
    back_args = (1.0 / scale_row, logs, scale)
    even, dots_even = attend_back(tab, qkv, heads_out, d_out, *back_args, 0)
    even = even.reshape(3, n, d // 2)
    even_theirs = flat_grad(theirs, [(after(attn_in, even), even)], d // 2)
    d_out = after(d_out, even_theirs)
    odd, dots_odd = attend_back(tab, qkv, heads_out, d_out, *back_args, 1)
    odd = odd.reshape(3, n, d // 2)
    wide_parts = columns_by_y(add_x(*held(wide_parts, odd)), ff)
    fc2_parts = rows_by_x(add_y(*held(fc2_parts, odd)))
    odd_theirs = flat_grad(theirs, [(after(attn_in, *wide_parts, *fc2_parts), odd)], d // 2)
    even_parts = flat_grad(mine, [(after(attn_in, odd_theirs), even)], d // 2, flip(even_theirs, 1))
    grad_sent, sums_sent = first_back(
        sent_at, after(even, *even_parts), odd, qkv_weight, tok_in, mid_sent, line(norm1_gain), 1, False
    )
    grad_back = exchange(grad_sent)
    fc2_parts = near_z(add_x(*held(fc2_parts, grad_sent)))
    wide_parts = near_z(add_y(*held(wide_parts, *fc2_parts)))
    tokens_grad, sums_kept = first_back(
        kept_at, after(even, *wide_parts), odd, qkv_weight, tokens, mid_kept, line(norm1_gain), 0, True
    )
    odd_parts = flat_grad(
        mine, [(after(attn_in, tokens_grad), odd)], d // 2, flip(odd_theirs, 1)
    )
    dots = jnp.stack([dots_even[:, 0].reshape(2, 4, head_dim), dots_odd[:, 0].reshape(2, 4, head_dim)], axis=1)
    head_scales_grad = jnp.sum(dots, axis=3).reshape(heads) / head_scales
    head_scales_grad = jnp.pad(head_scales_grad, (0, d - heads))
    total = jnp.concatenate(
        [
            (sums_sent + sums_kept)[:4],
            head_scales_grad[None],
            sums[:6],
            sums4.reshape(8 * ff // d, d)[: 3 * ff // d],
        ]
    )
    fc2_parts = far_z(add_z(4, *held(fc2_parts, tokens_grad)))
    even_parts = columns_by_y(add_x(*held(even_parts, tokens_grad)))
    total = after(total, *odd_parts)
    odd_parts = columns_by_y(add_x(*odd_parts))
    wide_parts = far_z(add_z(4, *held(wide_parts, *fc2_parts, *even_parts)))
    tokens_grad = fill(tokens_grad, grad_back)
    for move in (partial(flip, bit=1), partial(flip, bit=4), partial(flip, bit=8)):
        total = total + move(total)
    total = after(total, *odd_parts)
    for move in (partial(flip, bit=2), exchange):
        total = total + move(total)
    fc2_weight_grad = add_z(8, *fc2_parts)
    even_parts = near_z(add_y(*even_parts))
    wide_grad = add_z(8, *wide_parts)
    fc1_weight_grad, out_weight_grad = wide_grad[:, : ff // 2], wide_grad[:, ff // 2 :]
    even_parts = far_z(add_z(4, *even_parts))
    odd_parts = far_z(add_z(4, *near_z(add_y(*odd_parts))))
    even_grad, odd_grad = (add_z(8, *parts) for parts in (even_parts, odd_parts))
    first_sums, sums, sums4 = total[:5], total[5:11], total[11:].reshape(3, ff)
    run = d // 4
    qkv_weight_grad = jnp.stack(
        [even_grad.reshape(-1, 3, run), odd_grad.reshape(-1, 3, run)], axis=2
    ).reshape(-1, 6 * run)
    return (
        output,
        tokens_grad,
        first_sums[0],
        first_sums[1],
        qkv_weight_grad,
        first_sums[2],
        first_sums[3],
        first_sums[4, :heads],
        out_weight_grad,
        sums[0],
        sums[1],
        sums[2],
        sums[3],
        sums[4],
        fc1_weight_grad,
        sums4[0],
        sums4[1],
        sums4[2],
        fc2_weight_grad,
        sums[5],
    )


def solution(mesh):
    rows_fit = dict(mesh.shape) == {"dp": 16, "blk": 2}
    local = local_rows if rows_fit else local_general
    placed = (
        P("dp", "blk", None),
        P("dp", "blk", None),
        P("dp", None),
        P(),
        P(),
        P(),
        P(),
        P(),
        P(),
        P(),
        P(),
        P(),
        P(),
        P(),
        P(),
        P(),
        P(),
        P(),
        P(),
        P(),
        P(),
    )
    return jax.shard_map(
        local,
        mesh=mesh,
        in_specs=placed,
        out_specs=(
            P("dp", "blk", None),
            P("dp", "blk", None),
            P(),
            P(),
            P("dp", "blk"),
            P(),
            P(),
            P(),
            P("dp", "blk"),
            P(),
            P(),
            P(),
            P(),
            P(),
            P("dp", "blk"),
            P(),
            P(),
            P(),
            P("dp", "blk"),
            P(),
        ),
        check_vma=False,
    )
```

```python
from functools import partial

import jax
import jax.numpy as jnp
from jax import lax
from jax.experimental import pallas as pl
from jax.experimental.pallas import tpu as pltpu
from jax.sharding import PartitionSpec as P

f32 = jnp.float32
bf16 = jnp.bfloat16
eps = 1e-05
masked_score = -1e30
LANES = 128
NT = (((1,), (1,)), ((), ()))
NN = (((1,), (0,)), ((), ()))
TN = (((0,), (0,)), ((), ()))


def mm(a, b, dims=NN):
    return lax.dot_general(a, b, dims, preferred_element_type=f32)


def fold(x):
    total = x[:, :LANES]
    for c in range(LANES, x.shape[1], LANES):
        total = total + x[:, c : c + LANES]
    return total


def row_mean(x):
    return jnp.sum(fold(x), axis=1, keepdims=True) * (1.0 / x.shape[1])


def row_sum(x):
    return jnp.sum(x, axis=0, keepdims=True)


def norm_unit(v):
    centered = v - row_mean(v)
    inverse = lax.rsqrt(row_mean(centered * centered) + eps)
    return centered * inverse, inverse


def norm_back(grad_y, unit, inverse, gain):
    e = grad_y * gain
    return inverse * (e - row_mean(e) - unit * row_mean(e * unit))


def params(mib=None, **more):
    return pltpu.CompilerParams(vmem_limit_bytes=(mib or 60) * 2**20, **more)


def cost(flops, moved):
    return pl.CostEstimate(flops=flops, bytes_accessed=moved, transcendentals=0)


def whole(shape):
    return pl.BlockSpec(shape, lambda *_: (0,) * len(shape), pipeline_mode=pl.Buffered(1))


def core_split(x):
    low = lax.broadcasted_iota(jnp.int32, (x.shape[0], LANES), 1) < LANES // 2
    even, odd = [], []
    for c in range(0, x.shape[1], 2 * LANES):
        a = x[:, c : c + LANES].astype(f32)
        b = x[:, c + LANES : c + 2 * LANES].astype(f32)
        even.append(jnp.where(low, a, pltpu.roll(b, LANES // 2, 1)))
        odd.append(jnp.where(low, pltpu.roll(a, LANES // 2, 1), b))
    return (jnp.concatenate(y, axis=1).astype(bf16) for y in (even, odd))


def qkv_body(scale, at, tok, gain, shift, w, bias, *refs):
    attn_in, qkv, x, ws, sems = refs[-5:]
    step = pl.program_id(0)
    steps, d, cols = ws.shape
    half = cols // 2

    def fetch(k, h):
        columns = pl.ds(pl.multiple_of(k * cols + h * half, half), half)
        return pltpu.make_async_copy(
            w.at[:, columns], ws.at[k, :, pl.ds(h * half, half)], sems.at[k, h]
        )

    @pl.when(step == 0)
    def _():
        for k in range(steps):
            for h in range(2):
                fetch(k, h).start()
        unit, _ = norm_unit(tok[0].astype(f32))
        here = (unit * gain[...] + shift[...]).astype(bf16)
        x[...] = here
        attn_in[0], attn_in[1] = core_split(here)

    for h in range(2):
        fetch(step, h).wait()
    total = (mm(x[...], ws[step]) + bias[...]).astype(bf16)
    qkv[...] = (total.astype(f32) * jnp.where(step == 0, scale, 1.0)).astype(bf16)


def project_qkv(at, tok, gain, shift, w, bias, scale, slot, total, earlier=()):
    _, n, d = tok.shape
    held = pl.BlockSpec(memory_space=pl.ANY)
    return pl.pallas_call(
        partial(qkv_body, scale),
        name="project_qkv",
        grid_spec=pltpu.PrefetchScalarGridSpec(
            num_scalar_prefetch=1,
            grid=(3,),
            in_specs=[
                pl.BlockSpec((1, n, d), lambda i, at: (at[0], 0, 0), pipeline_mode=pl.Buffered(1)),
                whole(gain.shape),
                whole(shift.shape),
                held,
                pl.BlockSpec((1, d), lambda i, at: (0, i)),
            ]
            + [held] * len(earlier),
            out_specs=[
                pl.BlockSpec((2, n, d // 2), lambda i, at: (0, slot, 0)),
                pl.BlockSpec((n, d), lambda i, at: (slot, i)),
            ],
            scratch_shapes=[
                pltpu.VMEM((n, d), bf16),
                pltpu.VMEM((3, d, d), bf16),
                pltpu.SemaphoreType.DMA((3, 2)),
            ],
        ),
        out_shape=[
            jax.ShapeDtypeStruct((2, total, d // 2), bf16),
            jax.ShapeDtypeStruct((total, 3 * d), bf16),
        ],
        input_output_aliases={6 + k: k for k in range(len(earlier))},
        compiler_params=params(),
        cost_estimate=cost(2 * n * d * 3 * d, 6 * d * d + 10 * n * d),
    )(at, tok, gain, shift, w, bias, *earlier)


def half_slot(own, half):
    return own if half == 0 else 1 - own


def pick(ref, own, block, size):
    half, sub = divmod(block, 2)
    return ref[half_slot(own, half), sub * size : (sub + 1) * size, :]


def head_mask(size):
    return lax.broadcasted_iota(jnp.int32, (size, LANES), 1) < LANES // 2


def block_penalty(tab, i, j):
    return jnp.where(tab[1 + 4 * i + j] > 0, 0.0, masked_score).astype(f32)


def stack_heads(x, low):
    zero = jnp.zeros_like(x)
    return jnp.concatenate([jnp.where(low, x, zero), jnp.where(low, zero, x)], axis=0)


def place(ref, own, *targets):
    half = ref.shape[1]
    for h in range(2):
        targets[0][h * half : (h + 1) * half, :] = ref[half_slot(own, h)]


def attend_body(tab, q, k, v, head_scale, heads_out, lse, kp, vp):
    size = q.shape[1] // 2
    own = tab[0]
    low = head_mask(size)
    causal = lax.broadcasted_iota(jnp.int32, (2 * size, size), 0) % size >= lax.broadcasted_iota(
        jnp.int32, (2 * size, size), 1
    )
    lane = lax.broadcasted_iota(jnp.int32, (size, LANES), 1)
    place(k, own, kp)
    place(v, own, vp)
    for i in range(4):
        width = (i + 1) * size
        s = mm(stack_heads(pick(q, own, i, size), low), kp[:width, :], NT)
        parts = [s[:, j * size : (j + 1) * size] + block_penalty(tab, i, j) for j in range(i)]
        parts.append(jnp.where(causal, s[:, i * size :], masked_score))
        top = parts[0]
        for part in parts[1:]:
            top = jnp.maximum(top, part)
        top = jnp.max(top, axis=1, keepdims=True)
        parts = [jnp.exp(part - top) for part in parts]
        total = fold(parts[0])
        for part in parts[1:]:
            total = total + fold(part)
        total = jnp.sum(total, axis=1, keepdims=True)
        p = jnp.concatenate([part.astype(bf16) for part in parts], axis=1)
        out = mm(p, vp[:width, :]) * (1.0 / total)
        both = jnp.where(low, out[:size], out[size:]) * head_scale[...]
        half, sub = divmod(i, 2)
        heads_out[half_slot(own, half), sub * size : (sub + 1) * size, :] = both.astype(bf16)
        logs = top + jnp.log(total)
        columns = jnp.where(lane == 0, logs[:size], logs[size:])
        lse[0, i] = jnp.transpose(columns)[:8]


def attend(tab, qkv, head_scale_row):
    _, half_len, wide = qkv.shape
    d = wide // 3
    pairs = d // LANES
    size = half_len // 2

    def lanes(first):
        return pl.BlockSpec((2, half_len, LANES), lambda p, t: (0, 0, first + p))

    flops = 16 * half_len * half_len * pairs * LANES
    return pl.pallas_call(
        attend_body,
        name="attend",
        grid_spec=pltpu.PrefetchScalarGridSpec(
            num_scalar_prefetch=1,
            grid=(pairs,),
            in_specs=[
                lanes(0),
                lanes(pairs),
                lanes(2 * pairs),
                pl.BlockSpec((1, LANES), lambda p, t: (0, p)),
            ],
            out_specs=[
                lanes(0),
                pl.BlockSpec((1, 4, 8, size), lambda p, t: (p, 0, 0, 0)),
            ],
            scratch_shapes=[pltpu.VMEM((2 * half_len, LANES), bf16)] * 2,
        ),
        out_shape=[
            jax.ShapeDtypeStruct((2, half_len, d), bf16),
            jax.ShapeDtypeStruct((pairs, 4, 8, size), f32),
        ],
        compiler_params=params(),
        cost_estimate=cost(flops * 4, 8 * half_len * wide),
    )(tab, qkv, qkv, qkv, head_scale_row)


def attend_back_body(
    scale, tab, q, k, v, heads_out, d_out, inv_scale, lse, dqkv, dots, kp, vp, dk, dv
):
    size = q.shape[1] // 2
    own = tab[0]
    low = head_mask(size)
    causal = lax.broadcasted_iota(jnp.int32, (2 * size, size), 0) % size >= lax.broadcasted_iota(
        jnp.int32, (2 * size, size), 1
    )
    place(k, own, kp)
    place(v, own, vp)
    dots[...] = jnp.zeros_like(dots)
    for i in range(3, -1, -1):
        width = (i + 1) * size
        q2 = stack_heads(pick(q, own, i, size), low)
        gi = pick(d_out, own, i, size)
        g2 = stack_heads(gi, low)
        product = gi.astype(f32) * pick(heads_out, own, i, size).astype(f32) * inv_scale[...]
        dots[0, 0:1, :] += row_sum(product)
        zero = jnp.zeros_like(product)
        delta = jnp.concatenate(
            [
                jnp.sum(jnp.where(low, product, zero), axis=1, keepdims=True),
                jnp.sum(jnp.where(low, zero, product), axis=1, keepdims=True),
            ],
            axis=0,
        )
        columns = jnp.transpose(lse[0, i])
        logs = jnp.concatenate([columns[:, 0:1], columns[:, 1:2]], axis=0)
        s = mm(q2, kp[:width, :], NT)
        g = mm(g2, vp[:width, :], NT)
        ps, ds = [], []
        for j in range(i + 1):
            here = slice(j * size, (j + 1) * size)
            if j < i:
                p = jnp.exp(s[:, here] - (logs - block_penalty(tab, i, j)))
            else:
                p = jnp.exp(jnp.where(causal, s[:, here], masked_score) - logs)
            ps.append(p.astype(bf16))
            ds.append((p * (g[:, here] - delta)).astype(bf16))
        p = jnp.concatenate(ps, axis=1)
        d = jnp.concatenate(ds, axis=1)
        dv_part = mm(p, g2, TN)
        dk_part = mm(d, q2, TN)
        if i == 3:
            dv[...] = dv_part
            dk[...] = dk_part
        else:
            dv[:width, :] += dv_part
            dk[:width, :] += dk_part
        dq = mm(d, kp[:width, :]) * scale
        half, sub = divmod(i, 2)
        dqkv[0, half_slot(own, half), sub * size : (sub + 1) * size, :] = jnp.where(
            low, dq[:size], dq[size:]
        ).astype(bf16)
    for half in range(2):
        here = slice(half * 2 * size, (half + 1) * 2 * size)
        dqkv[1, half_slot(own, half)] = dk[here, :].astype(bf16)
        dqkv[2, half_slot(own, half)] = dv[here, :].astype(bf16)


def attend_back(tab, qkv, heads_out, d_out, inv_scale_row, lse, scale, group):
    _, half_len, wide = qkv.shape
    d = wide // 3
    every = d // LANES
    pairs = every // 2
    size = half_len // 2

    def pair(p):
        return p + 2 * (p // 2) + 2 * group

    def lanes(first):
        return pl.BlockSpec((2, half_len, LANES), lambda p, t: (0, 0, first + pair(p)))

    flops = 16 * half_len * half_len * pairs * LANES
    return pl.pallas_call(
        partial(attend_back_body, scale),
        name="attend_back",
        grid_spec=pltpu.PrefetchScalarGridSpec(
            num_scalar_prefetch=1,
            grid=(pairs,),
            in_specs=[
                lanes(0),
                lanes(every),
                lanes(2 * every),
                lanes(0),
                lanes(0),
                pl.BlockSpec((1, LANES), lambda p, t: (0, pair(p))),
                pl.BlockSpec((1, 4, 8, size), lambda p, t: (pair(p), 0, 0, 0)),
            ],
            out_specs=[
                pl.BlockSpec((3, 2, half_len, LANES), lambda p, t: (0, 0, 0, p)),
                pl.BlockSpec((1, 8, LANES), lambda p, t: (p, 0, 0)),
            ],
            scratch_shapes=[pltpu.VMEM((2 * half_len, LANES), bf16)] * 2
            + [pltpu.VMEM((2 * half_len, LANES), f32)] * 2,
        ),
        out_shape=[
            jax.ShapeDtypeStruct((3, 2, half_len, d // 2), bf16),
            jax.ShapeDtypeStruct((pairs, 8, LANES), f32),
        ],
        compiler_params=params(),
        cost_estimate=cost(flops * 10, 8 * half_len * wide),
    )(tab, qkv, qkv, qkv, heads_out, d_out, inv_scale_row, lse)


def gelu_parts(v):
    a = jnp.abs(v)
    t = 1.0 / (1.0 + (0.3275911 * 0.7071067811865476) * a)
    bell = jnp.exp(v * v * -0.5)
    poly = ((((1.061405429 * t - 1.453152027) * t + 1.421413741) * t - 0.284496736) * t + 0.254829592) * t
    tail = (0.5 * poly) * bell
    cdf = jnp.where(v < 0, tail, 1.0 - tail)
    return v * cdf, cdf + v * (bell * 0.3989422804014327)


def middle_body(
    at, ho, tok, cot, out_w, w1, w2, vec, vec4, *refs
):
    (
        output, grad_middle, sums, sums4, ffn_in, heads_in, mid_out, grad_hidden, grad_proj, d_out,
        act, slope, back, acc, unit_b, stats, total, total_u, w1s, w2s, sems,
    ) = refs[-21:]
    ho, tok, cot, d_out = (ref.at[0] for ref in (ho, tok, cot, d_out))
    output = output.at[0] if len(output.shape) == 3 else output
    step = pl.program_id(0)
    n, d = ho.shape
    chunks, _, fc = w1s.shape
    ff = fc * chunks
    c = step % chunks
    ahead = 2

    def fetch(k):
        columns = pl.ds(pl.multiple_of(k * fc, fc), fc)
        return (
            pltpu.make_async_copy(w1.at[:, columns], w1s.at[k], sems.at[0, k]),
            pltpu.make_async_copy(w2.at[columns, :], w2s.at[k], sems.at[1, k]),
        )
    strip = 128
    strips = n // strip

    def v(r):
        return vec[r : r + 1, :]

    def rows(t):
        return pl.ds(pl.multiple_of(t * strip, strip), strip)

    @pl.when(step == 0)
    def _():
        for k in range(ahead):
            for copy in fetch(k):
                copy.start()
        sums[...] = jnp.zeros_like(sums)
        acc[...] = mm(ho[...], out_w[...])

        def one(t, _):
            r = rows(t)
            unit_attn, inverse_attn = norm_unit(acc[r, :] + v(0))
            middle = tok[r, :].astype(f32) + (unit_attn * v(1) + v(2))
            unit_two, inverse_two = norm_unit(middle)
            x = (unit_two * v(3) + v(4)).astype(bf16)
            grad_middle[r, :] = unit_attn
            unit_b[r, :] = unit_two
            stats[r, 0:1] = inverse_attn
            stats[r, 1:2] = inverse_two
            acc[r, :] = middle + v(5)
            d_out[r, :] = x
            ffn_in[0, r, :], ffn_in[1, r, :] = core_split(x)
            heads_in[0, r, :], heads_in[1, r, :] = core_split(ho[r, :])
            return 0

        lax.fori_loop(0, strips, one, 0)

    @pl.when(step < chunks - ahead)
    def _():
        for copy in fetch(step + ahead):
            copy.start()

    @pl.when(step < chunks)
    def _():
        for copy in fetch(step):
            copy.wait()
        h = mm(d_out[...], w1s[c]) + vec4[0:1, :]
        back[c] = mm(cot[...], w2s[c], NT).astype(back.dtype)
        a, b = gelu_parts(h)
        act[c] = a
        slope[c] = b.astype(slope.dtype)

    @pl.when(step == 0)
    def _():
        total[...] = jnp.zeros_like(total)

    @pl.when(step < chunks)
    def _():
        total[...] += fold(act[c])

    @pl.when(step == chunks)
    def _():
        mean = jnp.sum(total[...], axis=1, keepdims=True) * (1.0 / ff)

        def one(k, t):
            centered = act[k] - mean
            return t + fold(centered * centered)

        square = lax.fori_loop(0, chunks, one, jnp.zeros_like(total))
        stats[:, 2:3] = mean
        stats[:, 3:4] = lax.rsqrt(jnp.sum(square, axis=1, keepdims=True) * (1.0 / ff) + eps)
        total[...] = jnp.zeros_like(total)
        total_u[...] = jnp.zeros_like(total_u)

    here = pl.ds(pl.multiple_of(c * fc, fc), fc)

    @pl.when((step >= chunks) & (step < 2 * chunks))
    def _():
        u = (act[c] - stats[:, 2:3]) * stats[:, 3:4]
        act[c] = u
        gain = vec4[1:2, :]
        m = (u * gain + vec4[2:3, :]).astype(bf16)
        mid_out[...] = m
        acc[...] += mm(m, w2s[c])
        gm = back[c].astype(f32)
        gmu = gm * u
        sums4[1:2, here] = row_sum(gmu)
        sums4[2:3, here] = row_sum(gm)
        total[...] += fold(gm * gain)
        total_u[...] += fold(gmu * gain)

    @pl.when(step == 2 * chunks)
    def _():
        stats[:, 4:5] = jnp.sum(total[...], axis=1, keepdims=True) * (1.0 / ff)
        stats[:, 5:6] = jnp.sum(total_u[...], axis=1, keepdims=True) * (1.0 / ff)
        output[...] = acc[...].astype(output.dtype)
        acc[...] = jnp.zeros_like(acc)

    @pl.when(step >= 2 * chunks)
    def _():
        e = back[c].astype(f32) * vec4[1:2, :]
        grad_act = stats[:, 3:4] * (e - stats[:, 4:5] - act[c] * stats[:, 5:6])
        gh = (grad_act * slope[c].astype(f32)).astype(bf16)
        grad_hidden[...] = gh
        sums4[0:1, here] = row_sum(gh.astype(f32))
        acc[...] += mm(gh, w1s[c], NT)

    @pl.when(step == 3 * chunks - 1)
    def _():
        def one(t, _):
            r = rows(t)
            grad_ffn_in = acc[r, :]
            unit_two = unit_b[r, :]
            unit_attn = grad_middle[r, :]
            gout = cot[r, :].astype(f32)
            sums[5:6, :] += row_sum(gout)
            sums[3:4, :] += row_sum(grad_ffn_in * unit_two)
            sums[4:5, :] += row_sum(grad_ffn_in)
            gmid = gout + norm_back(grad_ffn_in, unit_two, stats[r, 1:2], v(3))
            grad_middle[r, :] = gmid
            sums[1:2, :] += row_sum(gmid * unit_attn)
            sums[2:3, :] += row_sum(gmid)
            gp = norm_back(gmid, unit_attn, stats[r, 0:1], v(1)).astype(bf16)
            grad_proj[r, :] = gp
            sums[0:1, :] += row_sum(gp.astype(f32))
            return 0

        lax.fori_loop(0, strips, one, 0)
        d_out[...] = (mm(grad_proj[...], out_w[...], NT) * v(6)).astype(bf16)


def middle_pass(at, ho, tok, cot, out_w, w1, w2, vec, vec4, slot, last_part, earlier=(), fc=1024):
    _, n, d = ho.shape
    ff = w1.shape[1]
    chunks = ff // fc
    last = chunks - 1
    rows = whole((n, d))
    held = pl.BlockSpec(memory_space=pl.ANY)

    def once(shape, index):
        return pl.BlockSpec(shape, index, pipeline_mode=pl.Buffered(1))

    in_place = once((1, n, d), lambda t, at: (at[0], 0, 0))
    in_slot = once((1, n, d), lambda t, at: (slot, 0, 0))
    split = once((2, n, d // 2), lambda t, at: (0, slot, 0))
    kind = f32 if last_part else bf16
    return pl.pallas_call(
        middle_body,
        name="middle_pass",
        grid_spec=pltpu.PrefetchScalarGridSpec(
            num_scalar_prefetch=1,
            grid=(3 * chunks,),
            in_specs=[
                in_slot,
                in_place,
                in_place,
                whole(out_w.shape),
                held,
                held,
                whole(vec.shape),
                pl.BlockSpec((vec4.shape[0], fc), lambda t, at: (0, t % chunks)),
            ]
            + [held] * len(earlier),
            out_specs=[
                in_place if last_part else rows,
                rows,
                whole((8, d)),
                whole((8, ff)),
                split,
                split,
                pl.BlockSpec((n, fc), lambda t, at: (slot, jnp.clip(t - chunks, 0, last))),
                pl.BlockSpec((n, fc), lambda t, at: (slot, jnp.clip(t - 2 * chunks, 0, last))),
                once((n, d), lambda t, at: (slot, 0)),
                in_slot,
            ],
            scratch_shapes=[
                pltpu.VMEM((chunks, n, fc), f32),
                pltpu.VMEM((chunks, n, fc), bf16),
                pltpu.VMEM((chunks, n, fc), bf16),
                pltpu.VMEM((n, d), f32),
                pltpu.VMEM((n, d), f32),
                pltpu.VMEM((n, LANES), f32),
                pltpu.VMEM((n, LANES), f32),
                pltpu.VMEM((n, LANES), f32),
                pltpu.VMEM((chunks, d, fc), bf16),
                pltpu.VMEM((chunks, fc, d), bf16),
                pltpu.SemaphoreType.DMA((2, chunks)),
            ],
        ),
        out_shape=[
            jax.ShapeDtypeStruct((2, n, d) if last_part else (n, d), kind),
            jax.ShapeDtypeStruct((n, d), f32),
            jax.ShapeDtypeStruct((8, d), f32),
            jax.ShapeDtypeStruct((8, ff), f32),
            jax.ShapeDtypeStruct((2, 2 * n, d // 2), bf16),
            jax.ShapeDtypeStruct((2, 2 * n, d // 2), bf16),
            jax.ShapeDtypeStruct((2 * n, ff), bf16),
            jax.ShapeDtypeStruct((2 * n, ff), bf16),
            jax.ShapeDtypeStruct((2 * n, d), bf16),
            jax.ShapeDtypeStruct((2, n, d), bf16),
        ],
        input_output_aliases={9 + k: 4 + k for k in range(len(earlier))},
        compiler_params=params(62),
        cost_estimate=cost(
            8 * n * d * ff + 4 * n * d * d, 4 * d * ff + 2 * d * d + 4 * n * ff + 20 * n * d
        ),
    )(at, ho, tok, cot, out_w, w1, w2, vec, vec4, *earlier)


def first_back_body(at, even, odd, w, tok, grad_middle, gain, tokens_grad, sums):
    @pl.when(pl.program_id(0) == 0)
    def _():
        sums[...] = jnp.zeros_like(sums)

    d = w.shape[0]
    run = d // 4
    grad = None
    for part in range(3):
        for r in range(4):
            piece = (even, odd)[r % 2][part, :, (r // 2) * run : (r // 2 + 1) * run]
            here = r * run
            term = mm(piece, w[:, part * d + here : part * d + here + run], NT)
            grad = term if grad is None else grad + term
            if part != 1:
                at = 2 + part // 2
                sums[at : at + 1, here : here + run] += row_sum(piece.astype(f32))
    unit, inverse = norm_unit(tok[0].astype(f32))
    sums[0:1, :] += row_sum(grad * unit)
    sums[1:2, :] += row_sum(grad)
    whole_grad = grad_middle[...] + norm_back(grad, unit, inverse, gain[...])
    if len(tokens_grad.shape) == 3:
        tokens_grad[0] = whole_grad
    else:
        tokens_grad[...] = whole_grad.astype(tokens_grad.dtype)


def first_back(at, even, odd, w, tok, grad_middle, gain, slot, last_part, tb=256):
    d = w.shape[0]
    n = even.shape[1] // 2
    first = slot * (n // tb)
    half = pl.BlockSpec((3, tb, d // 2), lambda i, at: (0, first + i, 0))
    rows = pl.BlockSpec((tb, d), lambda i, at: (i, 0))
    in_place = pl.BlockSpec((1, tb, d), lambda i, at: (at[0], i, 0))
    return pl.pallas_call(
        first_back_body,
        name="first_back",
        grid_spec=pltpu.PrefetchScalarGridSpec(
            num_scalar_prefetch=1,
            grid=(n // tb,),
            in_specs=[half, half, whole(w.shape), in_place, rows, whole(gain.shape)],
            out_specs=[in_place if last_part else rows, whole((8, d))],
        ),
        out_shape=[
            jax.ShapeDtypeStruct((2, n, d), f32) if last_part else jax.ShapeDtypeStruct((n, d), bf16),
            jax.ShapeDtypeStruct((8, d), f32),
        ],
        compiler_params=params(),
        cost_estimate=cost(6 * n * d * d, 6 * d * d + 16 * n * d),
    )(at, even, odd, w, tok, grad_middle, gain)


def after(x, *others):
    return lax.optimization_barrier((x,) + others)[0]


def emit(at_low, low, high, received, outs):
    send, keep = jnp.where(at_low, high, low), jnp.where(at_low, low, high)
    if received is None:
        outs[-1][0] = send.astype(bf16)
        outs[-1][1] = keep.astype(bf16)
    else:
        outs[-2][...] = (send + received[0].astype(f32)).astype(bf16)
        outs[-1][...] = (keep + received[1].astype(f32)).astype(bf16)


def tall_grad_body(received_too, tab, *refs):
    runs, halves = refs[:2], refs[2:4]
    a = jnp.concatenate([r[...] for r in runs], axis=1)
    total = mm(a, jnp.concatenate([h[0] for h in halves], axis=0), TN)
    wide = total.shape[1] // 2
    emit(tab[2] == 0, total[:, :wide], total[:, wide:], refs[4] if received_too else None, refs)


def tall_grad(tab, a, b, received=None):
    n, wide = a.shape
    d = b[0].shape[2]
    tall = wide // 16
    steps = 4

    def run(k):
        return pl.BlockSpec((n, tall), lambda i, t: (0, (2 * i + k) * 2 + t[0]))

    in_specs = [
        run(0),
        run(1),
        pl.BlockSpec((1, n // 2, d), lambda i, t: (t[2], 0, 0), pipeline_mode=pl.Buffered(1)),
        pl.BlockSpec((1, n // 2, d), lambda i, t: (0, 0, 0), pipeline_mode=pl.Buffered(1)),
    ]
    both = pl.BlockSpec((2, 2 * tall, d // 2), lambda i, t: (0, i, 0))
    one = pl.BlockSpec((2 * tall, d // 2), lambda i, t: (i, 0))
    args = [tab, a, a, *b]
    if received is not None:
        in_specs.append(both)
        args.append(received)
    shape = (wide // 2, d // 2)
    return pl.pallas_call(
        partial(tall_grad_body, received is not None),
        name="tall_grad",
        grid_spec=pltpu.PrefetchScalarGridSpec(
            num_scalar_prefetch=1,
            grid=(steps,),
            in_specs=in_specs,
            out_specs=both if received is None else [one, one],
        ),
        out_shape=jax.ShapeDtypeStruct((2,) + shape, bf16)
        if received is None
        else [jax.ShapeDtypeStruct(shape, bf16)] * 2,
        compiler_params=params(),
        cost_estimate=cost(2 * n * wide * d // 2, n * wide + 2 * n * d + 8 * wide * d // 4),
    )(*args)


def flat_grad_body(counts, received_too, tab, *refs):
    step = pl.program_id(0)
    parts = len(counts)
    lhs, rhs = refs[:parts], refs[parts : 2 * parts]
    first = 0
    for k, count in enumerate(counts):

        @pl.when((step >= first) & (step < first + count))
        def _(k=k):
            b = rhs[k][0] if len(rhs[k].shape) == 3 else rhs[k][...]
            total = mm(lhs[k][0], b, TN)
            run = total.shape[0] // 8
            low, high = (
                jnp.concatenate([total[(2 * z + h) * run : (2 * z + h + 1) * run] for z in range(4)])
                for h in range(2)
            )
            emit(tab[1] == 0, low, high, refs[2 * parts] if received_too else None, refs)

        first += count


def flat_grad(tab, pairs, tn, received=None):
    counts = [b.shape[0] if b.ndim == 3 else b.shape[1] // tn for _, b in pairs]
    steps = sum(counts)
    n, wide = pairs[0][0].shape[1:]
    in_specs = [
        pl.BlockSpec((1, n, wide), lambda i, t: (t[0], 0, 0), pipeline_mode=pl.Buffered(1))
    ] * len(pairs)
    first = 0
    for (_, b), count in zip(pairs, counts):
        at = partial(lambda first, last, i: jnp.clip(i - first, 0, last), first, count - 1)
        if b.ndim == 3:
            in_specs.append(pl.BlockSpec((1, n, tn), lambda i, t, at=at: (at(i), 0, 0)))
        else:
            in_specs.append(pl.BlockSpec((n, tn), lambda i, t, at=at: (0, at(i))))
        first += count
    both = pl.BlockSpec((2, wide // 2, tn), lambda i, t: (0, 0, i))
    one = pl.BlockSpec((wide // 2, tn), lambda i, t: (0, i))
    args = [tab] + [a for a, _ in pairs] + [b for _, b in pairs]
    if received is not None:
        in_specs.append(both)
        args.append(received)
    shape = (wide // 2, steps * tn)
    weight = 16 if pairs[0][1].ndim == 3 else 1
    return pl.pallas_call(
        partial(flat_grad_body, counts, received is not None),
        name="flat_grad",
        grid_spec=pltpu.PrefetchScalarGridSpec(
            num_scalar_prefetch=1,
            grid=(steps,),
            in_specs=in_specs,
            out_specs=both if received is None else [one, one],
        ),
        out_shape=jax.ShapeDtypeStruct((2,) + shape, bf16)
        if received is None
        else [jax.ShapeDtypeStruct(shape, bf16)] * 2,
        compiler_params=params(),
        cost_estimate=cost(2 * n * wide * shape[1] // weight, (2 * n * (wide + shape[1]) + 8 * wide * shape[1]) // weight),
    )(*args)


def running_sums(lengths):
    count = lengths.shape[1]
    upto = jnp.arange(count)[:, None] >= jnp.arange(count)[None, :]
    return jnp.sum(jnp.where(upto[None], lengths[:, None, :], 0), axis=2).astype(jnp.int32)


def norm_forward(values, gain, shift):
    average = jnp.mean(values, axis=-1, keepdims=True)
    centered = values - average
    inverse = lax.rsqrt(jnp.mean(centered * centered, axis=-1, keepdims=True) + eps)
    normed = centered * inverse
    return (normed * gain + shift, normed, inverse)


def norm_backward(grad_y, normed, inverse, gain):
    scaled = grad_y * gain
    grad_in = inverse * (
        scaled
        - jnp.mean(scaled, axis=-1, keepdims=True)
        - normed * jnp.mean(scaled * normed, axis=-1, keepdims=True)
    )
    return (grad_in, jnp.sum(grad_y * normed, axis=(0, 1)), jnp.sum(grad_y, axis=(0, 1)))


def local_general(
    tokens,
    cotangent,
    doc_lengths,
    norm1_gain,
    norm1_shift,
    qkv_weight,
    query_bias,
    value_bias,
    head_scales,
    out_weight,
    out_bias,
    attn_gain,
    attn_shift,
    norm2_gain,
    norm2_shift,
    fc1_weight,
    fc1_bias,
    mid_gain,
    mid_shift,
    fc2_weight,
    fc2_bias,
):
    f32 = jnp.float32
    bf16 = jnp.bfloat16
    batch_size, local_len, model_width = tokens.shape
    head_count = head_scales.shape[0]
    head_dim = model_width // head_count
    score_scale = head_dim ** (-0.5)
    row_len = local_len * lax.axis_size("blk")
    row_first = lax.axis_index("blk") * local_len
    query_pos = row_first + jnp.arange(local_len, dtype=jnp.int32)
    doc_ends = running_sums(doc_lengths)
    starts = jnp.max(
        jnp.where(doc_ends[:, None, :] <= query_pos[None, :, None], doc_ends[:, None, :], 0), axis=2
    )
    lowest = jnp.min(starts[:, 0])
    query_last = row_first + local_len - 1
    inputs = tokens.astype(f32)
    attn_norm, unit_one, inverse_one = norm_forward(inputs, norm1_gain, norm1_shift)
    attn_in = attn_norm.astype(bf16)
    projected = jnp.dot(attn_in, qkv_weight, preferred_element_type=f32)
    queries = (
        (projected[..., :model_width] + query_bias)
        .astype(bf16)
        .reshape(batch_size, local_len, head_count, head_dim)
    )
    keys_low = projected[..., model_width : 2 * model_width].astype(bf16)
    values_low = (projected[..., 2 * model_width :] + value_bias).astype(bf16)

    def block_scores(key_piece, offset):
        key_len = key_piece.shape[1]
        keys_head = key_piece.reshape(batch_size, key_len, head_count, head_dim)
        raw_scores = (
            jnp.einsum("bqhd,bkhd->bhqk", queries, keys_head, preferred_element_type=f32)
            * score_scale
        )
        key_pos = offset + jnp.arange(key_len, dtype=jnp.int32)
        allowed = (key_pos[None, None, :] <= query_pos[None, :, None]) & (
            key_pos[None, None, :] >= starts[:, :, None]
        )
        return (jnp.where(allowed[:, None], raw_scores, masked_score), keys_head)

    def is_live(offset, key_len):
        return (offset <= query_last) & (offset + key_len - 1 >= lowest)

    def attend_slab(running, key_piece, value_piece, offset):
        key_len = key_piece.shape[1]

        def attend_compute(state):
            running_max, running_sum, weighted = state
            scores, keys_head = block_scores(key_piece, offset)
            new_max = jnp.maximum(running_max, jnp.max(scores, axis=3))
            rescale = jnp.exp(running_max - new_max)
            weights = jnp.exp(scores - new_max[..., None])
            values_head = value_piece.reshape(batch_size, key_len, head_count, head_dim)
            update = jnp.einsum(
                "bhqk,bkhd->bqhd", weights.astype(bf16), values_head, preferred_element_type=f32
            )
            rescale_t = jnp.transpose(rescale, (0, 2, 1))[..., None]
            return (
                new_max,
                running_sum * rescale + jnp.sum(weights, axis=3),
                weighted * rescale_t + update,
            )

        return lax.cond(is_live(offset, key_len), attend_compute, lambda state: state, running)

    start_state = (
        jnp.full((batch_size, head_count, local_len), masked_score, f32),
        jnp.zeros((batch_size, head_count, local_len), f32),
        jnp.zeros((batch_size, local_len, head_count, head_dim), f32),
    )
    key_piece = lax.all_gather(keys_low, "blk", axis=1, tiled=True)
    value_piece = lax.all_gather(values_low, "blk", axis=1, tiled=True)
    turns = key_piece.shape[1] // local_len

    def one_turn(index, state):
        begin = index * local_len
        key_slab = lax.dynamic_slice_in_dim(key_piece, begin, local_len, 1)
        value_slab = lax.dynamic_slice_in_dim(value_piece, begin, local_len, 1)
        return attend_slab(state, key_slab, value_slab, begin)

    running_max, running_sum, weighted = lax.fori_loop(0, turns, one_turn, start_state)
    attended = weighted / jnp.transpose(running_sum, (0, 2, 1))[..., None]
    log_total = running_max + jnp.log(running_sum)
    heads_out = (
        (attended * head_scales[:, None]).reshape(batch_size, local_len, model_width).astype(bf16)
    )
    projection = jnp.dot(heads_out, out_weight, preferred_element_type=f32) + out_bias
    branch, unit_attn, inverse_attn = norm_forward(projection, attn_gain, attn_shift)
    middle = inputs + branch
    ffn_norm, unit_two, inverse_two = norm_forward(middle, norm2_gain, norm2_shift)
    ffn_in = ffn_norm.astype(bf16)
    hidden = jnp.dot(ffn_in, fc1_weight, preferred_element_type=f32) + fc1_bias
    activated, gelu_grad = jax.vjp(partial(jax.nn.gelu, approximate=False), hidden)
    mid_norm, unit_mid, inverse_mid = norm_forward(activated, mid_gain, mid_shift)
    mid_out = mid_norm.astype(bf16)
    output = middle + jnp.dot(mid_out, fc2_weight, preferred_element_type=f32) + fc2_bias
    grad_output = cotangent.astype(f32)
    fc2_weight_grad = jnp.einsum("bcf,bcd->fd", mid_out, cotangent, preferred_element_type=f32)
    fc2_bias_grad = jnp.sum(grad_output, axis=(0, 1))
    grad_mid = jnp.einsum("bcd,fd->bcf", cotangent, fc2_weight, preferred_element_type=f32)
    grad_act, mid_gain_grad, mid_shift_grad = norm_backward(
        grad_mid, unit_mid, inverse_mid, mid_gain
    )
    grad_hidden = gelu_grad(grad_act)[0].astype(bf16)
    fc1_weight_grad = jnp.einsum("bcd,bcf->df", ffn_in, grad_hidden, preferred_element_type=f32)
    fc1_bias_grad = jnp.sum(grad_hidden.astype(f32), axis=(0, 1))
    grad_ffn_in = jnp.einsum("bcf,df->bcd", grad_hidden, fc1_weight, preferred_element_type=f32)
    grad_two, norm2_gain_grad, norm2_shift_grad = norm_backward(
        grad_ffn_in, unit_two, inverse_two, norm2_gain
    )
    grad_middle = grad_output + grad_two
    grad_proj_f, attn_gain_grad, attn_shift_grad = norm_backward(
        grad_middle, unit_attn, inverse_attn, attn_gain
    )
    grad_projection = grad_proj_f.astype(bf16)
    out_weight_grad = jnp.einsum(
        "bcd,bce->de", heads_out, grad_projection, preferred_element_type=f32
    )
    out_bias_grad = jnp.sum(grad_projection.astype(f32), axis=(0, 1))
    grad_heads = jnp.einsum(
        "bce,de->bcd", grad_projection, out_weight, preferred_element_type=f32
    ).reshape(batch_size, local_len, head_count, head_dim)
    head_scales_grad = jnp.sum(grad_heads * attended, axis=(0, 1, 3))
    grad_attended = (grad_heads * head_scales[:, None]).astype(bf16)
    row_dot = jnp.transpose(jnp.sum(grad_attended.astype(f32) * attended, axis=3), (0, 2, 1))

    def back_slab(running, key_piece, value_piece, offset):
        key_len = key_piece.shape[1]

        def back_compute(state):
            grad_queries, kv_buffer = state
            scores, keys_head = block_scores(key_piece, offset)
            attn_probs = jnp.exp(scores - log_total[..., None])
            values_head = value_piece.reshape(batch_size, key_len, head_count, head_dim)
            grad_probs = jnp.einsum(
                "bqhd,bkhd->bhqk", grad_attended, values_head, preferred_element_type=f32
            )
            grad_scores = (attn_probs * (grad_probs - row_dot[..., None])).astype(bf16)
            grad_queries = (
                grad_queries
                + jnp.einsum("bhqk,bkhd->bqhd", grad_scores, keys_head, preferred_element_type=f32)
                * score_scale
            )
            grad_keys = (
                jnp.einsum("bhqk,bqhd->bkhd", grad_scores, queries, preferred_element_type=f32)
                * score_scale
            )
            grad_values = jnp.einsum(
                "bhqk,bqhd->bkhd",
                attn_probs.astype(bf16),
                grad_attended,
                preferred_element_type=f32,
            )
            addition = jnp.concatenate(
                [
                    grad_keys.reshape(batch_size, key_len, model_width),
                    grad_values.reshape(batch_size, key_len, model_width),
                ],
                axis=2,
            )
            previous = lax.dynamic_slice_in_dim(kv_buffer, offset, key_len, 1)
            return (
                grad_queries,
                lax.dynamic_update_slice_in_dim(kv_buffer, previous + addition, offset, 1),
            )

        return lax.cond(is_live(offset, key_len), back_compute, lambda state: state, running)

    back_state = (
        jnp.zeros((batch_size, local_len, head_count, head_dim), f32),
        jnp.zeros((batch_size, row_len, 2 * model_width), f32),
    )
    attend_key_piece = lax.all_gather(keys_low, "blk", axis=1, tiled=True)
    attend_value_piece = lax.all_gather(values_low, "blk", axis=1, tiled=True)
    turns = attend_key_piece.shape[1] // local_len

    def one_turn(index, state):
        begin = index * local_len
        key_slab = lax.dynamic_slice_in_dim(attend_key_piece, begin, local_len, 1)
        value_slab = lax.dynamic_slice_in_dim(attend_value_piece, begin, local_len, 1)
        return back_slab(state, key_slab, value_slab, begin)

    grad_queries, kv_buffer = lax.fori_loop(0, turns, one_turn, back_state)
    grad_kv = lax.psum_scatter(
        kv_buffer.astype(jnp.bfloat16), "blk", scatter_dimension=1, tiled=True
    ).astype(jnp.float32)
    grad_qkv = jnp.concatenate(
        [grad_queries.reshape(batch_size, local_len, model_width), grad_kv], axis=2
    ).astype(bf16)
    qkv_weight_grad = jnp.einsum("bcd,bce->de", attn_in, grad_qkv, preferred_element_type=f32)
    query_bias_grad = jnp.sum(grad_qkv[..., :model_width].astype(f32), axis=(0, 1))
    value_bias_grad = jnp.sum(grad_qkv[..., 2 * model_width :].astype(f32), axis=(0, 1))
    grad_attn_in = jnp.einsum("bce,de->bcd", grad_qkv, qkv_weight, preferred_element_type=f32)
    grad_one, norm1_gain_grad, norm1_shift_grad = norm_backward(
        grad_attn_in, unit_one, inverse_one, norm1_gain
    )
    tokens_grad = grad_middle + grad_one
    matrix_grads = (qkv_weight_grad, out_weight_grad, fc1_weight_grad, fc2_weight_grad)
    reduced = (
        lax.psum_scatter(
            matrix_grads[0].astype(jnp.bfloat16), "dp", scatter_dimension=0, tiled=True
        ).astype(jnp.float32),
        lax.psum_scatter(
            matrix_grads[1].astype(jnp.bfloat16), "dp", scatter_dimension=0, tiled=True
        ).astype(jnp.float32),
        lax.psum_scatter(
            matrix_grads[2].astype(jnp.bfloat16), "dp", scatter_dimension=0, tiled=True
        ).astype(jnp.float32),
        lax.psum_scatter(
            matrix_grads[3].astype(jnp.bfloat16), "dp", scatter_dimension=0, tiled=True
        ).astype(jnp.float32),
    )
    reduced = (
        lax.psum_scatter(
            reduced[0].astype(jnp.bfloat16), "blk", scatter_dimension=1, tiled=True
        ).astype(jnp.float32),
        lax.psum_scatter(
            reduced[1].astype(jnp.bfloat16), "blk", scatter_dimension=1, tiled=True
        ).astype(jnp.float32),
        lax.psum_scatter(
            reduced[2].astype(jnp.bfloat16), "blk", scatter_dimension=1, tiled=True
        ).astype(jnp.float32),
        lax.psum_scatter(
            reduced[3].astype(jnp.bfloat16), "blk", scatter_dimension=1, tiled=True
        ).astype(jnp.float32),
    )
    small_sums = lax.psum(
        (
            norm1_gain_grad,
            norm1_shift_grad,
            query_bias_grad,
            value_bias_grad,
            head_scales_grad,
            out_bias_grad,
            attn_gain_grad,
            attn_shift_grad,
            norm2_gain_grad,
            norm2_shift_grad,
            fc1_bias_grad,
            mid_gain_grad,
            mid_shift_grad,
            fc2_bias_grad,
        ),
        ("dp", "blk"),
    )
    return (
        output,
        tokens_grad,
        small_sums[0],
        small_sums[1],
        reduced[0],
        small_sums[2],
        small_sums[3],
        small_sums[4],
        reduced[1],
        small_sums[5],
        small_sums[6],
        small_sums[7],
        small_sums[8],
        small_sums[9],
        reduced[2],
        small_sums[10],
        small_sums[11],
        small_sums[12],
        reduced[3],
        small_sums[13],
    )


swap = ((0, 1), (1, 0))


def exchange(x):
    return lax.ppermute(x, "blk", swap)


def flip(x, bit):
    return lax.ppermute(x, "dp", [(i, i ^ bit) for i in range(16)])


def local_rows(
    tokens,
    cotangent,
    doc_lengths,
    norm1_gain,
    norm1_shift,
    qkv_weight,
    query_bias,
    value_bias,
    head_scales,
    out_weight,
    out_bias,
    attn_gain,
    attn_shift,
    norm2_gain,
    norm2_shift,
    fc1_weight,
    fc1_bias,
    mid_gain,
    mid_shift,
    fc2_weight,
    fc2_bias,
):
    _, half_len, d = tokens.shape
    ff = fc1_weight.shape[1]
    heads = head_scales.shape[0]
    head_dim = d // heads
    scale = head_dim**-0.5
    n = 2 * half_len
    b = lax.axis_index("blk").astype(jnp.int32)
    dp = lax.axis_index("dp").astype(jnp.int32)
    core, x, z, y = dp % 2, (dp // 2) % 2, dp // 4, b

    tok_in = exchange(lax.dynamic_slice_in_dim(tokens, 1 - b, 1, 0))
    cot_in = exchange(lax.dynamic_slice_in_dim(cotangent, 1 - b, 1, 0))
    kept_at = b[None]
    sent_at = jnp.zeros((1,), jnp.int32)

    def line(v):
        return v.reshape(1, -1)

    qkv_bias = jnp.concatenate([query_bias, jnp.zeros_like(query_bias), value_bias])
    first_args = (line(norm1_gain), line(norm1_shift), qkv_weight, line(qkv_bias), scale)
    early = project_qkv(kept_at, tokens, *first_args, 0, n)

    def later(v):
        return after(v, early[0])

    lengths = lax.dynamic_slice_in_dim(later(doc_lengths), b, 1, 0)
    ends = running_sums(lengths)[0]
    firsts = (half_len // 2) * jnp.arange(4, dtype=jnp.int32)
    starts = jnp.max(jnp.where(ends[None, :] <= firsts[:, None], ends[None, :], 0), axis=1)
    allowed = (firsts[None, :] >= starts[:, None]).astype(jnp.int32)
    tab = jnp.concatenate([b[None], allowed.reshape(16)])
    theirs = jnp.stack([1 - core, x, y])
    mine = jnp.stack([core, x, y])
    head_scales = later(head_scales)
    scale_row = jnp.broadcast_to(head_scales[:, None], (heads, head_dim)).reshape(1, d)
    vec = jnp.stack(
        [later(out_bias), attn_gain, attn_shift, norm2_gain, norm2_shift, fc2_bias, scale_row[0], out_bias]
    )
    fc1_bias = later(fc1_bias)
    vec4 = jnp.stack([fc1_bias, mid_gain, mid_shift, fc1_bias])

    made = after(sent_at, tab, theirs, mine, scale_row, vec, vec4)
    attn_in, qkv = project_qkv(made, tok_in, *first_args, 1, n, early)
    qkv = qkv.reshape(2, half_len, 3 * d)
    heads_out, logs = attend(tab, qkv, scale_row)

    weights = (out_weight, fc1_weight, fc2_weight, vec, vec4)
    out_sent, mid_sent, *more = middle_pass(sent_at, heads_out, tok_in, cot_in, *weights, 1, False)
    sums, sums4, *earlier = more
    out_back = exchange(out_sent)
    output, mid_kept, *more = middle_pass(
        kept_at, heads_out, tokens, cotangent, *weights, 0, True, earlier
    )
    sums = sums + more[0]
    sums4 = sums4 + more[1]
    ffn_in, heads_in, mid_out, grad_hidden, grad_proj, d_out = more[2:]

    def fill(kept, back):
        return lax.dynamic_update_slice_in_dim(kept, back.astype(f32)[None], 1 - b, 0)

    def near_z(total):
        total = total.astype(bf16).reshape((2, 2) + total.shape[1:])
        odd = z % 2
        return (
            lax.dynamic_index_in_dim(total, 1 - odd, 1, keepdims=False),
            lax.dynamic_index_in_dim(total, odd, 1, keepdims=False),
        )

    def far_z(total):
        total = total.astype(bf16)
        high = z // 2
        return (
            lax.dynamic_index_in_dim(total, 1 - high, 0, keepdims=False),
            lax.dynamic_index_in_dim(total, high, 0, keepdims=False),
        )

    def add_z(move, send, keep):
        return keep.astype(f32) + flip(send, move).astype(f32)

    def held(parts, *others):
        return parts[0], after(parts[1], *others)

    def rows_by_x(total):
        total = total.astype(bf16).reshape(4, 2, -1, total.shape[1])
        return (
            lax.dynamic_index_in_dim(total, 1 - x, 1, keepdims=False),
            lax.dynamic_index_in_dim(total, x, 1, keepdims=False),
        )

    def columns_by_y(total, *cuts):
        total = total.astype(bf16).reshape(4, -1, total.shape[1])
        out = []
        for at in (1 - y, y):
            groups = []
            for first, last in zip((0,) + cuts, cuts + (total.shape[2],)):
                width = (last - first) // 2
                groups.append(lax.dynamic_slice_in_dim(total, first + at * width, width, 2))
            out.append(jnp.concatenate(groups, axis=2) if cuts else groups[0])
        return out

    def add_x(send, keep):
        return keep.astype(f32) + flip(send, 2).astype(f32)

    def add_y(send, keep):
        return keep.astype(f32) + exchange(send).astype(f32)

    cots = (cotangent, cot_in)
    output = fill(output, out_back)
    wide_pairs = [(after(ffn_in, output), grad_hidden), (heads_in, grad_proj)]
    wide_theirs = flat_grad(theirs, wide_pairs, d)
    fc2_theirs = tall_grad(theirs, after(mid_out, wide_theirs), cots)
    wide_pairs = [(after(ffn_in, fc2_theirs), grad_hidden), (heads_in, grad_proj)]
    wide_parts = flat_grad(mine, wide_pairs, d, flip(wide_theirs, 1))
    fc2_parts = tall_grad(mine, after(mid_out, *wide_parts), cots, flip(fc2_theirs, 1))
    d_out = after(d_out, *fc2_parts)
    back_args = (1.0 / scale_row, logs, scale)
    even, dots_even = attend_back(tab, qkv, heads_out, d_out, *back_args, 0)
    even = even.reshape(3, n, d // 2)
    even_theirs = flat_grad(theirs, [(after(attn_in, even), even)], d // 2)
    d_out = after(d_out, even_theirs)
    odd, dots_odd = attend_back(tab, qkv, heads_out, d_out, *back_args, 1)
    odd = odd.reshape(3, n, d // 2)
    wide_parts = columns_by_y(add_x(*held(wide_parts, odd)), ff)
    fc2_parts = rows_by_x(add_y(*held(fc2_parts, odd)))
    odd_theirs = flat_grad(theirs, [(after(attn_in, *wide_parts, *fc2_parts), odd)], d // 2)
    even_parts = flat_grad(mine, [(after(attn_in, odd_theirs), even)], d // 2, flip(even_theirs, 1))
    grad_sent, sums_sent = first_back(
        sent_at, after(even, *even_parts), odd, qkv_weight, tok_in, mid_sent, line(norm1_gain), 1, False
    )
    grad_back = exchange(grad_sent)
    fc2_parts = near_z(add_x(*held(fc2_parts, grad_sent)))
    odd_parts = flat_grad(
        mine, [(after(attn_in, grad_sent, *fc2_parts), odd)], d // 2, flip(odd_theirs, 1)
    )
    wide_parts = near_z(add_y(*held(wide_parts, *odd_parts)))
    tokens_grad, sums_kept = first_back(
        kept_at, after(even, *wide_parts), odd, qkv_weight, tokens, mid_kept, line(norm1_gain), 0, True
    )
    dots = jnp.stack([dots_even[:, 0].reshape(2, 4, head_dim), dots_odd[:, 0].reshape(2, 4, head_dim)], axis=1)
    head_scales_grad = jnp.sum(dots, axis=3).reshape(heads) / head_scales
    head_scales_grad = jnp.pad(head_scales_grad, (0, d - heads))
    total = jnp.concatenate(
        [
            (sums_sent + sums_kept)[:4],
            head_scales_grad[None],
            sums[:6],
            sums4.reshape(8 * ff // d, d)[: 3 * ff // d],
        ]
    )
    fc2_parts = far_z(add_z(4, *held(fc2_parts, tokens_grad)))
    even_parts = columns_by_y(add_x(*held(even_parts, tokens_grad)))
    wide_parts = far_z(add_z(4, *held(wide_parts, tokens_grad)))
    tokens_grad = fill(tokens_grad, grad_back)
    odd_parts = columns_by_y(add_x(*odd_parts))
    even_parts = near_z(add_y(*even_parts))
    odd_parts = near_z(add_y(*odd_parts))
    total = total + (partial(flip, bit=1))(total)
    total = total + (partial(flip, bit=4))(total)
    total = total + (partial(flip, bit=8))(total)
    total = after(total, *odd_parts)
    total = total + (partial(flip, bit=2))(total)
    total = total + (exchange)(total)
    even_parts = far_z(add_z(4, *even_parts))
    odd_parts = far_z(add_z(4, *odd_parts))
    fc2_weight_grad = add_z(8, *fc2_parts)
    wide_grad = add_z(8, *wide_parts)
    fc1_weight_grad, out_weight_grad = wide_grad[:, : ff // 2], wide_grad[:, ff // 2 :]
    even_grad, odd_grad = (add_z(8, *parts) for parts in (even_parts, odd_parts))
    first_sums, sums, sums4 = total[:5], total[5:11], total[11:].reshape(3, ff)
    run = d // 4
    qkv_weight_grad = jnp.stack(
        [even_grad.reshape(-1, 3, run), odd_grad.reshape(-1, 3, run)], axis=2
    ).reshape(-1, 6 * run)
    return (
        output,
        tokens_grad,
        first_sums[0],
        first_sums[1],
        qkv_weight_grad,
        first_sums[2],
        first_sums[3],
        first_sums[4, :heads],
        out_weight_grad,
        sums[0],
        sums[1],
        sums[2],
        sums[3],
        sums[4],
        fc1_weight_grad,
        sums4[0],
        sums4[1],
        sums4[2],
        fc2_weight_grad,
        sums[5],
    )


def solution(mesh):
    rows_fit = dict(mesh.shape) == {"dp": 16, "blk": 2}
    local = local_rows if rows_fit else local_general
    placed = (
        P("dp", "blk", None),
        P("dp", "blk", None),
        P("dp", None),
        P(),
        P(),
        P(),
        P(),
        P(),
        P(),
        P(),
        P(),
        P(),
        P(),
        P(),
        P(),
        P(),
        P(),
        P(),
        P(),
        P(),
        P(),
    )
    return jax.shard_map(
        local,
        mesh=mesh,
        in_specs=placed,
        out_specs=(
            P("dp", "blk", None),
            P("dp", "blk", None),
            P(),
            P(),
            P("dp", "blk"),
            P(),
            P(),
            P(),
            P("dp", "blk"),
            P(),
            P(),
            P(),
            P(),
            P(),
            P("dp", "blk"),
            P(),
            P(),
            P(),
            P("dp", "blk"),
            P(),
        ),
        check_vma=False,
    )
```

```python
from functools import partial

import jax
import jax.numpy as jnp
from jax import lax
from jax.experimental import pallas as pl
from jax.experimental.pallas import tpu as pltpu
from jax.sharding import PartitionSpec as P

f32 = jnp.float32
bf16 = jnp.bfloat16
eps = 1e-05
masked_score = -1e30
LANES = 128
NT = (((1,), (1,)), ((), ()))
NN = (((1,), (0,)), ((), ()))
TN = (((0,), (0,)), ((), ()))


def mm(a, b, dims=NN):
    return lax.dot_general(a, b, dims, preferred_element_type=f32)


def fold(x):
    total = x[:, :LANES]
    for c in range(LANES, x.shape[1], LANES):
        total = total + x[:, c : c + LANES]
    return total


def row_mean(x):
    return jnp.sum(fold(x), axis=1, keepdims=True) * (1.0 / x.shape[1])


def row_sum(x):
    return jnp.sum(x, axis=0, keepdims=True)


def norm_unit(v):
    centered = v - row_mean(v)
    inverse = lax.rsqrt(row_mean(centered * centered) + eps)
    return centered * inverse, inverse


def norm_back(grad_y, unit, inverse, gain):
    e = grad_y * gain
    return inverse * (e - row_mean(e) - unit * row_mean(e * unit))


def params(mib=None, **more):
    return pltpu.CompilerParams(vmem_limit_bytes=(mib or 60) * 2**20, **more)


def cost(flops, moved):
    return pl.CostEstimate(flops=flops, bytes_accessed=moved, transcendentals=0)


def whole(shape):
    return pl.BlockSpec(shape, lambda *_: (0,) * len(shape), pipeline_mode=pl.Buffered(1))


def core_split(x):
    low = lax.broadcasted_iota(jnp.int32, (x.shape[0], LANES), 1) < LANES // 2
    even, odd = [], []
    for c in range(0, x.shape[1], 2 * LANES):
        a = x[:, c : c + LANES].astype(f32)
        b = x[:, c + LANES : c + 2 * LANES].astype(f32)
        even.append(jnp.where(low, a, pltpu.roll(b, LANES // 2, 1)))
        odd.append(jnp.where(low, pltpu.roll(a, LANES // 2, 1), b))
    return (jnp.concatenate(y, axis=1).astype(bf16) for y in (even, odd))


def qkv_body(scale, at, tok, gain, shift, w, bias, *refs):
    attn_in, qkv, x, ws, sems = refs[-5:]
    step = pl.program_id(0)
    steps, d, cols = ws.shape
    half = cols // 2

    def fetch(k, h):
        columns = pl.ds(pl.multiple_of(k * cols + h * half, half), half)
        return pltpu.make_async_copy(
            w.at[:, columns], ws.at[k, :, pl.ds(h * half, half)], sems.at[k, h]
        )

    @pl.when(step == 0)
    def _():
        for k in range(steps):
            for h in range(2):
                fetch(k, h).start()
        unit, _ = norm_unit(tok[0].astype(f32))
        here = (unit * gain[...] + shift[...]).astype(bf16)
        x[...] = here
        attn_in[0], attn_in[1] = core_split(here)

    for h in range(2):
        fetch(step, h).wait()
    total = (mm(x[...], ws[step]) + bias[...]).astype(bf16)
    qkv[...] = (total.astype(f32) * jnp.where(step == 0, scale, 1.0)).astype(bf16)


def project_qkv(at, tok, gain, shift, w, bias, scale, slot, total, earlier=()):
    _, n, d = tok.shape
    held = pl.BlockSpec(memory_space=pl.ANY)
    return pl.pallas_call(
        partial(qkv_body, scale),
        name="project_qkv",
        grid_spec=pltpu.PrefetchScalarGridSpec(
            num_scalar_prefetch=1,
            grid=(3,),
            in_specs=[
                pl.BlockSpec((1, n, d), lambda i, at: (at[0], 0, 0), pipeline_mode=pl.Buffered(1)),
                whole(gain.shape),
                whole(shift.shape),
                held,
                pl.BlockSpec((1, d), lambda i, at: (0, i)),
            ]
            + [held] * len(earlier),
            out_specs=[
                pl.BlockSpec((2, n, d // 2), lambda i, at: (0, slot, 0)),
                pl.BlockSpec((n, d), lambda i, at: (slot, i)),
            ],
            scratch_shapes=[
                pltpu.VMEM((n, d), bf16),
                pltpu.VMEM((3, d, d), bf16),
                pltpu.SemaphoreType.DMA((3, 2)),
            ],
        ),
        out_shape=[
            jax.ShapeDtypeStruct((2, total, d // 2), bf16),
            jax.ShapeDtypeStruct((total, 3 * d), bf16),
        ],
        input_output_aliases={6 + k: k for k in range(len(earlier))},
        compiler_params=params(),
        cost_estimate=cost(2 * n * d * 3 * d, 6 * d * d + 10 * n * d),
    )(at, tok, gain, shift, w, bias, *earlier)


def half_slot(own, half):
    return own if half == 0 else 1 - own


def pick(ref, own, block, size):
    half, sub = divmod(block, 2)
    return ref[half_slot(own, half), sub * size : (sub + 1) * size, :]


def head_mask(size):
    return lax.broadcasted_iota(jnp.int32, (size, LANES), 1) < LANES // 2


def block_penalty(tab, i, j):
    return jnp.where(tab[1 + 4 * i + j] > 0, 0.0, masked_score).astype(f32)


def stack_heads(x, low):
    zero = jnp.zeros_like(x)
    return jnp.concatenate([jnp.where(low, x, zero), jnp.where(low, zero, x)], axis=0)


def place(ref, own, *targets):
    half = ref.shape[1]
    for h in range(2):
        targets[0][h * half : (h + 1) * half, :] = ref[half_slot(own, h)]


def attend_body(tab, q, k, v, head_scale, heads_out, lse, kp, vp):
    size = q.shape[1] // 2
    own = tab[0]
    low = head_mask(size)
    causal = lax.broadcasted_iota(jnp.int32, (2 * size, size), 0) % size >= lax.broadcasted_iota(
        jnp.int32, (2 * size, size), 1
    )
    lane = lax.broadcasted_iota(jnp.int32, (size, LANES), 1)
    place(k, own, kp)
    place(v, own, vp)
    for i in range(4):
        width = (i + 1) * size
        s = mm(stack_heads(pick(q, own, i, size), low), kp[:width, :], NT)
        parts = [s[:, j * size : (j + 1) * size] + block_penalty(tab, i, j) for j in range(i)]
        parts.append(jnp.where(causal, s[:, i * size :], masked_score))
        top = parts[0]
        for part in parts[1:]:
            top = jnp.maximum(top, part)
        top = jnp.max(top, axis=1, keepdims=True)
        parts = [jnp.exp(part - top) for part in parts]
        total = fold(parts[0])
        for part in parts[1:]:
            total = total + fold(part)
        total = jnp.sum(total, axis=1, keepdims=True)
        p = jnp.concatenate([part.astype(bf16) for part in parts], axis=1)
        out = mm(p, vp[:width, :]) * (1.0 / total)
        both = jnp.where(low, out[:size], out[size:]) * head_scale[...]
        half, sub = divmod(i, 2)
        heads_out[half_slot(own, half), sub * size : (sub + 1) * size, :] = both.astype(bf16)
        logs = top + jnp.log(total)
        columns = jnp.where(lane == 0, logs[:size], logs[size:])
        lse[0, i] = jnp.transpose(columns)[:8]


def attend(tab, qkv, head_scale_row):
    _, half_len, wide = qkv.shape
    d = wide // 3
    pairs = d // LANES
    size = half_len // 2

    def lanes(first):
        return pl.BlockSpec((2, half_len, LANES), lambda p, t: (0, 0, first + p))

    flops = 16 * half_len * half_len * pairs * LANES
    return pl.pallas_call(
        attend_body,
        name="attend",
        grid_spec=pltpu.PrefetchScalarGridSpec(
            num_scalar_prefetch=1,
            grid=(pairs,),
            in_specs=[
                lanes(0),
                lanes(pairs),
                lanes(2 * pairs),
                pl.BlockSpec((1, LANES), lambda p, t: (0, p)),
            ],
            out_specs=[
                lanes(0),
                pl.BlockSpec((1, 4, 8, size), lambda p, t: (p, 0, 0, 0)),
            ],
            scratch_shapes=[pltpu.VMEM((2 * half_len, LANES), bf16)] * 2,
        ),
        out_shape=[
            jax.ShapeDtypeStruct((2, half_len, d), bf16),
            jax.ShapeDtypeStruct((pairs, 4, 8, size), f32),
        ],
        compiler_params=params(),
        cost_estimate=cost(flops * 4, 8 * half_len * wide),
    )(tab, qkv, qkv, qkv, head_scale_row)


def attend_back_body(
    scale, tab, q, k, v, heads_out, d_out, inv_scale, lse, dqkv, dots, kp, vp, dk, dv
):
    size = q.shape[1] // 2
    own = tab[0]
    low = head_mask(size)
    causal = lax.broadcasted_iota(jnp.int32, (2 * size, size), 0) % size >= lax.broadcasted_iota(
        jnp.int32, (2 * size, size), 1
    )
    place(k, own, kp)
    place(v, own, vp)
    dots[...] = jnp.zeros_like(dots)
    for i in range(3, -1, -1):
        width = (i + 1) * size
        q2 = stack_heads(pick(q, own, i, size), low)
        gi = pick(d_out, own, i, size)
        g2 = stack_heads(gi, low)
        product = gi.astype(f32) * pick(heads_out, own, i, size).astype(f32) * inv_scale[...]
        dots[0, 0:1, :] += row_sum(product)
        zero = jnp.zeros_like(product)
        delta = jnp.concatenate(
            [
                jnp.sum(jnp.where(low, product, zero), axis=1, keepdims=True),
                jnp.sum(jnp.where(low, zero, product), axis=1, keepdims=True),
            ],
            axis=0,
        )
        columns = jnp.transpose(lse[0, i])
        logs = jnp.concatenate([columns[:, 0:1], columns[:, 1:2]], axis=0)
        s = mm(q2, kp[:width, :], NT)
        g = mm(g2, vp[:width, :], NT)
        ps, ds = [], []
        for j in range(i + 1):
            here = slice(j * size, (j + 1) * size)
            if j < i:
                p = jnp.exp(s[:, here] - (logs - block_penalty(tab, i, j)))
            else:
                p = jnp.exp(jnp.where(causal, s[:, here], masked_score) - logs)
            ps.append(p.astype(bf16))
            ds.append((p * (g[:, here] - delta)).astype(bf16))
        p = jnp.concatenate(ps, axis=1)
        d = jnp.concatenate(ds, axis=1)
        dv_part = mm(p, g2, TN)
        dk_part = mm(d, q2, TN)
        if i == 3:
            dv[...] = dv_part
            dk[...] = dk_part
        else:
            dv[:width, :] += dv_part
            dk[:width, :] += dk_part
        dq = mm(d, kp[:width, :]) * scale
        half, sub = divmod(i, 2)
        dqkv[0, half_slot(own, half), sub * size : (sub + 1) * size, :] = jnp.where(
            low, dq[:size], dq[size:]
        ).astype(bf16)
    for half in range(2):
        here = slice(half * 2 * size, (half + 1) * 2 * size)
        dqkv[1, half_slot(own, half)] = dk[here, :].astype(bf16)
        dqkv[2, half_slot(own, half)] = dv[here, :].astype(bf16)


def attend_back(tab, qkv, heads_out, d_out, inv_scale_row, lse, scale, group):
    _, half_len, wide = qkv.shape
    d = wide // 3
    every = d // LANES
    pairs = every // 2
    size = half_len // 2

    def pair(p):
        return p + 2 * (p // 2) + 2 * group

    def lanes(first):
        return pl.BlockSpec((2, half_len, LANES), lambda p, t: (0, 0, first + pair(p)))

    flops = 16 * half_len * half_len * pairs * LANES
    return pl.pallas_call(
        partial(attend_back_body, scale),
        name="attend_back",
        grid_spec=pltpu.PrefetchScalarGridSpec(
            num_scalar_prefetch=1,
            grid=(pairs,),
            in_specs=[
                lanes(0),
                lanes(every),
                lanes(2 * every),
                lanes(0),
                lanes(0),
                pl.BlockSpec((1, LANES), lambda p, t: (0, pair(p))),
                pl.BlockSpec((1, 4, 8, size), lambda p, t: (pair(p), 0, 0, 0)),
            ],
            out_specs=[
                pl.BlockSpec((3, 2, half_len, LANES), lambda p, t: (0, 0, 0, p)),
                pl.BlockSpec((1, 8, LANES), lambda p, t: (p, 0, 0)),
            ],
            scratch_shapes=[pltpu.VMEM((2 * half_len, LANES), bf16)] * 2
            + [pltpu.VMEM((2 * half_len, LANES), f32)] * 2,
        ),
        out_shape=[
            jax.ShapeDtypeStruct((3, 2, half_len, d // 2), bf16),
            jax.ShapeDtypeStruct((pairs, 8, LANES), f32),
        ],
        compiler_params=params(),
        cost_estimate=cost(flops * 10, 8 * half_len * wide),
    )(tab, qkv, qkv, qkv, heads_out, d_out, inv_scale_row, lse)


def gelu_parts(v):
    a = jnp.abs(v)
    t = 1.0 / (1.0 + (0.3275911 * 0.7071067811865476) * a)
    bell = jnp.exp(v * v * -0.5)
    poly = ((((1.061405429 * t - 1.453152027) * t + 1.421413741) * t - 0.284496736) * t + 0.254829592) * t
    tail = (0.5 * poly) * bell
    cdf = jnp.where(v < 0, tail, 1.0 - tail)
    return v * cdf, cdf + v * (bell * 0.3989422804014327)


def middle_body(
    at, ho, tok, cot, out_w, w1, w2, vec, vec4, *refs
):
    (
        output, grad_middle, sums, sums4, ffn_in, heads_in, mid_out, grad_hidden, grad_proj, d_out,
        act, slope, back, acc, unit_b, stats, total, total_u, w1s, w2s, sems,
    ) = refs[-21:]
    early_back = refs[0] if len(output.shape) == 3 else None
    ho, tok, cot, d_out = (ref.at[0] for ref in (ho, tok, cot, d_out))
    output = output.at[0] if len(output.shape) == 3 else output
    step = pl.program_id(0)
    n, d = ho.shape
    chunks, _, fc = w1s.shape
    ff = fc * chunks
    c = step % chunks
    ahead = 2

    def fetch(k):
        columns = pl.ds(pl.multiple_of(k * fc, fc), fc)
        copies = [
            pltpu.make_async_copy(w1.at[:, columns], w1s.at[k], sems.at[0, k]),
            pltpu.make_async_copy(w2.at[columns, :], w2s.at[k], sems.at[1, k]),
        ]
        if early_back is not None:
            copies.append(pltpu.make_async_copy(early_back.at[:, columns], back.at[k], sems.at[2, k]))
        return copies
    strip = 128
    strips = n // strip

    def v(r):
        return vec[r : r + 1, :]

    def rows(t):
        return pl.ds(pl.multiple_of(t * strip, strip), strip)

    @pl.when(step == 0)
    def _():
        for k in range(ahead):
            for copy in fetch(k):
                copy.start()
        sums[...] = jnp.zeros_like(sums)
        acc[...] = mm(ho[...], out_w[...])

        def one(t, _):
            r = rows(t)
            unit_attn, inverse_attn = norm_unit(acc[r, :] + v(0))
            middle = tok[r, :].astype(f32) + (unit_attn * v(1) + v(2))
            unit_two, inverse_two = norm_unit(middle)
            x = (unit_two * v(3) + v(4)).astype(bf16)
            grad_middle[r, :] = unit_attn
            unit_b[r, :] = unit_two
            stats[r, 0:1] = inverse_attn
            stats[r, 1:2] = inverse_two
            acc[r, :] = middle + v(5)
            d_out[r, :] = x
            ffn_in[0, r, :], ffn_in[1, r, :] = core_split(x)
            heads_in[0, r, :], heads_in[1, r, :] = core_split(ho[r, :])
            return 0

        lax.fori_loop(0, strips, one, 0)

    @pl.when(step < chunks - ahead)
    def _():
        for copy in fetch(step + ahead):
            copy.start()

    @pl.when(step < chunks)
    def _():
        for copy in fetch(step):
            copy.wait()
        h = mm(d_out[...], w1s[c]) + vec4[0:1, :]
        if early_back is None:
            back[c] = mm(cot[...], w2s[c], NT).astype(back.dtype)
        a, b = gelu_parts(h)
        act[c] = a
        slope[c] = b.astype(slope.dtype)

    @pl.when(step == 0)
    def _():
        total[...] = jnp.zeros_like(total)

    @pl.when(step < chunks)
    def _():
        total[...] += fold(act[c])

    @pl.when(step == chunks)
    def _():
        mean = jnp.sum(total[...], axis=1, keepdims=True) * (1.0 / ff)

        def one(k, t):
            centered = act[k] - mean
            return t + fold(centered * centered)

        square = lax.fori_loop(0, chunks, one, jnp.zeros_like(total))
        stats[:, 2:3] = mean
        stats[:, 3:4] = lax.rsqrt(jnp.sum(square, axis=1, keepdims=True) * (1.0 / ff) + eps)
        total[...] = jnp.zeros_like(total)
        total_u[...] = jnp.zeros_like(total_u)

    here = pl.ds(pl.multiple_of(c * fc, fc), fc)

    @pl.when((step >= chunks) & (step < 2 * chunks))
    def _():
        u = (act[c] - stats[:, 2:3]) * stats[:, 3:4]
        act[c] = u
        gain = vec4[1:2, :]
        m = (u * gain + vec4[2:3, :]).astype(bf16)
        mid_out[...] = m
        acc[...] += mm(m, w2s[c])
        gm = back[c].astype(f32)
        gmu = gm * u
        sums4[1:2, here] = row_sum(gmu)
        sums4[2:3, here] = row_sum(gm)
        total[...] += fold(gm * gain)
        total_u[...] += fold(gmu * gain)

    @pl.when(step == 2 * chunks)
    def _():
        stats[:, 4:5] = jnp.sum(total[...], axis=1, keepdims=True) * (1.0 / ff)
        stats[:, 5:6] = jnp.sum(total_u[...], axis=1, keepdims=True) * (1.0 / ff)
        output[...] = acc[...].astype(output.dtype)
        acc[...] = jnp.zeros_like(acc)

    @pl.when(step >= 2 * chunks)
    def _():
        e = back[c].astype(f32) * vec4[1:2, :]
        grad_act = stats[:, 3:4] * (e - stats[:, 4:5] - act[c] * stats[:, 5:6])
        gh = (grad_act * slope[c].astype(f32)).astype(bf16)
        grad_hidden[...] = gh
        sums4[0:1, here] = row_sum(gh.astype(f32))
        acc[...] += mm(gh, w1s[c], NT)

    @pl.when(step == 3 * chunks - 1)
    def _():
        def one(t, _):
            r = rows(t)
            grad_ffn_in = acc[r, :]
            unit_two = unit_b[r, :]
            unit_attn = grad_middle[r, :]
            gout = cot[r, :].astype(f32)
            sums[5:6, :] += row_sum(gout)
            sums[3:4, :] += row_sum(grad_ffn_in * unit_two)
            sums[4:5, :] += row_sum(grad_ffn_in)
            gmid = gout + norm_back(grad_ffn_in, unit_two, stats[r, 1:2], v(3))
            grad_middle[r, :] = gmid
            sums[1:2, :] += row_sum(gmid * unit_attn)
            sums[2:3, :] += row_sum(gmid)
            gp = norm_back(gmid, unit_attn, stats[r, 0:1], v(1)).astype(bf16)
            grad_proj[r, :] = gp
            sums[0:1, :] += row_sum(gp.astype(f32))
            return 0

        lax.fori_loop(0, strips, one, 0)
        d_out[...] = (mm(grad_proj[...], out_w[...], NT) * v(6)).astype(bf16)


def middle_pass(at, ho, tok, cot, out_w, w1, w2, vec, vec4, slot, last_part, earlier=(), early_back=(), fc=1024):
    _, n, d = ho.shape
    ff = w1.shape[1]
    chunks = ff // fc
    last = chunks - 1
    rows = whole((n, d))
    held = pl.BlockSpec(memory_space=pl.ANY)

    def once(shape, index):
        return pl.BlockSpec(shape, index, pipeline_mode=pl.Buffered(1))

    in_place = once((1, n, d), lambda t, at: (at[0], 0, 0))
    in_slot = once((1, n, d), lambda t, at: (slot, 0, 0))
    split = once((2, n, d // 2), lambda t, at: (0, slot, 0))
    kind = f32 if last_part else bf16
    return pl.pallas_call(
        middle_body,
        name="middle_pass",
        grid_spec=pltpu.PrefetchScalarGridSpec(
            num_scalar_prefetch=1,
            grid=(3 * chunks,),
            in_specs=[
                in_slot,
                in_place,
                in_place,
                whole(out_w.shape),
                held,
                held,
                whole(vec.shape),
                pl.BlockSpec((vec4.shape[0], fc), lambda t, at: (0, t % chunks)),
            ]
            + [held] * (len(early_back) + len(earlier)),
            out_specs=[
                in_place if last_part else rows,
                rows,
                whole((8, d)),
                whole((8, ff)),
                split,
                split,
                pl.BlockSpec((n, fc), lambda t, at: (slot, jnp.clip(t - chunks, 0, last))),
                pl.BlockSpec((n, fc), lambda t, at: (slot, jnp.clip(t - 2 * chunks, 0, last))),
                once((n, d), lambda t, at: (slot, 0)),
                in_slot,
            ],
            scratch_shapes=[
                pltpu.VMEM((chunks, n, fc), f32),
                pltpu.VMEM((chunks, n, fc), bf16),
                pltpu.VMEM((chunks, n, fc), bf16),
                pltpu.VMEM((n, d), f32),
                pltpu.VMEM((n, d), f32),
                pltpu.VMEM((n, LANES), f32),
                pltpu.VMEM((n, LANES), f32),
                pltpu.VMEM((n, LANES), f32),
                pltpu.VMEM((chunks, d, fc), bf16),
                pltpu.VMEM((chunks, fc, d), bf16),
                pltpu.SemaphoreType.DMA((3, chunks)),
            ],
        ),
        out_shape=[
            jax.ShapeDtypeStruct((2, n, d) if last_part else (n, d), kind),
            jax.ShapeDtypeStruct((n, d), f32),
            jax.ShapeDtypeStruct((8, d), f32),
            jax.ShapeDtypeStruct((8, ff), f32),
            jax.ShapeDtypeStruct((2, 2 * n, d // 2), bf16),
            jax.ShapeDtypeStruct((2, 2 * n, d // 2), bf16),
            jax.ShapeDtypeStruct((2 * n, ff), bf16),
            jax.ShapeDtypeStruct((2 * n, ff), bf16),
            jax.ShapeDtypeStruct((2 * n, d), bf16),
            jax.ShapeDtypeStruct((2, n, d), bf16),
        ],
        input_output_aliases={9 + len(early_back) + k: 4 + k for k in range(len(earlier))},
        compiler_params=params(62),
        cost_estimate=cost(
            8 * n * d * ff + 4 * n * d * d, 4 * d * ff + 2 * d * d + 4 * n * ff + 20 * n * d
        ),
    )(at, ho, tok, cot, out_w, w1, w2, vec, vec4, *early_back, *earlier)


def grad_mid_body(at, cot, w, out):
    out[...] = mm(cot[0], w[...], NT).astype(bf16)


def grad_mid(at, cot, w, fc=1024):
    _, n, d = cot.shape
    ff = w.shape[0]
    return pl.pallas_call(
        grad_mid_body,
        name="grad_mid",
        grid_spec=pltpu.PrefetchScalarGridSpec(
            num_scalar_prefetch=1,
            grid=(ff // fc,),
            in_specs=[
                pl.BlockSpec((1, n, d), lambda t, at: (at[0], 0, 0), pipeline_mode=pl.Buffered(1)),
                pl.BlockSpec((fc, d), lambda t, at: (t, 0)),
            ],
            out_specs=pl.BlockSpec((n, fc), lambda t, at: (0, t)),
        ),
        out_shape=jax.ShapeDtypeStruct((n, ff), bf16),
        compiler_params=params(),
        cost_estimate=cost(2 * n * d * ff, 2 * (n * d + d * ff + n * ff)),
    )(at, cot, w)


def first_back_body(at, even, odd, w, tok, grad_middle, gain, tokens_grad, sums):
    @pl.when(pl.program_id(0) == 0)
    def _():
        sums[...] = jnp.zeros_like(sums)

    d = w.shape[0]
    run = d // 4
    grad = None
    for part in range(3):
        for r in range(4):
            piece = (even, odd)[r % 2][part, :, (r // 2) * run : (r // 2 + 1) * run]
            here = r * run
            term = mm(piece, w[:, part * d + here : part * d + here + run], NT)
            grad = term if grad is None else grad + term
            if part != 1:
                at = 2 + part // 2
                sums[at : at + 1, here : here + run] += row_sum(piece.astype(f32))
    unit, inverse = norm_unit(tok[0].astype(f32))
    sums[0:1, :] += row_sum(grad * unit)
    sums[1:2, :] += row_sum(grad)
    whole_grad = grad_middle[...] + norm_back(grad, unit, inverse, gain[...])
    if len(tokens_grad.shape) == 3:
        tokens_grad[0] = whole_grad
    else:
        tokens_grad[...] = whole_grad.astype(tokens_grad.dtype)


def first_back(at, even, odd, w, tok, grad_middle, gain, slot, last_part, tb=256):
    d = w.shape[0]
    n = even.shape[1] // 2
    first = slot * (n // tb)
    half = pl.BlockSpec((3, tb, d // 2), lambda i, at: (0, first + i, 0))
    rows = pl.BlockSpec((tb, d), lambda i, at: (i, 0))
    in_place = pl.BlockSpec((1, tb, d), lambda i, at: (at[0], i, 0))
    return pl.pallas_call(
        first_back_body,
        name="first_back",
        grid_spec=pltpu.PrefetchScalarGridSpec(
            num_scalar_prefetch=1,
            grid=(n // tb,),
            in_specs=[half, half, whole(w.shape), in_place, rows, whole(gain.shape)],
            out_specs=[in_place if last_part else rows, whole((8, d))],
        ),
        out_shape=[
            jax.ShapeDtypeStruct((2, n, d), f32) if last_part else jax.ShapeDtypeStruct((n, d), bf16),
            jax.ShapeDtypeStruct((8, d), f32),
        ],
        compiler_params=params(),
        cost_estimate=cost(6 * n * d * d, 6 * d * d + 16 * n * d),
    )(at, even, odd, w, tok, grad_middle, gain)


def after(x, *others):
    return lax.optimization_barrier((x,) + others)[0]


def emit(at_low, low, high, received, outs):
    send, keep = jnp.where(at_low, high, low), jnp.where(at_low, low, high)
    if received is None:
        outs[-1][0] = send.astype(bf16)
        outs[-1][1] = keep.astype(bf16)
    else:
        outs[-2][...] = (send + received[0].astype(f32)).astype(bf16)
        outs[-1][...] = (keep + received[1].astype(f32)).astype(bf16)


def tall_grad_body(received_too, tab, *refs):
    runs, halves = refs[:2], refs[2:4]
    a = jnp.concatenate([r[...] for r in runs], axis=1)
    total = mm(a, jnp.concatenate([h[0] for h in halves], axis=0), TN)
    wide = total.shape[1] // 2
    emit(tab[2] == 0, total[:, :wide], total[:, wide:], refs[4] if received_too else None, refs)


def tall_grad(tab, a, b, received=None):
    n, wide = a.shape
    d = b[0].shape[2]
    tall = wide // 16
    steps = 4

    def run(k):
        return pl.BlockSpec((n, tall), lambda i, t: (0, (2 * i + k) * 2 + t[0]))

    in_specs = [
        run(0),
        run(1),
        pl.BlockSpec((1, n // 2, d), lambda i, t: (t[2], 0, 0), pipeline_mode=pl.Buffered(1)),
        pl.BlockSpec((1, n // 2, d), lambda i, t: (0, 0, 0), pipeline_mode=pl.Buffered(1)),
    ]
    both = pl.BlockSpec((2, 2 * tall, d // 2), lambda i, t: (0, i, 0))
    one = pl.BlockSpec((2 * tall, d // 2), lambda i, t: (i, 0))
    args = [tab, a, a, *b]
    if received is not None:
        in_specs.append(both)
        args.append(received)
    shape = (wide // 2, d // 2)
    return pl.pallas_call(
        partial(tall_grad_body, received is not None),
        name="tall_grad",
        grid_spec=pltpu.PrefetchScalarGridSpec(
            num_scalar_prefetch=1,
            grid=(steps,),
            in_specs=in_specs,
            out_specs=both if received is None else [one, one],
        ),
        out_shape=jax.ShapeDtypeStruct((2,) + shape, bf16)
        if received is None
        else [jax.ShapeDtypeStruct(shape, bf16)] * 2,
        compiler_params=params(),
        cost_estimate=cost(2 * n * wide * d // 2, n * wide + 2 * n * d + 8 * wide * d // 4),
    )(*args)


def flat_grad_body(counts, received_too, tab, *refs):
    step = pl.program_id(0)
    parts = len(counts)
    lhs, rhs = refs[:parts], refs[parts : 2 * parts]
    first = 0
    for k, count in enumerate(counts):

        @pl.when((step >= first) & (step < first + count))
        def _(k=k):
            b = rhs[k][0] if len(rhs[k].shape) == 3 else rhs[k][...]
            total = mm(lhs[k][0], b, TN)
            run = total.shape[0] // 8
            low, high = (
                jnp.concatenate([total[(2 * z + h) * run : (2 * z + h + 1) * run] for z in range(4)])
                for h in range(2)
            )
            emit(tab[1] == 0, low, high, refs[2 * parts] if received_too else None, refs)

        first += count


def flat_grad(tab, pairs, tn, received=None):
    counts = [b.shape[0] if b.ndim == 3 else b.shape[1] // tn for _, b in pairs]
    steps = sum(counts)
    n, wide = pairs[0][0].shape[1:]
    in_specs = [
        pl.BlockSpec((1, n, wide), lambda i, t: (t[0], 0, 0), pipeline_mode=pl.Buffered(1))
    ] * len(pairs)
    first = 0
    for (_, b), count in zip(pairs, counts):
        at = partial(lambda first, last, i: jnp.clip(i - first, 0, last), first, count - 1)
        if b.ndim == 3:
            in_specs.append(pl.BlockSpec((1, n, tn), lambda i, t, at=at: (at(i), 0, 0)))
        else:
            in_specs.append(pl.BlockSpec((n, tn), lambda i, t, at=at: (0, at(i))))
        first += count
    both = pl.BlockSpec((2, wide // 2, tn), lambda i, t: (0, 0, i))
    one = pl.BlockSpec((wide // 2, tn), lambda i, t: (0, i))
    args = [tab] + [a for a, _ in pairs] + [b for _, b in pairs]
    if received is not None:
        in_specs.append(both)
        args.append(received)
    shape = (wide // 2, steps * tn)
    weight = 16 if pairs[0][1].ndim == 3 else 1
    return pl.pallas_call(
        partial(flat_grad_body, counts, received is not None),
        name="flat_grad",
        grid_spec=pltpu.PrefetchScalarGridSpec(
            num_scalar_prefetch=1,
            grid=(steps,),
            in_specs=in_specs,
            out_specs=both if received is None else [one, one],
        ),
        out_shape=jax.ShapeDtypeStruct((2,) + shape, bf16)
        if received is None
        else [jax.ShapeDtypeStruct(shape, bf16)] * 2,
        compiler_params=params(),
        cost_estimate=cost(2 * n * wide * shape[1] // weight, (2 * n * (wide + shape[1]) + 8 * wide * shape[1]) // weight),
    )(*args)


def running_sums(lengths):
    count = lengths.shape[1]
    upto = jnp.arange(count)[:, None] >= jnp.arange(count)[None, :]
    return jnp.sum(jnp.where(upto[None], lengths[:, None, :], 0), axis=2).astype(jnp.int32)


def norm_forward(values, gain, shift):
    average = jnp.mean(values, axis=-1, keepdims=True)
    centered = values - average
    inverse = lax.rsqrt(jnp.mean(centered * centered, axis=-1, keepdims=True) + eps)
    normed = centered * inverse
    return (normed * gain + shift, normed, inverse)


def norm_backward(grad_y, normed, inverse, gain):
    scaled = grad_y * gain
    grad_in = inverse * (
        scaled
        - jnp.mean(scaled, axis=-1, keepdims=True)
        - normed * jnp.mean(scaled * normed, axis=-1, keepdims=True)
    )
    return (grad_in, jnp.sum(grad_y * normed, axis=(0, 1)), jnp.sum(grad_y, axis=(0, 1)))


def local_general(
    tokens,
    cotangent,
    doc_lengths,
    norm1_gain,
    norm1_shift,
    qkv_weight,
    query_bias,
    value_bias,
    head_scales,
    out_weight,
    out_bias,
    attn_gain,
    attn_shift,
    norm2_gain,
    norm2_shift,
    fc1_weight,
    fc1_bias,
    mid_gain,
    mid_shift,
    fc2_weight,
    fc2_bias,
):
    f32 = jnp.float32
    bf16 = jnp.bfloat16
    batch_size, local_len, model_width = tokens.shape
    head_count = head_scales.shape[0]
    head_dim = model_width // head_count
    score_scale = head_dim ** (-0.5)
    row_len = local_len * lax.axis_size("blk")
    row_first = lax.axis_index("blk") * local_len
    query_pos = row_first + jnp.arange(local_len, dtype=jnp.int32)
    doc_ends = running_sums(doc_lengths)
    starts = jnp.max(
        jnp.where(doc_ends[:, None, :] <= query_pos[None, :, None], doc_ends[:, None, :], 0), axis=2
    )
    lowest = jnp.min(starts[:, 0])
    query_last = row_first + local_len - 1
    inputs = tokens.astype(f32)
    attn_norm, unit_one, inverse_one = norm_forward(inputs, norm1_gain, norm1_shift)
    attn_in = attn_norm.astype(bf16)
    projected = jnp.dot(attn_in, qkv_weight, preferred_element_type=f32)
    queries = (
        (projected[..., :model_width] + query_bias)
        .astype(bf16)
        .reshape(batch_size, local_len, head_count, head_dim)
    )
    keys_low = projected[..., model_width : 2 * model_width].astype(bf16)
    values_low = (projected[..., 2 * model_width :] + value_bias).astype(bf16)

    def block_scores(key_piece, offset):
        key_len = key_piece.shape[1]
        keys_head = key_piece.reshape(batch_size, key_len, head_count, head_dim)
        raw_scores = (
            jnp.einsum("bqhd,bkhd->bhqk", queries, keys_head, preferred_element_type=f32)
            * score_scale
        )
        key_pos = offset + jnp.arange(key_len, dtype=jnp.int32)
        allowed = (key_pos[None, None, :] <= query_pos[None, :, None]) & (
            key_pos[None, None, :] >= starts[:, :, None]
        )
        return (jnp.where(allowed[:, None], raw_scores, masked_score), keys_head)

    def is_live(offset, key_len):
        return (offset <= query_last) & (offset + key_len - 1 >= lowest)

    def attend_slab(running, key_piece, value_piece, offset):
        key_len = key_piece.shape[1]

        def attend_compute(state):
            running_max, running_sum, weighted = state
            scores, keys_head = block_scores(key_piece, offset)
            new_max = jnp.maximum(running_max, jnp.max(scores, axis=3))
            rescale = jnp.exp(running_max - new_max)
            weights = jnp.exp(scores - new_max[..., None])
            values_head = value_piece.reshape(batch_size, key_len, head_count, head_dim)
            update = jnp.einsum(
                "bhqk,bkhd->bqhd", weights.astype(bf16), values_head, preferred_element_type=f32
            )
            rescale_t = jnp.transpose(rescale, (0, 2, 1))[..., None]
            return (
                new_max,
                running_sum * rescale + jnp.sum(weights, axis=3),
                weighted * rescale_t + update,
            )

        return lax.cond(is_live(offset, key_len), attend_compute, lambda state: state, running)

    start_state = (
        jnp.full((batch_size, head_count, local_len), masked_score, f32),
        jnp.zeros((batch_size, head_count, local_len), f32),
        jnp.zeros((batch_size, local_len, head_count, head_dim), f32),
    )
    key_piece = lax.all_gather(keys_low, "blk", axis=1, tiled=True)
    value_piece = lax.all_gather(values_low, "blk", axis=1, tiled=True)
    turns = key_piece.shape[1] // local_len

    def one_turn(index, state):
        begin = index * local_len
        key_slab = lax.dynamic_slice_in_dim(key_piece, begin, local_len, 1)
        value_slab = lax.dynamic_slice_in_dim(value_piece, begin, local_len, 1)
        return attend_slab(state, key_slab, value_slab, begin)

    running_max, running_sum, weighted = lax.fori_loop(0, turns, one_turn, start_state)
    attended = weighted / jnp.transpose(running_sum, (0, 2, 1))[..., None]
    log_total = running_max + jnp.log(running_sum)
    heads_out = (
        (attended * head_scales[:, None]).reshape(batch_size, local_len, model_width).astype(bf16)
    )
    projection = jnp.dot(heads_out, out_weight, preferred_element_type=f32) + out_bias
    branch, unit_attn, inverse_attn = norm_forward(projection, attn_gain, attn_shift)
    middle = inputs + branch
    ffn_norm, unit_two, inverse_two = norm_forward(middle, norm2_gain, norm2_shift)
    ffn_in = ffn_norm.astype(bf16)
    hidden = jnp.dot(ffn_in, fc1_weight, preferred_element_type=f32) + fc1_bias
    activated, gelu_grad = jax.vjp(partial(jax.nn.gelu, approximate=False), hidden)
    mid_norm, unit_mid, inverse_mid = norm_forward(activated, mid_gain, mid_shift)
    mid_out = mid_norm.astype(bf16)
    output = middle + jnp.dot(mid_out, fc2_weight, preferred_element_type=f32) + fc2_bias
    grad_output = cotangent.astype(f32)
    fc2_weight_grad = jnp.einsum("bcf,bcd->fd", mid_out, cotangent, preferred_element_type=f32)
    fc2_bias_grad = jnp.sum(grad_output, axis=(0, 1))
    grad_mid = jnp.einsum("bcd,fd->bcf", cotangent, fc2_weight, preferred_element_type=f32)
    grad_act, mid_gain_grad, mid_shift_grad = norm_backward(
        grad_mid, unit_mid, inverse_mid, mid_gain
    )
    grad_hidden = gelu_grad(grad_act)[0].astype(bf16)
    fc1_weight_grad = jnp.einsum("bcd,bcf->df", ffn_in, grad_hidden, preferred_element_type=f32)
    fc1_bias_grad = jnp.sum(grad_hidden.astype(f32), axis=(0, 1))
    grad_ffn_in = jnp.einsum("bcf,df->bcd", grad_hidden, fc1_weight, preferred_element_type=f32)
    grad_two, norm2_gain_grad, norm2_shift_grad = norm_backward(
        grad_ffn_in, unit_two, inverse_two, norm2_gain
    )
    grad_middle = grad_output + grad_two
    grad_proj_f, attn_gain_grad, attn_shift_grad = norm_backward(
        grad_middle, unit_attn, inverse_attn, attn_gain
    )
    grad_projection = grad_proj_f.astype(bf16)
    out_weight_grad = jnp.einsum(
        "bcd,bce->de", heads_out, grad_projection, preferred_element_type=f32
    )
    out_bias_grad = jnp.sum(grad_projection.astype(f32), axis=(0, 1))
    grad_heads = jnp.einsum(
        "bce,de->bcd", grad_projection, out_weight, preferred_element_type=f32
    ).reshape(batch_size, local_len, head_count, head_dim)
    head_scales_grad = jnp.sum(grad_heads * attended, axis=(0, 1, 3))
    grad_attended = (grad_heads * head_scales[:, None]).astype(bf16)
    row_dot = jnp.transpose(jnp.sum(grad_attended.astype(f32) * attended, axis=3), (0, 2, 1))

    def back_slab(running, key_piece, value_piece, offset):
        key_len = key_piece.shape[1]

        def back_compute(state):
            grad_queries, kv_buffer = state
            scores, keys_head = block_scores(key_piece, offset)
            attn_probs = jnp.exp(scores - log_total[..., None])
            values_head = value_piece.reshape(batch_size, key_len, head_count, head_dim)
            grad_probs = jnp.einsum(
                "bqhd,bkhd->bhqk", grad_attended, values_head, preferred_element_type=f32
            )
            grad_scores = (attn_probs * (grad_probs - row_dot[..., None])).astype(bf16)
            grad_queries = (
                grad_queries
                + jnp.einsum("bhqk,bkhd->bqhd", grad_scores, keys_head, preferred_element_type=f32)
                * score_scale
            )
            grad_keys = (
                jnp.einsum("bhqk,bqhd->bkhd", grad_scores, queries, preferred_element_type=f32)
                * score_scale
            )
            grad_values = jnp.einsum(
                "bhqk,bqhd->bkhd",
                attn_probs.astype(bf16),
                grad_attended,
                preferred_element_type=f32,
            )
            addition = jnp.concatenate(
                [
                    grad_keys.reshape(batch_size, key_len, model_width),
                    grad_values.reshape(batch_size, key_len, model_width),
                ],
                axis=2,
            )
            previous = lax.dynamic_slice_in_dim(kv_buffer, offset, key_len, 1)
            return (
                grad_queries,
                lax.dynamic_update_slice_in_dim(kv_buffer, previous + addition, offset, 1),
            )

        return lax.cond(is_live(offset, key_len), back_compute, lambda state: state, running)

    back_state = (
        jnp.zeros((batch_size, local_len, head_count, head_dim), f32),
        jnp.zeros((batch_size, row_len, 2 * model_width), f32),
    )
    attend_key_piece = lax.all_gather(keys_low, "blk", axis=1, tiled=True)
    attend_value_piece = lax.all_gather(values_low, "blk", axis=1, tiled=True)
    turns = attend_key_piece.shape[1] // local_len

    def one_turn(index, state):
        begin = index * local_len
        key_slab = lax.dynamic_slice_in_dim(attend_key_piece, begin, local_len, 1)
        value_slab = lax.dynamic_slice_in_dim(attend_value_piece, begin, local_len, 1)
        return back_slab(state, key_slab, value_slab, begin)

    grad_queries, kv_buffer = lax.fori_loop(0, turns, one_turn, back_state)
    grad_kv = lax.psum_scatter(
        kv_buffer.astype(jnp.bfloat16), "blk", scatter_dimension=1, tiled=True
    ).astype(jnp.float32)
    grad_qkv = jnp.concatenate(
        [grad_queries.reshape(batch_size, local_len, model_width), grad_kv], axis=2
    ).astype(bf16)
    qkv_weight_grad = jnp.einsum("bcd,bce->de", attn_in, grad_qkv, preferred_element_type=f32)
    query_bias_grad = jnp.sum(grad_qkv[..., :model_width].astype(f32), axis=(0, 1))
    value_bias_grad = jnp.sum(grad_qkv[..., 2 * model_width :].astype(f32), axis=(0, 1))
    grad_attn_in = jnp.einsum("bce,de->bcd", grad_qkv, qkv_weight, preferred_element_type=f32)
    grad_one, norm1_gain_grad, norm1_shift_grad = norm_backward(
        grad_attn_in, unit_one, inverse_one, norm1_gain
    )
    tokens_grad = grad_middle + grad_one
    matrix_grads = (qkv_weight_grad, out_weight_grad, fc1_weight_grad, fc2_weight_grad)
    reduced = (
        lax.psum_scatter(
            matrix_grads[0].astype(jnp.bfloat16), "dp", scatter_dimension=0, tiled=True
        ).astype(jnp.float32),
        lax.psum_scatter(
            matrix_grads[1].astype(jnp.bfloat16), "dp", scatter_dimension=0, tiled=True
        ).astype(jnp.float32),
        lax.psum_scatter(
            matrix_grads[2].astype(jnp.bfloat16), "dp", scatter_dimension=0, tiled=True
        ).astype(jnp.float32),
        lax.psum_scatter(
            matrix_grads[3].astype(jnp.bfloat16), "dp", scatter_dimension=0, tiled=True
        ).astype(jnp.float32),
    )
    reduced = (
        lax.psum_scatter(
            reduced[0].astype(jnp.bfloat16), "blk", scatter_dimension=1, tiled=True
        ).astype(jnp.float32),
        lax.psum_scatter(
            reduced[1].astype(jnp.bfloat16), "blk", scatter_dimension=1, tiled=True
        ).astype(jnp.float32),
        lax.psum_scatter(
            reduced[2].astype(jnp.bfloat16), "blk", scatter_dimension=1, tiled=True
        ).astype(jnp.float32),
        lax.psum_scatter(
            reduced[3].astype(jnp.bfloat16), "blk", scatter_dimension=1, tiled=True
        ).astype(jnp.float32),
    )
    small_sums = lax.psum(
        (
            norm1_gain_grad,
            norm1_shift_grad,
            query_bias_grad,
            value_bias_grad,
            head_scales_grad,
            out_bias_grad,
            attn_gain_grad,
            attn_shift_grad,
            norm2_gain_grad,
            norm2_shift_grad,
            fc1_bias_grad,
            mid_gain_grad,
            mid_shift_grad,
            fc2_bias_grad,
        ),
        ("dp", "blk"),
    )
    return (
        output,
        tokens_grad,
        small_sums[0],
        small_sums[1],
        reduced[0],
        small_sums[2],
        small_sums[3],
        small_sums[4],
        reduced[1],
        small_sums[5],
        small_sums[6],
        small_sums[7],
        small_sums[8],
        small_sums[9],
        reduced[2],
        small_sums[10],
        small_sums[11],
        small_sums[12],
        reduced[3],
        small_sums[13],
    )


swap = ((0, 1), (1, 0))


def exchange(x):
    return lax.ppermute(x, "blk", swap)


def flip(x, bit):
    return lax.ppermute(x, "dp", [(i, i ^ bit) for i in range(16)])


def local_rows(
    tokens,
    cotangent,
    doc_lengths,
    norm1_gain,
    norm1_shift,
    qkv_weight,
    query_bias,
    value_bias,
    head_scales,
    out_weight,
    out_bias,
    attn_gain,
    attn_shift,
    norm2_gain,
    norm2_shift,
    fc1_weight,
    fc1_bias,
    mid_gain,
    mid_shift,
    fc2_weight,
    fc2_bias,
):
    _, half_len, d = tokens.shape
    ff = fc1_weight.shape[1]
    heads = head_scales.shape[0]
    head_dim = d // heads
    scale = head_dim**-0.5
    n = 2 * half_len
    b = lax.axis_index("blk").astype(jnp.int32)
    dp = lax.axis_index("dp").astype(jnp.int32)
    core, x, z, y = dp % 2, (dp // 2) % 2, dp // 4, b

    tok_in = exchange(lax.dynamic_slice_in_dim(tokens, 1 - b, 1, 0))
    cot_in = exchange(lax.dynamic_slice_in_dim(cotangent, 1 - b, 1, 0))
    kept_at = b[None]
    sent_at = jnp.zeros((1,), jnp.int32)

    def line(v):
        return v.reshape(1, -1)

    qkv_bias = jnp.concatenate([query_bias, jnp.zeros_like(query_bias), value_bias])
    first_args = (line(norm1_gain), line(norm1_shift), qkv_weight, line(qkv_bias), scale)
    early = project_qkv(kept_at, tokens, *first_args, 0, n)

    def later(v):
        return after(v, early[0])

    lengths = lax.dynamic_slice_in_dim(later(doc_lengths), b, 1, 0)
    ends = running_sums(lengths)[0]
    firsts = (half_len // 2) * jnp.arange(4, dtype=jnp.int32)
    starts = jnp.max(jnp.where(ends[None, :] <= firsts[:, None], ends[None, :], 0), axis=1)
    allowed = (firsts[None, :] >= starts[:, None]).astype(jnp.int32)
    tab = jnp.concatenate([b[None], allowed.reshape(16)])
    theirs = jnp.stack([1 - core, x, y])
    mine = jnp.stack([core, x, y])
    head_scales = later(head_scales)
    scale_row = jnp.broadcast_to(head_scales[:, None], (heads, head_dim)).reshape(1, d)
    vec = jnp.stack(
        [later(out_bias), attn_gain, attn_shift, norm2_gain, norm2_shift, fc2_bias, scale_row[0], out_bias]
    )
    fc1_bias = later(fc1_bias)
    vec4 = jnp.stack([fc1_bias, mid_gain, mid_shift, fc1_bias])

    early_back = grad_mid(later(kept_at), cotangent, fc2_weight)
    made = after(sent_at, early_back, tab, theirs, mine, scale_row, vec, vec4)
    attn_in, qkv = project_qkv(made, tok_in, *first_args, 1, n, early)
    qkv = qkv.reshape(2, half_len, 3 * d)
    heads_out, logs = attend(tab, qkv, scale_row)

    weights = (out_weight, fc1_weight, fc2_weight, vec, vec4)
    out_sent, mid_sent, *more = middle_pass(sent_at, heads_out, tok_in, cot_in, *weights, 1, False)
    sums, sums4, *earlier = more
    out_back = exchange(out_sent)
    output, mid_kept, *more = middle_pass(
        kept_at, heads_out, tokens, cotangent, *weights, 0, True, earlier, (early_back,)
    )
    sums = sums + more[0]
    sums4 = sums4 + more[1]
    ffn_in, heads_in, mid_out, grad_hidden, grad_proj, d_out = more[2:]

    def fill(kept, back):
        return lax.dynamic_update_slice_in_dim(kept, back.astype(f32)[None], 1 - b, 0)

    def near_z(total):
        total = total.astype(bf16).reshape((2, 2) + total.shape[1:])
        odd = z % 2
        return (
            lax.dynamic_index_in_dim(total, 1 - odd, 1, keepdims=False),
            lax.dynamic_index_in_dim(total, odd, 1, keepdims=False),
        )

    def far_z(total):
        total = total.astype(bf16)
        high = z // 2
        return (
            lax.dynamic_index_in_dim(total, 1 - high, 0, keepdims=False),
            lax.dynamic_index_in_dim(total, high, 0, keepdims=False),
        )

    def add_z(move, send, keep):
        return keep.astype(f32) + flip(send, move).astype(f32)

    def held(parts, *others):
        return parts[0], after(parts[1], *others)

    def rows_by_x(total):
        total = total.astype(bf16).reshape(4, 2, -1, total.shape[1])
        return (
            lax.dynamic_index_in_dim(total, 1 - x, 1, keepdims=False),
            lax.dynamic_index_in_dim(total, x, 1, keepdims=False),
        )

    def columns_by_y(total, *cuts):
        total = total.astype(bf16).reshape(4, -1, total.shape[1])
        out = []
        for at in (1 - y, y):
            groups = []
            for first, last in zip((0,) + cuts, cuts + (total.shape[2],)):
                width = (last - first) // 2
                groups.append(lax.dynamic_slice_in_dim(total, first + at * width, width, 2))
            out.append(jnp.concatenate(groups, axis=2) if cuts else groups[0])
        return out

    def add_x(send, keep):
        return keep.astype(f32) + flip(send, 2).astype(f32)

    def add_y(send, keep):
        return keep.astype(f32) + exchange(send).astype(f32)

    cots = (cotangent, cot_in)
    output = fill(output, out_back)
    wide_pairs = [(after(ffn_in, output), grad_hidden), (heads_in, grad_proj)]
    wide_theirs = flat_grad(theirs, wide_pairs, d)
    fc2_theirs = tall_grad(theirs, after(mid_out, wide_theirs), cots)
    wide_pairs = [(after(ffn_in, fc2_theirs), grad_hidden), (heads_in, grad_proj)]
    wide_parts = flat_grad(mine, wide_pairs, d, flip(wide_theirs, 1))
    fc2_parts = tall_grad(mine, after(mid_out, *wide_parts), cots, flip(fc2_theirs, 1))
    d_out = after(d_out, *fc2_parts)
    back_args = (1.0 / scale_row, logs, scale)
    even, dots_even = attend_back(tab, qkv, heads_out, d_out, *back_args, 0)
    even = even.reshape(3, n, d // 2)
    even_theirs = flat_grad(theirs, [(after(attn_in, even), even)], d // 2)
    d_out = after(d_out, even_theirs)
    odd, dots_odd = attend_back(tab, qkv, heads_out, d_out, *back_args, 1)
    odd = odd.reshape(3, n, d // 2)
    wide_parts = columns_by_y(add_x(*held(wide_parts, odd)), ff)
    fc2_parts = rows_by_x(add_y(*held(fc2_parts, odd)))
    odd_theirs = flat_grad(theirs, [(after(attn_in, *wide_parts, *fc2_parts), odd)], d // 2)
    even_parts = flat_grad(mine, [(after(attn_in, odd_theirs), even)], d // 2, flip(even_theirs, 1))
    grad_sent, sums_sent = first_back(
        sent_at, after(even, *even_parts), odd, qkv_weight, tok_in, mid_sent, line(norm1_gain), 1, False
    )
    grad_back = exchange(grad_sent)
    fc2_parts = near_z(add_x(*held(fc2_parts, grad_sent)))
    odd_parts = flat_grad(
        mine, [(after(attn_in, grad_sent, *fc2_parts), odd)], d // 2, flip(odd_theirs, 1)
    )
    wide_parts = near_z(add_y(*held(wide_parts, *odd_parts)))
    tokens_grad, sums_kept = first_back(
        kept_at, after(even, *wide_parts), odd, qkv_weight, tokens, mid_kept, line(norm1_gain), 0, True
    )
    dots = jnp.stack([dots_even[:, 0].reshape(2, 4, head_dim), dots_odd[:, 0].reshape(2, 4, head_dim)], axis=1)
    head_scales_grad = jnp.sum(dots, axis=3).reshape(heads) / head_scales
    head_scales_grad = jnp.pad(head_scales_grad, (0, d - heads))
    total = jnp.concatenate(
        [
            (sums_sent + sums_kept)[:4],
            head_scales_grad[None],
            sums[:6],
            sums4.reshape(8 * ff // d, d)[: 3 * ff // d],
        ]
    )
    fc2_parts = far_z(add_z(4, *held(fc2_parts, tokens_grad)))
    even_parts = columns_by_y(add_x(*held(even_parts, tokens_grad)))
    wide_parts = far_z(add_z(4, *held(wide_parts, tokens_grad)))
    tokens_grad = fill(tokens_grad, grad_back)
    odd_parts = columns_by_y(add_x(*odd_parts))
    even_parts = near_z(add_y(*even_parts))
    odd_parts = near_z(add_y(*odd_parts))
    total = total + (partial(flip, bit=1))(total)
    total = total + (partial(flip, bit=4))(total)
    total = total + (partial(flip, bit=8))(total)
    total = after(total, *odd_parts)
    total = total + (partial(flip, bit=2))(total)
    total = total + (exchange)(total)
    even_parts = far_z(add_z(4, *even_parts))
    odd_parts = far_z(add_z(4, *odd_parts))
    fc2_weight_grad = add_z(8, *fc2_parts)
    wide_grad = add_z(8, *wide_parts)
    fc1_weight_grad, out_weight_grad = wide_grad[:, : ff // 2], wide_grad[:, ff // 2 :]
    even_grad, odd_grad = (add_z(8, *parts) for parts in (even_parts, odd_parts))
    first_sums, sums, sums4 = total[:5], total[5:11], total[11:].reshape(3, ff)
    run = d // 4
    qkv_weight_grad = jnp.stack(
        [even_grad.reshape(-1, 3, run), odd_grad.reshape(-1, 3, run)], axis=2
    ).reshape(-1, 6 * run)
    return (
        output,
        tokens_grad,
        first_sums[0],
        first_sums[1],
        qkv_weight_grad,
        first_sums[2],
        first_sums[3],
        first_sums[4, :heads],
        out_weight_grad,
        sums[0],
        sums[1],
        sums[2],
        sums[3],
        sums[4],
        fc1_weight_grad,
        sums4[0],
        sums4[1],
        sums4[2],
        fc2_weight_grad,
        sums[5],
    )


def solution(mesh):
    rows_fit = dict(mesh.shape) == {"dp": 16, "blk": 2}
    local = local_rows if rows_fit else local_general
    placed = (
        P("dp", "blk", None),
        P("dp", "blk", None),
        P("dp", None),
        P(),
        P(),
        P(),
        P(),
        P(),
        P(),
        P(),
        P(),
        P(),
        P(),
        P(),
        P(),
        P(),
        P(),
        P(),
        P(),
        P(),
        P(),
    )
    return jax.shard_map(
        local,
        mesh=mesh,
        in_specs=placed,
        out_specs=(
            P("dp", "blk", None),
            P("dp", "blk", None),
            P(),
            P(),
            P("dp", "blk"),
            P(),
            P(),
            P(),
            P("dp", "blk"),
            P(),
            P(),
            P(),
            P(),
            P(),
            P("dp", "blk"),
            P(),
            P(),
            P(),
            P("dp", "blk"),
            P(),
        ),
        check_vma=False,
    )
```

```python
from functools import partial

import jax
import jax.numpy as jnp
from jax import lax
from jax.experimental import pallas as pl
from jax.experimental.pallas import tpu as pltpu
from jax.sharding import PartitionSpec as P

f32 = jnp.float32
bf16 = jnp.bfloat16
eps = 1e-05
masked_score = -1e30
LANES = 128
NT = (((1,), (1,)), ((), ()))
NN = (((1,), (0,)), ((), ()))
TN = (((0,), (0,)), ((), ()))


def mm(a, b, dims=NN):
    return lax.dot_general(a, b, dims, preferred_element_type=f32)


def fold(x):
    total = x[:, :LANES]
    for c in range(LANES, x.shape[1], LANES):
        total = total + x[:, c : c + LANES]
    return total


def row_mean(x):
    return jnp.sum(fold(x), axis=1, keepdims=True) * (1.0 / x.shape[1])


def row_sum(x):
    return jnp.sum(x, axis=0, keepdims=True)


def norm_unit(v):
    centered = v - row_mean(v)
    inverse = lax.rsqrt(row_mean(centered * centered) + eps)
    return centered * inverse, inverse


def norm_back(grad_y, unit, inverse, gain):
    e = grad_y * gain
    return inverse * (e - row_mean(e) - unit * row_mean(e * unit))


def params(mib=None, **more):
    return pltpu.CompilerParams(vmem_limit_bytes=(mib or 60) * 2**20, **more)


def cost(flops, moved):
    return pl.CostEstimate(flops=flops, bytes_accessed=moved, transcendentals=0)


def whole(shape):
    return pl.BlockSpec(shape, lambda *_: (0,) * len(shape), pipeline_mode=pl.Buffered(1))


def core_split(x):
    low = lax.broadcasted_iota(jnp.int32, (x.shape[0], LANES), 1) < LANES // 2
    even, odd = [], []
    for c in range(0, x.shape[1], 2 * LANES):
        a = x[:, c : c + LANES].astype(f32)
        b = x[:, c + LANES : c + 2 * LANES].astype(f32)
        even.append(jnp.where(low, a, pltpu.roll(b, LANES // 2, 1)))
        odd.append(jnp.where(low, pltpu.roll(a, LANES // 2, 1), b))
    return (jnp.concatenate(y, axis=1).astype(bf16) for y in (even, odd))


def qkv_body(scale, at, tok, gain, shift, w, bias, *refs):
    attn_in, qkv, x, ws, sems = refs[-5:]
    step = pl.program_id(0)
    steps, d, cols = ws.shape
    half = cols // 2

    def fetch(k, h):
        columns = pl.ds(pl.multiple_of(k * cols + h * half, half), half)
        return pltpu.make_async_copy(
            w.at[:, columns], ws.at[k, :, pl.ds(h * half, half)], sems.at[k, h]
        )

    @pl.when(step == 0)
    def _():
        for k in range(steps):
            for h in range(2):
                fetch(k, h).start()
        unit, _ = norm_unit(tok[0].astype(f32))
        here = (unit * gain[...] + shift[...]).astype(bf16)
        x[...] = here
        attn_in[0], attn_in[1] = core_split(here)

    for h in range(2):
        fetch(step, h).wait()
    total = (mm(x[...], ws[step]) + bias[...]).astype(bf16)
    qkv[...] = (total.astype(f32) * jnp.where(step == 0, scale, 1.0)).astype(bf16)


def project_qkv(at, tok, gain, shift, w, bias, scale, slot, total, earlier=()):
    _, n, d = tok.shape
    held = pl.BlockSpec(memory_space=pl.ANY)
    return pl.pallas_call(
        partial(qkv_body, scale),
        name="project_qkv",
        grid_spec=pltpu.PrefetchScalarGridSpec(
            num_scalar_prefetch=1,
            grid=(3,),
            in_specs=[
                pl.BlockSpec((1, n, d), lambda i, at: (at[0], 0, 0), pipeline_mode=pl.Buffered(1)),
                whole(gain.shape),
                whole(shift.shape),
                held,
                pl.BlockSpec((1, d), lambda i, at: (0, i)),
            ]
            + [held] * len(earlier),
            out_specs=[
                pl.BlockSpec((2, n, d // 2), lambda i, at: (0, slot, 0)),
                pl.BlockSpec((n, d), lambda i, at: (slot, i)),
            ],
            scratch_shapes=[
                pltpu.VMEM((n, d), bf16),
                pltpu.VMEM((3, d, d), bf16),
                pltpu.SemaphoreType.DMA((3, 2)),
            ],
        ),
        out_shape=[
            jax.ShapeDtypeStruct((2, total, d // 2), bf16),
            jax.ShapeDtypeStruct((total, 3 * d), bf16),
        ],
        input_output_aliases={6 + k: k for k in range(len(earlier))},
        compiler_params=params(),
        cost_estimate=cost(2 * n * d * 3 * d, 6 * d * d + 10 * n * d),
    )(at, tok, gain, shift, w, bias, *earlier)


def half_slot(own, half):
    return own if half == 0 else 1 - own


def pick(ref, own, block, size):
    half, sub = divmod(block, 2)
    return ref[half_slot(own, half), sub * size : (sub + 1) * size, :]


def head_mask(size):
    return lax.broadcasted_iota(jnp.int32, (size, LANES), 1) < LANES // 2


def block_penalty(tab, i, j):
    return jnp.where(tab[1 + 4 * i + j] > 0, 0.0, masked_score).astype(f32)


def stack_heads(x, low):
    zero = jnp.zeros_like(x)
    return jnp.concatenate([jnp.where(low, x, zero), jnp.where(low, zero, x)], axis=0)


def place(ref, own, *targets):
    half = ref.shape[1]
    for h in range(2):
        targets[0][h * half : (h + 1) * half, :] = ref[half_slot(own, h)]


def attend_body(tab, q, k, v, head_scale, heads_out, lse, kp, vp):
    size = q.shape[1] // 2
    own = tab[0]
    low = head_mask(size)
    causal = lax.broadcasted_iota(jnp.int32, (2 * size, size), 0) % size >= lax.broadcasted_iota(
        jnp.int32, (2 * size, size), 1
    )
    lane = lax.broadcasted_iota(jnp.int32, (size, LANES), 1)
    place(k, own, kp)
    place(v, own, vp)
    for i in range(4):
        width = (i + 1) * size
        s = mm(stack_heads(pick(q, own, i, size), low), kp[:width, :], NT)
        parts = [s[:, j * size : (j + 1) * size] + block_penalty(tab, i, j) for j in range(i)]
        parts.append(jnp.where(causal, s[:, i * size :], masked_score))
        top = parts[0]
        for part in parts[1:]:
            top = jnp.maximum(top, part)
        top = jnp.max(top, axis=1, keepdims=True)
        parts = [jnp.exp(part - top) for part in parts]
        total = fold(parts[0])
        for part in parts[1:]:
            total = total + fold(part)
        total = jnp.sum(total, axis=1, keepdims=True)
        p = jnp.concatenate([part.astype(bf16) for part in parts], axis=1)
        out = mm(p, vp[:width, :]) * (1.0 / total)
        both = jnp.where(low, out[:size], out[size:]) * head_scale[...]
        half, sub = divmod(i, 2)
        heads_out[half_slot(own, half), sub * size : (sub + 1) * size, :] = both.astype(bf16)
        logs = top + jnp.log(total)
        columns = jnp.where(lane == 0, logs[:size], logs[size:])
        lse[0, i] = jnp.transpose(columns)[:8]


def attend(tab, qkv, head_scale_row):
    _, half_len, wide = qkv.shape
    d = wide // 3
    pairs = d // LANES
    size = half_len // 2

    def lanes(first):
        return pl.BlockSpec((2, half_len, LANES), lambda p, t: (0, 0, first + p))

    flops = 16 * half_len * half_len * pairs * LANES
    return pl.pallas_call(
        attend_body,
        name="attend",
        grid_spec=pltpu.PrefetchScalarGridSpec(
            num_scalar_prefetch=1,
            grid=(pairs,),
            in_specs=[
                lanes(0),
                lanes(pairs),
                lanes(2 * pairs),
                pl.BlockSpec((1, LANES), lambda p, t: (0, p)),
            ],
            out_specs=[
                lanes(0),
                pl.BlockSpec((1, 4, 8, size), lambda p, t: (p, 0, 0, 0)),
            ],
            scratch_shapes=[pltpu.VMEM((2 * half_len, LANES), bf16)] * 2,
        ),
        out_shape=[
            jax.ShapeDtypeStruct((2, half_len, d), bf16),
            jax.ShapeDtypeStruct((pairs, 4, 8, size), f32),
        ],
        compiler_params=params(),
        cost_estimate=cost(flops * 4, 8 * half_len * wide),
    )(tab, qkv, qkv, qkv, head_scale_row)


def attend_back_body(
    scale, tab, q, k, v, heads_out, d_out, inv_scale, lse, dqkv, dots, kp, vp, dk, dv
):
    size = q.shape[1] // 2
    own = tab[0]
    low = head_mask(size)
    causal = lax.broadcasted_iota(jnp.int32, (2 * size, size), 0) % size >= lax.broadcasted_iota(
        jnp.int32, (2 * size, size), 1
    )
    place(k, own, kp)
    place(v, own, vp)
    dots[...] = jnp.zeros_like(dots)
    for i in range(3, -1, -1):
        width = (i + 1) * size
        q2 = stack_heads(pick(q, own, i, size), low)
        gi = pick(d_out, own, i, size)
        g2 = stack_heads(gi, low)
        product = gi.astype(f32) * pick(heads_out, own, i, size).astype(f32) * inv_scale[...]
        dots[0, 0:1, :] += row_sum(product)
        zero = jnp.zeros_like(product)
        delta = jnp.concatenate(
            [
                jnp.sum(jnp.where(low, product, zero), axis=1, keepdims=True),
                jnp.sum(jnp.where(low, zero, product), axis=1, keepdims=True),
            ],
            axis=0,
        )
        columns = jnp.transpose(lse[0, i])
        logs = jnp.concatenate([columns[:, 0:1], columns[:, 1:2]], axis=0)
        s = mm(q2, kp[:width, :], NT)
        g = mm(g2, vp[:width, :], NT)
        ps, ds = [], []
        for j in range(i + 1):
            here = slice(j * size, (j + 1) * size)
            if j < i:
                p = jnp.exp(s[:, here] - (logs - block_penalty(tab, i, j)))
            else:
                p = jnp.exp(jnp.where(causal, s[:, here], masked_score) - logs)
            ps.append(p.astype(bf16))
            ds.append((p * (g[:, here] - delta)).astype(bf16))
        p = jnp.concatenate(ps, axis=1)
        d = jnp.concatenate(ds, axis=1)
        dv_part = mm(p, g2, TN)
        dk_part = mm(d, q2, TN)
        if i == 3:
            dv[...] = dv_part
            dk[...] = dk_part
        else:
            dv[:width, :] += dv_part
            dk[:width, :] += dk_part
        dq = mm(d, kp[:width, :]) * scale
        half, sub = divmod(i, 2)
        dqkv[0, half_slot(own, half), sub * size : (sub + 1) * size, :] = jnp.where(
            low, dq[:size], dq[size:]
        ).astype(bf16)
    for half in range(2):
        here = slice(half * 2 * size, (half + 1) * 2 * size)
        dqkv[1, half_slot(own, half)] = dk[here, :].astype(bf16)
        dqkv[2, half_slot(own, half)] = dv[here, :].astype(bf16)


def attend_back(tab, qkv, heads_out, d_out, inv_scale_row, lse, scale, group):
    _, half_len, wide = qkv.shape
    d = wide // 3
    every = d // LANES
    pairs = every // 2
    size = half_len // 2

    def pair(p):
        return p + 2 * (p // 2) + 2 * group

    def lanes(first):
        return pl.BlockSpec((2, half_len, LANES), lambda p, t: (0, 0, first + pair(p)))

    flops = 16 * half_len * half_len * pairs * LANES
    return pl.pallas_call(
        partial(attend_back_body, scale),
        name="attend_back",
        grid_spec=pltpu.PrefetchScalarGridSpec(
            num_scalar_prefetch=1,
            grid=(pairs,),
            in_specs=[
                lanes(0),
                lanes(every),
                lanes(2 * every),
                lanes(0),
                lanes(0),
                pl.BlockSpec((1, LANES), lambda p, t: (0, pair(p))),
                pl.BlockSpec((1, 4, 8, size), lambda p, t: (pair(p), 0, 0, 0)),
            ],
            out_specs=[
                pl.BlockSpec((3, 2, half_len, LANES), lambda p, t: (0, 0, 0, p)),
                pl.BlockSpec((1, 8, LANES), lambda p, t: (p, 0, 0)),
            ],
            scratch_shapes=[pltpu.VMEM((2 * half_len, LANES), bf16)] * 2
            + [pltpu.VMEM((2 * half_len, LANES), f32)] * 2,
        ),
        out_shape=[
            jax.ShapeDtypeStruct((3, 2, half_len, d // 2), bf16),
            jax.ShapeDtypeStruct((pairs, 8, LANES), f32),
        ],
        compiler_params=params(20),
        cost_estimate=cost(flops * 10, 8 * half_len * wide),
    )(tab, qkv, qkv, qkv, heads_out, d_out, inv_scale_row, lse)


def gelu_parts(v):
    a = jnp.abs(v)
    t = 1.0 / (1.0 + (0.3275911 * 0.7071067811865476) * a)
    bell = jnp.exp(v * v * -0.5)
    poly = ((((1.061405429 * t - 1.453152027) * t + 1.421413741) * t - 0.284496736) * t + 0.254829592) * t
    tail = (0.5 * poly) * bell
    cdf = jnp.where(v < 0, tail, 1.0 - tail)
    return v * cdf, cdf + v * (bell * 0.3989422804014327)


def middle_body(
    at, ho, tok, cot, out_w, w1, w2, vec, vec4, *refs
):
    (
        output, grad_middle, sums, sums4, ffn_in, heads_in, mid_out, grad_hidden, grad_proj, d_out,
        act, slope, back, acc, unit_b, stats, total, total_u, w1s, w2s, sems,
    ) = refs[-21:]
    early_back = refs[0] if len(output.shape) == 3 else None
    ho, tok, cot, d_out = (ref.at[0] for ref in (ho, tok, cot, d_out))
    output = output.at[0] if len(output.shape) == 3 else output
    step = pl.program_id(0)
    n, d = ho.shape
    chunks, _, fc = w1s.shape
    ff = fc * chunks
    c = step % chunks
    ahead = 2

    def fetch(k):
        columns = pl.ds(pl.multiple_of(k * fc, fc), fc)
        copies = [
            pltpu.make_async_copy(w1.at[:, columns], w1s.at[k], sems.at[0, k]),
            pltpu.make_async_copy(w2.at[columns, :], w2s.at[k], sems.at[1, k]),
        ]
        if early_back is not None:
            copies.append(pltpu.make_async_copy(early_back.at[:, columns], back.at[k], sems.at[2, k]))
        return copies
    strip = 128
    strips = n // strip

    def v(r):
        return vec[r : r + 1, :]

    def rows(t):
        return pl.ds(pl.multiple_of(t * strip, strip), strip)

    @pl.when(step == 0)
    def _():
        for k in range(ahead):
            for copy in fetch(k):
                copy.start()
        sums[...] = jnp.zeros_like(sums)
        acc[...] = mm(ho[...], out_w[...])

        def one(t, _):
            r = rows(t)
            unit_attn, inverse_attn = norm_unit(acc[r, :] + v(0))
            middle = tok[r, :].astype(f32) + (unit_attn * v(1) + v(2))
            unit_two, inverse_two = norm_unit(middle)
            x = (unit_two * v(3) + v(4)).astype(bf16)
            grad_middle[r, :] = unit_attn
            unit_b[r, :] = unit_two
            stats[r, 0:1] = inverse_attn
            stats[r, 1:2] = inverse_two
            acc[r, :] = middle + v(5)
            d_out[r, :] = x
            ffn_in[0, r, :], ffn_in[1, r, :] = core_split(x)
            heads_in[0, r, :], heads_in[1, r, :] = core_split(ho[r, :])
            return 0

        lax.fori_loop(0, strips, one, 0)

    @pl.when(step < chunks - ahead)
    def _():
        for copy in fetch(step + ahead):
            copy.start()

    @pl.when(step < chunks)
    def _():
        for copy in fetch(step):
            copy.wait()
        h = mm(d_out[...], w1s[c]) + vec4[0:1, :]
        if early_back is None:
            back[c] = mm(cot[...], w2s[c], NT).astype(back.dtype)
        a, b = gelu_parts(h)
        act[c] = a
        slope[c] = b.astype(slope.dtype)

    @pl.when(step == 0)
    def _():
        total[...] = jnp.zeros_like(total)

    @pl.when(step < chunks)
    def _():
        total[...] += fold(act[c])

    @pl.when(step == chunks)
    def _():
        mean = jnp.sum(total[...], axis=1, keepdims=True) * (1.0 / ff)

        def one(k, t):
            centered = act[k] - mean
            return t + fold(centered * centered)

        square = lax.fori_loop(0, chunks, one, jnp.zeros_like(total))
        stats[:, 2:3] = mean
        stats[:, 3:4] = lax.rsqrt(jnp.sum(square, axis=1, keepdims=True) * (1.0 / ff) + eps)
        total[...] = jnp.zeros_like(total)
        total_u[...] = jnp.zeros_like(total_u)

    here = pl.ds(pl.multiple_of(c * fc, fc), fc)

    @pl.when((step >= chunks) & (step < 2 * chunks))
    def _():
        u = (act[c] - stats[:, 2:3]) * stats[:, 3:4]
        act[c] = u
        gain = vec4[1:2, :]
        m = (u * gain + vec4[2:3, :]).astype(bf16)
        mid_out[...] = m
        acc[...] += mm(m, w2s[c])
        gm = back[c].astype(f32)
        gmu = gm * u
        sums4[1:2, here] = row_sum(gmu)
        sums4[2:3, here] = row_sum(gm)
        total[...] += fold(gm * gain)
        total_u[...] += fold(gmu * gain)

    @pl.when(step == 2 * chunks)
    def _():
        stats[:, 4:5] = jnp.sum(total[...], axis=1, keepdims=True) * (1.0 / ff)
        stats[:, 5:6] = jnp.sum(total_u[...], axis=1, keepdims=True) * (1.0 / ff)
        output[...] = acc[...].astype(output.dtype)
        acc[...] = jnp.zeros_like(acc)

    @pl.when(step >= 2 * chunks)
    def _():
        e = back[c].astype(f32) * vec4[1:2, :]
        grad_act = stats[:, 3:4] * (e - stats[:, 4:5] - act[c] * stats[:, 5:6])
        gh = (grad_act * slope[c].astype(f32)).astype(bf16)
        grad_hidden[...] = gh
        sums4[0:1, here] = row_sum(gh.astype(f32))
        acc[...] += mm(gh, w1s[c], NT)

    @pl.when(step == 3 * chunks - 1)
    def _():
        def one(t, _):
            r = rows(t)
            grad_ffn_in = acc[r, :]
            unit_two = unit_b[r, :]
            unit_attn = grad_middle[r, :]
            gout = cot[r, :].astype(f32)
            sums[5:6, :] += row_sum(gout)
            sums[3:4, :] += row_sum(grad_ffn_in * unit_two)
            sums[4:5, :] += row_sum(grad_ffn_in)
            gmid = gout + norm_back(grad_ffn_in, unit_two, stats[r, 1:2], v(3))
            grad_middle[r, :] = gmid
            sums[1:2, :] += row_sum(gmid * unit_attn)
            sums[2:3, :] += row_sum(gmid)
            gp = norm_back(gmid, unit_attn, stats[r, 0:1], v(1)).astype(bf16)
            grad_proj[r, :] = gp
            sums[0:1, :] += row_sum(gp.astype(f32))
            return 0

        lax.fori_loop(0, strips, one, 0)
        d_out[...] = (mm(grad_proj[...], out_w[...], NT) * v(6)).astype(bf16)


def middle_pass(at, ho, tok, cot, out_w, w1, w2, vec, vec4, slot, last_part, earlier=(), early_back=(), fc=1024):
    _, n, d = ho.shape
    ff = w1.shape[1]
    chunks = ff // fc
    last = chunks - 1
    rows = whole((n, d))
    held = pl.BlockSpec(memory_space=pl.ANY)

    def once(shape, index):
        return pl.BlockSpec(shape, index, pipeline_mode=pl.Buffered(1))

    in_place = once((1, n, d), lambda t, at: (at[0], 0, 0))
    in_slot = once((1, n, d), lambda t, at: (slot, 0, 0))
    split = once((2, n, d // 2), lambda t, at: (0, slot, 0))
    kind = f32 if last_part else bf16
    return pl.pallas_call(
        middle_body,
        name="middle_pass",
        grid_spec=pltpu.PrefetchScalarGridSpec(
            num_scalar_prefetch=1,
            grid=(3 * chunks,),
            in_specs=[
                in_slot,
                in_place,
                in_place,
                whole(out_w.shape),
                held,
                held,
                whole(vec.shape),
                pl.BlockSpec((vec4.shape[0], fc), lambda t, at: (0, t % chunks)),
            ]
            + [held] * (len(early_back) + len(earlier)),
            out_specs=[
                in_place if last_part else rows,
                rows,
                whole((8, d)),
                whole((8, ff)),
                split,
                split,
                pl.BlockSpec((n, fc), lambda t, at: (slot, jnp.clip(t - chunks, 0, last))),
                pl.BlockSpec((n, fc), lambda t, at: (slot, jnp.clip(t - 2 * chunks, 0, last))),
                once((n, d), lambda t, at: (slot, 0)),
                in_slot,
            ],
            scratch_shapes=[
                pltpu.VMEM((chunks, n, fc), f32),
                pltpu.VMEM((chunks, n, fc), bf16),
                pltpu.VMEM((chunks, n, fc), bf16),
                pltpu.VMEM((n, d), f32),
                pltpu.VMEM((n, d), f32),
                pltpu.VMEM((n, LANES), f32),
                pltpu.VMEM((n, LANES), f32),
                pltpu.VMEM((n, LANES), f32),
                pltpu.VMEM((chunks, d, fc), bf16),
                pltpu.VMEM((chunks, fc, d), bf16),
                pltpu.SemaphoreType.DMA((3, chunks)),
            ],
        ),
        out_shape=[
            jax.ShapeDtypeStruct((2, n, d) if last_part else (n, d), kind),
            jax.ShapeDtypeStruct((n, d), f32),
            jax.ShapeDtypeStruct((8, d), f32),
            jax.ShapeDtypeStruct((8, ff), f32),
            jax.ShapeDtypeStruct((2, 2 * n, d // 2), bf16),
            jax.ShapeDtypeStruct((2, 2 * n, d // 2), bf16),
            jax.ShapeDtypeStruct((2 * n, ff), bf16),
            jax.ShapeDtypeStruct((2 * n, ff), bf16),
            jax.ShapeDtypeStruct((2 * n, d), bf16),
            jax.ShapeDtypeStruct((2, n, d), bf16),
        ],
        input_output_aliases={9 + len(early_back) + k: 4 + k for k in range(len(earlier))},
        compiler_params=params(62),
        cost_estimate=cost(
            8 * n * d * ff + 4 * n * d * d, 4 * d * ff + 2 * d * d + 4 * n * ff + 20 * n * d
        ),
    )(at, ho, tok, cot, out_w, w1, w2, vec, vec4, *early_back, *earlier)


def grad_mid_body(at, cot, w, out):
    out[...] = mm(cot[0], w[...], NT).astype(bf16)


def grad_mid(at, cot, w, fc=1024):
    _, n, d = cot.shape
    ff = w.shape[0]
    return pl.pallas_call(
        grad_mid_body,
        name="grad_mid",
        grid_spec=pltpu.PrefetchScalarGridSpec(
            num_scalar_prefetch=1,
            grid=(ff // fc,),
            in_specs=[
                pl.BlockSpec((1, n, d), lambda t, at: (at[0], 0, 0), pipeline_mode=pl.Buffered(1)),
                pl.BlockSpec((fc, d), lambda t, at: (t, 0)),
            ],
            out_specs=pl.BlockSpec((n, fc), lambda t, at: (0, t)),
        ),
        out_shape=jax.ShapeDtypeStruct((n, ff), bf16),
        compiler_params=params(),
        cost_estimate=cost(2 * n * d * ff, 2 * (n * d + d * ff + n * ff)),
    )(at, cot, w)


def first_back_body(at, even, odd, w, tok, grad_middle, gain, tokens_grad, sums):
    @pl.when(pl.program_id(0) == 0)
    def _():
        sums[...] = jnp.zeros_like(sums)

    d = w.shape[0]
    run = d // 4
    grad = None
    for part in range(3):
        for r in range(4):
            piece = (even, odd)[r % 2][part, :, (r // 2) * run : (r // 2 + 1) * run]
            here = r * run
            term = mm(piece, w[:, part * d + here : part * d + here + run], NT)
            grad = term if grad is None else grad + term
            if part != 1:
                at = 2 + part // 2
                sums[at : at + 1, here : here + run] += row_sum(piece.astype(f32))
    unit, inverse = norm_unit(tok[0].astype(f32))
    sums[0:1, :] += row_sum(grad * unit)
    sums[1:2, :] += row_sum(grad)
    whole_grad = grad_middle[...] + norm_back(grad, unit, inverse, gain[...])
    if len(tokens_grad.shape) == 3:
        tokens_grad[0] = whole_grad
    else:
        tokens_grad[...] = whole_grad.astype(tokens_grad.dtype)


def first_back(at, even, odd, w, tok, grad_middle, gain, slot, last_part, tb=256):
    d = w.shape[0]
    n = even.shape[1] // 2
    first = slot * (n // tb)
    half = pl.BlockSpec((3, tb, d // 2), lambda i, at: (0, first + i, 0))
    rows = pl.BlockSpec((tb, d), lambda i, at: (i, 0))
    in_place = pl.BlockSpec((1, tb, d), lambda i, at: (at[0], i, 0))
    return pl.pallas_call(
        first_back_body,
        name="first_back",
        grid_spec=pltpu.PrefetchScalarGridSpec(
            num_scalar_prefetch=1,
            grid=(n // tb,),
            in_specs=[half, half, whole(w.shape), in_place, rows, whole(gain.shape)],
            out_specs=[in_place if last_part else rows, whole((8, d))],
        ),
        out_shape=[
            jax.ShapeDtypeStruct((2, n, d), f32) if last_part else jax.ShapeDtypeStruct((n, d), bf16),
            jax.ShapeDtypeStruct((8, d), f32),
        ],
        compiler_params=params(30),
        cost_estimate=cost(6 * n * d * d, 6 * d * d + 16 * n * d),
    )(at, even, odd, w, tok, grad_middle, gain)


def after(x, *others):
    return lax.optimization_barrier((x,) + others)[0]


def emit(at_low, low, high, received, outs):
    send, keep = jnp.where(at_low, high, low), jnp.where(at_low, low, high)
    if received is None:
        outs[-1][0] = send.astype(bf16)
        outs[-1][1] = keep.astype(bf16)
    else:
        outs[-2][...] = (send + received[0].astype(f32)).astype(bf16)
        outs[-1][...] = (keep + received[1].astype(f32)).astype(bf16)


def tall_grad_body(received_too, tab, *refs):
    runs, halves = refs[:2], refs[2:4]
    a = jnp.concatenate([r[...] for r in runs], axis=1)
    total = mm(a, jnp.concatenate([h[0] for h in halves], axis=0), TN)
    wide = total.shape[1] // 2
    emit(tab[2] == 0, total[:, :wide], total[:, wide:], refs[4] if received_too else None, refs)


def tall_grad(tab, a, b, received=None):
    n, wide = a.shape
    d = b[0].shape[2]
    tall = wide // 16
    steps = 4

    def run(k):
        return pl.BlockSpec((n, tall), lambda i, t: (0, (2 * i + k) * 2 + t[0]))

    in_specs = [
        run(0),
        run(1),
        pl.BlockSpec((1, n // 2, d), lambda i, t: (t[2], 0, 0), pipeline_mode=pl.Buffered(1)),
        pl.BlockSpec((1, n // 2, d), lambda i, t: (0, 0, 0), pipeline_mode=pl.Buffered(1)),
    ]
    both = pl.BlockSpec((2, 2 * tall, d // 2), lambda i, t: (0, i, 0))
    one = pl.BlockSpec((2 * tall, d // 2), lambda i, t: (i, 0))
    args = [tab, a, a, *b]
    if received is not None:
        in_specs.append(both)
        args.append(received)
    shape = (wide // 2, d // 2)
    return pl.pallas_call(
        partial(tall_grad_body, received is not None),
        name="tall_grad",
        grid_spec=pltpu.PrefetchScalarGridSpec(
            num_scalar_prefetch=1,
            grid=(steps,),
            in_specs=in_specs,
            out_specs=both if received is None else [one, one],
        ),
        out_shape=jax.ShapeDtypeStruct((2,) + shape, bf16)
        if received is None
        else [jax.ShapeDtypeStruct(shape, bf16)] * 2,
        compiler_params=params(26),
        cost_estimate=cost(2 * n * wide * d // 2, n * wide + 2 * n * d + 8 * wide * d // 4),
    )(*args)


def flat_grad_body(counts, received_too, tab, *refs):
    step = pl.program_id(0)
    parts = len(counts)
    lhs, rhs = refs[:parts], refs[parts : 2 * parts]
    first = 0
    for k, count in enumerate(counts):

        @pl.when((step >= first) & (step < first + count))
        def _(k=k):
            b = rhs[k][0] if len(rhs[k].shape) == 3 else rhs[k][...]
            total = mm(lhs[k][0], b, TN)
            run = total.shape[0] // 8
            low, high = (
                jnp.concatenate([total[(2 * z + h) * run : (2 * z + h + 1) * run] for z in range(4)])
                for h in range(2)
            )
            emit(tab[1] == 0, low, high, refs[2 * parts] if received_too else None, refs)

        first += count


def flat_grad(tab, pairs, tn, received=None):
    counts = [b.shape[0] if b.ndim == 3 else b.shape[1] // tn for _, b in pairs]
    steps = sum(counts)
    n, wide = pairs[0][0].shape[1:]
    in_specs = [
        pl.BlockSpec((1, n, wide), lambda i, t: (t[0], 0, 0), pipeline_mode=pl.Buffered(1))
    ] * len(pairs)
    first = 0
    for (_, b), count in zip(pairs, counts):
        at = partial(lambda first, last, i: jnp.clip(i - first, 0, last), first, count - 1)
        if b.ndim == 3:
            in_specs.append(pl.BlockSpec((1, n, tn), lambda i, t, at=at: (at(i), 0, 0)))
        else:
            in_specs.append(pl.BlockSpec((n, tn), lambda i, t, at=at: (0, at(i))))
        first += count
    both = pl.BlockSpec((2, wide // 2, tn), lambda i, t: (0, 0, i))
    one = pl.BlockSpec((wide // 2, tn), lambda i, t: (0, i))
    args = [tab] + [a for a, _ in pairs] + [b for _, b in pairs]
    if received is not None:
        in_specs.append(both)
        args.append(received)
    shape = (wide // 2, steps * tn)
    weight = 16 if pairs[0][1].ndim == 3 else 1
    return pl.pallas_call(
        partial(flat_grad_body, counts, received is not None),
        name="flat_grad",
        grid_spec=pltpu.PrefetchScalarGridSpec(
            num_scalar_prefetch=1,
            grid=(steps,),
            in_specs=in_specs,
            out_specs=both if received is None else [one, one],
        ),
        out_shape=jax.ShapeDtypeStruct((2,) + shape, bf16)
        if received is None
        else [jax.ShapeDtypeStruct(shape, bf16)] * 2,
        compiler_params=params(30 if weight > 1 else 60),
        cost_estimate=cost(2 * n * wide * shape[1] // weight, (2 * n * (wide + shape[1]) + 8 * wide * shape[1]) // weight),
    )(*args)


def running_sums(lengths):
    count = lengths.shape[1]
    upto = jnp.arange(count)[:, None] >= jnp.arange(count)[None, :]
    return jnp.sum(jnp.where(upto[None], lengths[:, None, :], 0), axis=2).astype(jnp.int32)


def norm_forward(values, gain, shift):
    average = jnp.mean(values, axis=-1, keepdims=True)
    centered = values - average
    inverse = lax.rsqrt(jnp.mean(centered * centered, axis=-1, keepdims=True) + eps)
    normed = centered * inverse
    return (normed * gain + shift, normed, inverse)


def norm_backward(grad_y, normed, inverse, gain):
    scaled = grad_y * gain
    grad_in = inverse * (
        scaled
        - jnp.mean(scaled, axis=-1, keepdims=True)
        - normed * jnp.mean(scaled * normed, axis=-1, keepdims=True)
    )
    return (grad_in, jnp.sum(grad_y * normed, axis=(0, 1)), jnp.sum(grad_y, axis=(0, 1)))


def local_general(
    tokens,
    cotangent,
    doc_lengths,
    norm1_gain,
    norm1_shift,
    qkv_weight,
    query_bias,
    value_bias,
    head_scales,
    out_weight,
    out_bias,
    attn_gain,
    attn_shift,
    norm2_gain,
    norm2_shift,
    fc1_weight,
    fc1_bias,
    mid_gain,
    mid_shift,
    fc2_weight,
    fc2_bias,
):
    f32 = jnp.float32
    bf16 = jnp.bfloat16
    batch_size, local_len, model_width = tokens.shape
    head_count = head_scales.shape[0]
    head_dim = model_width // head_count
    score_scale = head_dim ** (-0.5)
    row_len = local_len * lax.axis_size("blk")
    row_first = lax.axis_index("blk") * local_len
    query_pos = row_first + jnp.arange(local_len, dtype=jnp.int32)
    doc_ends = running_sums(doc_lengths)
    starts = jnp.max(
        jnp.where(doc_ends[:, None, :] <= query_pos[None, :, None], doc_ends[:, None, :], 0), axis=2
    )
    lowest = jnp.min(starts[:, 0])
    query_last = row_first + local_len - 1
    inputs = tokens.astype(f32)
    attn_norm, unit_one, inverse_one = norm_forward(inputs, norm1_gain, norm1_shift)
    attn_in = attn_norm.astype(bf16)
    projected = jnp.dot(attn_in, qkv_weight, preferred_element_type=f32)
    queries = (
        (projected[..., :model_width] + query_bias)
        .astype(bf16)
        .reshape(batch_size, local_len, head_count, head_dim)
    )
    keys_low = projected[..., model_width : 2 * model_width].astype(bf16)
    values_low = (projected[..., 2 * model_width :] + value_bias).astype(bf16)

    def block_scores(key_piece, offset):
        key_len = key_piece.shape[1]
        keys_head = key_piece.reshape(batch_size, key_len, head_count, head_dim)
        raw_scores = (
            jnp.einsum("bqhd,bkhd->bhqk", queries, keys_head, preferred_element_type=f32)
            * score_scale
        )
        key_pos = offset + jnp.arange(key_len, dtype=jnp.int32)
        allowed = (key_pos[None, None, :] <= query_pos[None, :, None]) & (
            key_pos[None, None, :] >= starts[:, :, None]
        )
        return (jnp.where(allowed[:, None], raw_scores, masked_score), keys_head)

    def is_live(offset, key_len):
        return (offset <= query_last) & (offset + key_len - 1 >= lowest)

    def attend_slab(running, key_piece, value_piece, offset):
        key_len = key_piece.shape[1]

        def attend_compute(state):
            running_max, running_sum, weighted = state
            scores, keys_head = block_scores(key_piece, offset)
            new_max = jnp.maximum(running_max, jnp.max(scores, axis=3))
            rescale = jnp.exp(running_max - new_max)
            weights = jnp.exp(scores - new_max[..., None])
            values_head = value_piece.reshape(batch_size, key_len, head_count, head_dim)
            update = jnp.einsum(
                "bhqk,bkhd->bqhd", weights.astype(bf16), values_head, preferred_element_type=f32
            )
            rescale_t = jnp.transpose(rescale, (0, 2, 1))[..., None]
            return (
                new_max,
                running_sum * rescale + jnp.sum(weights, axis=3),
                weighted * rescale_t + update,
            )

        return lax.cond(is_live(offset, key_len), attend_compute, lambda state: state, running)

    start_state = (
        jnp.full((batch_size, head_count, local_len), masked_score, f32),
        jnp.zeros((batch_size, head_count, local_len), f32),
        jnp.zeros((batch_size, local_len, head_count, head_dim), f32),
    )
    key_piece = lax.all_gather(keys_low, "blk", axis=1, tiled=True)
    value_piece = lax.all_gather(values_low, "blk", axis=1, tiled=True)
    turns = key_piece.shape[1] // local_len

    def one_turn(index, state):
        begin = index * local_len
        key_slab = lax.dynamic_slice_in_dim(key_piece, begin, local_len, 1)
        value_slab = lax.dynamic_slice_in_dim(value_piece, begin, local_len, 1)
        return attend_slab(state, key_slab, value_slab, begin)

    running_max, running_sum, weighted = lax.fori_loop(0, turns, one_turn, start_state)
    attended = weighted / jnp.transpose(running_sum, (0, 2, 1))[..., None]
    log_total = running_max + jnp.log(running_sum)
    heads_out = (
        (attended * head_scales[:, None]).reshape(batch_size, local_len, model_width).astype(bf16)
    )
    projection = jnp.dot(heads_out, out_weight, preferred_element_type=f32) + out_bias
    branch, unit_attn, inverse_attn = norm_forward(projection, attn_gain, attn_shift)
    middle = inputs + branch
    ffn_norm, unit_two, inverse_two = norm_forward(middle, norm2_gain, norm2_shift)
    ffn_in = ffn_norm.astype(bf16)
    hidden = jnp.dot(ffn_in, fc1_weight, preferred_element_type=f32) + fc1_bias
    activated, gelu_grad = jax.vjp(partial(jax.nn.gelu, approximate=False), hidden)
    mid_norm, unit_mid, inverse_mid = norm_forward(activated, mid_gain, mid_shift)
    mid_out = mid_norm.astype(bf16)
    output = middle + jnp.dot(mid_out, fc2_weight, preferred_element_type=f32) + fc2_bias
    grad_output = cotangent.astype(f32)
    fc2_weight_grad = jnp.einsum("bcf,bcd->fd", mid_out, cotangent, preferred_element_type=f32)
    fc2_bias_grad = jnp.sum(grad_output, axis=(0, 1))
    grad_mid = jnp.einsum("bcd,fd->bcf", cotangent, fc2_weight, preferred_element_type=f32)
    grad_act, mid_gain_grad, mid_shift_grad = norm_backward(
        grad_mid, unit_mid, inverse_mid, mid_gain
    )
    grad_hidden = gelu_grad(grad_act)[0].astype(bf16)
    fc1_weight_grad = jnp.einsum("bcd,bcf->df", ffn_in, grad_hidden, preferred_element_type=f32)
    fc1_bias_grad = jnp.sum(grad_hidden.astype(f32), axis=(0, 1))
    grad_ffn_in = jnp.einsum("bcf,df->bcd", grad_hidden, fc1_weight, preferred_element_type=f32)
    grad_two, norm2_gain_grad, norm2_shift_grad = norm_backward(
        grad_ffn_in, unit_two, inverse_two, norm2_gain
    )
    grad_middle = grad_output + grad_two
    grad_proj_f, attn_gain_grad, attn_shift_grad = norm_backward(
        grad_middle, unit_attn, inverse_attn, attn_gain
    )
    grad_projection = grad_proj_f.astype(bf16)
    out_weight_grad = jnp.einsum(
        "bcd,bce->de", heads_out, grad_projection, preferred_element_type=f32
    )
    out_bias_grad = jnp.sum(grad_projection.astype(f32), axis=(0, 1))
    grad_heads = jnp.einsum(
        "bce,de->bcd", grad_projection, out_weight, preferred_element_type=f32
    ).reshape(batch_size, local_len, head_count, head_dim)
    head_scales_grad = jnp.sum(grad_heads * attended, axis=(0, 1, 3))
    grad_attended = (grad_heads * head_scales[:, None]).astype(bf16)
    row_dot = jnp.transpose(jnp.sum(grad_attended.astype(f32) * attended, axis=3), (0, 2, 1))

    def back_slab(running, key_piece, value_piece, offset):
        key_len = key_piece.shape[1]

        def back_compute(state):
            grad_queries, kv_buffer = state
            scores, keys_head = block_scores(key_piece, offset)
            attn_probs = jnp.exp(scores - log_total[..., None])
            values_head = value_piece.reshape(batch_size, key_len, head_count, head_dim)
            grad_probs = jnp.einsum(
                "bqhd,bkhd->bhqk", grad_attended, values_head, preferred_element_type=f32
            )
            grad_scores = (attn_probs * (grad_probs - row_dot[..., None])).astype(bf16)
            grad_queries = (
                grad_queries
                + jnp.einsum("bhqk,bkhd->bqhd", grad_scores, keys_head, preferred_element_type=f32)
                * score_scale
            )
            grad_keys = (
                jnp.einsum("bhqk,bqhd->bkhd", grad_scores, queries, preferred_element_type=f32)
                * score_scale
            )
            grad_values = jnp.einsum(
                "bhqk,bqhd->bkhd",
                attn_probs.astype(bf16),
                grad_attended,
                preferred_element_type=f32,
            )
            addition = jnp.concatenate(
                [
                    grad_keys.reshape(batch_size, key_len, model_width),
                    grad_values.reshape(batch_size, key_len, model_width),
                ],
                axis=2,
            )
            previous = lax.dynamic_slice_in_dim(kv_buffer, offset, key_len, 1)
            return (
                grad_queries,
                lax.dynamic_update_slice_in_dim(kv_buffer, previous + addition, offset, 1),
            )

        return lax.cond(is_live(offset, key_len), back_compute, lambda state: state, running)

    back_state = (
        jnp.zeros((batch_size, local_len, head_count, head_dim), f32),
        jnp.zeros((batch_size, row_len, 2 * model_width), f32),
    )
    attend_key_piece = lax.all_gather(keys_low, "blk", axis=1, tiled=True)
    attend_value_piece = lax.all_gather(values_low, "blk", axis=1, tiled=True)
    turns = attend_key_piece.shape[1] // local_len

    def one_turn(index, state):
        begin = index * local_len
        key_slab = lax.dynamic_slice_in_dim(attend_key_piece, begin, local_len, 1)
        value_slab = lax.dynamic_slice_in_dim(attend_value_piece, begin, local_len, 1)
        return back_slab(state, key_slab, value_slab, begin)

    grad_queries, kv_buffer = lax.fori_loop(0, turns, one_turn, back_state)
    grad_kv = lax.psum_scatter(
        kv_buffer.astype(jnp.bfloat16), "blk", scatter_dimension=1, tiled=True
    ).astype(jnp.float32)
    grad_qkv = jnp.concatenate(
        [grad_queries.reshape(batch_size, local_len, model_width), grad_kv], axis=2
    ).astype(bf16)
    qkv_weight_grad = jnp.einsum("bcd,bce->de", attn_in, grad_qkv, preferred_element_type=f32)
    query_bias_grad = jnp.sum(grad_qkv[..., :model_width].astype(f32), axis=(0, 1))
    value_bias_grad = jnp.sum(grad_qkv[..., 2 * model_width :].astype(f32), axis=(0, 1))
    grad_attn_in = jnp.einsum("bce,de->bcd", grad_qkv, qkv_weight, preferred_element_type=f32)
    grad_one, norm1_gain_grad, norm1_shift_grad = norm_backward(
        grad_attn_in, unit_one, inverse_one, norm1_gain
    )
    tokens_grad = grad_middle + grad_one
    matrix_grads = (qkv_weight_grad, out_weight_grad, fc1_weight_grad, fc2_weight_grad)
    reduced = (
        lax.psum_scatter(
            matrix_grads[0].astype(jnp.bfloat16), "dp", scatter_dimension=0, tiled=True
        ).astype(jnp.float32),
        lax.psum_scatter(
            matrix_grads[1].astype(jnp.bfloat16), "dp", scatter_dimension=0, tiled=True
        ).astype(jnp.float32),
        lax.psum_scatter(
            matrix_grads[2].astype(jnp.bfloat16), "dp", scatter_dimension=0, tiled=True
        ).astype(jnp.float32),
        lax.psum_scatter(
            matrix_grads[3].astype(jnp.bfloat16), "dp", scatter_dimension=0, tiled=True
        ).astype(jnp.float32),
    )
    reduced = (
        lax.psum_scatter(
            reduced[0].astype(jnp.bfloat16), "blk", scatter_dimension=1, tiled=True
        ).astype(jnp.float32),
        lax.psum_scatter(
            reduced[1].astype(jnp.bfloat16), "blk", scatter_dimension=1, tiled=True
        ).astype(jnp.float32),
        lax.psum_scatter(
            reduced[2].astype(jnp.bfloat16), "blk", scatter_dimension=1, tiled=True
        ).astype(jnp.float32),
        lax.psum_scatter(
            reduced[3].astype(jnp.bfloat16), "blk", scatter_dimension=1, tiled=True
        ).astype(jnp.float32),
    )
    small_sums = lax.psum(
        (
            norm1_gain_grad,
            norm1_shift_grad,
            query_bias_grad,
            value_bias_grad,
            head_scales_grad,
            out_bias_grad,
            attn_gain_grad,
            attn_shift_grad,
            norm2_gain_grad,
            norm2_shift_grad,
            fc1_bias_grad,
            mid_gain_grad,
            mid_shift_grad,
            fc2_bias_grad,
        ),
        ("dp", "blk"),
    )
    return (
        output,
        tokens_grad,
        small_sums[0],
        small_sums[1],
        reduced[0],
        small_sums[2],
        small_sums[3],
        small_sums[4],
        reduced[1],
        small_sums[5],
        small_sums[6],
        small_sums[7],
        small_sums[8],
        small_sums[9],
        reduced[2],
        small_sums[10],
        small_sums[11],
        small_sums[12],
        reduced[3],
        small_sums[13],
    )


swap = ((0, 1), (1, 0))


def exchange(x):
    return lax.ppermute(x, "blk", swap)


def flip(x, bit):
    return lax.ppermute(x, "dp", [(i, i ^ bit) for i in range(16)])


def local_rows(
    tokens,
    cotangent,
    doc_lengths,
    norm1_gain,
    norm1_shift,
    qkv_weight,
    query_bias,
    value_bias,
    head_scales,
    out_weight,
    out_bias,
    attn_gain,
    attn_shift,
    norm2_gain,
    norm2_shift,
    fc1_weight,
    fc1_bias,
    mid_gain,
    mid_shift,
    fc2_weight,
    fc2_bias,
):
    _, half_len, d = tokens.shape
    ff = fc1_weight.shape[1]
    heads = head_scales.shape[0]
    head_dim = d // heads
    scale = head_dim**-0.5
    n = 2 * half_len
    b = lax.axis_index("blk").astype(jnp.int32)
    dp = lax.axis_index("dp").astype(jnp.int32)
    core, x, z, y = dp % 2, (dp // 2) % 2, dp // 4, b

    tok_in = exchange(lax.dynamic_slice_in_dim(tokens, 1 - b, 1, 0))
    cot_in = exchange(lax.dynamic_slice_in_dim(cotangent, 1 - b, 1, 0))
    kept_at = b[None]
    sent_at = jnp.zeros((1,), jnp.int32)

    def line(v):
        return v.reshape(1, -1)

    qkv_bias = jnp.concatenate([query_bias, jnp.zeros_like(query_bias), value_bias])
    first_args = (line(norm1_gain), line(norm1_shift), qkv_weight, line(qkv_bias), scale)
    early = project_qkv(kept_at, tokens, *first_args, 0, n)

    def later(v):
        return after(v, early[0])

    lengths = lax.dynamic_slice_in_dim(later(doc_lengths), b, 1, 0)
    ends = running_sums(lengths)[0]
    firsts = (half_len // 2) * jnp.arange(4, dtype=jnp.int32)
    starts = jnp.max(jnp.where(ends[None, :] <= firsts[:, None], ends[None, :], 0), axis=1)
    allowed = (firsts[None, :] >= starts[:, None]).astype(jnp.int32)
    tab = jnp.concatenate([b[None], allowed.reshape(16)])
    theirs = jnp.stack([1 - core, x, y])
    mine = jnp.stack([core, x, y])
    head_scales = later(head_scales)
    scale_row = jnp.broadcast_to(head_scales[:, None], (heads, head_dim)).reshape(1, d)
    vec = jnp.stack(
        [later(out_bias), attn_gain, attn_shift, norm2_gain, norm2_shift, fc2_bias, scale_row[0], out_bias]
    )
    fc1_bias = later(fc1_bias)
    vec4 = jnp.stack([fc1_bias, mid_gain, mid_shift, fc1_bias])

    early_back = grad_mid(later(kept_at), cotangent, fc2_weight)
    made = after(sent_at, early_back, tab, theirs, mine, scale_row, vec, vec4)
    attn_in, qkv = project_qkv(made, tok_in, *first_args, 1, n, early)
    qkv = qkv.reshape(2, half_len, 3 * d)
    heads_out, logs = attend(tab, qkv, scale_row)

    weights = (out_weight, fc1_weight, fc2_weight, vec, vec4)
    out_sent, mid_sent, *more = middle_pass(sent_at, heads_out, tok_in, cot_in, *weights, 1, False)
    sums, sums4, *earlier = more
    out_back = exchange(out_sent)
    output, mid_kept, *more = middle_pass(
        kept_at, heads_out, tokens, cotangent, *weights, 0, True, earlier, (early_back,)
    )
    sums = sums + more[0]
    sums4 = sums4 + more[1]
    ffn_in, heads_in, mid_out, grad_hidden, grad_proj, d_out = more[2:]

    def fill(kept, back):
        return lax.dynamic_update_slice_in_dim(kept, back.astype(f32)[None], 1 - b, 0)

    def near_z(total):
        total = total.astype(bf16).reshape((2, 2) + total.shape[1:])
        odd = z % 2
        return (
            lax.dynamic_index_in_dim(total, 1 - odd, 1, keepdims=False),
            lax.dynamic_index_in_dim(total, odd, 1, keepdims=False),
        )

    def far_z(total):
        total = total.astype(bf16)
        high = z // 2
        return (
            lax.dynamic_index_in_dim(total, 1 - high, 0, keepdims=False),
            lax.dynamic_index_in_dim(total, high, 0, keepdims=False),
        )

    def add_z(move, send, keep):
        return keep.astype(f32) + flip(send, move).astype(f32)

    def held(parts, *others):
        return parts[0], after(parts[1], *others)

    def rows_by_x(total):
        total = total.astype(bf16).reshape(4, 2, -1, total.shape[1])
        return (
            lax.dynamic_index_in_dim(total, 1 - x, 1, keepdims=False),
            lax.dynamic_index_in_dim(total, x, 1, keepdims=False),
        )

    def columns_by_y(total, *cuts):
        total = total.astype(bf16).reshape(4, -1, total.shape[1])
        out = []
        for at in (1 - y, y):
            groups = []
            for first, last in zip((0,) + cuts, cuts + (total.shape[2],)):
                width = (last - first) // 2
                groups.append(lax.dynamic_slice_in_dim(total, first + at * width, width, 2))
            out.append(jnp.concatenate(groups, axis=2) if cuts else groups[0])
        return out

    def add_x(send, keep):
        return keep.astype(f32) + flip(send, 2).astype(f32)

    def add_y(send, keep):
        return keep.astype(f32) + exchange(send).astype(f32)

    cots = (cotangent, cot_in)
    output = fill(output, out_back)
    wide_pairs = [(after(ffn_in, output), grad_hidden), (heads_in, grad_proj)]
    wide_theirs = flat_grad(theirs, wide_pairs, d)
    fc2_theirs = tall_grad(theirs, after(mid_out, wide_theirs), cots)
    wide_pairs = [(after(ffn_in, fc2_theirs), grad_hidden), (heads_in, grad_proj)]
    wide_parts = flat_grad(mine, wide_pairs, d, flip(wide_theirs, 1))
    fc2_parts = tall_grad(mine, after(mid_out, *wide_parts), cots, flip(fc2_theirs, 1))
    d_out = after(d_out, *fc2_parts)
    back_args = (1.0 / scale_row, logs, scale)
    even, dots_even = attend_back(tab, qkv, heads_out, d_out, *back_args, 0)
    even = even.reshape(3, n, d // 2)
    even_theirs = flat_grad(theirs, [(after(attn_in, even), even)], d // 2)
    d_out = after(d_out, even_theirs)
    odd, dots_odd = attend_back(tab, qkv, heads_out, d_out, *back_args, 1)
    odd = odd.reshape(3, n, d // 2)
    wide_parts = columns_by_y(add_x(*held(wide_parts, odd)), ff)
    fc2_parts = rows_by_x(add_y(*held(fc2_parts, odd)))
    odd_theirs = flat_grad(theirs, [(after(attn_in, *wide_parts, *fc2_parts), odd)], d // 2)
    even_parts = flat_grad(mine, [(after(attn_in, odd_theirs), even)], d // 2, flip(even_theirs, 1))
    grad_sent, sums_sent = first_back(
        sent_at, after(even, *even_parts), odd, qkv_weight, tok_in, mid_sent, line(norm1_gain), 1, False
    )
    grad_back = exchange(grad_sent)
    fc2_parts = near_z(add_x(*held(fc2_parts, grad_sent)))
    odd_parts = flat_grad(
        mine, [(after(attn_in, grad_sent, *fc2_parts), odd)], d // 2, flip(odd_theirs, 1)
    )
    wide_parts = near_z(add_y(*held(wide_parts, *odd_parts)))
    tokens_grad, sums_kept = first_back(
        kept_at, after(even, *wide_parts), odd, qkv_weight, tokens, mid_kept, line(norm1_gain), 0, True
    )
    dots = jnp.stack([dots_even[:, 0].reshape(2, 4, head_dim), dots_odd[:, 0].reshape(2, 4, head_dim)], axis=1)
    head_scales_grad = jnp.sum(dots, axis=3).reshape(heads) / head_scales
    head_scales_grad = jnp.pad(head_scales_grad, (0, d - heads))
    total = jnp.concatenate(
        [
            (sums_sent + sums_kept)[:4],
            head_scales_grad[None],
            sums[:6],
            sums4.reshape(8 * ff // d, d)[: 3 * ff // d],
        ]
    )
    fc2_parts = far_z(add_z(4, *held(fc2_parts, tokens_grad)))
    even_parts = columns_by_y(add_x(*held(even_parts, tokens_grad)))
    wide_parts = far_z(add_z(4, *held(wide_parts, tokens_grad)))
    tokens_grad = fill(tokens_grad, grad_back)
    odd_parts = columns_by_y(add_x(*odd_parts))
    even_parts = near_z(add_y(*even_parts))
    odd_parts = near_z(add_y(*odd_parts))
    total = total + (partial(flip, bit=1))(total)
    total = total + (partial(flip, bit=4))(total)
    total = total + (partial(flip, bit=8))(total)
    total = after(total, *odd_parts)
    total = total + (partial(flip, bit=2))(total)
    total = total + (exchange)(total)
    even_parts = far_z(add_z(4, *even_parts))
    odd_parts = far_z(add_z(4, *odd_parts))
    fc2_weight_grad = add_z(8, *fc2_parts)
    wide_grad = add_z(8, *wide_parts)
    fc1_weight_grad, out_weight_grad = wide_grad[:, : ff // 2], wide_grad[:, ff // 2 :]
    even_grad, odd_grad = (add_z(8, *parts) for parts in (even_parts, odd_parts))
    first_sums, sums, sums4 = total[:5], total[5:11], total[11:].reshape(3, ff)
    run = d // 4
    qkv_weight_grad = jnp.stack(
        [even_grad.reshape(-1, 3, run), odd_grad.reshape(-1, 3, run)], axis=2
    ).reshape(-1, 6 * run)
    return (
        output,
        tokens_grad,
        first_sums[0],
        first_sums[1],
        qkv_weight_grad,
        first_sums[2],
        first_sums[3],
        first_sums[4, :heads],
        out_weight_grad,
        sums[0],
        sums[1],
        sums[2],
        sums[3],
        sums[4],
        fc1_weight_grad,
        sums4[0],
        sums4[1],
        sums4[2],
        fc2_weight_grad,
        sums[5],
    )


def solution(mesh):
    rows_fit = dict(mesh.shape) == {"dp": 16, "blk": 2}
    local = local_rows if rows_fit else local_general
    placed = (
        P("dp", "blk", None),
        P("dp", "blk", None),
        P("dp", None),
        P(),
        P(),
        P(),
        P(),
        P(),
        P(),
        P(),
        P(),
        P(),
        P(),
        P(),
        P(),
        P(),
        P(),
        P(),
        P(),
        P(),
        P(),
    )
    return jax.shard_map(
        local,
        mesh=mesh,
        in_specs=placed,
        out_specs=(
            P("dp", "blk", None),
            P("dp", "blk", None),
            P(),
            P(),
            P("dp", "blk"),
            P(),
            P(),
            P(),
            P("dp", "blk"),
            P(),
            P(),
            P(),
            P(),
            P(),
            P("dp", "blk"),
            P(),
            P(),
            P(),
            P("dp", "blk"),
            P(),
        ),
        check_vma=False,
    )
```
